32 devices in a mesh: dp: 8 (over y, x, core), seq: 4 (over z).
Axes of the slice: x: 2, y: 2, z: 4, core: 2. Of those that a mesh axis runs over, the one named last changes fastest.
Arguments:
- hidden: bfloat16 [16, 1024, 768], P('dp', 'seq'), may hold values from -6 to 6
- cotangent: bfloat16 [16, 1024, 768], P('dp', 'seq'), may hold values from -6 to 6
- w_proj: bfloat16 [768, 1920], P(('dp', 'seq')), may hold values from -0.3125 to 0.3125
- w_depth: bfloat16 [768, 9], P(('dp', 'seq')), may hold values from -2 to 2
- w_kernel: bfloat16 [384, 54], replicated, may hold values from -0.3125 to 0.3125
- b_kernel: bfloat16 [54], replicated, may hold values from -3 to 3
- w_out: bfloat16 [768, 768], P(('dp', 'seq')), may hold values from -0.4375 to 0.4375
- w_up: bfloat16 [768, 1536], P(('dp', 'seq')), may hold values from -0.3125 to 0.3125
- w_down: bfloat16 [3072, 384], P(('dp', 'seq')), may hold values from -0.21875 to 0.21875
- b_proj: bfloat16 [1536], P(('dp', 'seq')), may hold values from -3 to 3
- b_up: bfloat16 [3072], P(('dp', 'seq')), may hold values from -3 to 3
- b_out: bfloat16 [768], P(('dp', 'seq')), may hold values from -3 to 3
- ln1_gain: bfloat16 [768], P(('dp', 'seq')), may hold values from 0.5 to 1.5
- ln1_bias: bfloat16 [768], P(('dp', 'seq')), may hold values from -3 to 3
- b_down: bfloat16 [768], P(('dp', 'seq')), may hold values from -3 to 3
- ln2_gain: bfloat16 [768], P(('dp', 'seq')), may hold values from 0.5 to 1.5
- ln2_bias: bfloat16 [768], P(('dp', 'seq')), may hold values from -3 to 3
Outputs:
- output: bfloat16 [16, 1024, 768], P('dp', 'seq')
- grad_hidden: float32 [16, 1024, 768], P('dp', 'seq')
- grad_w_proj: float32 [768, 1920], P(('dp', 'seq'))
- grad_w_depth: float32 [768, 9], P(('dp', 'seq'))
- grad_w_kernel: float32 [384, 54], replicated
- grad_b_kernel: float32 [54], replicated
- grad_w_out: float32 [768, 768], P(('dp', 'seq'))
- grad_w_up: float32 [768, 1536], P(('dp', 'seq'))
- grad_w_down: float32 [3072, 384], P(('dp', 'seq'))
- grad_b_proj: float32 [1536], P(('dp', 'seq'))
- grad_b_up: float32 [3072], P(('dp', 'seq'))
- grad_b_out: float32 [768], P(('dp', 'seq'))
- grad_ln1_gain: float32 [768], P(('dp', 'seq'))
- grad_ln1_bias: float32 [768], P(('dp', 'seq'))
- grad_b_down: float32 [768], P(('dp', 'seq'))
- grad_ln2_gain: float32 [768], P(('dp', 'seq'))
- grad_ln2_bias: float32 [768], P(('dp', 'seq'))
The draws below stay inside these ranges and needn't reach their ends.
All inputs are finite; a program needn't handle non-finite values.
Results may differ from the reference program's by a relative error of at most 0.014.
The reference program's roundings to bfloat16 on the way count: a program that leaves them out, or rounds other values in their place, can miss the bound.
Values may be sent and summed in bfloat16 or wider, within the bound.
A program may use at most 256 MiB of HBM per device.

```python
from functools import partial
import jax
import jax.numpy as jnp
from jax import lax

D = 768
HEADS = 6
HEAD = 64
KERNEL = 9
FF = 3072
GROUPS = 2
CHAN = 384
BATCH = 16
LENGTH = 1024


def steps_of(own_key, shape, shards, smallest, high):
    def one(axis_at, blocks):
        heights = jax.random.uniform(jax.random.fold_in(jax.random.fold_in(own_key, 6), axis_at), (blocks,), jnp.float32, smallest / len(shards), high / len(shards))
        return jnp.repeat(jnp.exp(heights), shape[axis_at] // blocks).reshape((-1,) + (1,) * (len(shape) - axis_at - 1))

    factor_of = one(*shards[0])
    for cut in shards[1:]:
        factor_of = factor_of * one(*cut)
    return factor_of


def scatter_about(key, shape, scale, bound, split=(), kind=jnp.bfloat16):
    entries = scale * jax.random.normal(key, shape, jnp.float32)
    if split:
        entries = entries * steps_of(key, shape, split, -0.22, 0.18)
    return jnp.clip(entries, -bound, bound).astype(kind)


def setup_inputs(seed: int = 0) -> dict:
    splits = jax.random.split(jax.random.key(seed), 18)
    return {
        "hidden": scatter_about(splits[0], (BATCH, LENGTH, D), 1.0, 6.0, ((0, 8), (1, 4))),
        "cotangent": scatter_about(splits[1], (BATCH, LENGTH, D), 1.0, 6.0, ((0, 8), (1, 4))),
        "w_proj": scatter_about(splits[2], (D, 5 * CHAN), (D // 2) ** -0.5, 0.3125, ((0, 32),)),
        "w_depth": scatter_about(splits[3], (D, KERNEL), KERNEL ** -0.5, 2.0, ((0, 32),)),
        "w_kernel": scatter_about(splits[4], (CHAN, HEADS * KERNEL), CHAN ** -0.5, 0.3125),
        "b_kernel": scatter_about(splits[5], (HEADS * KERNEL,), 0.5, 3.0),
        "w_out": scatter_about(splits[6], (D, D), (D // 4) ** -0.5, 0.4375, ((0, 32),)),
        "w_up": scatter_about(splits[7], (D, FF // GROUPS), (D // GROUPS) ** -0.5, 0.3125, ((0, 32),)),
        "w_down": scatter_about(splits[8], (FF, D // GROUPS), (FF // (2 * GROUPS)) ** -0.5, 0.21875, ((0, 32),)),
        "b_proj": scatter_about(splits[9], (4 * CHAN,), 0.5, 3.0, ((0, 32),)),
        "b_up": scatter_about(splits[10], (FF,), 0.5, 3.0, ((0, 32),)),
        "b_out": scatter_about(splits[11], (D,), 0.5, 3.0, ((0, 32),)),
        "ln1_gain": jnp.clip(1.0 + 0.1 * jax.random.normal(splits[12], (D,), jnp.float32), 0.5, 1.5).astype(jnp.bfloat16),
        "ln1_bias": scatter_about(splits[13], (D,), 0.5, 3.0, ((0, 32),)),
        "b_down": scatter_about(splits[14], (D,), 0.5, 3.0, ((0, 32),)),
        "ln2_gain": jnp.clip(1.0 + 0.1 * jax.random.normal(splits[15], (D,), jnp.float32), 0.5, 1.5).astype(jnp.bfloat16),
        "ln2_bias": scatter_about(splits[16], (D,), 0.5, 3.0, ((0, 32),)),
    }


HIGH = lax.Precision.HIGHEST
norm_eps = 1e-12

@jax.custom_vjp
def low(v):
    return lax.optimization_barrier(v.astype(jnp.bfloat16)).astype(jnp.float32)

@jax.custom_vjp
def low_back(v):
    return v

def low_keep(v):
    return (low(v), None)

def low_pass(kept, grad):
    return (grad,)

def back_keep(v):
    return (v, None)

def back_low(kept, grad):
    return (low(grad),)
low.defvjp(low_keep, low_pass)
low_back.defvjp(back_keep, back_low)

def matmul(left, right):
    return jnp.dot(left, right, precision=HIGH, preferred_element_type=jnp.float32)

def layer_norm(inputs, gain_vec, shift_vec):
    centre = inputs - lax.optimization_barrier(jnp.mean(inputs, axis=-1, keepdims=True))
    variance = lax.optimization_barrier(jnp.mean(centre * centre, axis=-1, keepdims=True))
    return centre * lax.rsqrt(variance + norm_eps) * gain_vec + shift_vec

def attend_block(query_block, key_rows, value_rows):
    scores = low_back(jnp.einsum('ihe,jhe->hij', query_block, key_rows, precision=HIGH) * HEAD ** (-0.5))
    norm_log = jax.nn.logsumexp(scores, axis=-1, keepdims=True)
    weights_low = low(jnp.exp(scores - norm_log))
    return jnp.einsum('hij,jhe->ihe', weights_low, value_rows, precision=HIGH)

def one_sequence(param_set, tokens):
    w_proj, w_depth, w_kernel, b_kernel, w_out, w_up, w_down, b_proj, b_up, b_out, ln1_gain, ln1_bias, b_down, ln2_gain, ln2_bias = param_set
    half_kernel = KERNEL // 2
    projected = matmul(tokens, w_proj[:, :4 * CHAN])
    queries = low_back(low(projected[:, :CHAN] + b_proj[:CHAN]))
    key_rows = low_back(low(projected[:, CHAN:2 * CHAN]))
    value_rows = low_back(low(projected[:, 2 * CHAN:3 * CHAN] + b_proj[CHAN:2 * CHAN]))
    conv_input = low_back(projected[:, 3 * CHAN:]) + b_proj[2 * CHAN:3 * CHAN]
    padded = jnp.pad(tokens, ((half_kernel, half_kernel), (0, 0)))
    depth_sum = jnp.zeros((LENGTH, D), jnp.float32)
    for tap_index in range(KERNEL):
        depth_sum = depth_sum + padded[tap_index:tap_index + LENGTH] * w_depth[:, tap_index]
    spread = low(depth_sum)
    key_conv = low_back(matmul(spread, w_proj[:, 4 * CHAN:])) + b_proj[3 * CHAN:]
    mixed_key = low(key_conv * queries)
    logits = low_back(matmul(mixed_key, w_kernel)) + b_kernel
    tap_weights = jax.nn.softmax(logits.reshape(LENGTH, HEADS, KERNEL), axis=-1)
    conv_pad = jnp.pad(conv_input, ((half_kernel, half_kernel), (0, 0))).reshape(LENGTH + 2 * half_kernel, HEADS, HEAD)
    conv_mix = jnp.zeros((LENGTH, HEADS, HEAD), jnp.float32)
    for tap_index in range(KERNEL):
        conv_mix = conv_mix + tap_weights[:, :, tap_index, None] * conv_pad[tap_index:tap_index + LENGTH]
    block_rows = min(512, LENGTH)
    query_blocks = queries.reshape(LENGTH // block_rows, block_rows, HEADS, HEAD)
    keys_three = key_rows.reshape(LENGTH, HEADS, HEAD)
    values_three = value_rows.reshape(LENGTH, HEADS, HEAD)

    def block_step(query_block):
        return attend_block(query_block, keys_three, values_three)
    context = lax.map(jax.checkpoint(block_step), query_blocks).reshape(LENGTH, CHAN)
    context = low_back(low(context))
    joined = jnp.concatenate([context, low(conv_mix.reshape(LENGTH, CHAN))], axis=-1)
    after_mix = low_back(matmul(joined, w_out)) + b_out + tokens
    first_norm = layer_norm(after_mix, ln1_gain, ln1_bias)
    group_in = low(first_norm).reshape(LENGTH, GROUPS, D // GROUPS)
    up_sum = jnp.einsum('ngd,gdf->ngf', group_in, w_up.reshape(GROUPS, D // GROUPS, FF // GROUPS), precision=HIGH)
    pre_act = low_back(up_sum.reshape(LENGTH, FF)) + b_up
    activated = low(jax.nn.gelu(pre_act, approximate=False))
    down_sum = jnp.einsum('ngf,gfd->ngd', activated.reshape(LENGTH, GROUPS, FF // GROUPS), w_down.reshape(GROUPS, FF // GROUPS, D // GROUPS), precision=HIGH)
    summed = low_back(down_sum.reshape(LENGTH, D)) + b_down + first_norm
    return layer_norm(summed, ln2_gain, ln2_bias)

def reference(hidden, cotangent, w_proj, w_depth, w_kernel, b_kernel, w_out, w_up, w_down, b_proj, b_up, b_out, ln1_gain, ln1_bias, b_down, ln2_gain, ln2_bias):
    param_set = tuple((array_in.astype(jnp.float32) for array_in in (w_proj, w_depth, w_kernel, b_kernel, w_out, w_up, w_down, b_proj, b_up, b_out, ln1_gain, ln1_bias, b_down, ln2_gain, ln2_bias)))

    def forward(tokens_all, params_in):
        return lax.map(partial(one_sequence, params_in), tokens_all)
    output, pullback = jax.vjp(forward, hidden.astype(jnp.float32), param_set)
    grad_hidden, grads = pullback(cotangent.astype(jnp.float32))
    return (output.astype(jnp.bfloat16), grad_hidden, grads[0], grads[1], grads[2], grads[3], grads[4], grads[5], grads[6], grads[7], grads[8], grads[9], grads[10], grads[11], grads[12], grads[13], grads[14])
```

```python
from functools import partial

import jax
import jax.numpy as jnp
from jax import lax
from jax.experimental import pallas as pl
from jax.experimental.pallas import tpu as pltpu
from jax.sharding import PartitionSpec as P

MESH = pl.DeviceIdType.MESH


class Grid:
    def __init__(self, dp, seq):
        self.C = 2 if dp % 2 == 0 else 1
        rest = dp // self.C
        y = 1
        while (2 * y) * (2 * y) <= rest and rest % (2 * y) == 0:
            y *= 2
        self.Y, self.X, self.Z = y, rest // y, seq
        d = lax.axis_index("dp")
        self.z = lax.axis_index("seq")
        self.c = d % self.C
        self.x = (d // self.C) % self.X
        self.y = d // (self.C * self.X)
        self.dp = d
    def size(self, ax):
        return getattr(self, ax.upper())
    def at(self, **off):
        g = {a: (getattr(self, a) + off.get(a, 0)) % self.size(a) if off.get(a, 0) else getattr(self, a) for a in "yxcz"}
        return g
    def dpof(self, g):
        return (g["y"] * self.X + g["x"]) * self.C + g["c"]
    def dev(self, **off):
        g = self.at(**off)
        return (self.dpof(g), g["z"])


def peers(grid):
    out = []
    for a in "zxyc":
        for o in range(1, grid.size(a)):
            out.append(grid.dev(**{a: o}))
    return out


def entry_barrier(grid):
    b = pltpu.get_barrier_semaphore()
    ps = peers(grid)
    for p in ps:
        pl.semaphore_signal(b, inc=1, device_id=p, device_id_type=MESH)
    pl.semaphore_wait(b, len(ps))


class Gather:
    def __init__(self, grid, src, buf, order, ssem, rsem, lsem):
        self.g, self.src, self.buf, self.ssem, self.rsem, self.lsem = grid, src, buf, ssem, rsem, lsem
        self.u, self.v = order[1], order[2]
        self.ns = 0
        self.sent = []
        self.recv = {}
        g = grid
        k = 0
        self.slot = {}
        for o in range(1, g.Z):
            self.slot["z", o] = k; k += 1
        for o in range(1, g.size(self.u)):
            self.slot["u", o] = k; k += 1
        for o in range(1, g.size(self.v)):
            for q in range(g.size(self.u)):
                self.slot["v", o, q] = k; k += 1
        for o in range(1, g.C):
            for q in range(g.size(self.u)):
                for w in range(g.size(self.v)):
                    self.slot["c", o, q, w] = k; k += 1
        self.count = k

    @staticmethod
    def slots(Z, X, Y, C):
        return (Z - 1) + X * Y * C - 1

    def block(self, uo, vo, co=0):
        g = self.g.at(**{self.u: uo, self.v: vo, "c": co})
        return self.buf.at[pl.ds(self.g.dpof(g) * self.g.Z, self.g.Z)]

    def _send(self, src, dst, slot, dev):
        k = self.slot[slot]
        cp = pltpu.make_async_remote_copy(src_ref=src, dst_ref=dst, send_sem=self.ssem.at[k], recv_sem=self.rsem.at[k],
                                          device_id=dev, device_id_type=MESH)
        cp.start()
        self.sent.append(cp)

    def start(self):
        g = self.g
        me = g.dp * g.Z + g.z
        self.local = pltpu.make_async_copy(self.src, self.buf.at[me], self.lsem)
        self.local.start()
        for o in range(1, g.Z):
            self._send(self.src, self.buf.at[me], ("z", o), g.dev(z=o))

    def _wait_recv(self, ref, slot):
        k = self.slot[slot]
        pltpu.make_async_remote_copy(src_ref=ref, dst_ref=ref, send_sem=self.ssem.at[k], recv_sem=self.rsem.at[k],
                                     device_id=self.g.dev(z=1) if self.g.Z > 1 else self.g.dev(c=1), device_id_type=MESH).wait_recv()

    def step1(self):
        g = self.g
        self.local.wait()
        for o in range(1, g.Z):
            self._wait_recv(self.buf.at[g.dp * g.Z + (g.z + g.Z - o) % g.Z], ("z", o))
        blk = self.block(0, 0)
        for o in range(1, g.size(self.u)):
            self._send(blk, blk, ("u", o), g.dev(**{self.u: o}))
        for o in range(1, g.size(self.v)):
            self._send(blk, blk, ("v", o, 0), g.dev(**{self.v: o}))
        for o in range(1, g.C):
            self._send(blk, blk, ("c", o, 0, 0), g.dev(c=o))

    def step2(self):
        g = self.g
        U, V = g.size(self.u), g.size(self.v)
        for q in range(1, U):
            blk = self.block(U - q, 0)
            self._wait_recv(blk, ("u", q))
            for o in range(1, V):
                self._send(blk, blk, ("v", o, q), g.dev(**{self.v: o}))
            for o in range(1, g.C):
                self._send(blk, blk, ("c", o, q, 0), g.dev(c=o))

    def step3(self):
        g = self.g
        U, V = g.size(self.u), g.size(self.v)
        for q in range(U):
            for w in range(1, V):
                blk = self.block((U - q) % U, V - w)
                self._wait_recv(blk, ("v", w, q))
                for o in range(1, g.C):
                    self._send(blk, blk, ("c", o, q, w), g.dev(c=o))

    def step4(self):
        g = self.g
        U, V = g.size(self.u), g.size(self.v)
        for q in range(U):
            for w in range(V):
                for o in range(1, g.C):
                    self._wait_recv(self.block((U - q) % U, (V - w) % V, g.C - o), ("c", o, q, w))

    def finish(self):
        for cp in self.sent:
            cp.wait_send()


def run_gathers(gs):
    n = len(gs)
    for g in gs:
        g.start()
    steps = [lambda g: g.step1(), lambda g: g.step2(), lambda g: g.step3(), lambda g: g.step4()]
    for t in range(n + 3):
        for s in range(4):
            i = t - s
            if 0 <= i < n:
                steps[s](gs[i])
    for g in gs:
        g.finish()

class Scatter:
    def __init__(self, grid, part, order, bufs, acc, out, ssem, rsem):
        self.g, self.part, self.acc, self.out, self.ssem, self.rsem = grid, part, acc, out, ssem, rsem
        self.rc, self.rv, self.ru, self.rz = bufs
        self.u, self.v = order[1], order[2]
        g = grid
        U, V = g.size(self.u), g.size(self.v)
        self.U, self.V = U, V
        k = 0
        self.slot = {}
        for o in range(1, g.C):
            for q in range(U):
                for w in range(V):
                    self.slot["c", o, q, w] = k; k += 1
        for o in range(1, V):
            for q in range(U):
                self.slot["v", o, q] = k; k += 1
        for o in range(1, U):
            self.slot["u", o] = k; k += 1
        for o in range(1, g.Z):
            self.slot["z", o] = k; k += 1
        self.sent = []

    def first(self, uo, vo, co=0):
        g = self.g.at(**{self.u: uo, self.v: vo, "c": co})
        return self.g.dpof(g) * self.g.Z

    def block(self, uo, vo, co=0):
        return self.part.at[pl.ds(self.first(uo, vo, co), self.g.Z)]

    def _copy(self, src, dst, slot, dev):
        k = self.slot[slot]
        return pltpu.make_async_remote_copy(src_ref=src, dst_ref=dst, send_sem=self.ssem.at[k], recv_sem=self.rsem.at[k],
                                            device_id=dev, device_id_type=MESH)

    def _send(self, src, dst, slot, dev):
        cp = self._copy(src, dst, slot, dev)
        cp.start()
        self.sent.append((src, dst, slot, dev))

    def _wait(self, dst, slot, dev):
        self._copy(dst, dst, slot, dev).wait_recv()

    def start(self):
        g = self.g
        for o in range(1, g.C):
            for w in list(range(1, self.V)) + [0]:
                for q in list(range(1, self.U)) + [0]:
                    self._send(self.block(q, w, o), self.rc.at[o - 1, q * self.V + w], ("c", o, q, w), g.dev(c=o))

    def step1(self):
        g = self.g
        f = jnp.float32
        for w in list(range(1, self.V)) + [0]:
            for q in list(range(1, self.U)) + [0]:
                for o in range(1, g.C):
                    self._wait(self.rc.at[o - 1, q * self.V + w], ("c", o, q, w), g.dev(c=o))
                at = self.first(q, w)
                def body(i, _):
                    s = self.part[at + i].astype(f)
                    for o in range(1, g.C):
                        s = s + self.rc[o - 1, q * self.V + w, i].astype(f)
                    if w:
                        self.part[at + i] = s.astype(self.part.dtype)
                    else:
                        self.acc[q, i] = s
                    return 0
                lax.fori_loop(0, g.Z, body, 0)
                if w:
                    self._send(self.block(q, w), self.rv.at[w - 1, q], ("v", w, q), g.dev(**{self.v: w}))

    def step2(self):
        g = self.g
        f = jnp.float32
        for q in list(range(1, self.U)) + [0]:
            for w in range(1, self.V):
                self._wait(self.rv.at[w - 1, q], ("v", w, q), g.dev(**{self.v: w}))
            at = self.first(q, 0)
            def body(i, _):
                s = self.acc[q, i]
                for w in range(1, self.V):
                    s = s + self.rv[w - 1, q, i].astype(f)
                if q:
                    self.part[at + i] = s.astype(self.part.dtype)
                else:
                    self.acc[q, i] = s
                return 0
            lax.fori_loop(0, g.Z, body, 0)
            if q:
                self._send(self.block(q, 0), self.ru.at[q - 1], ("u", q), g.dev(**{self.u: q}))

    def step3(self):
        g = self.g
        f = jnp.float32
        for q in range(1, self.U):
            self._wait(self.ru.at[q - 1], ("u", q), g.dev(**{self.u: q}))
        at = self.first(0, 0)
        for o in list(range(1, g.Z)) + [0]:
            i = (g.z + o) % g.Z
            s = self.acc[0, i]
            for q in range(1, self.U):
                s = s + self.ru[q - 1, i].astype(f)
            if o:
                self.part[at + i] = s.astype(self.part.dtype)
                self._send(self.part.at[at + i], self.rz.at[o - 1], ("z", o), g.dev(z=o))
            else:
                self.acc[0, i] = s

    def step4(self):
        g = self.g
        s = self.acc[0, g.z]
        for o in range(1, g.Z):
            self._wait(self.rz.at[o - 1], ("z", o), g.dev(z=o))
            s = s + self.rz[o - 1].astype(jnp.float32)
        self.out[...] = s

    def finish(self):
        for a in self.sent:
            self._copy(*a).wait_send()


def scatter_scratch(grid_sizes, shape, dtype, order):
    Z, S = grid_sizes["z"], grid_sizes
    U, V, C = S[order[1]], S[order[2]], S["c"]
    t = tuple(shape)
    m = lambda n: max(n, 1)
    return [pltpu.VMEM((m(C - 1), U * V, Z) + t, dtype), pltpu.VMEM((m(V - 1), U, Z) + t, dtype), pltpu.VMEM((m(U - 1), Z) + t, dtype),
            pltpu.VMEM((m(Z - 1),) + t, dtype), pltpu.VMEM((U, Z) + t, jnp.float32)]


def run_scatters(gs):
    n = len(gs)
    for g in gs:
        g.start()
    for t in range(n + 3):
        for s in range(4):
            i = t - s
            if 0 <= i < n:
                [gs[i].step1, gs[i].step2, gs[i].step3, gs[i].step4][s]()
    for g in gs:
        g.finish()


ORDERS = ("zxyc", "zyxc", "zyxc", "zxyc", "zyxc", "zxyc")
VMEM_CAP = 60 << 20


def sizes_of(dp, seq):
    C = 2 if dp % 2 == 0 else 1
    rest = dp // C
    y = 1
    while (2 * y) * (2 * y) <= rest and rest % (2 * y) == 0:
        y *= 2
    return dict(y=y, x=rest // y, c=C, z=seq)


def tiled(shard):
    rows, cols = shard.shape
    return shard.reshape((rows // 8, 8, cols) if rows % 8 == 0 else (1, rows, cols))


def gather_kernel(dp, seq, orders, *refs):
    n = len(orders)
    ins, outs = refs[:n], refs[n : 2 * n]
    ssem, rsem, lsem = refs[2 * n :]
    grid = Grid(dp, seq)
    entry_barrier(grid)
    run_gathers(
        [
            Gather(grid, ins[i], outs[i], orders[i], ssem.at[i], rsem.at[i], lsem.at[i])
            for i in range(n)
        ]
    )


def gather_all(dp, seq, shards):
    n = len(shards)
    sems = pltpu.SemaphoreType.DMA((n, dp * seq - 1))
    blocks = [tiled(s) for s in shards]
    outs = pl.pallas_call(
        partial(gather_kernel, dp, seq, ORDERS[:n]),
        out_shape=[jax.ShapeDtypeStruct((dp * seq,) + b.shape, b.dtype) for b in blocks],
        in_specs=[pl.BlockSpec(memory_space=pl.ANY)] * n,
        out_specs=[pl.BlockSpec(memory_space=pl.ANY)] * n,
        scratch_shapes=[sems, sems, pltpu.SemaphoreType.DMA((n,))],
        compiler_params=pltpu.CompilerParams(collective_id=0, has_side_effects=True),
        name="gather",
    )(*blocks)
    return [o.reshape((-1, s.shape[1])) for o, s in zip(outs, shards)]


def scatter_kernel(dp, seq, orders, count, *refs):
    n = len(orders)
    ins, outs, total, rest = refs[:n], refs[n : 2 * n], refs[2 * n], refs[2 * n + 1 :]
    parts, rest = rest[:n], rest[n:]
    ssem, rsem, lsem, gs, gr = rest[-5:]
    tail = rest[-6]
    grid = Grid(dp, seq)
    copies = [pltpu.make_async_copy(ins[i], parts[i], lsem.at[i]) for i in range(n)]
    for c in copies:
        c.start()
    entry_barrier(grid)
    for c in copies:
        c.wait()
    run_scatters(
        [
            Scatter(
                grid, parts[i], orders[i], rest[5 * i : 5 * i + 4], rest[5 * i + 4], outs[i],
                ssem.at[i], rsem.at[i],
            )
            for i in range(n)
        ]
    )
    tail[...] = outs[n - 1][1:]
    run_gathers([Gather(grid, tail, total, "zxyc", gs, gr, lsem.at[n])])


def scatter_all(dp, seq, parts, orders):
    n = len(parts)
    N = dp * seq
    sizes = sizes_of(dp, seq)
    scratch = [pltpu.VMEM(p.shape, p.dtype) for p in parts]
    for p, o in zip(parts, orders):
        scratch += scatter_scratch(sizes, p.shape[1:], p.dtype, o)
    last = parts[-1].shape[1:]
    tail = (last[0] - 1,) + last[1:]
    sems = pltpu.SemaphoreType.DMA((n, N - 1))
    one = pltpu.SemaphoreType.DMA((N - 1,))
    return pl.pallas_call(
        partial(scatter_kernel, dp, seq, orders, n),
        out_shape=[jax.ShapeDtypeStruct(p.shape[1:], jnp.float32) for p in parts]
        + [jax.ShapeDtypeStruct((N,) + tail, jnp.float32)],
        in_specs=[pl.BlockSpec(memory_space=pl.ANY)] * n,
        out_specs=[pl.BlockSpec(memory_space=pltpu.VMEM)] * (n + 1),
        scratch_shapes=scratch
        + [
            pltpu.VMEM(tail, jnp.float32), sems, sems, pltpu.SemaphoreType.DMA((n + 1,)), one, one,
        ],
        compiler_params=pltpu.CompilerParams(
            collective_id=1, has_side_effects=True, vmem_limit_bytes=VMEM_CAP
        ),
        name="scatter",
    )(*parts)


def lanes(flat, rows):
    return jnp.pad(flat, ((0, 0), (0, rows * 1024 - flat.shape[1]))).reshape(-1, rows, 8, 128)


def cut(rows, widths):
    out, at = [], 0
    for w in widths:
        out.append(rows[:, at : at + w])
        at += w
    return out


HEADS = 6
HEAD = 64
KERNEL = 9
FF = 3072
GROUPS = 2


norm_eps = 1e-12


def with_halo(cells, sides, width):
    for axis, dim in sides:
        count = lax.axis_size(axis)
        ends = count - 1
        head = lax.slice_in_dim(cells, 0, width, axis=dim)
        tail = lax.slice_in_dim(cells, cells.shape[dim] - width, cells.shape[dim], axis=dim)
        cells = jnp.concatenate(
            [
                lax.ppermute(tail, axis, [(i, (i + 1) % count) for i in range(ends)]),
                cells,
                lax.ppermute(head, axis, [((i + 1) % count, i) for i in range(ends)]),
            ],
            axis=dim,
        )
    return cells


def layer_norm(inputs, gain_vec, shift_vec):
    centre = inputs - jnp.mean(inputs, axis=-1, keepdims=True)
    variance = jnp.mean(centre * centre, axis=-1, keepdims=True)
    return centre * lax.rsqrt(variance + norm_eps) * gain_vec + shift_vec


def attend(queries, key_rows, value_rows, score_scale):
    scores = (
        jnp.einsum("ihe,jhe->hij", queries, key_rows, preferred_element_type=jnp.float32)
        * score_scale
    )
    row_max = jnp.max(scores, axis=-1, keepdims=True)
    norm_log = row_max + jnp.log(jnp.sum(jnp.exp(scores - row_max), axis=-1, keepdims=True))
    weights_low = jnp.exp(scores - norm_log).astype(jnp.bfloat16)
    context = jnp.einsum(
        "hij,jhe->ihe", weights_low, value_rows, preferred_element_type=jnp.float32
    )
    return (context.astype(jnp.bfloat16), norm_log[..., 0])


def attend_back(queries, grad_context, norm_log, key_rows, value_rows, row_delta, score_scale):
    scores = (
        jnp.einsum("ihe,jhe->hij", queries, key_rows, preferred_element_type=jnp.float32)
        * score_scale
    )
    soft_rows = jnp.exp(scores - norm_log[..., None])
    grad_soft = jnp.einsum(
        "ihe,jhe->hij", grad_context, value_rows, preferred_element_type=jnp.float32
    )
    row_delta = jnp.sum(soft_rows * grad_soft, axis=-1)
    grad_scores = (soft_rows * (grad_soft - row_delta[..., None])).astype(jnp.bfloat16)
    grad_queries = (
        jnp.einsum("hij,jhe->ihe", grad_scores, key_rows, preferred_element_type=jnp.float32)
        * score_scale
    )
    grad_keys = (
        jnp.einsum("hij,ihe->jhe", grad_scores, queries, preferred_element_type=jnp.float32)
        * score_scale
    )
    grad_values = jnp.einsum(
        "hij,ihe->jhe",
        soft_rows.astype(jnp.bfloat16),
        grad_context,
        preferred_element_type=jnp.float32,
    )
    return (grad_queries, grad_keys, grad_values, row_delta)


def body(
    hidden,
    cotangent,
    w_proj,
    w_depth,
    w_kernel,
    b_kernel,
    w_out,
    w_up,
    w_down,
    b_proj,
    b_up,
    b_out,
    ln1_gain,
    ln1_bias,
    b_down,
    ln2_gain,
    ln2_bias,
):
    seq_count, local_rows, model_width = hidden.shape
    total_rows = seq_count * local_rows
    head_count = HEADS
    head_size = HEAD
    all_width = head_count * head_size
    tap_count = KERNEL
    half_kernel = KERNEL // 2
    group_count = GROUPS
    hidden_units = FF
    ext_rows = local_rows + 2 * half_kernel
    score_scale = head_size ** (-0.5)
    dp, seq = lax.axis_size("dp"), lax.axis_size("seq")
    devices = dp * seq
    vectors = (b_proj, b_up, b_out, ln1_gain, ln1_bias, b_down, ln2_gain, ln2_bias)
    widths = [w_depth.shape[0] * KERNEL] + [v.shape[0] for v in vectors]
    small = jnp.concatenate([w_depth.reshape(-1)] + list(vectors))
    small = jnp.pad(small, (0, 1024 - small.shape[0])).reshape(8, 128)
    full_proj, full_out, full_up, full_down, small = gather_all(
        dp, seq, [w_proj, w_out, w_up, w_down, small]
    )
    small = cut(small.reshape(devices, 1024), widths)
    full_depth = small[0].reshape(-1, KERNEL)
    (
        full_bproj,
        full_bup,
        full_bout,
        gain_one,
        shift_one,
        full_bdown,
        gain_two,
        shift_two,
    ) = [v.reshape(-1) for v in small[1:]]
    bias_proj = full_bproj.astype(jnp.float32)
    gain_first = gain_one.astype(jnp.float32)
    shift_first = shift_one.astype(jnp.float32)
    gain_second = gain_two.astype(jnp.float32)
    shift_second = shift_two.astype(jnp.float32)
    tokens_flat = hidden.reshape(total_rows, model_width)
    first_proj = jnp.dot(
        tokens_flat, full_proj[:, : 3 * all_width], preferred_element_type=jnp.float32
    )
    queries = (first_proj[:, :all_width] + bias_proj[:all_width]).astype(jnp.bfloat16)
    key_rows = first_proj[:, all_width : 2 * all_width].astype(jnp.bfloat16)
    value_rows = (first_proj[:, 2 * all_width :] + bias_proj[all_width : 2 * all_width]).astype(
        jnp.bfloat16
    )
    extended = with_halo(hidden, (("seq", 1),), half_kernel)
    position = lax.axis_index("seq") * local_rows + jnp.arange(ext_rows) - half_kernel
    inside = ((position >= 0) & (position < local_rows * lax.axis_size("seq"))).astype(jnp.float32)
    conv_input = jnp.dot(
        extended.reshape(seq_count * ext_rows, model_width),
        full_proj[:, 3 * all_width : 4 * all_width],
        preferred_element_type=jnp.float32,
    )
    conv_input = (conv_input + bias_proj[2 * all_width : 3 * all_width]).reshape(
        seq_count, ext_rows, all_width
    ) * inside[None, :, None]
    depth_weights = full_depth.astype(jnp.float32)
    depth_sum = jnp.zeros((seq_count, local_rows, model_width), jnp.float32)
    for tap_index in range(tap_count):
        depth_sum = (
            depth_sum
            + extended[:, tap_index : tap_index + local_rows].astype(jnp.float32)
            * depth_weights[:, tap_index]
        )
    spread = depth_sum.astype(jnp.bfloat16).reshape(total_rows, model_width)
    key_conv = (
        jnp.dot(spread, full_proj[:, 4 * all_width :], preferred_element_type=jnp.float32)
        + bias_proj[3 * all_width :]
    )
    mixed_key = (key_conv * queries.astype(jnp.float32)).astype(jnp.bfloat16)
    logits = jnp.dot(mixed_key, w_kernel, preferred_element_type=jnp.float32) + b_kernel.astype(
        jnp.float32
    )
    tap_weights = jax.nn.softmax(
        logits.reshape(seq_count, local_rows, head_count, tap_count), axis=-1
    )
    conv_heads = conv_input.reshape(seq_count, ext_rows, head_count, head_size)
    conv_mix = jnp.zeros((seq_count, local_rows, head_count, head_size), jnp.float32)
    for tap_index in range(tap_count):
        conv_mix = (
            conv_mix
            + tap_weights[..., tap_index, None] * conv_heads[:, tap_index : tap_index + local_rows]
        )
    queries_seq = queries.reshape(seq_count, local_rows, all_width)
    all_keys, all_values = (
        lax.all_gather(
            key_rows.reshape(seq_count, local_rows, all_width), "seq", axis=1, tiled=True
        ),
        lax.all_gather(
            value_rows.reshape(seq_count, local_rows, all_width), "seq", axis=1, tiled=True
        ),
    )
    full_length = all_keys.shape[1]

    def forward_one(item_set):
        query_seq, key_seq, value_seq = item_set
        return attend(
            query_seq.reshape(local_rows, head_count, head_size),
            key_seq.reshape(full_length, head_count, head_size),
            value_seq.reshape(full_length, head_count, head_size),
            score_scale,
        )

    context, norm_log = lax.map(forward_one, (queries_seq, all_keys, all_values))
    joined = jnp.concatenate(
        [
            context.reshape(total_rows, all_width),
            conv_mix.reshape(total_rows, all_width).astype(jnp.bfloat16),
        ],
        axis=-1,
    )
    after_mix = (
        jnp.dot(joined, full_out, preferred_element_type=jnp.float32)
        + full_bout.astype(jnp.float32)
        + tokens_flat.astype(jnp.float32)
    )
    first_norm, first_pull = jax.vjp(layer_norm, after_mix, gain_first, shift_first)
    grouped_in = first_norm.astype(jnp.bfloat16).reshape(
        total_rows, group_count, model_width // group_count
    )
    up_groups = full_up.reshape(
        group_count, model_width // group_count, hidden_units // group_count
    )
    pre_act = jnp.einsum(
        "ngd,gdf->ngf", grouped_in, up_groups, preferred_element_type=jnp.float32
    ).reshape(total_rows, hidden_units) + full_bup.astype(jnp.float32)
    activated, gelu_pull = jax.vjp(partial(jax.nn.gelu, approximate=False), pre_act)
    act_low = activated.astype(jnp.bfloat16).reshape(
        total_rows, group_count, hidden_units // group_count
    )
    down_groups = full_down.reshape(
        group_count, hidden_units // group_count, model_width // group_count
    )
    summed = jnp.einsum(
        "ngf,gfd->ngd", act_low, down_groups, preferred_element_type=jnp.float32
    ).reshape(total_rows, model_width)
    summed = summed + full_bdown.astype(jnp.float32) + first_norm
    out_value, second_pull = jax.vjp(layer_norm, summed, gain_second, shift_second)
    output = out_value.astype(jnp.bfloat16).reshape(seq_count, local_rows, model_width)
    back_proj = full_proj
    back_depth = full_depth.astype(jnp.float32)
    back_out = full_out
    back_up = up_groups
    back_down = down_groups
    grad_summed, grad_gain_two, grad_shift_two = second_pull(
        cotangent.reshape(total_rows, model_width).astype(jnp.float32)
    )
    grad_bdown = jnp.sum(grad_summed, axis=0)
    summed_low = grad_summed.astype(jnp.bfloat16).reshape(
        total_rows, group_count, model_width // group_count
    )
    grad_activ = jnp.einsum(
        "ngd,gfd->ngf", summed_low, back_down, preferred_element_type=jnp.float32
    ).reshape(total_rows, hidden_units)
    grad_wdown = jnp.einsum(
        "ngf,ngd->gfd", act_low, summed_low, preferred_element_type=jnp.float32
    ).reshape(hidden_units, model_width // group_count)
    grad_pre = gelu_pull(grad_activ)[0]
    grad_bup = jnp.sum(grad_pre, axis=0)
    pre_low = grad_pre.astype(jnp.bfloat16).reshape(
        total_rows, group_count, hidden_units // group_count
    )
    grad_wup = jnp.einsum(
        "ngd,ngf->gdf", grouped_in, pre_low, preferred_element_type=jnp.float32
    ).reshape(model_width, hidden_units // group_count)
    grad_first = grad_summed + jnp.einsum(
        "ngf,gdf->ngd", pre_low, back_up, preferred_element_type=jnp.float32
    ).reshape(total_rows, model_width)
    grad_after, grad_gain_one, grad_shift_one = first_pull(grad_first)
    grad_bout = jnp.sum(grad_after, axis=0)
    after_low = grad_after.astype(jnp.bfloat16)
    grad_wout = jnp.dot(joined.T, after_low, preferred_element_type=jnp.float32)
    grad_joined = jnp.dot(after_low, back_out.T, preferred_element_type=jnp.float32)
    grad_context = (
        grad_joined[:, :all_width].astype(jnp.bfloat16).reshape(seq_count, local_rows, all_width)
    )
    grad_mix = grad_joined[:, all_width:].reshape(seq_count, local_rows, head_count, head_size)

    def back_one(item_set):
        query_seq, grad_seq, norm_seq, key_seq, value_seq = item_set
        grad_query, grad_key, grad_value, unused_delta = attend_back(
            query_seq.reshape(local_rows, head_count, head_size),
            grad_seq.reshape(local_rows, head_count, head_size),
            norm_seq,
            key_seq.reshape(full_length, head_count, head_size),
            value_seq.reshape(full_length, head_count, head_size),
            None,
            score_scale,
        )
        key_value = jnp.concatenate(
            [grad_key.reshape(full_length, all_width), grad_value.reshape(full_length, all_width)],
            axis=-1,
        )
        return (grad_query.reshape(local_rows, all_width), key_value)

    grad_query_att, kv_terms = lax.map(
        back_one, (queries_seq, grad_context, norm_log, all_keys, all_values)
    )
    own_kv = lax.psum_scatter(
        kv_terms.astype(jnp.bfloat16), "seq", scatter_dimension=1, tiled=True
    ).astype(jnp.float32)
    grad_keys_low = own_kv[..., :all_width].reshape(total_rows, all_width).astype(jnp.bfloat16)
    grad_values_low = own_kv[..., all_width:].reshape(total_rows, all_width).astype(jnp.bfloat16)
    grad_taps = jnp.stack(
        [
            jnp.sum(grad_mix * conv_heads[:, tap_index : tap_index + local_rows], axis=-1)
            for tap_index in range(tap_count)
        ],
        axis=-1,
    )
    grad_conv_ext = jnp.zeros((seq_count, ext_rows, head_count, head_size), jnp.float32)
    for tap_index in range(tap_count):
        grad_conv_ext = grad_conv_ext + jnp.pad(
            tap_weights[..., tap_index, None] * grad_mix,
            ((0, 0), (tap_index, 2 * half_kernel - tap_index), (0, 0), (0, 0)),
        )
    grad_logits = tap_weights * (
        grad_taps - jnp.sum(tap_weights * grad_taps, axis=-1, keepdims=True)
    )
    grad_logits = grad_logits.reshape(total_rows, head_count * tap_count)
    grad_bkernel = jnp.sum(grad_logits, axis=0)
    logits_low = grad_logits.astype(jnp.bfloat16)
    grad_wkernel = jnp.dot(mixed_key.T, logits_low, preferred_element_type=jnp.float32)
    grad_mixed = jnp.dot(logits_low, w_kernel.T, preferred_element_type=jnp.float32)
    grad_queries = (grad_query_att.reshape(total_rows, all_width) + grad_mixed * key_conv).astype(
        jnp.bfloat16
    )
    grad_key_conv = grad_mixed * queries.astype(jnp.float32)
    grad_bpt = jnp.sum(grad_key_conv, axis=0)
    key_conv_low = grad_key_conv.astype(jnp.bfloat16)
    grad_wpt = jnp.dot(spread.T, key_conv_low, preferred_element_type=jnp.float32)
    grad_spread = jnp.dot(
        key_conv_low, back_proj[:, 4 * all_width :].T, preferred_element_type=jnp.float32
    ).reshape(seq_count, local_rows, model_width)
    grad_wdepth = jnp.stack(
        [
            jnp.sum(
                extended[:, tap_index : tap_index + local_rows].astype(jnp.float32) * grad_spread,
                axis=(0, 1),
            )
            for tap_index in range(tap_count)
        ],
        axis=-1,
    )
    grad_ext_depth = jnp.zeros((seq_count, ext_rows, model_width), jnp.float32)
    for tap_index in range(tap_count):
        grad_ext_depth = grad_ext_depth + jnp.pad(
            back_depth[:, tap_index] * grad_spread,
            ((0, 0), (tap_index, 2 * half_kernel - tap_index), (0, 0)),
        )
    combined = jnp.concatenate(
        [grad_conv_ext.reshape(seq_count, ext_rows, all_width), grad_ext_depth], axis=-1
    )
    received = with_halo(combined.astype(jnp.bfloat16), (("seq", 1),), half_kernel).astype(
        combined.dtype
    )
    own_part = combined[:, half_kernel : half_kernel + local_rows]
    own_part = own_part.at[:, :half_kernel].add(received[:, :half_kernel])
    own_part = own_part.at[:, local_rows - half_kernel :].add(
        received[:, received.shape[1] - half_kernel :]
    )
    grad_conv_own = own_part[..., :all_width].reshape(total_rows, all_width)
    grad_depth_x = own_part[..., all_width:].reshape(total_rows, model_width)
    grad_bconv = jnp.sum(grad_conv_own, axis=0)
    conv_low = grad_conv_own.astype(jnp.bfloat16)
    stacked = jnp.concatenate([grad_queries, grad_keys_low, grad_values_low, conv_low], axis=-1)
    grad_wfirst = jnp.dot(tokens_flat.T, stacked, preferred_element_type=jnp.float32)
    grad_tokens = (
        grad_after
        + jnp.dot(stacked, back_proj[:, : 4 * all_width].T, preferred_element_type=jnp.float32)
        + grad_depth_x
    )
    grad_wproj = jnp.concatenate([grad_wfirst, grad_wpt], axis=1)
    grad_bproj = jnp.concatenate(
        [
            jnp.sum(grad_queries.astype(jnp.float32), axis=0),
            jnp.sum(grad_values_low.astype(jnp.float32), axis=0),
            grad_bconv,
            grad_bpt,
        ]
    )
    def blocks(grad, shard):
        return grad.astype(jnp.bfloat16).reshape((devices,) + tiled(shard).shape)

    per_device = [
        g.reshape(devices, -1)
        for g in (
            grad_wdepth, grad_bproj, grad_bup, grad_bout, grad_gain_one, grad_shift_one,
            grad_bdown, grad_gain_two, grad_shift_two,
        )
    ]
    kernel_flat = jnp.concatenate([grad_wkernel.reshape(-1), grad_bkernel])
    kernel_len = kernel_flat.shape[0]
    kernel_each = -(-kernel_len // devices)
    kernel_flat = jnp.pad(kernel_flat, (0, kernel_each * devices - kernel_len))
    small_grad = jnp.concatenate(
        [
            lanes(jnp.concatenate(per_device, axis=1), 1),
            lanes(kernel_flat.reshape(devices, kernel_each), 1),
        ],
        axis=1,
    )
    sum_down, sum_up, sum_out, sum_proj, sum_small, sum_kernel = scatter_all(
        dp,
        seq,
        [
            blocks(grad_wdown, w_down), blocks(grad_wup, w_up), blocks(grad_wout, w_out),
            blocks(grad_wproj, w_proj), small_grad,
        ],
        ("zxyc", "zyxc", "zxyc", "zyxc", "zxyc"),
    )
    mine = cut(sum_small[:1].reshape(1, 1024), widths)
    shards = [sum_proj.reshape(w_proj.shape), mine[0].reshape(w_depth.shape)]
    shards += [
        sum_out.reshape(w_out.shape), sum_up.reshape(w_up.shape), sum_down.reshape(w_down.shape),
    ]
    shards += [m.reshape(-1) for m in mine[1:]]
    kernel_sum = sum_kernel.reshape(devices, 1024)[:, :kernel_each].reshape(-1)
    kernel_total = (
        kernel_sum[: grad_wkernel.size].reshape(grad_wkernel.shape),
        kernel_sum[grad_wkernel.size : kernel_len],
    )
    return (
        output,
        grad_tokens.reshape(seq_count, local_rows, model_width),
        shards[0],
        shards[1],
        kernel_total[0],
        kernel_total[1],
        shards[2],
        shards[3],
        shards[4],
        shards[5],
        shards[6],
        shards[7],
        shards[8],
        shards[9],
        shards[10],
        shards[11],
        shards[12],
    )


def solution(mesh):
    placed = (
        P("dp", "seq", None),
        P("dp", "seq", None),
        P(("dp", "seq"), None),
        P(("dp", "seq"), None),
        P(),
        P(),
        P(("dp", "seq"), None),
        P(("dp", "seq"), None),
        P(("dp", "seq"), None),
        P(("dp", "seq")),
        P(("dp", "seq")),
        P(("dp", "seq")),
        P(("dp", "seq")),
        P(("dp", "seq")),
        P(("dp", "seq")),
        P(("dp", "seq")),
        P(("dp", "seq")),
    )
    return jax.shard_map(
        body,
        mesh=mesh,
        in_specs=placed,
        out_specs=(
            P("dp", "seq", None),
            P("dp", "seq", None),
            P(("dp", "seq"), None),
            P(("dp", "seq"), None),
            P(),
            P(),
            P(("dp", "seq"), None),
            P(("dp", "seq"), None),
            P(("dp", "seq"), None),
            P(("dp", "seq")),
            P(("dp", "seq")),
            P(("dp", "seq")),
            P(("dp", "seq")),
            P(("dp", "seq")),
            P(("dp", "seq")),
            P(("dp", "seq")),
            P(("dp", "seq")),
        ),
        check_vma=False,
    )
```

```python
from functools import partial

import jax
import jax.numpy as jnp
from jax import lax
from jax.experimental import pallas as pl
from jax.experimental.pallas import tpu as pltpu
from jax.sharding import PartitionSpec as P

MESH = pl.DeviceIdType.MESH


class Grid:
    def __init__(self, dp, seq):
        self.C = 2 if dp % 2 == 0 else 1
        rest = dp // self.C
        y = 1
        while (2 * y) * (2 * y) <= rest and rest % (2 * y) == 0:
            y *= 2
        self.Y, self.X, self.Z = y, rest // y, seq
        d = lax.axis_index("dp")
        self.z = lax.axis_index("seq")
        self.c = d % self.C
        self.x = (d // self.C) % self.X
        self.y = d // (self.C * self.X)
        self.dp = d
    def size(self, ax):
        return getattr(self, ax.upper())
    def at(self, **off):
        g = {a: (getattr(self, a) + off.get(a, 0)) % self.size(a) if off.get(a, 0) else getattr(self, a) for a in "yxcz"}
        return g
    def dpof(self, g):
        return (g["y"] * self.X + g["x"]) * self.C + g["c"]
    def dev(self, **off):
        g = self.at(**off)
        return (self.dpof(g), g["z"])


def peers(grid):
    out = []
    for a in "zxyc":
        for o in range(1, grid.size(a)):
            out.append(grid.dev(**{a: o}))
    return out


def entry_barrier(grid):
    b = pltpu.get_barrier_semaphore()
    ps = peers(grid)
    for p in ps:
        pl.semaphore_signal(b, inc=1, device_id=p, device_id_type=MESH)
    pl.semaphore_wait(b, len(ps))


class Gather:
    def __init__(self, grid, src, buf, order, ssem, rsem, lsem):
        self.g, self.src, self.buf, self.ssem, self.rsem, self.lsem = grid, src, buf, ssem, rsem, lsem
        self.u, self.v = order[1], order[2]
        self.ns = 0
        self.sent = []
        self.recv = {}
        g = grid
        k = 0
        self.slot = {}
        for o in range(1, g.Z):
            self.slot["z", o] = k; k += 1
        for o in range(1, g.size(self.u)):
            self.slot["u", o] = k; k += 1
        for o in range(1, g.size(self.v)):
            for q in range(g.size(self.u)):
                self.slot["v", o, q] = k; k += 1
        for o in range(1, g.C):
            for q in range(g.size(self.u)):
                for w in range(g.size(self.v)):
                    self.slot["c", o, q, w] = k; k += 1
        self.count = k

    @staticmethod
    def slots(Z, X, Y, C):
        return (Z - 1) + X * Y * C - 1

    def block(self, uo, vo, co=0):
        g = self.g.at(**{self.u: uo, self.v: vo, "c": co})
        return self.buf.at[pl.ds(self.g.dpof(g) * self.g.Z, self.g.Z)]

    def _send(self, src, dst, slot, dev):
        k = self.slot[slot]
        cp = pltpu.make_async_remote_copy(src_ref=src, dst_ref=dst, send_sem=self.ssem.at[k], recv_sem=self.rsem.at[k],
                                          device_id=dev, device_id_type=MESH)
        cp.start()
        self.sent.append(cp)

    def start(self):
        g = self.g
        me = g.dp * g.Z + g.z
        self.local = pltpu.make_async_copy(self.src, self.buf.at[me], self.lsem)
        self.local.start()
        for o in range(1, g.Z):
            self._send(self.src, self.buf.at[me], ("z", o), g.dev(z=o))

    def _wait_recv(self, ref, slot):
        k = self.slot[slot]
        pltpu.make_async_remote_copy(src_ref=ref, dst_ref=ref, send_sem=self.ssem.at[k], recv_sem=self.rsem.at[k],
                                     device_id=self.g.dev(z=1) if self.g.Z > 1 else self.g.dev(c=1), device_id_type=MESH).wait_recv()

    def step1(self):
        g = self.g
        self.local.wait()
        for o in range(1, g.Z):
            self._wait_recv(self.buf.at[g.dp * g.Z + (g.z + g.Z - o) % g.Z], ("z", o))
        blk = self.block(0, 0)
        for o in range(1, g.size(self.u)):
            self._send(blk, blk, ("u", o), g.dev(**{self.u: o}))
        for o in range(1, g.size(self.v)):
            self._send(blk, blk, ("v", o, 0), g.dev(**{self.v: o}))
        for o in range(1, g.C):
            self._send(blk, blk, ("c", o, 0, 0), g.dev(c=o))

    def step2(self):
        g = self.g
        U, V = g.size(self.u), g.size(self.v)
        for q in range(1, U):
            blk = self.block(U - q, 0)
            self._wait_recv(blk, ("u", q))
            for o in range(1, V):
                self._send(blk, blk, ("v", o, q), g.dev(**{self.v: o}))
            for o in range(1, g.C):
                self._send(blk, blk, ("c", o, q, 0), g.dev(c=o))

    def step3(self):
        g = self.g
        U, V = g.size(self.u), g.size(self.v)
        for q in range(U):
            for w in range(1, V):
                blk = self.block((U - q) % U, V - w)
                self._wait_recv(blk, ("v", w, q))
                for o in range(1, g.C):
                    self._send(blk, blk, ("c", o, q, w), g.dev(c=o))

    def step4(self):
        g = self.g
        U, V = g.size(self.u), g.size(self.v)
        for q in range(U):
            for w in range(V):
                for o in range(1, g.C):
                    self._wait_recv(self.block((U - q) % U, (V - w) % V, g.C - o), ("c", o, q, w))

    def finish(self):
        for cp in self.sent:
            cp.wait_send()


def run_gathers(gs):
    n = len(gs)
    for g in gs:
        g.start()
    steps = [lambda g: g.step1(), lambda g: g.step2(), lambda g: g.step3(), lambda g: g.step4()]
    for t in range(n + 3):
        for s in range(4):
            i = t - s
            if 0 <= i < n:
                steps[s](gs[i])
    for g in gs:
        g.finish()

class Scatter:
    def __init__(self, grid, part, order, bufs, out, ssem, rsem):
        self.g, self.part, self.out, self.ssem, self.rsem = grid, part, out, ssem, rsem
        self.rc, self.rv, self.ru, self.rz = bufs
        self.u, self.v = order[1], order[2]
        g = grid
        U, V = g.size(self.u), g.size(self.v)
        self.U, self.V = U, V
        k = 0
        self.slot = {}
        for o in range(1, g.C):
            for q in range(U):
                for w in range(V):
                    self.slot["c", o, q, w] = k; k += 1
        for o in range(1, V):
            for q in range(U):
                self.slot["v", o, q] = k; k += 1
        for o in range(1, U):
            self.slot["u", o] = k; k += 1
        for o in range(1, g.Z):
            self.slot["z", o] = k; k += 1
        self.sent = []

    def first(self, uo, vo, co=0):
        g = self.g.at(**{self.u: uo, self.v: vo, "c": co})
        return self.g.dpof(g) * self.g.Z

    def block(self, uo, vo, co=0):
        return self.part.at[pl.ds(self.first(uo, vo, co), self.g.Z)]

    def _copy(self, src, dst, slot, dev):
        k = self.slot[slot]
        return pltpu.make_async_remote_copy(src_ref=src, dst_ref=dst, send_sem=self.ssem.at[k], recv_sem=self.rsem.at[k],
                                            device_id=dev, device_id_type=MESH)

    def _send(self, src, dst, slot, dev):
        cp = self._copy(src, dst, slot, dev)
        cp.start()
        self.sent.append((src, dst, slot, dev))

    def _wait(self, dst, slot, dev):
        self._copy(dst, dst, slot, dev).wait_recv()

    def start(self):
        g = self.g
        for o in range(1, g.C):
            for w in list(range(1, self.V)) + [0]:
                for q in list(range(1, self.U)) + [0]:
                    self._send(self.block(q, w, o), self.rc.at[o - 1, q * self.V + w], ("c", o, q, w), g.dev(c=o))

    def _total(self, q, w, i):
        f = jnp.float32
        s = self.part[self.first(q, w) + i].astype(f)
        for o in range(1, self.g.C):
            s = s + self.rc[o - 1, q * self.V + w, i].astype(f)
        if w == 0:
            for k in range(1, self.V):
                s = s + self.rv[k - 1, q, i].astype(f)
            if q == 0:
                for k in range(1, self.U):
                    s = s + self.ru[k - 1, i].astype(f)
        return s

    def _wait_c(self, q, w):
        for o in range(1, self.g.C):
            self._wait(self.rc.at[o - 1, q * self.V + w], ("c", o, q, w), self.g.dev(c=o))

    def _reduce(self, q, w):
        at = self.first(q, w)

        def body(i, _):
            self.part[at + i] = self._total(q, w, i).astype(self.part.dtype)
            return 0

        lax.fori_loop(0, self.g.Z, body, 0)

    def step1(self):
        for w in range(1, self.V):
            for q in list(range(1, self.U)) + [0]:
                self._wait_c(q, w)
                self._reduce(q, w)
                self._send(self.block(q, w), self.rv.at[w - 1, q], ("v", w, q), self.g.dev(**{self.v: w}))

    def step2(self):
        for q in range(1, self.U):
            self._wait_c(q, 0)
            for w in range(1, self.V):
                self._wait(self.rv.at[w - 1, q], ("v", w, q), self.g.dev(**{self.v: w}))
            self._reduce(q, 0)
            self._send(self.block(q, 0), self.ru.at[q - 1], ("u", q), self.g.dev(**{self.u: q}))

    def step3(self):
        g = self.g
        self._wait_c(0, 0)
        for w in range(1, self.V):
            self._wait(self.rv.at[w - 1, 0], ("v", w, 0), g.dev(**{self.v: w}))
        for q in range(1, self.U):
            self._wait(self.ru.at[q - 1], ("u", q), g.dev(**{self.u: q}))
        at = self.first(0, 0)
        for o in range(1, g.Z):
            i = (g.z + o) % g.Z
            self.part[at + i] = self._total(0, 0, i).astype(self.part.dtype)
            self._send(self.part.at[at + i], self.rz.at[o - 1], ("z", o), g.dev(z=o))

    def step4(self):
        g = self.g
        s = self._total(0, 0, g.z)
        for o in range(1, g.Z):
            self._wait(self.rz.at[o - 1], ("z", o), g.dev(z=o))
            s = s + self.rz[o - 1].astype(jnp.float32)
        self.out[...] = s

    def finish(self):
        for a in self.sent:
            self._copy(*a).wait_send()


def scatter_scratch(grid_sizes, shape, dtype, order):
    Z, S = grid_sizes["z"], grid_sizes
    U, V, C = S[order[1]], S[order[2]], S["c"]
    t = tuple(shape)
    m = lambda n: max(n, 1)
    return [pltpu.VMEM((m(C - 1), U * V, Z) + t, dtype), pltpu.VMEM((m(V - 1), U, Z) + t, dtype), pltpu.VMEM((m(U - 1), Z) + t, dtype),
            pltpu.VMEM((m(Z - 1),) + t, dtype)]


def run_scatters(gs):
    n = len(gs)
    for g in gs:
        g.start()
    for t in range(n + 3):
        for s in range(4):
            i = t - s
            if 0 <= i < n:
                [gs[i].step1, gs[i].step2, gs[i].step3, gs[i].step4][s]()
    for g in gs:
        g.finish()


ORDERS = ("zxyc", "zyxc", "zyxc", "zxyc", "zyxc", "zxyc")
VMEM_CAP = 60 << 20


def sizes_of(dp, seq):
    C = 2 if dp % 2 == 0 else 1
    rest = dp // C
    y = 1
    while (2 * y) * (2 * y) <= rest and rest % (2 * y) == 0:
        y *= 2
    return dict(y=y, x=rest // y, c=C, z=seq)


def tiled(shard):
    rows, cols = shard.shape
    return shard.reshape((rows // 8, 8, cols) if rows % 8 == 0 else (1, rows, cols))


def gather_kernel(dp, seq, orders, *refs):
    n = len(orders)
    ins, outs = refs[:n], refs[n : 2 * n]
    ssem, rsem, lsem = refs[2 * n :]
    grid = Grid(dp, seq)
    entry_barrier(grid)
    run_gathers(
        [
            Gather(grid, ins[i], outs[i], orders[i], ssem.at[i], rsem.at[i], lsem.at[i])
            for i in range(n)
        ]
    )


def gather_all(dp, seq, shards):
    n = len(shards)
    sems = pltpu.SemaphoreType.DMA((n, dp * seq - 1))
    blocks = [tiled(s) for s in shards]
    outs = pl.pallas_call(
        partial(gather_kernel, dp, seq, ORDERS[:n]),
        out_shape=[jax.ShapeDtypeStruct((dp * seq,) + b.shape, b.dtype) for b in blocks],
        in_specs=[pl.BlockSpec(memory_space=pl.ANY)] * n,
        out_specs=[pl.BlockSpec(memory_space=pl.ANY)] * n,
        scratch_shapes=[sems, sems, pltpu.SemaphoreType.DMA((n,))],
        compiler_params=pltpu.CompilerParams(collective_id=0, has_side_effects=True),
        name="gather",
    )(*blocks)
    return [o.reshape((-1, s.shape[1])) for o, s in zip(outs, shards)]


def scatter_kernel(dp, seq, orders, count, *refs):
    n = len(orders)
    ins, outs, total, rest = refs[:n], refs[n : 2 * n], refs[2 * n], refs[2 * n + 1 :]
    parts, rest = rest[:n], rest[n:]
    ssem, rsem, lsem, gs, gr = rest[-5:]
    tail = rest[-6]
    grid = Grid(dp, seq)
    copies = [pltpu.make_async_copy(ins[i], parts[i], lsem.at[i]) for i in range(n)]
    for c in copies:
        c.start()
    entry_barrier(grid)
    for c in copies:
        c.wait()
    run_scatters(
        [
            Scatter(
                grid, parts[i], orders[i], rest[4 * i : 4 * i + 4], outs[i],
                ssem.at[i], rsem.at[i],
            )
            for i in range(n)
        ]
    )
    tail[...] = outs[n - 1][1:]
    run_gathers([Gather(grid, tail, total, "zxyc", gs, gr, lsem.at[n])])


def scatter_all(dp, seq, parts, orders):
    n = len(parts)
    N = dp * seq
    sizes = sizes_of(dp, seq)
    scratch = [pltpu.VMEM(p.shape, p.dtype) for p in parts]
    for p, o in zip(parts, orders):
        scratch += scatter_scratch(sizes, p.shape[1:], p.dtype, o)
    last = parts[-1].shape[1:]
    tail = (last[0] - 1,) + last[1:]
    sems = pltpu.SemaphoreType.DMA((n, N - 1))
    one = pltpu.SemaphoreType.DMA((N - 1,))
    return pl.pallas_call(
        partial(scatter_kernel, dp, seq, orders, n),
        out_shape=[jax.ShapeDtypeStruct(p.shape[1:], jnp.float32) for p in parts]
        + [jax.ShapeDtypeStruct((N,) + tail, jnp.float32)],
        in_specs=[pl.BlockSpec(memory_space=pl.ANY)] * n,
        out_specs=[pl.BlockSpec(memory_space=pltpu.VMEM)] * (n + 1),
        scratch_shapes=scratch
        + [
            pltpu.VMEM(tail, jnp.float32), sems, sems, pltpu.SemaphoreType.DMA((n + 1,)), one, one,
        ],
        compiler_params=pltpu.CompilerParams(
            collective_id=1, has_side_effects=True, vmem_limit_bytes=VMEM_CAP
        ),
        name="scatter",
    )(*parts)


def lanes(flat, rows):
    return jnp.pad(flat, ((0, 0), (0, rows * 1024 - flat.shape[1]))).reshape(-1, rows, 8, 128)


def cut(rows, widths):
    out, at = [], 0
    for w in widths:
        out.append(rows[:, at : at + w])
        at += w
    return out


HEADS = 6
HEAD = 64
KERNEL = 9
FF = 3072
GROUPS = 2


norm_eps = 1e-12


def with_halo(cells, sides, width):
    for axis, dim in sides:
        count = lax.axis_size(axis)
        ends = count - 1
        head = lax.slice_in_dim(cells, 0, width, axis=dim)
        tail = lax.slice_in_dim(cells, cells.shape[dim] - width, cells.shape[dim], axis=dim)
        cells = jnp.concatenate(
            [
                lax.ppermute(tail, axis, [(i, (i + 1) % count) for i in range(ends)]),
                cells,
                lax.ppermute(head, axis, [((i + 1) % count, i) for i in range(ends)]),
            ],
            axis=dim,
        )
    return cells


def layer_norm(inputs, gain_vec, shift_vec):
    centre = inputs - jnp.mean(inputs, axis=-1, keepdims=True)
    variance = jnp.mean(centre * centre, axis=-1, keepdims=True)
    return centre * lax.rsqrt(variance + norm_eps) * gain_vec + shift_vec


def attend(queries, key_rows, value_rows, score_scale):
    scores = (
        jnp.einsum("ihe,jhe->hij", queries, key_rows, preferred_element_type=jnp.float32)
        * score_scale
    )
    row_max = jnp.max(scores, axis=-1, keepdims=True)
    norm_log = row_max + jnp.log(jnp.sum(jnp.exp(scores - row_max), axis=-1, keepdims=True))
    weights_low = jnp.exp(scores - norm_log).astype(jnp.bfloat16)
    context = jnp.einsum(
        "hij,jhe->ihe", weights_low, value_rows, preferred_element_type=jnp.float32
    )
    return (context.astype(jnp.bfloat16), norm_log[..., 0])


def attend_back(queries, grad_context, norm_log, key_rows, value_rows, row_delta, score_scale):
    scores = (
        jnp.einsum("ihe,jhe->hij", queries, key_rows, preferred_element_type=jnp.float32)
        * score_scale
    )
    soft_rows = jnp.exp(scores - norm_log[..., None])
    grad_soft = jnp.einsum(
        "ihe,jhe->hij", grad_context, value_rows, preferred_element_type=jnp.float32
    )
    row_delta = jnp.sum(soft_rows * grad_soft, axis=-1)
    grad_scores = (soft_rows * (grad_soft - row_delta[..., None])).astype(jnp.bfloat16)
    grad_queries = (
        jnp.einsum("hij,jhe->ihe", grad_scores, key_rows, preferred_element_type=jnp.float32)
        * score_scale
    )
    grad_keys = (
        jnp.einsum("hij,ihe->jhe", grad_scores, queries, preferred_element_type=jnp.float32)
        * score_scale
    )
    grad_values = jnp.einsum(
        "hij,ihe->jhe",
        soft_rows.astype(jnp.bfloat16),
        grad_context,
        preferred_element_type=jnp.float32,
    )
    return (grad_queries, grad_keys, grad_values, row_delta)


def dot(a, b):
    return jnp.dot(a, b, preferred_element_type=jnp.float32)


def dot_nt(a, b):
    return lax.dot_general(a, b, (((1,), (1,)), ((), ())), preferred_element_type=jnp.float32)


def dot_tn(a, b):
    return lax.dot_general(a, b, (((0,), (0,)), ((), ())), preferred_element_type=jnp.float32)


def centred(v):
    centre = v - jnp.mean(v, axis=-1, keepdims=True)
    inv = lax.rsqrt(jnp.mean(centre * centre, axis=-1, keepdims=True) + norm_eps)
    return centre * inv, inv


def norm_back(grad, normed, inv):
    return inv * (
        grad
        - jnp.mean(grad, axis=-1, keepdims=True)
        - normed * jnp.mean(grad * normed, axis=-1, keepdims=True)
    )


def rows_sum(v):
    return jnp.sum(v, axis=0, keepdims=True)


V_BOUT, V_G1, V_S1, V_BDOWN, V_G2, V_S2 = range(9, 15)
HALF_GELU = 0.7071067811865476
PDF = 0.3989422804014327
BLOCK = 128
CHUNK = 512


def ffn_kernel(
    cbuf, cm, x, cot, wout, wup, wdown, vec, bup,
    out, gafter, dctx, gmix, gwout, gwup, gwdown, vecg, gbup,
    act, slope, gp, fnb, gsb, gab,
):
    f32, bf16 = jnp.float32, jnp.bfloat16
    total = x.shape[0]
    width = x.shape[1]
    local = cbuf.shape[1]
    half = cbuf.shape[2]
    gw = width // GROUPS
    gf = FF // GROUPS
    per = local // BLOCK
    vecg[...] = jnp.zeros_like(vecg)
    gbup[...] = jnp.zeros_like(gbup)

    def block(r, _):
        rows = pl.ds(pl.multiple_of(r * BLOCK, BLOCK), BLOCK)
        s = r // per
        o = pl.ds(pl.multiple_of((r % per) * BLOCK, BLOCK), BLOCK)
        row = lambda i: vec[i : i + 1, :]
        after = dot(cbuf[2 * s, o], wout[:half]) + dot(cbuf[2 * s + 1, o], wout[half : 2 * half])
        after = after + dot(cm[rows], wout[2 * half :]) + row(V_BOUT) + x[rows].astype(f32)
        n1, inv1 = centred(after)
        first = n1 * row(V_G1) + row(V_S1)
        low = first.astype(bf16)
        fnb[rows] = low
        parts = []
        for g in range(GROUPS):
            acc = jnp.zeros((BLOCK, gw), f32)
            for j in range(gf // CHUNK):
                cols = slice(g * gf + j * CHUNK, g * gf + (j + 1) * CHUNK)
                pre = dot(
                    low[:, g * gw : (g + 1) * gw],
                    wup[g * gw : (g + 1) * gw, j * CHUNK : (j + 1) * CHUNK],
                ) + bup[:, cols]
                cdf = 0.5 + 0.5 * lax.erf(pre * HALF_GELU)
                a = (pre * cdf).astype(bf16)
                act[rows, cols] = a
                slope[:, cols] = cdf + pre * (PDF * jnp.exp(pre * pre * -0.5))
                acc = acc + dot(a, wdown[cols])
            parts.append(acc)
        summed = jnp.concatenate(parts, axis=-1) + row(V_BDOWN) + first
        n2, inv2 = centred(summed)
        out[rows] = (n2 * row(V_G2) + row(V_S2)).astype(bf16)
        c = cot[rows].astype(f32)
        gs = norm_back(c * row(V_G2), n2, inv2)
        glow = gs.astype(bf16)
        gsb[rows] = glow
        parts = []
        for g in range(GROUPS):
            acc = jnp.zeros((BLOCK, gw), f32)
            for j in range(gf // CHUNK):
                cols = slice(g * gf + j * CHUNK, g * gf + (j + 1) * CHUNK)
                pre = dot_nt(glow[:, g * gw : (g + 1) * gw], wdown[cols]) * slope[:, cols]
                gbup[:, cols] += rows_sum(pre)
                p = pre.astype(bf16)
                gp[rows, cols] = p
                acc = acc + dot_nt(
                    p, wup[g * gw : (g + 1) * gw, j * CHUNK : (j + 1) * CHUNK]
                )
            parts.append(acc)
        gfirst = gs + jnp.concatenate(parts, axis=-1)
        ga = norm_back(gfirst * row(V_G1), n1, inv1)
        gafter[rows] = ga
        alow = ga.astype(bf16)
        gab[rows] = alow
        for h in range(2):
            dctx[2 * s + h, o] = dot_nt(alow, wout[h * half : (h + 1) * half]).astype(bf16)
        gmix[rows] = dot_nt(alow, wout[2 * half :])
        for i, v in (
            (V_BOUT, ga), (V_G1, gfirst * n1), (V_S1, gfirst), (V_BDOWN, gs), (V_G2, c * n2),
            (V_S2, c),
        ):
            vecg[i : i + 1, :] += rows_sum(v)
        return 0

    lax.fori_loop(0, total // BLOCK, block, 0)
    seqs = total // local
    for h in range(2):
        acc = jnp.zeros((half, width), f32)
        for s in range(seqs):
            acc = acc + dot_tn(cbuf[2 * s + h], gab[s * local : (s + 1) * local])
        gwout[h * half : (h + 1) * half] = acc.astype(bf16)
    gwout[2 * half :] = dot_tn(cm[...], gab[...]).astype(bf16)
    for g in range(GROUPS):
        for j in range(gf // CHUNK):
            cols = slice(g * gf + j * CHUNK, g * gf + (j + 1) * CHUNK)
            gwdown[cols] = dot_tn(act[:, cols], gsb[:, g * gw : (g + 1) * gw]).astype(bf16)
            gwup[g * gw : (g + 1) * gw, j * CHUNK : (j + 1) * CHUNK] = dot_tn(
                fnb[:, g * gw : (g + 1) * gw], gp[:, cols]
            ).astype(bf16)


def ffn(cbuf, cm, x, cot, wout, wup, wdown, vec, bup):
    f32, bf16 = jnp.float32, jnp.bfloat16
    total, width = x.shape
    shape = jax.ShapeDtypeStruct
    return pl.pallas_call(
        ffn_kernel,
        out_shape=[
            shape((total, width), bf16),
            shape((total, width), f32),
            shape(cbuf.shape, bf16),
            shape(cm.shape, f32),
            shape(wout.shape, bf16),
            shape(wup.shape, bf16),
            shape(wdown.shape, bf16),
            shape(vec.shape, f32),
            shape(bup.shape, f32),
        ],
        in_specs=[pl.BlockSpec(memory_space=pltpu.VMEM)] * 9,
        out_specs=[pl.BlockSpec(memory_space=pltpu.VMEM)] * 9,
        scratch_shapes=[
            pltpu.VMEM((total, FF), bf16),
            pltpu.VMEM((BLOCK, FF), f32),
            pltpu.VMEM((total, FF), bf16),
            pltpu.VMEM((total, width), bf16),
            pltpu.VMEM((total, width), bf16),
            pltpu.VMEM((total, width), bf16),
        ],
        compiler_params=pltpu.CompilerParams(vmem_limit_bytes=VMEM_CAP),
        name="ffn",
    )(cbuf, cm, x, cot, wout, wup, wdown, vec, bup)


HEADS_PER = HEADS // 2
PART = HEADS_PER * HEAD
EDGE = 8
TAPS = KERNEL
CHAN = HEADS * HEAD


def iota(shape, dim):
    return lax.broadcasted_iota(jnp.int32, shape, dim)


def expander(rows, cols, width):
    return (iota((rows, cols), 1) % width == iota((rows, cols), 0)).astype(jnp.bfloat16)


def owned(stack, width):
    keep = iota(stack.shape, 2) // width == iota(stack.shape, 0)
    return jnp.sum(jnp.where(keep, stack, 0.0), axis=0)


def unpack_small(gsmall, vec, bproj, bup, widths):
    n = gsmall.shape[0]
    w, wp, wu = widths
    flat = gsmall[:, :2].reshape(n * 16, 128).astype(jnp.bfloat16)
    cols = vec.shape[1]
    vec[...] = owned(dot(flat, expander(128, cols, w)).reshape(n, 16, cols), w)
    flat = gsmall[:, 2].reshape(n * 8, 128).astype(jnp.bfloat16)
    cols = bproj.shape[1]
    bproj[...] = owned(dot(flat, expander(128, cols, wp)).reshape(n, 8, cols), wp)[:1]
    cols = bup.shape[1]
    bup[...] = owned(dot(flat, expander(128, cols, wu)).reshape(n, 8, cols), wu)[1:2]


def tap_logits(mixed, wkx, bkx, logits):
    for t in range(TAPS):
        logits[t] = dot(mixed, wkx[t]) + bkx[t : t + 1]


def softmax_taps(logits, rows):
    ls = [logits[t, rows] for t in range(TAPS)]
    top = ls[0]
    for v in ls[1:]:
        top = jnp.maximum(top, v)
    es = [jnp.exp(v - top) for v in ls]
    total = es[0]
    for v in es[1:]:
        total = total + v
    inv = 1.0 / total
    return [e * inv for e in es]


def expand_kernel_weights(w_kernel, b_kernel, wkx, bkx):
    cols = wkx.shape[2]
    wk, bk = w_kernel[...], b_kernel[...]
    for t in range(TAPS):
        k = wk.shape[1]
        pick = (iota((k, cols), 0) == iota((k, cols), 1) // HEAD * TAPS + t).astype(jnp.bfloat16)
        wkx[t] = dot(wk, pick).astype(jnp.bfloat16)
        bkx[t : t + 1] = dot(bk, pick)


def load_whole(gathered, whole, sem):
    cp = pltpu.make_async_copy(gathered.reshape(whole.shape), whole, sem)
    cp.start()
    return cp


ROW = 16


def front_kernel(
    dp, seq, widths,
    x, wproj, wout, wup, wdown, small, w_kernel, b_kernel,
    gqkv, gcp, gout, gup, gdown,
    qh, kh, vh, stats, cbuf, cm, qn, xe, convin, keyconv, mixed, spread, vec, bup, wkx, bkx,
    pqkv, pcp, gsmall, wq, wcp, xf, edges, inedge, qkv, abuf, csend, logits, bproj,
    ssem, rsem, lsem, asend, arecv, bsend, brecv, esend, erecv, wsem,
):
    f32, bf16 = jnp.float32, jnp.bfloat16
    grid = Grid(dp, seq)
    z, Z = grid.z, seq
    seqs, local, width = x.shape
    total = seqs * local

    w = wproj[...].astype(f32)
    cols = []
    for h in range(2):
        for p in range(3):
            at = p * CHAN + h * PART
            cols.append(w[:, at : at + PART])
    shard = pqkv.shape
    pqkv[...] = jnp.concatenate(cols, axis=1).reshape(shard).astype(bf16)
    pcp[...] = w[:, 3 * CHAN :].reshape(pcp.shape).astype(bf16)
    for s in range(seqs):
        edges[0, s] = x[s, :EDGE].astype(f32)
        edges[1, s] = x[s, local - EDGE :].astype(f32)

    entry_barrier(grid)
    mk = lambda i, src, buf, order: Gather(
        grid, src, buf, order, ssem.at[i], rsem.at[i], lsem.at[i]
    )
    gs = mk(0, small, gsmall, "zxyc")
    g1 = mk(1, pqkv, gqkv, "zxyc")
    g2 = mk(2, pcp, gcp, "zyxc")
    g3 = mk(3, wout, gout, "zyxc")
    g4 = mk(4, wup, gup, "zxyc")
    g5 = mk(5, wdown, gdown, "zyxc")
    gs.start()
    g1.start()
    g2.start()
    hops = []
    for i, o in ((0, seq - 1), (1, 1)):
        cp = pltpu.make_async_remote_copy(
            src_ref=edges.at[i], dst_ref=inedge.at[i], send_sem=esend.at[i],
            recv_sem=erecv.at[i], device_id=grid.dev(z=o), device_id_type=MESH,
        )
        cp.start()
        hops.append(cp)
    expand_kernel_weights(w_kernel, b_kernel, wkx, bkx)
    gs.step1()
    g1.step1()
    g2.step1()
    g3.start()
    gs.step2()
    g1.step2()
    g2.step2()
    gs.step3()
    g1.step3()
    g2.step3()
    gs.step4()
    unpack_small(gsmall, vec, bproj, bup, widths)
    g1.step4()
    c1 = load_whole(gqkv, wq, wsem.at[0])
    g3.step1()
    g4.start()
    c1.wait()

    bias = bproj[...]
    zero = jnp.zeros((1, PART), f32)
    qkv_bias = jnp.concatenate(
        [bias[:, 0:PART], zero, bias[:, CHAN : CHAN + PART],
         bias[:, PART:CHAN], zero, bias[:, CHAN + PART : 2 * CHAN]], axis=1,
    )
    for s in range(seqs):
        val = (dot(x[s], wq[...]) + qkv_bias).astype(bf16)
        rows = slice(s * local, (s + 1) * local)
        qkv[2 * s] = val[:, : 3 * PART]
        qkv[2 * s + 1] = val[:, 3 * PART :]
        qn[rows] = jnp.concatenate([val[:, :PART], val[:, 3 * PART : 4 * PART]], axis=1)
    sends = []
    for o in range(1, Z):
        to = (z + o) % Z
        cp = pltpu.make_async_remote_copy(
            src_ref=qkv.at[to], dst_ref=abuf.at[z], send_sem=asend.at[o - 1],
            recv_sem=arecv.at[o - 1], device_id=grid.dev(z=o), device_id_type=MESH,
        )
        cp.start()
        sends.append(cp)
    abuf[z] = qkv[z]

    g2.step4()
    c2 = load_whole(gcp, wcp, wsem.at[1])
    g3.step2()
    for cp in hops:
        cp.wait_recv()
    for s in range(seqs):
        top = jnp.where(z > 0, inedge[1, s], 0.0)
        low = jnp.where(z < Z - 1, inedge[0, s], 0.0)
        xf[s, :EDGE] = top
        xf[s, EDGE : EDGE + local] = x[s].astype(f32)
        xf[s, EDGE + local :] = low
        xe[s] = xf[s].astype(bf16)
    ext = local + 2 * EDGE
    spread_rows(xf, vec, spread, seqs, local)
    c2.wait()
    at = iota((ext, 1), 0)
    inside = ((at >= EDGE) | (z > 0)) & ((at < EDGE + local) | (z < Z - 1))
    for s in range(seqs):
        val = dot(xe[s], wcp[:, :CHAN]) + bias[:, 2 * CHAN : 3 * CHAN]
        convin[s] = jnp.where(inside, val, 0.0)
    for s in range(seqs):
        rows = slice(s * local, (s + 1) * local)
        kc = dot(spread[rows], wcp[:, CHAN:]) + bias[:, 3 * CHAN :]
        keyconv[rows] = kc
        mixed[rows] = (kc * qn[rows].astype(f32)).astype(bf16)
    g3.step3()
    g4.step1()
    g5.start()
    for s in range(seqs):
        tap_logits(mixed[s * local : (s + 1) * local], wkx, bkx, logits)

        def mix(i, _):
            r = pl.ds(pl.multiple_of(i * ROW, ROW), ROW)
            win = convin[s, pl.ds(pl.multiple_of(i * ROW, ROW), 2 * ROW)]
            tw = softmax_taps(logits, r)
            acc = jnp.zeros((ROW, CHAN), f32)
            for t in range(TAPS):
                a = EDGE - TAPS // 2 + t
                acc = acc + tw[t] * win[a : a + ROW]
            cm[pl.ds(pl.multiple_of(s * local + i * ROW, ROW), ROW)] = acc.astype(bf16)
            return 0

        lax.fori_loop(0, local // ROW, mix, 0)
    g4.step2()
    g5.step1()

    for o in range(1, Z):
        sends[o - 1].wait_recv()
    for b in range(Z):
        val = abuf[b]
        rows = slice(b * local, (b + 1) * local)
        for h in range(HEADS_PER):
            for p, ref in enumerate((qh, kh, vh)):
                ref[h, rows] = val[:, p * PART + h * HEAD : p * PART + (h + 1) * HEAD]
    sends += attend_units(grid, qh, kh, vh, stats, csend, cbuf, bsend, brecv)
    g4.step3()
    g5.step2()
    g5.step3()
    g3.step4()
    g4.step4()
    g5.step4()
    for cp in sends[Z - 1 :]:
        cp.wait_recv()
    for cp in sends + hops:
        cp.wait_send()
    for g in (gs, g1, g2, g3, g4, g5):
        g.finish()


def spread_rows(xf, vec, spread, seqs, local):
    width = xf.shape[2]
    step = 256

    def body(i, _):
        for s in range(seqs):
            for c in range(width // step):
                cols = slice(c * step, (c + 1) * step)
                win = xf[s, pl.ds(pl.multiple_of(i * ROW, ROW), 2 * ROW), cols]
                acc = jnp.zeros((ROW, step), jnp.float32)
                for t in range(TAPS):
                    a = EDGE - TAPS // 2 + t
                    acc = acc + win[a : a + ROW] * vec[t : t + 1, cols]
                r = pl.ds(pl.multiple_of(s * local + i * ROW, ROW), ROW)
                spread[r, cols] = acc.astype(spread.dtype)
        return 0

    lax.fori_loop(0, local // ROW, body, 0)


def attend_units(grid, qh, kh, vh, stats, csend, cbuf, bsend, brecv):
    f32, bf16 = jnp.float32, jnp.bfloat16
    z, Z = grid.z, grid.Z
    local = csend.shape[1]
    sends = []
    scale = jnp.asarray(HEAD ** (-0.5), bf16)
    for o in list(range(1, Z)) + [0]:
        b = (z + o) % Z
        rows = pl.ds(pl.multiple_of(b * local, local), local)
        outs = []
        for h in range(HEADS_PER):
            st = dot_nt(kh[h], qh[h, rows] * scale)
            top = jnp.max(st, axis=0, keepdims=True)
            e = jnp.exp(st - top)
            den = jnp.sum(e, axis=0, keepdims=True)
            stats[h, b] = top + jnp.log(den)
            ct = dot_tn(vh[h], e.astype(bf16)) / den
            outs.append(ct.T)
        val = jnp.concatenate(outs, axis=1).astype(bf16)
        if o:
            csend[o - 1] = val
            cp = pltpu.make_async_remote_copy(
                src_ref=csend.at[o - 1], dst_ref=cbuf.at[z], send_sem=bsend.at[o - 1],
                recv_sem=brecv.at[o - 1], device_id=grid.dev(z=o), device_id_type=MESH,
            )
            cp.start()
            sends.append(cp)
        else:
            cbuf[z] = val
    return sends


def front(dp, seq, x, w_proj, w_out, w_up, w_down, small, w_kernel, b_kernel, widths):
    f32, bf16 = jnp.float32, jnp.bfloat16
    seqs, local, width = x.shape
    total = seqs * local
    length = seq * local
    N = dp * seq
    rows = w_proj.shape[0]
    lead = tiled(w_proj).shape[:2]
    shape = jax.ShapeDtypeStruct
    wide = 6 * PART
    ext = local + 2 * EDGE
    vm = pl.BlockSpec(memory_space=pltpu.VMEM)
    hb = pl.BlockSpec(memory_space=pl.ANY)
    other = [tiled(a) for a in (w_out, w_up, w_down)]
    hbm_out = [shape((N,) + lead + (wide,), bf16), shape((N,) + lead + (2 * CHAN,), bf16)]
    hbm_out += [shape((N,) + a.shape, bf16) for a in other]
    vm_out = [
        shape((HEADS_PER, length, HEAD), bf16),
        shape((HEADS_PER, length, HEAD), bf16),
        shape((HEADS_PER, length, HEAD), bf16),
        shape((HEADS_PER, seq, 1, local), f32),
        shape((seq, local, PART), bf16),
        shape((total, CHAN), bf16),
        shape((total, CHAN), bf16),
        shape((seqs, ext, width), bf16),
        shape((seqs, ext, CHAN), f32),
        shape((total, CHAN), f32),
        shape((total, CHAN), bf16),
        shape((total, width), bf16),
        shape((16, width), f32),
        shape((1, FF), f32),
        shape((TAPS, CHAN, CHAN), bf16),
        shape((16, CHAN), f32),
    ]
    sem = lambda *s: pltpu.SemaphoreType.DMA(s)
    return pl.pallas_call(
        partial(front_kernel, dp, seq, widths),
        out_shape=hbm_out + vm_out,
        in_specs=[vm, vm, hb, hb, hb, vm, vm, vm],
        out_specs=[hb] * len(hbm_out) + [vm] * len(vm_out),
        scratch_shapes=[
            pltpu.VMEM(lead + (wide,), bf16),
            pltpu.VMEM(lead + (2 * CHAN,), bf16),
            pltpu.VMEM((N,) + small.shape, f32),
            pltpu.VMEM((width, wide), bf16),
            pltpu.VMEM((width, 2 * CHAN), bf16),
            pltpu.VMEM((seqs, ext, width), f32),
            pltpu.VMEM((2, seqs, EDGE, width), f32),
            pltpu.VMEM((2, seqs, EDGE, width), f32),
            pltpu.VMEM((seq, local, 3 * PART), bf16),
            pltpu.VMEM((seq, local, 3 * PART), bf16),
            pltpu.VMEM((seq - 1, local, PART), bf16),
            pltpu.VMEM((TAPS, local, CHAN), f32),
            pltpu.VMEM((1, 4 * CHAN), f32),
            sem(6, N - 1), sem(6, N - 1), sem(6),
            sem(seq - 1), sem(seq - 1), sem(seq - 1), sem(seq - 1), sem(2), sem(2), sem(2),
        ],
        compiler_params=pltpu.CompilerParams(
            collective_id=2, has_side_effects=True, vmem_limit_bytes=VMEM_CAP
        ),
        name="front",
    )(x, w_proj, *other, small, w_kernel, b_kernel)


def pack_small(w_depth, vectors, b_proj, b_up):
    rows = [(i, v) for i, v in enumerate([w_depth[:, t] for t in range(TAPS)] + list(vectors))]
    rows += [(16, b_proj), (17, b_up)]
    out = jnp.zeros((24, 128), jnp.float32)
    for i, v in rows:
        out = out + jnp.pad(v.astype(jnp.float32)[None], ((i, 23 - i), (0, 128 - v.shape[0])))
    return out.reshape(3, 8, 128)


def unhalve(w):
    w = w.reshape(w.shape[:-1] + (2, 3, PART))
    return jnp.swapaxes(w, -3, -2).reshape(w.shape[:-3] + (3 * CHAN,))


PAD = 16


def to_owners(v, width, n):
    r, cols = v.shape
    keep = iota((n, r, cols), 2) // width == iota((n, r, cols), 0)
    stack = jnp.where(keep, v[None], 0.0).reshape(n * r, cols)
    pick = (iota((128, cols), 1) % width == iota((128, cols), 0)).astype(jnp.float32)
    out = lax.dot_general(
        stack, pick, (((1,), (1,)), ((), ())), precision=lax.Precision.HIGHEST,
        preferred_element_type=jnp.float32,
    )
    return out.reshape(n, r, 128)


def conv_back(
    s, local, gmix, convin, keyconv, mixed, qn, wkx, bkx, wkp, wpt,
    tw, gt, gl, gpad, gsp, gqm, gk, gci_ext, gwk, gbk, gbpoint,
):
    f32, bf16 = jnp.float32, jnp.bfloat16
    rows = slice(s * local, (s + 1) * local)
    body_rows = slice(PAD, PAD + local)
    for t in range(TAPS):
        tw[t, body_rows] = dot(mixed[rows], wkx[t]) + bkx[t : t + 1]
    gpad[body_rows] = gmix[rows]
    same = (iota((CHAN, CHAN), 0) // HEAD == iota((CHAN, CHAN), 1) // HEAD).astype(bf16)
    for t in range(TAPS):
        a = EDGE - TAPS // 2 + t
        p = gmix[rows] * convin[s, a : a + local]
        hi = p.astype(bf16)
        lo = (p - hi.astype(f32)).astype(bf16)
        gt[t] = dot(hi, same) + dot(lo, same)

    def taps(i, _):
        r = pl.ds(pl.multiple_of(i * ROW, ROW), ROW)
        rp = pl.ds(pl.multiple_of(PAD + i * ROW, ROW), ROW)
        ws = softmax_taps(tw, rp)
        gs = [gt[t, r] for t in range(TAPS)]
        mean = ws[0] * gs[0]
        for t in range(1, TAPS):
            mean = mean + ws[t] * gs[t]
        for t in range(TAPS):
            tw[t, rp] = ws[t]
            g = ws[t] * (gs[t] - mean)
            gl[t, r] = g.astype(bf16)
            gbk[t] += g[:8] + g[8:]
        return 0

    lax.fori_loop(0, local // ROW, taps, 0)

    def spread_back(i, _):
        w = pl.ds(pl.multiple_of(i * ROW, ROW), 2 * ROW)
        g = gpad[w]
        acc = jnp.zeros((ROW, CHAN), f32)
        for t in range(TAPS):
            a = PAD - TAPS // 2 - t
            acc = acc + (tw[t, w] * g)[a : a + ROW]
        gci_ext[s, pl.ds(pl.multiple_of(i * ROW, ROW), ROW)] = acc
        return 0

    lax.fori_loop(0, (local + 2 * EDGE) // ROW, spread_back, 0)
    compact = jnp.zeros((local, 128), f32)
    for t in range(TAPS):
        pick = (
            (iota((CHAN, 128), 0) == iota((CHAN, 128), 1) // TAPS * HEAD)
            & (iota((CHAN, 128), 1) % TAPS == t)
            & (iota((CHAN, 128), 1) < HEADS * TAPS)
        ).astype(bf16)
        compact = compact + dot(gl[t], pick)
    low = compact.astype(bf16)
    gwk[...] += dot_tn(mixed[rows], low)
    gmixed = dot_nt(low, wkp[...])
    gqm[rows] = gmixed * keyconv[rows]
    gkc = gmixed * qn[rows].astype(f32)
    gbpoint[...] += rows_sum(gkc)
    glow = gkc.astype(bf16)
    gk[rows] = glow
    gsp[s, body_rows] = dot_nt(glow, wpt)


def depth_back(local, seqs, gsp, xe, vec, gdx_ext, gwd):
    f32 = jnp.float32
    width = gsp.shape[2]
    step = 256

    def grads(i, _):
        w = pl.ds(pl.multiple_of(i * ROW, ROW), 2 * ROW)
        for s in range(seqs):
            for c in range(width // step):
                cols = slice(c * step, (c + 1) * step)
                g = gsp[s, w, cols]
                acc = jnp.zeros((ROW, step), f32)
                for t in range(TAPS):
                    a = PAD - TAPS // 2 - t
                    acc = acc + g[a : a + ROW] * vec[t : t + 1, cols]
                gdx_ext[s, pl.ds(pl.multiple_of(i * ROW, ROW), ROW), cols] = acc
        return 0

    lax.fori_loop(0, (local + 2 * EDGE) // ROW, grads, 0)

    def weights(i, _):
        w = pl.ds(pl.multiple_of(i * ROW, ROW), 2 * ROW)
        for s in range(seqs):
            for c in range(width // step):
                cols = slice(c * step, (c + 1) * step)
                win = xe[s, w, cols].astype(f32)
                g = gsp[s, pl.ds(pl.multiple_of(PAD + i * ROW, ROW), ROW), cols]
                for t in range(TAPS):
                    a = EDGE - TAPS // 2 + t
                    p = win[a : a + ROW] * g
                    gwd[t, :, cols] += p[:8] + p[8:]
        return 0

    lax.fori_loop(0, local // ROW, weights, 0)


def attend_back_block(b, h, qh, kh, vh, kt, stats, dbuf, dqb, dkv, local, first):
    f32, bf16 = jnp.float32, jnp.bfloat16
    scale = HEAD ** (-0.5)
    rows = pl.ds(pl.multiple_of(b * local, local), local)
    q = qh[h, rows]
    do = dbuf[b][:, h * HEAD : (h + 1) * HEAD]
    st = dot_nt(kh[h], q * jnp.asarray(scale, bf16))
    p = jnp.exp(st - stats[h, b])
    dp = dot_nt(vh[h], do)
    delta = jnp.sum(p * dp, axis=0, keepdims=True)
    ds = (p * (dp - delta)).astype(bf16)
    dk = dot(ds, q)
    dv = dot(p.astype(bf16), do)
    if first:
        dkv[0, h] = dk
        dkv[1, h] = dv
    else:
        dkv[0, h] += dk
        dkv[1, h] += dv
    return (dot(kt[h], ds) * scale).T


def back_kernel(
    dp, seq, widths,
    dctx, qh, kh, vh, stats, gmix, convin, keyconv, mixed, qn, spread, xe, vec, wkx, bkx, w_kernel,
    vecg, gbup, gafter, gqkv, gcp, gwdown, gwup, gwout,
    gx, o_proj, o_depth, o_kernel, o_bkernel, o_out, o_up, o_down, o_bproj, o_bup, o_vecs,
    *rest,
):
    f32, bf16 = jnp.float32, jnp.bfloat16
    pieces = 7
    parts, rest = rest[:pieces], rest[pieces:]
    bufs, rest = rest[: 4 * pieces], rest[4 * pieces :]
    souts, rest = (o_down, o_up, o_out) + rest[:4], rest[4:]
    (
        dbuf, gsend, grecv, wq, wcp, grads, tw, gt, gl, gpad, gsp, gqm, gk, gci_ext, gcl, gdx_ext,
        gwd, gwk, gbk, gbpoint, wkp, hsend, hrecv, kt, dqb, dkv, ktail, kall, vsum, bprow,
        ssem, rsem, gssem, grsem, lsem, asend, arecv, bsend, brecv, esend, erecv, wsem,
    ) = rest
    grid = Grid(dp, seq)
    z, Z = grid.z, seq
    N = dp * seq
    seqs = xe.shape[0]
    local = dctx.shape[1]
    total = seqs * local
    width = xe.shape[2]
    w1, wp, wu = widths

    loads = [
        pltpu.make_async_copy(src, dst, wsem.at[i])
        for i, (src, dst) in enumerate(
            ((gwdown, parts[0]), (gwup, parts[1]), (gwout, parts[2]))
        )
    ]
    loads.append(pltpu.make_async_copy(gcp.reshape(wcp.shape), wcp, wsem.at[3]))
    loads.append(pltpu.make_async_copy(gqkv.reshape(wq.shape), wq, wsem.at[4]))
    loads.append(pltpu.make_async_copy(gafter, gx, wsem.at[5]))
    for cp in loads:
        cp.start()
    entry_barrier(grid)
    sends = []
    for o in range(1, Z):
        to = (z + o) % Z
        cp = pltpu.make_async_remote_copy(
            src_ref=dctx.at[to], dst_ref=dbuf.at[z], send_sem=bsend.at[o - 1],
            recv_sem=brecv.at[o - 1], device_id=grid.dev(z=o), device_id_type=MESH,
        )
        cp.start()
        sends.append(cp)
    dbuf[z] = dctx[z]
    sc = [
        Scatter(
            grid, parts[i], ("zxyc", "zyxc", "zxyc", "zyxc", "zxyc", "zyxc", "zxyc")[i],
            bufs[4 * i : 4 * i + 4], souts[i], ssem.at[i], rsem.at[i],
        )
        for i in range(pieces)
    ]
    sdown, sup, sout, scp, sqkv, skern, svec = sc
    for i in range(3):
        loads[i].wait()
        sc[i].start()

    wk = w_kernel[...]
    wkp[...] = dot(
        wk, (iota((wk.shape[1], 128), 0) == iota((wk.shape[1], 128), 1)).astype(bf16)
    ).astype(bf16)
    gwk[...] = jnp.zeros_like(gwk)
    gbk[...] = jnp.zeros_like(gbk)
    gwd[...] = jnp.zeros_like(gwd)
    gbpoint[...] = jnp.zeros_like(gbpoint)
    gpad[...] = jnp.zeros_like(gpad)
    zeros = jnp.zeros((PAD, CHAN), f32)
    for t in range(TAPS):
        tw[t, :PAD] = zeros
        tw[t, PAD + local :] = zeros
    zeros = jnp.zeros((PAD, width), f32)
    for s in range(seqs):
        gsp[s, :PAD] = zeros
        gsp[s, PAD + local :] = zeros
    loads[3].wait()
    wpt = wcp[:, CHAN:]
    for s in range(seqs):
        conv_back(
            s, local, gmix, convin, keyconv, mixed, qn, wkx, bkx, wkp, wpt,
            tw, gt, gl, gpad, gsp, gqm, gk, gci_ext, gwk, gbk, gbpoint,
        )
        if s == 0:
            sdown.step1()
    depth_back(local, seqs, gsp, xe, vec, gdx_ext, gwd)
    for i, at in ((0, 0), (1, EDGE + local)):
        for s in range(seqs):
            hsend[i, s, :, :CHAN] = gci_ext[s, at : at + EDGE]
            hsend[i, s, :, CHAN:] = gdx_ext[s, at : at + EDGE]
    hops = []
    for i, o in ((0, seq - 1), (1, 1)):
        cp = pltpu.make_async_remote_copy(
            src_ref=hsend.at[i], dst_ref=hrecv.at[i], send_sem=esend.at[i],
            recv_sem=erecv.at[i], device_id=grid.dev(z=o), device_id_type=MESH,
        )
        cp.start()
        hops.append(cp)
    rows = parts[5].shape[0] * parts[5].shape[1] * 8
    bias_row = jnp.zeros((1, 128), f32)
    for t in range(TAPS):
        pick = (
            (iota((CHAN, 128), 0) == iota((CHAN, 128), 1) // TAPS * HEAD)
            & (iota((CHAN, 128), 1) % TAPS == t)
            & (iota((CHAN, 128), 1) < HEADS * TAPS)
        ).astype(f32)
        bias_row = bias_row + jnp.dot(
            rows_sum(gbk[t]), pick, precision=lax.Precision.HIGHEST, preferred_element_type=f32
        )
    tail = jnp.where(iota((rows - CHAN, 128), 0) == 0, bias_row, 0.0)
    parts[5][...] = jnp.concatenate([gwk[...], tail], axis=0).reshape(parts[5].shape)
    skern.start()
    sup.step1()
    sout.step1()
    sdown.step2()
    gw = dot_tn(spread[...], gk[...])
    gate = lambda v: v.reshape(parts[3].shape[:3] + (CHAN,)).astype(bf16)
    parts[3][:, :, :, CHAN:] = gate(gw)

    for h in range(HEADS_PER):
        kt[h] = kh[h].T
    for n, o in enumerate(range(Z)):
        b = (z + Z - o) % Z
        if o:
            sends[o - 1].wait_recv()
        outs = [
            attend_back_block(b, h, qh, kh, vh, kt, stats, dbuf, dqb, dkv, local, n == 0)
            for h in range(HEADS_PER)
        ]
        dqb[b] = jnp.concatenate(outs, axis=1).astype(bf16)
        if n == 0:
            sup.step2()
            sout.step2()
            sdown.step3()
            skern.step1()
        if n == 1:
            sup.step3()
            sout.step3()
            skern.step2()
            sdown.step4()
        if n == 2:
            skern.step3()
            sup.step4()
            sout.step4()
    scale = HEAD ** (-0.5)
    back = []
    for o in list(range(1, Z)) + [0]:
        b = (z + o) % Z
        r = pl.ds(pl.multiple_of(b * local, local), local)
        val = jnp.concatenate(
            [dqb[b]]
            + [(dkv[0, h, r] * scale).astype(bf16) for h in range(HEADS_PER)]
            + [dkv[1, h, r].astype(bf16) for h in range(HEADS_PER)],
            axis=1,
        )
        if o:
            gsend[o - 1] = val
            cp = pltpu.make_async_remote_copy(
                src_ref=gsend.at[o - 1], dst_ref=grecv.at[z], send_sem=asend.at[o - 1],
                recv_sem=arecv.at[o - 1], device_id=grid.dev(z=o), device_id_type=MESH,
            )
            cp.start()
            back.append(cp)
        else:
            grecv[z] = val

    for cp in hops:
        cp.wait_recv()
    gbconv = jnp.zeros((1, CHAN), f32)
    for s in range(seqs):
        for i, at, ok in ((0, local, z < Z - 1), (1, EDGE, z > 0)):
            add = jnp.where(ok, hrecv[i, s], 0.0)
            gci_ext[s, at : at + EDGE] += add[:, :CHAN]
            gdx_ext[s, at : at + EDGE] += add[:, CHAN:]
        own = gci_ext[s, EDGE : EDGE + local]
        gbconv = gbconv + rows_sum(own)
        gcl[s * local : (s + 1) * local] = own.astype(bf16)
    xs = [xe[s, EDGE : EDGE + local] for s in range(seqs)]
    gw = jnp.zeros((width, CHAN), f32)
    for s in range(seqs):
        gw = gw + dot_tn(xs[s], gcl[s * local : (s + 1) * local])
    parts[3][:, :, :, :CHAN] = gate(gw)
    scp.start()
    loads[5].wait()
    for s in range(seqs):
        r = slice(s * local, (s + 1) * local)
        gx[r] += gdx_ext[s, EDGE : EDGE + local] + dot_nt(gcl[r], wcp[:, :CHAN])
    taps = jnp.concatenate([rows_sum(gwd[t]) for t in range(TAPS)], axis=0)
    head = jnp.concatenate([taps, vecg[TAPS:16]], axis=0)
    own = to_owners(head, w1, N)
    parts[6][:, 0] = own[:, :8]
    parts[6][:, 1] = own[:, 8:]
    up_rows = to_owners(jnp.where(iota((8, FF), 0) == 1, gbup[...], 0.0), wu, N)
    scp.step1()
    skern.step4()
    gk_tail = Gather(grid, souts[5], kall, "zxyc", gssem, grsem, lsem)
    gk_tail.start()
    gk_tail.step1()
    scp.step2()
    gk_tail.step2()

    loads[4].wait()
    for cp in back:
        cp.wait_recv()
    sums = [jnp.zeros((1, PART), f32) for _ in range(4)]
    for s in range(seqs):
        r = slice(s * local, (s + 1) * local)
        vals = []
        for h in range(2):
            val = grecv[2 * s + h]
            q = (
                val[:, :PART].astype(f32) + gqm[r, h * PART : (h + 1) * PART]
            ).astype(bf16)
            sums[h] = sums[h] + rows_sum(q.astype(f32))
            sums[2 + h] = sums[2 + h] + rows_sum(val[:, 2 * PART :].astype(f32))
            vals += [q, val[:, PART:]]
        grads[r] = jnp.concatenate(vals, axis=1)
    step = width // 2
    for c in range(2):
        cols = slice(c * step, (c + 1) * step)
        gw = jnp.zeros((step, 6 * PART), f32)
        for s in range(seqs):
            gw = gw + dot_tn(xe[s, EDGE : EDGE + local, cols], grads[s * local : (s + 1) * local])
        n = N // 2
        parts[4][c * n : (c + 1) * n] = gw.reshape((n,) + parts[4].shape[1:]).astype(bf16)
    sqkv.start()
    bprow[...] = jnp.concatenate(sums + [gbconv, gbpoint[...]], axis=1)
    own = to_owners(jnp.where(iota((8, 4 * CHAN), 0) == 0, bprow[...], 0.0), wp, N)
    parts[6][:, 2] = own + up_rows
    svec.start()
    for s in range(seqs):
        r = slice(s * local, (s + 1) * local)
        gx[r] += dot_nt(grads[r], wq[...])
    sqkv.step1()
    svec.step1()
    scp.step3()
    gk_tail.step3()
    sqkv.step2()
    svec.step2()
    scp.step4()
    gk_tail.step4()
    sqkv.step3()
    svec.step3()
    every = kall[...].reshape(rows, 128)
    o_kernel[...] = every[:CHAN, : HEADS * TAPS]
    o_bkernel[...] = every[CHAN : CHAN + 1, : HEADS * TAPS]
    sqkv.step4()
    svec.step4()
    flat = souts[4][...].reshape(w1, 6 * PART)
    cols = []
    for p in range(3):
        for h in range(2):
            cols.append(flat[:, h * 3 * PART + p * PART : h * 3 * PART + (p + 1) * PART])
    o_proj[:, : 3 * CHAN] = jnp.concatenate(cols, axis=1)
    o_proj[:, 3 * CHAN :] = souts[3][...].reshape(w1, 2 * CHAN)
    small = souts[6][...]
    o_depth[...] = small[:2].reshape(16, 128).T[:w1, :TAPS]
    o_vecs[...] = small[1]
    o_bproj[...] = small[2, 0:1, :wp]
    o_bup[...] = small[2, 1:2, :wu]
    for cp in sends + back + hops:
        cp.wait_send()
    for g in sc:
        g.finish()
    gk_tail.finish()


def back(dp, seq, widths, values, gathered, wgrads, shards):
    f32, bf16 = jnp.float32, jnp.bfloat16
    (
        dctx, qh, kh, vh, stats, gmix, convin, keyconv, mixed, qn, spread, xe, vec, wkx, bkx,
        w_kernel, vecg, gbup,
    ) = values
    N = dp * seq
    w1, wp, wu = widths
    seqs, ext, width = xe.shape
    local = dctx.shape[1]
    total = seqs * local
    length = kh.shape[1]
    sizes = sizes_of(dp, seq)
    shape = jax.ShapeDtypeStruct
    vm = pl.BlockSpec(memory_space=pltpu.VMEM)
    hb = pl.BlockSpec(memory_space=pl.ANY)
    t_down, t_up, t_out = [tiled(a).shape for a in shards]
    lead = t_out[:2]
    kr = -(-(CHAN + 1) // (8 * N))
    piece = [
        (t_down, bf16), (t_up, bf16), (t_out, bf16), (lead + (2 * CHAN,), bf16),
        (lead + (6 * PART,), bf16), ((kr, 8, 128), f32), ((3, 8, 128), f32),
    ]
    wgrads = [g.reshape((N,) + p[0]) for g, p in zip(wgrads, piece)]
    scratch = [pltpu.VMEM((N,) + p, d) for p, d in piece]
    for p, d in piece:
        scratch += scatter_scratch(sizes, p, d, "zxyc")
    scratch += [pltpu.VMEM(p, f32) for p, d in piece[3:]]
    V = pltpu.VMEM
    scratch += [
        V((seq, local, PART), bf16),
        V((seq - 1, local, 3 * PART), bf16),
        V((seq, local, 3 * PART), bf16),
        V((width, 6 * PART), bf16),
        V((width, 2 * CHAN), bf16),
        V((total, 6 * PART), bf16),
        V((TAPS, local + 2 * PAD, CHAN), f32),
        V((TAPS, local, CHAN), f32),
        V((TAPS, local, CHAN), bf16),
        V((local + 2 * PAD, CHAN), f32),
        V((seqs, local + 2 * PAD, width), f32),
        V((total, CHAN), f32),
        V((total, CHAN), bf16),
        V((seqs, ext, CHAN), f32),
        V((total, CHAN), bf16),
        V((seqs, ext, width), f32),
        V((TAPS, 8, width), f32),
        V((CHAN, 128), f32),
        V((TAPS, 8, CHAN), f32),
        V((1, CHAN), f32),
        V((CHAN, 128), bf16),
        V((2, seqs, EDGE, CHAN + width), f32),
        V((2, seqs, EDGE, CHAN + width), f32),
        V((HEADS_PER, HEAD, length), bf16),
        V((seq, local, PART), bf16),
        V((2, HEADS_PER, length, HEAD), f32),
        V((kr, 8, 128), f32),
        V((N, kr, 8, 128), f32),
        V((1, 8, 128), f32),
        V((1, 4 * CHAN), f32),
    ]
    sem = lambda *s: pltpu.SemaphoreType.DMA(s)
    scratch += [
        sem(7, N - 1), sem(7, N - 1), sem(N - 1), sem(N - 1), sem(),
        sem(seq - 1), sem(seq - 1), sem(seq - 1), sem(seq - 1), sem(2), sem(2), sem(6),
    ]
    outs = [
        shape((total, width), f32),
        shape((w1, 5 * CHAN), f32),
        shape((w1, TAPS), f32),
        shape((CHAN, HEADS * TAPS), f32),
        shape((1, HEADS * TAPS), f32),
        shape(t_out, f32),
        shape(t_up, f32),
        shape(t_down, f32),
        shape((1, wp), f32),
        shape((1, wu), f32),
        shape((8, 128), f32),
    ]
    return pl.pallas_call(
        partial(back_kernel, dp, seq, widths),
        out_shape=outs,
        in_specs=[vm] * len(values) + [hb] * 6,
        out_specs=[vm] * len(outs),
        scratch_shapes=scratch,
        compiler_params=pltpu.CompilerParams(
            collective_id=3, has_side_effects=True, vmem_limit_bytes=62 << 20
        ),
        name="back",
    )(*values, *gathered, *wgrads)


def fast_body(
    hidden, cotangent, w_proj, w_depth, w_kernel, b_kernel, w_out, w_up, w_down, b_proj, b_up,
    b_out, ln1_gain, ln1_bias, b_down, ln2_gain, ln2_bias,
):
    dp, seq = lax.axis_size("dp"), lax.axis_size("seq")
    seqs, local, width = hidden.shape
    total = seqs * local
    widths = (w_out.shape[0], b_proj.shape[0], b_up.shape[0])
    small = pack_small(
        w_depth, (b_out, ln1_gain, ln1_bias, b_down, ln2_gain, ln2_bias), b_proj, b_up
    )
    (
        gqkv, gcp, gout, gup, gdown, qh, kh, vh, stats, cbuf, cm, qn, xe, convin, keyconv, mixed,
        spread, vec, bup, wkx, bkx,
    ) = front(
        dp, seq, hidden, w_proj, w_out, w_up, w_down, small, w_kernel, b_kernel[None], widths
    )
    out, gafter, dctx, gmix, gwout, gwup, gwdown, vecg, gbup = ffn(
        cbuf, cm, hidden.reshape(total, width), cotangent.reshape(total, width),
        gout.reshape(-1, w_out.shape[1]), gup.reshape(-1, w_up.shape[1]),
        gdown.reshape(-1, w_down.shape[1]), vec, bup,
    )
    (
        gx, g_proj, g_depth, g_kernel, g_bkernel, g_out, g_up, g_down, g_bproj, g_bup, g_vecs,
    ) = back(
        dp, seq, widths,
        (
            dctx, qh, kh, vh, stats, gmix, convin, keyconv, mixed, qn, spread, xe, vec, wkx, bkx,
            w_kernel, vecg, gbup,
        ),
        (gafter, gqkv, gcp), (gwdown, gwup, gwout), (w_down, w_up, w_out),
    )
    w1 = widths[0]
    vecs = [g_vecs[i - 8, :w1] for i in range(V_BOUT, V_S2 + 1)]
    return (
        out.reshape(hidden.shape),
        gx.reshape(hidden.shape),
        g_proj,
        g_depth,
        g_kernel,
        g_bkernel[0],
        g_out.reshape(w_out.shape),
        g_up.reshape(w_up.shape),
        g_down.reshape(w_down.shape),
        g_bproj[0],
        g_bup[0],
    ) + tuple(vecs)


def fits(mesh):
    return mesh.shape["seq"] == 4 and mesh.shape["dp"] == 8


def body(
    hidden,
    cotangent,
    w_proj,
    w_depth,
    w_kernel,
    b_kernel,
    w_out,
    w_up,
    w_down,
    b_proj,
    b_up,
    b_out,
    ln1_gain,
    ln1_bias,
    b_down,
    ln2_gain,
    ln2_bias,
):
    seq_count, local_rows, model_width = hidden.shape
    total_rows = seq_count * local_rows
    head_count = HEADS
    head_size = HEAD
    all_width = head_count * head_size
    tap_count = KERNEL
    half_kernel = KERNEL // 2
    group_count = GROUPS
    hidden_units = FF
    ext_rows = local_rows + 2 * half_kernel
    score_scale = head_size ** (-0.5)
    dp, seq = lax.axis_size("dp"), lax.axis_size("seq")
    devices = dp * seq
    vectors = (b_proj, b_up, b_out, ln1_gain, ln1_bias, b_down, ln2_gain, ln2_bias)
    widths = [w_depth.shape[0] * KERNEL] + [v.shape[0] for v in vectors]
    small = jnp.concatenate([w_depth.reshape(-1)] + list(vectors))
    small = jnp.pad(small, (0, 1024 - small.shape[0])).reshape(8, 128)
    full_proj, full_out, full_up, full_down, small = gather_all(
        dp, seq, [w_proj, w_out, w_up, w_down, small]
    )
    small = cut(small.reshape(devices, 1024), widths)
    full_depth = small[0].reshape(-1, KERNEL)
    (
        full_bproj,
        full_bup,
        full_bout,
        gain_one,
        shift_one,
        full_bdown,
        gain_two,
        shift_two,
    ) = [v.reshape(-1) for v in small[1:]]
    bias_proj = full_bproj.astype(jnp.float32)
    gain_first = gain_one.astype(jnp.float32)
    shift_first = shift_one.astype(jnp.float32)
    gain_second = gain_two.astype(jnp.float32)
    shift_second = shift_two.astype(jnp.float32)
    tokens_flat = hidden.reshape(total_rows, model_width)
    first_proj = jnp.dot(
        tokens_flat, full_proj[:, : 3 * all_width], preferred_element_type=jnp.float32
    )
    queries = (first_proj[:, :all_width] + bias_proj[:all_width]).astype(jnp.bfloat16)
    key_rows = first_proj[:, all_width : 2 * all_width].astype(jnp.bfloat16)
    value_rows = (first_proj[:, 2 * all_width :] + bias_proj[all_width : 2 * all_width]).astype(
        jnp.bfloat16
    )
    extended = with_halo(hidden, (("seq", 1),), half_kernel)
    position = lax.axis_index("seq") * local_rows + jnp.arange(ext_rows) - half_kernel
    inside = ((position >= 0) & (position < local_rows * lax.axis_size("seq"))).astype(jnp.float32)
    conv_input = jnp.dot(
        extended.reshape(seq_count * ext_rows, model_width),
        full_proj[:, 3 * all_width : 4 * all_width],
        preferred_element_type=jnp.float32,
    )
    conv_input = (conv_input + bias_proj[2 * all_width : 3 * all_width]).reshape(
        seq_count, ext_rows, all_width
    ) * inside[None, :, None]
    depth_weights = full_depth.astype(jnp.float32)
    depth_sum = jnp.zeros((seq_count, local_rows, model_width), jnp.float32)
    for tap_index in range(tap_count):
        depth_sum = (
            depth_sum
            + extended[:, tap_index : tap_index + local_rows].astype(jnp.float32)
            * depth_weights[:, tap_index]
        )
    spread = depth_sum.astype(jnp.bfloat16).reshape(total_rows, model_width)
    key_conv = (
        jnp.dot(spread, full_proj[:, 4 * all_width :], preferred_element_type=jnp.float32)
        + bias_proj[3 * all_width :]
    )
    mixed_key = (key_conv * queries.astype(jnp.float32)).astype(jnp.bfloat16)
    logits = jnp.dot(mixed_key, w_kernel, preferred_element_type=jnp.float32) + b_kernel.astype(
        jnp.float32
    )
    tap_weights = jax.nn.softmax(
        logits.reshape(seq_count, local_rows, head_count, tap_count), axis=-1
    )
    conv_heads = conv_input.reshape(seq_count, ext_rows, head_count, head_size)
    conv_mix = jnp.zeros((seq_count, local_rows, head_count, head_size), jnp.float32)
    for tap_index in range(tap_count):
        conv_mix = (
            conv_mix
            + tap_weights[..., tap_index, None] * conv_heads[:, tap_index : tap_index + local_rows]
        )
    queries_seq = queries.reshape(seq_count, local_rows, all_width)
    all_keys, all_values = (
        lax.all_gather(
            key_rows.reshape(seq_count, local_rows, all_width), "seq", axis=1, tiled=True
        ),
        lax.all_gather(
            value_rows.reshape(seq_count, local_rows, all_width), "seq", axis=1, tiled=True
        ),
    )
    full_length = all_keys.shape[1]

    def forward_one(item_set):
        query_seq, key_seq, value_seq = item_set
        return attend(
            query_seq.reshape(local_rows, head_count, head_size),
            key_seq.reshape(full_length, head_count, head_size),
            value_seq.reshape(full_length, head_count, head_size),
            score_scale,
        )

    context, norm_log = lax.map(forward_one, (queries_seq, all_keys, all_values))
    joined = jnp.concatenate(
        [
            context.reshape(total_rows, all_width),
            conv_mix.reshape(total_rows, all_width).astype(jnp.bfloat16),
        ],
        axis=-1,
    )
    after_mix = (
        jnp.dot(joined, full_out, preferred_element_type=jnp.float32)
        + full_bout.astype(jnp.float32)
        + tokens_flat.astype(jnp.float32)
    )
    first_norm, first_pull = jax.vjp(layer_norm, after_mix, gain_first, shift_first)
    grouped_in = first_norm.astype(jnp.bfloat16).reshape(
        total_rows, group_count, model_width // group_count
    )
    up_groups = full_up.reshape(
        group_count, model_width // group_count, hidden_units // group_count
    )
    pre_act = jnp.einsum(
        "ngd,gdf->ngf", grouped_in, up_groups, preferred_element_type=jnp.float32
    ).reshape(total_rows, hidden_units) + full_bup.astype(jnp.float32)
    activated, gelu_pull = jax.vjp(partial(jax.nn.gelu, approximate=False), pre_act)
    act_low = activated.astype(jnp.bfloat16).reshape(
        total_rows, group_count, hidden_units // group_count
    )
    down_groups = full_down.reshape(
        group_count, hidden_units // group_count, model_width // group_count
    )
    summed = jnp.einsum(
        "ngf,gfd->ngd", act_low, down_groups, preferred_element_type=jnp.float32
    ).reshape(total_rows, model_width)
    summed = summed + full_bdown.astype(jnp.float32) + first_norm
    out_value, second_pull = jax.vjp(layer_norm, summed, gain_second, shift_second)
    output = out_value.astype(jnp.bfloat16).reshape(seq_count, local_rows, model_width)
    back_proj = full_proj
    back_depth = full_depth.astype(jnp.float32)
    back_out = full_out
    back_up = up_groups
    back_down = down_groups
    grad_summed, grad_gain_two, grad_shift_two = second_pull(
        cotangent.reshape(total_rows, model_width).astype(jnp.float32)
    )
    grad_bdown = jnp.sum(grad_summed, axis=0)
    summed_low = grad_summed.astype(jnp.bfloat16).reshape(
        total_rows, group_count, model_width // group_count
    )
    grad_activ = jnp.einsum(
        "ngd,gfd->ngf", summed_low, back_down, preferred_element_type=jnp.float32
    ).reshape(total_rows, hidden_units)
    grad_wdown = jnp.einsum(
        "ngf,ngd->gfd", act_low, summed_low, preferred_element_type=jnp.float32
    ).reshape(hidden_units, model_width // group_count)
    grad_pre = gelu_pull(grad_activ)[0]
    grad_bup = jnp.sum(grad_pre, axis=0)
    pre_low = grad_pre.astype(jnp.bfloat16).reshape(
        total_rows, group_count, hidden_units // group_count
    )
    grad_wup = jnp.einsum(
        "ngd,ngf->gdf", grouped_in, pre_low, preferred_element_type=jnp.float32
    ).reshape(model_width, hidden_units // group_count)
    grad_first = grad_summed + jnp.einsum(
        "ngf,gdf->ngd", pre_low, back_up, preferred_element_type=jnp.float32
    ).reshape(total_rows, model_width)
    grad_after, grad_gain_one, grad_shift_one = first_pull(grad_first)
    grad_bout = jnp.sum(grad_after, axis=0)
    after_low = grad_after.astype(jnp.bfloat16)
    grad_wout = jnp.dot(joined.T, after_low, preferred_element_type=jnp.float32)
    grad_joined = jnp.dot(after_low, back_out.T, preferred_element_type=jnp.float32)
    grad_context = (
        grad_joined[:, :all_width].astype(jnp.bfloat16).reshape(seq_count, local_rows, all_width)
    )
    grad_mix = grad_joined[:, all_width:].reshape(seq_count, local_rows, head_count, head_size)

    def back_one(item_set):
        query_seq, grad_seq, norm_seq, key_seq, value_seq = item_set
        grad_query, grad_key, grad_value, unused_delta = attend_back(
            query_seq.reshape(local_rows, head_count, head_size),
            grad_seq.reshape(local_rows, head_count, head_size),
            norm_seq,
            key_seq.reshape(full_length, head_count, head_size),
            value_seq.reshape(full_length, head_count, head_size),
            None,
            score_scale,
        )
        key_value = jnp.concatenate(
            [grad_key.reshape(full_length, all_width), grad_value.reshape(full_length, all_width)],
            axis=-1,
        )
        return (grad_query.reshape(local_rows, all_width), key_value)

    grad_query_att, kv_terms = lax.map(
        back_one, (queries_seq, grad_context, norm_log, all_keys, all_values)
    )
    own_kv = lax.psum_scatter(
        kv_terms.astype(jnp.bfloat16), "seq", scatter_dimension=1, tiled=True
    ).astype(jnp.float32)
    grad_keys_low = own_kv[..., :all_width].reshape(total_rows, all_width).astype(jnp.bfloat16)
    grad_values_low = own_kv[..., all_width:].reshape(total_rows, all_width).astype(jnp.bfloat16)
    grad_taps = jnp.stack(
        [
            jnp.sum(grad_mix * conv_heads[:, tap_index : tap_index + local_rows], axis=-1)
            for tap_index in range(tap_count)
        ],
        axis=-1,
    )
    grad_conv_ext = jnp.zeros((seq_count, ext_rows, head_count, head_size), jnp.float32)
    for tap_index in range(tap_count):
        grad_conv_ext = grad_conv_ext + jnp.pad(
            tap_weights[..., tap_index, None] * grad_mix,
            ((0, 0), (tap_index, 2 * half_kernel - tap_index), (0, 0), (0, 0)),
        )
    grad_logits = tap_weights * (
        grad_taps - jnp.sum(tap_weights * grad_taps, axis=-1, keepdims=True)
    )
    grad_logits = grad_logits.reshape(total_rows, head_count * tap_count)
    grad_bkernel = jnp.sum(grad_logits, axis=0)
    logits_low = grad_logits.astype(jnp.bfloat16)
    grad_wkernel = jnp.dot(mixed_key.T, logits_low, preferred_element_type=jnp.float32)
    grad_mixed = jnp.dot(logits_low, w_kernel.T, preferred_element_type=jnp.float32)
    grad_queries = (grad_query_att.reshape(total_rows, all_width) + grad_mixed * key_conv).astype(
        jnp.bfloat16
    )
    grad_key_conv = grad_mixed * queries.astype(jnp.float32)
    grad_bpt = jnp.sum(grad_key_conv, axis=0)
    key_conv_low = grad_key_conv.astype(jnp.bfloat16)
    grad_wpt = jnp.dot(spread.T, key_conv_low, preferred_element_type=jnp.float32)
    grad_spread = jnp.dot(
        key_conv_low, back_proj[:, 4 * all_width :].T, preferred_element_type=jnp.float32
    ).reshape(seq_count, local_rows, model_width)
    grad_wdepth = jnp.stack(
        [
            jnp.sum(
                extended[:, tap_index : tap_index + local_rows].astype(jnp.float32) * grad_spread,
                axis=(0, 1),
            )
            for tap_index in range(tap_count)
        ],
        axis=-1,
    )
    grad_ext_depth = jnp.zeros((seq_count, ext_rows, model_width), jnp.float32)
    for tap_index in range(tap_count):
        grad_ext_depth = grad_ext_depth + jnp.pad(
            back_depth[:, tap_index] * grad_spread,
            ((0, 0), (tap_index, 2 * half_kernel - tap_index), (0, 0)),
        )
    combined = jnp.concatenate(
        [grad_conv_ext.reshape(seq_count, ext_rows, all_width), grad_ext_depth], axis=-1
    )
    received = with_halo(combined.astype(jnp.bfloat16), (("seq", 1),), half_kernel).astype(
        combined.dtype
    )
    own_part = combined[:, half_kernel : half_kernel + local_rows]
    own_part = own_part.at[:, :half_kernel].add(received[:, :half_kernel])
    own_part = own_part.at[:, local_rows - half_kernel :].add(
        received[:, received.shape[1] - half_kernel :]
    )
    grad_conv_own = own_part[..., :all_width].reshape(total_rows, all_width)
    grad_depth_x = own_part[..., all_width:].reshape(total_rows, model_width)
    grad_bconv = jnp.sum(grad_conv_own, axis=0)
    conv_low = grad_conv_own.astype(jnp.bfloat16)
    stacked = jnp.concatenate([grad_queries, grad_keys_low, grad_values_low, conv_low], axis=-1)
    grad_wfirst = jnp.dot(tokens_flat.T, stacked, preferred_element_type=jnp.float32)
    grad_tokens = (
        grad_after
        + jnp.dot(stacked, back_proj[:, : 4 * all_width].T, preferred_element_type=jnp.float32)
        + grad_depth_x
    )
    grad_wproj = jnp.concatenate([grad_wfirst, grad_wpt], axis=1)
    grad_bproj = jnp.concatenate(
        [
            jnp.sum(grad_queries.astype(jnp.float32), axis=0),
            jnp.sum(grad_values_low.astype(jnp.float32), axis=0),
            grad_bconv,
            grad_bpt,
        ]
    )
    def blocks(grad, shard):
        return grad.astype(jnp.bfloat16).reshape((devices,) + tiled(shard).shape)

    per_device = [
        g.reshape(devices, -1)
        for g in (
            grad_wdepth, grad_bproj, grad_bup, grad_bout, grad_gain_one, grad_shift_one,
            grad_bdown, grad_gain_two, grad_shift_two,
        )
    ]
    kernel_flat = jnp.concatenate([grad_wkernel.reshape(-1), grad_bkernel])
    kernel_len = kernel_flat.shape[0]
    kernel_each = -(-kernel_len // devices)
    kernel_flat = jnp.pad(kernel_flat, (0, kernel_each * devices - kernel_len))
    small_grad = jnp.concatenate(
        [
            lanes(jnp.concatenate(per_device, axis=1), 1),
            lanes(kernel_flat.reshape(devices, kernel_each), 1),
        ],
        axis=1,
    )
    sum_down, sum_up, sum_out, sum_proj, sum_small, sum_kernel = scatter_all(
        dp,
        seq,
        [
            blocks(grad_wdown, w_down), blocks(grad_wup, w_up), blocks(grad_wout, w_out),
            blocks(grad_wproj, w_proj), small_grad,
        ],
        ("zxyc", "zyxc", "zxyc", "zyxc", "zxyc"),
    )
    mine = cut(sum_small[:1].reshape(1, 1024), widths)
    shards = [sum_proj.reshape(w_proj.shape), mine[0].reshape(w_depth.shape)]
    shards += [
        sum_out.reshape(w_out.shape), sum_up.reshape(w_up.shape), sum_down.reshape(w_down.shape),
    ]
    shards += [m.reshape(-1) for m in mine[1:]]
    kernel_sum = sum_kernel.reshape(devices, 1024)[:, :kernel_each].reshape(-1)
    kernel_total = (
        kernel_sum[: grad_wkernel.size].reshape(grad_wkernel.shape),
        kernel_sum[grad_wkernel.size : kernel_len],
    )
    return (
        output,
        grad_tokens.reshape(seq_count, local_rows, model_width),
        shards[0],
        shards[1],
        kernel_total[0],
        kernel_total[1],
        shards[2],
        shards[3],
        shards[4],
        shards[5],
        shards[6],
        shards[7],
        shards[8],
        shards[9],
        shards[10],
        shards[11],
        shards[12],
    )


def solution(mesh):
    placed = (
        P("dp", "seq", None),
        P("dp", "seq", None),
        P(("dp", "seq"), None),
        P(("dp", "seq"), None),
        P(),
        P(),
        P(("dp", "seq"), None),
        P(("dp", "seq"), None),
        P(("dp", "seq"), None),
        P(("dp", "seq")),
        P(("dp", "seq")),
        P(("dp", "seq")),
        P(("dp", "seq")),
        P(("dp", "seq")),
        P(("dp", "seq")),
        P(("dp", "seq")),
        P(("dp", "seq")),
    )
    return jax.shard_map(
        fast_body if fits(mesh) else body,
        mesh=mesh,
        in_specs=placed,
        out_specs=(
            P("dp", "seq", None),
            P("dp", "seq", None),
            P(("dp", "seq"), None),
            P(("dp", "seq"), None),
            P(),
            P(),
            P(("dp", "seq"), None),
            P(("dp", "seq"), None),
            P(("dp", "seq"), None),
            P(("dp", "seq")),
            P(("dp", "seq")),
            P(("dp", "seq")),
            P(("dp", "seq")),
            P(("dp", "seq")),
            P(("dp", "seq")),
            P(("dp", "seq")),
            P(("dp", "seq")),
        ),
        check_vma=False,
    )
```

```python
from functools import partial

import jax
import jax.numpy as jnp
from jax import lax
from jax.experimental import pallas as pl
from jax.experimental.pallas import tpu as pltpu
from jax.sharding import PartitionSpec as P

MESH = pl.DeviceIdType.MESH


class Grid:
    def __init__(self, dp, seq):
        self.C = 2 if dp % 2 == 0 else 1
        rest = dp // self.C
        y = 1
        while (2 * y) * (2 * y) <= rest and rest % (2 * y) == 0:
            y *= 2
        self.Y, self.X, self.Z = y, rest // y, seq
        d = lax.axis_index("dp")
        self.z = lax.axis_index("seq")
        self.c = d % self.C
        self.x = (d // self.C) % self.X
        self.y = d // (self.C * self.X)
        self.dp = d
    def size(self, ax):
        return getattr(self, ax.upper())
    def at(self, **off):
        g = {a: (getattr(self, a) + off.get(a, 0)) % self.size(a) if off.get(a, 0) else getattr(self, a) for a in "yxcz"}
        return g
    def dpof(self, g):
        return (g["y"] * self.X + g["x"]) * self.C + g["c"]
    def dev(self, **off):
        g = self.at(**off)
        return (self.dpof(g), g["z"])


def peers(grid):
    out = []
    for a in "zxyc":
        for o in range(1, grid.size(a)):
            out.append(grid.dev(**{a: o}))
    return out


def entry_barrier(grid):
    b = pltpu.get_barrier_semaphore()
    ps = peers(grid)
    for p in ps:
        pl.semaphore_signal(b, inc=1, device_id=p, device_id_type=MESH)
    pl.semaphore_wait(b, len(ps))


class Gather:
    def __init__(self, grid, src, buf, order, ssem, rsem, lsem):
        self.g, self.src, self.buf, self.ssem, self.rsem, self.lsem = grid, src, buf, ssem, rsem, lsem
        self.u, self.v = order[1], order[2]
        self.ns = 0
        self.sent = []
        self.recv = {}
        g = grid
        k = 0
        self.slot = {}
        for o in range(1, g.Z):
            self.slot["z", o] = k; k += 1
        for o in range(1, g.size(self.u)):
            self.slot["u", o] = k; k += 1
        for o in range(1, g.size(self.v)):
            for q in range(g.size(self.u)):
                self.slot["v", o, q] = k; k += 1
        for o in range(1, g.C):
            for q in range(g.size(self.u)):
                for w in range(g.size(self.v)):
                    self.slot["c", o, q, w] = k; k += 1
        self.count = k

    @staticmethod
    def slots(Z, X, Y, C):
        return (Z - 1) + X * Y * C - 1

    def block(self, uo, vo, co=0):
        g = self.g.at(**{self.u: uo, self.v: vo, "c": co})
        return self.buf.at[pl.ds(self.g.dpof(g) * self.g.Z, self.g.Z)]

    def _send(self, src, dst, slot, dev):
        k = self.slot[slot]
        cp = pltpu.make_async_remote_copy(src_ref=src, dst_ref=dst, send_sem=self.ssem.at[k], recv_sem=self.rsem.at[k],
                                          device_id=dev, device_id_type=MESH)
        cp.start()
        self.sent.append(cp)

    def start(self):
        g = self.g
        me = g.dp * g.Z + g.z
        self.local = pltpu.make_async_copy(self.src, self.buf.at[me], self.lsem)
        self.local.start()
        for o in range(1, g.Z):
            self._send(self.src, self.buf.at[me], ("z", o), g.dev(z=o))

    def _wait_recv(self, ref, slot):
        k = self.slot[slot]
        pltpu.make_async_remote_copy(src_ref=ref, dst_ref=ref, send_sem=self.ssem.at[k], recv_sem=self.rsem.at[k],
                                     device_id=self.g.dev(z=1) if self.g.Z > 1 else self.g.dev(c=1), device_id_type=MESH).wait_recv()

    def step1(self):
        g = self.g
        self.local.wait()
        for o in range(1, g.Z):
            self._wait_recv(self.buf.at[g.dp * g.Z + (g.z + g.Z - o) % g.Z], ("z", o))
        blk = self.block(0, 0)
        for o in range(1, g.size(self.u)):
            self._send(blk, blk, ("u", o), g.dev(**{self.u: o}))
        for o in range(1, g.size(self.v)):
            self._send(blk, blk, ("v", o, 0), g.dev(**{self.v: o}))
        for o in range(1, g.C):
            self._send(blk, blk, ("c", o, 0, 0), g.dev(c=o))

    def step2(self):
        g = self.g
        U, V = g.size(self.u), g.size(self.v)
        for q in range(1, U):
            blk = self.block(U - q, 0)
            self._wait_recv(blk, ("u", q))
            for o in range(1, V):
                self._send(blk, blk, ("v", o, q), g.dev(**{self.v: o}))
            for o in range(1, g.C):
                self._send(blk, blk, ("c", o, q, 0), g.dev(c=o))

    def step3(self):
        g = self.g
        U, V = g.size(self.u), g.size(self.v)
        for q in range(U):
            for w in range(1, V):
                blk = self.block((U - q) % U, V - w)
                self._wait_recv(blk, ("v", w, q))
                for o in range(1, g.C):
                    self._send(blk, blk, ("c", o, q, w), g.dev(c=o))

    def step4(self):
        g = self.g
        U, V = g.size(self.u), g.size(self.v)
        for q in range(U):
            for w in range(V):
                for o in range(1, g.C):
                    self._wait_recv(self.block((U - q) % U, (V - w) % V, g.C - o), ("c", o, q, w))

    def finish(self):
        for cp in self.sent:
            cp.wait_send()


def run_gathers(gs):
    n = len(gs)
    for g in gs:
        g.start()
    steps = [lambda g: g.step1(), lambda g: g.step2(), lambda g: g.step3(), lambda g: g.step4()]
    for t in range(n + 3):
        for s in range(4):
            i = t - s
            if 0 <= i < n:
                steps[s](gs[i])
    for g in gs:
        g.finish()

class Scatter:
    def __init__(self, grid, part, order, bufs, out, ssem, rsem):
        self.g, self.part, self.out, self.ssem, self.rsem = grid, part, out, ssem, rsem
        self.rc, self.rv, self.ru, self.rz = bufs
        self.u, self.v = order[1], order[2]
        g = grid
        U, V = g.size(self.u), g.size(self.v)
        self.U, self.V = U, V
        k = 0
        self.slot = {}
        for o in range(1, g.C):
            for q in range(U):
                for w in range(V):
                    self.slot["c", o, q, w] = k; k += 1
        for o in range(1, V):
            for q in range(U):
                self.slot["v", o, q] = k; k += 1
        for o in range(1, U):
            self.slot["u", o] = k; k += 1
        for o in range(1, g.Z):
            self.slot["z", o] = k; k += 1
        self.sent = []

    def first(self, uo, vo, co=0):
        g = self.g.at(**{self.u: uo, self.v: vo, "c": co})
        return self.g.dpof(g) * self.g.Z

    def block(self, uo, vo, co=0):
        return self.part.at[pl.ds(self.first(uo, vo, co), self.g.Z)]

    def _copy(self, src, dst, slot, dev):
        k = self.slot[slot]
        return pltpu.make_async_remote_copy(src_ref=src, dst_ref=dst, send_sem=self.ssem.at[k], recv_sem=self.rsem.at[k],
                                            device_id=dev, device_id_type=MESH)

    def _send(self, src, dst, slot, dev):
        cp = self._copy(src, dst, slot, dev)
        cp.start()
        self.sent.append((src, dst, slot, dev))

    def _wait(self, dst, slot, dev):
        self._copy(dst, dst, slot, dev).wait_recv()

    def start(self):
        g = self.g
        for o in range(1, g.C):
            for w in list(range(1, self.V)) + [0]:
                for q in list(range(1, self.U)) + [0]:
                    self._send(self.block(q, w, o), self.rc.at[o - 1, q * self.V + w], ("c", o, q, w), g.dev(c=o))

    def _total(self, q, w, i):
        f = jnp.float32
        s = self.part[self.first(q, w) + i].astype(f)
        for o in range(1, self.g.C):
            s = s + self.rc[o - 1, q * self.V + w, i].astype(f)
        if w == 0:
            for k in range(1, self.V):
                s = s + self.rv[k - 1, q, i].astype(f)
            if q == 0:
                for k in range(1, self.U):
                    s = s + self.ru[k - 1, i].astype(f)
        return s

    def _wait_c(self, q, w):
        for o in range(1, self.g.C):
            self._wait(self.rc.at[o - 1, q * self.V + w], ("c", o, q, w), self.g.dev(c=o))

    def _reduce(self, q, w):
        at = self.first(q, w)

        def body(i, _):
            self.part[at + i] = self._total(q, w, i).astype(self.part.dtype)
            return 0

        lax.fori_loop(0, self.g.Z, body, 0)

    def step1(self):
        for w in range(1, self.V):
            for q in list(range(1, self.U)) + [0]:
                self._wait_c(q, w)
                self._reduce(q, w)
                self._send(self.block(q, w), self.rv.at[w - 1, q], ("v", w, q), self.g.dev(**{self.v: w}))

    def step2(self):
        for q in range(1, self.U):
            self._wait_c(q, 0)
            for w in range(1, self.V):
                self._wait(self.rv.at[w - 1, q], ("v", w, q), self.g.dev(**{self.v: w}))
            self._reduce(q, 0)
            self._send(self.block(q, 0), self.ru.at[q - 1], ("u", q), self.g.dev(**{self.u: q}))

    def step3(self):
        g = self.g
        self._wait_c(0, 0)
        for w in range(1, self.V):
            self._wait(self.rv.at[w - 1, 0], ("v", w, 0), g.dev(**{self.v: w}))
        for q in range(1, self.U):
            self._wait(self.ru.at[q - 1], ("u", q), g.dev(**{self.u: q}))
        at = self.first(0, 0)
        for o in range(1, g.Z):
            i = (g.z + o) % g.Z
            self.part[at + i] = self._total(0, 0, i).astype(self.part.dtype)
            self._send(self.part.at[at + i], self.rz.at[o - 1], ("z", o), g.dev(z=o))

    def step4(self):
        g = self.g
        s = self._total(0, 0, g.z)
        for o in range(1, g.Z):
            self._wait(self.rz.at[o - 1], ("z", o), g.dev(z=o))
            s = s + self.rz[o - 1].astype(jnp.float32)
        self.out[...] = s

    def finish(self):
        for a in self.sent:
            self._copy(*a).wait_send()


def scatter_scratch(grid_sizes, shape, dtype, order):
    Z, S = grid_sizes["z"], grid_sizes
    U, V, C = S[order[1]], S[order[2]], S["c"]
    t = tuple(shape)
    m = lambda n: max(n, 1)
    return [pltpu.VMEM((m(C - 1), U * V, Z) + t, dtype), pltpu.VMEM((m(V - 1), U, Z) + t, dtype), pltpu.VMEM((m(U - 1), Z) + t, dtype),
            pltpu.VMEM((m(Z - 1),) + t, dtype)]


def run_scatters(gs):
    n = len(gs)
    for g in gs:
        g.start()
    for t in range(n + 3):
        for s in range(4):
            i = t - s
            if 0 <= i < n:
                [gs[i].step1, gs[i].step2, gs[i].step3, gs[i].step4][s]()
    for g in gs:
        g.finish()


ORDERS = ("zxyc", "zyxc", "zyxc", "zxyc", "zyxc", "zxyc")
VMEM_CAP = 60 << 20


def sizes_of(dp, seq):
    C = 2 if dp % 2 == 0 else 1
    rest = dp // C
    y = 1
    while (2 * y) * (2 * y) <= rest and rest % (2 * y) == 0:
        y *= 2
    return dict(y=y, x=rest // y, c=C, z=seq)


def tiled(shard):
    rows, cols = shard.shape
    return shard.reshape((rows // 8, 8, cols) if rows % 8 == 0 else (1, rows, cols))


def gather_kernel(dp, seq, orders, *refs):
    n = len(orders)
    ins, outs = refs[:n], refs[n : 2 * n]
    ssem, rsem, lsem = refs[2 * n :]
    grid = Grid(dp, seq)
    entry_barrier(grid)
    run_gathers(
        [
            Gather(grid, ins[i], outs[i], orders[i], ssem.at[i], rsem.at[i], lsem.at[i])
            for i in range(n)
        ]
    )


def gather_all(dp, seq, shards):
    n = len(shards)
    sems = pltpu.SemaphoreType.DMA((n, dp * seq - 1))
    blocks = [tiled(s) for s in shards]
    outs = pl.pallas_call(
        partial(gather_kernel, dp, seq, ORDERS[:n]),
        out_shape=[jax.ShapeDtypeStruct((dp * seq,) + b.shape, b.dtype) for b in blocks],
        in_specs=[pl.BlockSpec(memory_space=pl.ANY)] * n,
        out_specs=[pl.BlockSpec(memory_space=pl.ANY)] * n,
        scratch_shapes=[sems, sems, pltpu.SemaphoreType.DMA((n,))],
        compiler_params=pltpu.CompilerParams(collective_id=0, has_side_effects=True),
        name="gather",
    )(*blocks)
    return [o.reshape((-1, s.shape[1])) for o, s in zip(outs, shards)]


def scatter_kernel(dp, seq, orders, count, *refs):
    n = len(orders)
    ins, outs, total, rest = refs[:n], refs[n : 2 * n], refs[2 * n], refs[2 * n + 1 :]
    parts, rest = rest[:n], rest[n:]
    ssem, rsem, lsem, gs, gr = rest[-5:]
    tail = rest[-6]
    grid = Grid(dp, seq)
    copies = [pltpu.make_async_copy(ins[i], parts[i], lsem.at[i]) for i in range(n)]
    for c in copies:
        c.start()
    entry_barrier(grid)
    for c in copies:
        c.wait()
    run_scatters(
        [
            Scatter(
                grid, parts[i], orders[i], rest[4 * i : 4 * i + 4], outs[i],
                ssem.at[i], rsem.at[i],
            )
            for i in range(n)
        ]
    )
    tail[...] = outs[n - 1][1:]
    run_gathers([Gather(grid, tail, total, "zxyc", gs, gr, lsem.at[n])])


def scatter_all(dp, seq, parts, orders):
    n = len(parts)
    N = dp * seq
    sizes = sizes_of(dp, seq)
    scratch = [pltpu.VMEM(p.shape, p.dtype) for p in parts]
    for p, o in zip(parts, orders):
        scratch += scatter_scratch(sizes, p.shape[1:], p.dtype, o)
    last = parts[-1].shape[1:]
    tail = (last[0] - 1,) + last[1:]
    sems = pltpu.SemaphoreType.DMA((n, N - 1))
    one = pltpu.SemaphoreType.DMA((N - 1,))
    return pl.pallas_call(
        partial(scatter_kernel, dp, seq, orders, n),
        out_shape=[jax.ShapeDtypeStruct(p.shape[1:], jnp.float32) for p in parts]
        + [jax.ShapeDtypeStruct((N,) + tail, jnp.float32)],
        in_specs=[pl.BlockSpec(memory_space=pl.ANY)] * n,
        out_specs=[pl.BlockSpec(memory_space=pltpu.VMEM)] * (n + 1),
        scratch_shapes=scratch
        + [
            pltpu.VMEM(tail, jnp.float32), sems, sems, pltpu.SemaphoreType.DMA((n + 1,)), one, one,
        ],
        compiler_params=pltpu.CompilerParams(
            collective_id=1, has_side_effects=True, vmem_limit_bytes=VMEM_CAP
        ),
        name="scatter",
    )(*parts)


def lanes(flat, rows):
    return jnp.pad(flat, ((0, 0), (0, rows * 1024 - flat.shape[1]))).reshape(-1, rows, 8, 128)


def cut(rows, widths):
    out, at = [], 0
    for w in widths:
        out.append(rows[:, at : at + w])
        at += w
    return out


HEADS = 6
HEAD = 64
KERNEL = 9
FF = 3072
GROUPS = 2


norm_eps = 1e-12


def with_halo(cells, sides, width):
    for axis, dim in sides:
        count = lax.axis_size(axis)
        ends = count - 1
        head = lax.slice_in_dim(cells, 0, width, axis=dim)
        tail = lax.slice_in_dim(cells, cells.shape[dim] - width, cells.shape[dim], axis=dim)
        cells = jnp.concatenate(
            [
                lax.ppermute(tail, axis, [(i, (i + 1) % count) for i in range(ends)]),
                cells,
                lax.ppermute(head, axis, [((i + 1) % count, i) for i in range(ends)]),
            ],
            axis=dim,
        )
    return cells


def layer_norm(inputs, gain_vec, shift_vec):
    centre = inputs - jnp.mean(inputs, axis=-1, keepdims=True)
    variance = jnp.mean(centre * centre, axis=-1, keepdims=True)
    return centre * lax.rsqrt(variance + norm_eps) * gain_vec + shift_vec


def attend(queries, key_rows, value_rows, score_scale):
    scores = (
        jnp.einsum("ihe,jhe->hij", queries, key_rows, preferred_element_type=jnp.float32)
        * score_scale
    )
    row_max = jnp.max(scores, axis=-1, keepdims=True)
    norm_log = row_max + jnp.log(jnp.sum(jnp.exp(scores - row_max), axis=-1, keepdims=True))
    weights_low = jnp.exp(scores - norm_log).astype(jnp.bfloat16)
    context = jnp.einsum(
        "hij,jhe->ihe", weights_low, value_rows, preferred_element_type=jnp.float32
    )
    return (context.astype(jnp.bfloat16), norm_log[..., 0])


def attend_back(queries, grad_context, norm_log, key_rows, value_rows, row_delta, score_scale):
    scores = (
        jnp.einsum("ihe,jhe->hij", queries, key_rows, preferred_element_type=jnp.float32)
        * score_scale
    )
    soft_rows = jnp.exp(scores - norm_log[..., None])
    grad_soft = jnp.einsum(
        "ihe,jhe->hij", grad_context, value_rows, preferred_element_type=jnp.float32
    )
    row_delta = jnp.sum(soft_rows * grad_soft, axis=-1)
    grad_scores = (soft_rows * (grad_soft - row_delta[..., None])).astype(jnp.bfloat16)
    grad_queries = (
        jnp.einsum("hij,jhe->ihe", grad_scores, key_rows, preferred_element_type=jnp.float32)
        * score_scale
    )
    grad_keys = (
        jnp.einsum("hij,ihe->jhe", grad_scores, queries, preferred_element_type=jnp.float32)
        * score_scale
    )
    grad_values = jnp.einsum(
        "hij,ihe->jhe",
        soft_rows.astype(jnp.bfloat16),
        grad_context,
        preferred_element_type=jnp.float32,
    )
    return (grad_queries, grad_keys, grad_values, row_delta)


def dot(a, b):
    return jnp.dot(a, b, preferred_element_type=jnp.float32)


def dot_nt(a, b):
    return lax.dot_general(a, b, (((1,), (1,)), ((), ())), preferred_element_type=jnp.float32)


def dot_tn(a, b):
    return lax.dot_general(a, b, (((0,), (0,)), ((), ())), preferred_element_type=jnp.float32)


def centred(v):
    centre = v - jnp.mean(v, axis=-1, keepdims=True)
    inv = lax.rsqrt(jnp.mean(centre * centre, axis=-1, keepdims=True) + norm_eps)
    return centre * inv, inv


def norm_back(grad, normed, inv):
    return inv * (
        grad
        - jnp.mean(grad, axis=-1, keepdims=True)
        - normed * jnp.mean(grad * normed, axis=-1, keepdims=True)
    )


def rows_sum(v):
    return jnp.sum(v, axis=0, keepdims=True)


V_BOUT, V_G1, V_S1, V_BDOWN, V_G2, V_S2 = range(9, 15)
HALF_GELU = 0.7071067811865476
PDF = 0.3989422804014327
BLOCK = 128
CHUNK = 512


def ffn_kernel(
    joined, x, cot, wout, wup, wdown, vec, bup,
    out, gafter, dctx, gmix, gwout, gwup, gwdown, vecg, gbup,
    act, slope, gp, fnb, gsb, gab,
):
    f32, bf16 = jnp.float32, jnp.bfloat16
    total = x.shape[0]
    width = x.shape[1]
    chan = width // 2
    gw = width // GROUPS
    gf = FF // GROUPS
    vecg[...] = jnp.zeros_like(vecg)
    gbup[...] = jnp.zeros_like(gbup)

    def block(r, _):
        rows = pl.ds(pl.multiple_of(r * BLOCK, BLOCK), BLOCK)
        row = lambda i: vec[i : i + 1, :]
        after = dot(joined[rows], wout[...]) + row(V_BOUT) + x[rows].astype(f32)
        n1, inv1 = centred(after)
        first = n1 * row(V_G1) + row(V_S1)
        low = first.astype(bf16)
        fnb[rows] = low
        parts = []
        for g in range(GROUPS):
            acc = jnp.zeros((BLOCK, gw), f32)
            for j in range(gf // CHUNK):
                cols = slice(g * gf + j * CHUNK, g * gf + (j + 1) * CHUNK)
                pre = dot(
                    low[:, g * gw : (g + 1) * gw],
                    wup[g * gw : (g + 1) * gw, j * CHUNK : (j + 1) * CHUNK],
                ) + bup[:, cols]
                cdf = 0.5 + 0.5 * lax.erf(pre * HALF_GELU)
                a = (pre * cdf).astype(bf16)
                act[rows, cols] = a
                slope[:, cols] = cdf + pre * (PDF * jnp.exp(pre * pre * -0.5))
                acc = acc + dot(a, wdown[cols])
            parts.append(acc)
        summed = jnp.concatenate(parts, axis=-1) + row(V_BDOWN) + first
        n2, inv2 = centred(summed)
        out[rows] = (n2 * row(V_G2) + row(V_S2)).astype(bf16)
        c = cot[rows].astype(f32)
        gs = norm_back(c * row(V_G2), n2, inv2)
        glow = gs.astype(bf16)
        gsb[rows] = glow
        parts = []
        for g in range(GROUPS):
            acc = jnp.zeros((BLOCK, gw), f32)
            for j in range(gf // CHUNK):
                cols = slice(g * gf + j * CHUNK, g * gf + (j + 1) * CHUNK)
                pre = dot_nt(glow[:, g * gw : (g + 1) * gw], wdown[cols]) * slope[:, cols]
                gbup[:, cols] += rows_sum(pre)
                p = pre.astype(bf16)
                gp[rows, cols] = p
                acc = acc + dot_nt(
                    p, wup[g * gw : (g + 1) * gw, j * CHUNK : (j + 1) * CHUNK]
                )
            parts.append(acc)
        gfirst = gs + jnp.concatenate(parts, axis=-1)
        ga = norm_back(gfirst * row(V_G1), n1, inv1)
        gafter[rows] = ga
        alow = ga.astype(bf16)
        gab[rows] = alow
        gj = dot_nt(alow, wout[...])
        dctx[rows] = gj[:, :chan].astype(bf16)
        gmix[rows] = gj[:, chan:]
        for i, v in (
            (V_BOUT, ga), (V_G1, gfirst * n1), (V_S1, gfirst), (V_BDOWN, gs), (V_G2, c * n2),
            (V_S2, c),
        ):
            vecg[i : i + 1, :] += rows_sum(v)
        return 0

    lax.fori_loop(0, total // BLOCK, block, 0)
    gwout[...] = dot_tn(joined[...], gab[...]).astype(bf16)
    for g in range(GROUPS):
        for j in range(gf // CHUNK):
            cols = slice(g * gf + j * CHUNK, g * gf + (j + 1) * CHUNK)
            gwdown[cols] = dot_tn(act[:, cols], gsb[:, g * gw : (g + 1) * gw]).astype(bf16)
            gwup[g * gw : (g + 1) * gw, j * CHUNK : (j + 1) * CHUNK] = dot_tn(
                fnb[:, g * gw : (g + 1) * gw], gp[:, cols]
            ).astype(bf16)


def ffn(joined, x, cot, wout, wup, wdown, vec, bup):
    f32, bf16 = jnp.float32, jnp.bfloat16
    total, width = x.shape
    shape = jax.ShapeDtypeStruct
    return pl.pallas_call(
        ffn_kernel,
        out_shape=[
            shape((total, width), bf16),
            shape((total, width), f32),
            shape((total, width // 2), bf16),
            shape((total, width // 2), f32),
            shape(wout.shape, bf16),
            shape(wup.shape, bf16),
            shape(wdown.shape, bf16),
            shape(vec.shape, f32),
            shape(bup.shape, f32),
        ],
        in_specs=[pl.BlockSpec(memory_space=pltpu.VMEM)] * 8,
        out_specs=[pl.BlockSpec(memory_space=pltpu.VMEM)] * 9,
        scratch_shapes=[
            pltpu.VMEM((total, FF), bf16),
            pltpu.VMEM((BLOCK, FF), f32),
            pltpu.VMEM((total, FF), bf16),
            pltpu.VMEM((total, width), bf16),
            pltpu.VMEM((total, width), bf16),
            pltpu.VMEM((total, width), bf16),
        ],
        compiler_params=pltpu.CompilerParams(vmem_limit_bytes=VMEM_CAP),
        name="ffn",
    )(joined, x, cot, wout, wup, wdown, vec, bup)


HEADS_PER = HEADS // 2
PART = HEADS_PER * HEAD
EDGE = 8
TAPS = KERNEL
CHAN = HEADS * HEAD


def iota(shape, dim):
    return lax.broadcasted_iota(jnp.int32, shape, dim)


def expander(rows, cols, width):
    return (iota((rows, cols), 1) % width == iota((rows, cols), 0)).astype(jnp.bfloat16)


def owned(stack, width):
    keep = iota(stack.shape, 2) // width == iota(stack.shape, 0)
    return jnp.sum(jnp.where(keep, stack, 0.0), axis=0)


def unpack_small(gsmall, vec, bproj, bup, widths):
    n = gsmall.shape[0]
    w, wp, wu = widths
    flat = gsmall[:, :2].reshape(n * 16, 128).astype(jnp.bfloat16)
    cols = vec.shape[1]
    vec[...] = owned(dot(flat, expander(128, cols, w)).reshape(n, 16, cols), w)
    flat = gsmall[:, 2].reshape(n * 8, 128).astype(jnp.bfloat16)
    cols = bproj.shape[1]
    bproj[...] = owned(dot(flat, expander(128, cols, wp)).reshape(n, 8, cols), wp)[:1]
    cols = bup.shape[1]
    bup[...] = owned(dot(flat, expander(128, cols, wu)).reshape(n, 8, cols), wu)[1:2]


def pack(v):
    r = v.shape[0] // 2
    return jnp.concatenate([v[:r], v[r:]], axis=1)


def unpack(v):
    c = v.shape[1] // 2
    return jnp.concatenate([v[:, :c], v[:, c:]], axis=0)


def tap_logits(mixed, wkx, bkx, logits):
    for t in range(TAPS):
        logits[t] = dot(mixed, wkx[t]) + bkx[t : t + 1]


def softmax_taps(logits, rows):
    ls = [logits[t, rows] for t in range(TAPS)]
    top = ls[0]
    for v in ls[1:]:
        top = jnp.maximum(top, v)
    es = [jnp.exp(v - top) for v in ls]
    total = es[0]
    for v in es[1:]:
        total = total + v
    inv = 1.0 / total
    return [e * inv for e in es]


def expand_kernel_weights(w_kernel, b_kernel, wkx, bkx):
    cols = wkx.shape[2]
    wk, bk = w_kernel[...], b_kernel[...]
    for t in range(TAPS):
        k = wk.shape[0]
        pick = (iota((k, cols), 0) == iota((k, cols), 1) // HEAD * TAPS + t).astype(jnp.bfloat16)
        wkx[t] = dot_tn(wk, pick).astype(jnp.bfloat16)
        bkx[t : t + 1] = dot(bk, pick)


def load_whole(gathered, whole, sem):
    cp = pltpu.make_async_copy(gathered.reshape(whole.shape), whole, sem)
    cp.start()
    return cp


ROW = 16


def front_kernel(
    dp, seq, widths,
    x, wproj, wout, wup, wdown, small, w_kernel, b_kernel,
    gq0, gq1, gq2, gcp, gout, gup, gdown,
    qh, kh, vh, stats, joined, qn, xe, convin, keyconv, mixed, spread, vec, bup, wkx, bkx,
    pq, pcp, gsmall, wq, wcp, xf, edges, inedge, qkv, abuf, csend, cbuf, logits, bproj,
    ssem, rsem, lsem, asend, arecv, bsend, brecv, esend, erecv, wsem,
):
    f32, bf16 = jnp.float32, jnp.bfloat16
    grid = Grid(dp, seq)
    z, Z = grid.z, seq
    seqs, local, width = x.shape
    total = seqs * local

    w = wproj[...].astype(f32)
    for j in range(HEADS_PER):
        cols = []
        for n in (j, HEADS_PER + j):
            for p in range(3):
                at = p * CHAN + n * HEAD
                cols.append(w[:, at : at + HEAD])
        pq[j] = jnp.concatenate(cols, axis=1).reshape(pq.shape[1:]).astype(bf16)
    pcp[...] = w[:, 3 * CHAN :].reshape(pcp.shape).astype(bf16)
    for s in range(seqs):
        edges[0, s] = x[s, :EDGE].astype(f32)
        edges[1, s] = x[s, local - EDGE :].astype(f32)

    entry_barrier(grid)
    mk = lambda i, src, buf, order: Gather(
        grid, src, buf, order, ssem.at[i], rsem.at[i], lsem.at[i]
    )
    gs = mk(0, small, gsmall, "zxyc")
    gq = [
        mk(1, pq.at[0], gq0, "zxyc"), mk(2, pq.at[1], gq1, "zyxc"), mk(3, pq.at[2], gq2, "zxyc")
    ]
    g2 = mk(4, pcp, gcp, "zyxc")
    g3 = mk(5, wout, gout, "zxyc")
    g4 = mk(6, wup, gup, "zyxc")
    g5 = mk(7, wdown, gdown, "zxyc")
    gs.start()
    for g in gq:
        g.start()
    hops = []
    for i, o in ((0, seq - 1), (1, 1)):
        cp = pltpu.make_async_remote_copy(
            src_ref=edges.at[i], dst_ref=inedge.at[i], send_sem=esend.at[i],
            recv_sem=erecv.at[i], device_id=grid.dev(z=o), device_id_type=MESH,
        )
        cp.start()
        hops.append(cp)
    expand_kernel_weights(w_kernel, b_kernel, wkx, bkx)
    early = [gs] + gq
    for g in early:
        g.step1()
    g2.start()
    g3.start()
    g4.start()
    g5.start()
    for g in early:
        g.step2()
    for g in early:
        g.step3()
    gs.step4()
    unpack_small(gsmall, vec, bproj, bup, widths)
    bias = bproj[...]
    zero = jnp.zeros((1, HEAD), f32)
    for j in range(HEADS_PER):
        gq[j].step4()
        pltpu.make_async_copy(
            (gq0, gq1, gq2)[j].reshape((width, 2 * PART)), wq.at[j], wsem.at[j]
        ).start()
    g2.step1()

    sends = []
    heads = {}
    for j in range(HEADS_PER):
        pltpu.make_async_copy(
            (gq0, gq1, gq2)[j].reshape((width, 2 * PART)), wq.at[j], wsem.at[j]
        ).wait()
        cols = []
        for n in (j, HEADS_PER + j):
            at = n * HEAD
            cols += [bias[:, at : at + HEAD], zero, bias[:, CHAN + at : CHAN + at + HEAD]]
        qkv_bias = jnp.concatenate(cols, axis=1)
        for s in range(seqs):
            val = (dot(x[s], wq[j]) + qkv_bias).astype(bf16)
            for h in range(2):
                qkv[2 * s + h, j] = pack(val[:, h * PART : (h + 1) * PART])
                heads[s, h * HEADS_PER + j] = val[:, h * PART : h * PART + HEAD]
        for o in range(1, Z):
            to = (z + o) % Z
            cp = pltpu.make_async_remote_copy(
                src_ref=qkv.at[to, j], dst_ref=abuf.at[j, z], send_sem=asend.at[j, o - 1],
                recv_sem=arecv.at[j, o - 1], device_id=grid.dev(z=o), device_id_type=MESH,
            )
            cp.start()
            sends.append(cp)
        abuf[j, z] = qkv[z, j]
    for s in range(seqs):
        qn[s * local : (s + 1) * local] = jnp.concatenate(
            [heads[s, n] for n in range(HEADS)], axis=1
        )

    g2.step2()
    g3.step1()
    for cp in hops:
        cp.wait_recv()
    for s in range(seqs):
        top = jnp.where(z > 0, inedge[1, s], 0.0)
        low = jnp.where(z < Z - 1, inedge[0, s], 0.0)
        xf[s, :EDGE] = top
        xf[s, EDGE : EDGE + local] = x[s].astype(f32)
        xf[s, EDGE + local :] = low
        xe[s] = xf[s].astype(bf16)
    ext = local + 2 * EDGE
    spread_rows(xf, vec, spread, seqs, local)
    g4.step1()
    g5.step1()
    g2.step3()
    g2.step4()
    c2 = load_whole(gcp, wcp, wsem.at[HEADS_PER])
    c2.wait()
    at = iota((ext, 1), 0)
    inside = ((at >= EDGE) | (z > 0)) & ((at < EDGE + local) | (z < Z - 1))
    for s in range(seqs):
        val = dot(xe[s], wcp[:, :CHAN]) + bias[:, 2 * CHAN : 3 * CHAN]
        convin[s] = jnp.where(inside, val, 0.0)
    for s in range(seqs):
        rows = slice(s * local, (s + 1) * local)
        kc = dot(spread[rows], wcp[:, CHAN:]) + bias[:, 3 * CHAN :]
        keyconv[rows] = kc
        mixed[rows] = (kc * qn[rows].astype(f32)).astype(bf16)
    g3.step2()
    for s in range(seqs):
        tap_logits(mixed[s * local : (s + 1) * local], wkx, bkx, logits)

        def mix(i, _):
            r = pl.ds(pl.multiple_of(i * ROW, ROW), ROW)
            win = convin[s, pl.ds(pl.multiple_of(i * ROW, ROW), 2 * ROW)]
            tw = softmax_taps(logits, r)
            acc = jnp.zeros((ROW, CHAN), f32)
            for t in range(TAPS):
                a = EDGE - TAPS // 2 + t
                acc = acc + tw[t] * win[a : a + ROW]
            joined[pl.ds(pl.multiple_of(s * local + i * ROW, ROW), ROW), CHAN:] = acc.astype(bf16)
            return 0

        lax.fori_loop(0, local // ROW, mix, 0)
    g4.step2()
    g3.step3()
    g5.step2()

    for j in range(HEADS_PER):
        for o in range(1, Z):
            sends[j * (Z - 1) + o - 1].wait_recv()
        for b in range(Z):
            val = unpack(abuf[j, b])
            rows = slice(b * local, (b + 1) * local)
            for p, ref in enumerate((qh, kh, vh)):
                ref[j, rows] = val[:, p * HEAD : (p + 1) * HEAD]
        sends += attend_unit(grid, j, qh, kh, vh, stats, csend, cbuf, bsend, brecv)
        if j == 0:
            g4.step3()
            g5.step3()
            g3.step4()
    g4.step4()
    g5.step4()
    for cp in sends[HEADS_PER * (Z - 1) :]:
        cp.wait_recv()
    for s in range(seqs):
        outs = []
        for n in range(HEADS):
            v = cbuf[n % HEADS_PER, 2 * s + n // HEADS_PER]
            outs.append(unpack(unpack(v)))
        joined[s * local : (s + 1) * local, :CHAN] = jnp.concatenate(outs, axis=1)
    for cp in sends + hops:
        cp.wait_send()
    for g in early + [g2, g3, g4, g5]:
        g.finish()


def spread_rows(xf, vec, spread, seqs, local):
    width = xf.shape[2]
    step = 256

    def body(i, _):
        for s in range(seqs):
            for c in range(width // step):
                cols = slice(c * step, (c + 1) * step)
                win = xf[s, pl.ds(pl.multiple_of(i * ROW, ROW), 2 * ROW), cols]
                acc = jnp.zeros((ROW, step), jnp.float32)
                for t in range(TAPS):
                    a = EDGE - TAPS // 2 + t
                    acc = acc + win[a : a + ROW] * vec[t : t + 1, cols]
                r = pl.ds(pl.multiple_of(s * local + i * ROW, ROW), ROW)
                spread[r, cols] = acc.astype(spread.dtype)
        return 0

    lax.fori_loop(0, local // ROW, body, 0)


def attend_unit(grid, h, qh, kh, vh, stats, csend, cbuf, bsend, brecv):
    f32, bf16 = jnp.float32, jnp.bfloat16
    z, Z = grid.z, grid.Z
    local = qh.shape[1] // Z
    sends = []
    scale = jnp.asarray(HEAD ** (-0.5), bf16)
    keys = kh[h]
    vt = vh[h].T
    for o in list(range(1, Z)) + [0]:
        b = (z + o) % Z
        rows = pl.ds(pl.multiple_of(b * local, local), local)
        st = dot_nt(keys, qh[h, rows] * scale)
        top = jnp.max(st, axis=0, keepdims=True)
        e = jnp.exp(st - top)
        den = jnp.sum(e, axis=0, keepdims=True)
        stats[h, b] = top + jnp.log(den)
        ct = dot(vt, e.astype(bf16)) / den
        val = pack(pack(ct.T.astype(bf16)))
        if o:
            csend[h, o - 1] = val
            cp = pltpu.make_async_remote_copy(
                src_ref=csend.at[h, o - 1], dst_ref=cbuf.at[h, z], send_sem=bsend.at[h, o - 1],
                recv_sem=brecv.at[h, o - 1], device_id=grid.dev(z=o), device_id_type=MESH,
            )
            cp.start()
            sends.append(cp)
        else:
            cbuf[h, z] = val
    return sends


def front(dp, seq, x, w_proj, w_out, w_up, w_down, small, w_kernel, b_kernel, widths):
    f32, bf16 = jnp.float32, jnp.bfloat16
    seqs, local, width = x.shape
    total = seqs * local
    length = seq * local
    N = dp * seq
    rows = w_proj.shape[0]
    lead = tiled(w_proj).shape[:2]
    shape = jax.ShapeDtypeStruct
    wide = 6 * PART
    ext = local + 2 * EDGE
    vm = pl.BlockSpec(memory_space=pltpu.VMEM)
    hb = pl.BlockSpec(memory_space=pl.ANY)
    other = [tiled(a) for a in (w_out, w_up, w_down)]
    hbm_out = [
        shape((N,) + lead + (c,), bf16) for c in (2 * PART,) * HEADS_PER + (2 * CHAN,)
    ]
    hbm_out += [shape((N,) + a.shape, bf16) for a in other]
    vm_out = [
        shape((HEADS_PER, length, HEAD), bf16),
        shape((HEADS_PER, length, HEAD), bf16),
        shape((HEADS_PER, length, HEAD), bf16),
        shape((HEADS_PER, seq, 1, local), f32),
        shape((total, width), bf16),
        shape((total, CHAN), bf16),
        shape((seqs, ext, width), bf16),
        shape((seqs, ext, CHAN), f32),
        shape((total, CHAN), f32),
        shape((total, CHAN), bf16),
        shape((total, width), bf16),
        shape((16, width), f32),
        shape((1, FF), f32),
        shape((TAPS, CHAN, CHAN), bf16),
        shape((16, CHAN), f32),
    ]
    sem = lambda *s: pltpu.SemaphoreType.DMA(s)
    return pl.pallas_call(
        partial(front_kernel, dp, seq, widths),
        out_shape=hbm_out + vm_out,
        in_specs=[vm, vm, hb, hb, hb, vm, vm, vm],
        out_specs=[hb] * len(hbm_out) + [vm] * len(vm_out),
        scratch_shapes=[
            pltpu.VMEM((HEADS_PER,) + lead + (2 * PART,), bf16),
            pltpu.VMEM(lead + (2 * CHAN,), bf16),
            pltpu.VMEM((N,) + small.shape, f32),
            pltpu.VMEM((HEADS_PER, width, 2 * PART), bf16),
            pltpu.VMEM((width, 2 * CHAN), bf16),
            pltpu.VMEM((seqs, ext, width), f32),
            pltpu.VMEM((2, seqs, EDGE, width), f32),
            pltpu.VMEM((2, seqs, EDGE, width), f32),
            pltpu.VMEM((seq, HEADS_PER, local // 2, 2 * PART), bf16),
            pltpu.VMEM((HEADS_PER, seq, local // 2, 2 * PART), bf16),
            pltpu.VMEM((HEADS_PER, seq - 1, local // 4, 4 * HEAD), bf16),
            pltpu.VMEM((HEADS_PER, seq, local // 4, 4 * HEAD), bf16),
            pltpu.VMEM((TAPS, local, CHAN), f32),
            pltpu.VMEM((1, 4 * CHAN), f32),
            sem(8, N - 1), sem(8, N - 1), sem(8),
            sem(HEADS_PER, seq - 1), sem(HEADS_PER, seq - 1),
            sem(HEADS_PER, seq - 1), sem(HEADS_PER, seq - 1), sem(2), sem(2), sem(HEADS_PER + 1),
        ],
        compiler_params=pltpu.CompilerParams(
            collective_id=2, has_side_effects=True, vmem_limit_bytes=VMEM_CAP
        ),
        name="front",
    )(x, w_proj, *other, small, w_kernel, b_kernel)


def pack_small(w_depth, vectors, b_proj, b_up):
    rows = [(i, v) for i, v in enumerate([w_depth[:, t] for t in range(TAPS)] + list(vectors))]
    rows += [(16, b_proj), (17, b_up)]
    out = jnp.zeros((24, 128), jnp.float32)
    for i, v in rows:
        out = out + jnp.pad(v.astype(jnp.float32)[None], ((i, 23 - i), (0, 128 - v.shape[0])))
    return out.reshape(3, 8, 128)


def unhalve(w):
    w = w.reshape(w.shape[:-1] + (2, 3, PART))
    return jnp.swapaxes(w, -3, -2).reshape(w.shape[:-3] + (3 * CHAN,))


PAD = 16


def to_owners(v, width, n):
    r, cols = v.shape
    keep = iota((n, r, cols), 2) // width == iota((n, r, cols), 0)
    stack = jnp.where(keep, v[None], 0.0).reshape(n * r, cols)
    pick = (iota((128, cols), 1) % width == iota((128, cols), 0)).astype(jnp.float32)
    out = lax.dot_general(
        stack, pick, (((1,), (1,)), ((), ())), precision=lax.Precision.HIGHEST,
        preferred_element_type=jnp.float32,
    )
    return out.reshape(n, r, 128)


def conv_back(
    s, local, gmix, convin, keyconv, mixed, qn, wkx, bkx, wkp, wpt,
    tw, gt, gl, gpad, gsp, gqm, gk, gci_ext, gwk, gbk, gbpoint,
):
    f32, bf16 = jnp.float32, jnp.bfloat16
    rows = slice(s * local, (s + 1) * local)
    body_rows = slice(PAD, PAD + local)
    for t in range(TAPS):
        tw[t, body_rows] = dot(mixed[rows], wkx[t]) + bkx[t : t + 1]
    gpad[body_rows] = gmix[rows]
    same = (iota((CHAN, CHAN), 0) // HEAD == iota((CHAN, CHAN), 1) // HEAD).astype(bf16)
    for t in range(TAPS):
        a = EDGE - TAPS // 2 + t
        p = gmix[rows] * convin[s, a : a + local]
        hi = p.astype(bf16)
        lo = (p - hi.astype(f32)).astype(bf16)
        gt[t] = dot(hi, same) + dot(lo, same)

    def taps(i, _):
        r = pl.ds(pl.multiple_of(i * ROW, ROW), ROW)
        rp = pl.ds(pl.multiple_of(PAD + i * ROW, ROW), ROW)
        ws = softmax_taps(tw, rp)
        gs = [gt[t, r] for t in range(TAPS)]
        mean = ws[0] * gs[0]
        for t in range(1, TAPS):
            mean = mean + ws[t] * gs[t]
        for t in range(TAPS):
            tw[t, rp] = ws[t]
            g = ws[t] * (gs[t] - mean)
            gl[t, r] = g.astype(bf16)
            gbk[t] += g[:8] + g[8:]
        return 0

    lax.fori_loop(0, local // ROW, taps, 0)

    def spread_back(i, _):
        w = pl.ds(pl.multiple_of(i * ROW, ROW), 2 * ROW)
        g = gpad[w]
        acc = jnp.zeros((ROW, CHAN), f32)
        for t in range(TAPS):
            a = PAD - TAPS // 2 - t
            acc = acc + (tw[t, w] * g)[a : a + ROW]
        gci_ext[s, pl.ds(pl.multiple_of(i * ROW, ROW), ROW)] = acc
        return 0

    lax.fori_loop(0, (local + 2 * EDGE) // ROW, spread_back, 0)
    compact = jnp.zeros((local, 128), f32)
    for t in range(TAPS):
        pick = (
            (iota((CHAN, 128), 0) == iota((CHAN, 128), 1) // TAPS * HEAD)
            & (iota((CHAN, 128), 1) % TAPS == t)
            & (iota((CHAN, 128), 1) < HEADS * TAPS)
        ).astype(bf16)
        compact = compact + dot(gl[t], pick)
    low = compact.astype(bf16)
    gwk[...] += dot_tn(low, mixed[rows])
    gmixed = dot(low, wkp[...])
    gqm[rows] = gmixed * keyconv[rows]
    gkc = gmixed * qn[rows].astype(f32)
    gbpoint[...] += rows_sum(gkc)
    glow = gkc.astype(bf16)
    gk[rows] = glow
    gsp[s, body_rows] = dot_nt(glow, wpt)


def depth_back(local, seqs, gsp, xe, vec, gdx_ext, gwd):
    f32 = jnp.float32
    width = gsp.shape[2]
    step = 256

    def grads(i, _):
        w = pl.ds(pl.multiple_of(i * ROW, ROW), 2 * ROW)
        for s in range(seqs):
            for c in range(width // step):
                cols = slice(c * step, (c + 1) * step)
                g = gsp[s, w, cols]
                acc = jnp.zeros((ROW, step), f32)
                for t in range(TAPS):
                    a = PAD - TAPS // 2 - t
                    acc = acc + g[a : a + ROW] * vec[t : t + 1, cols]
                gdx_ext[s, pl.ds(pl.multiple_of(i * ROW, ROW), ROW), cols] = acc
        return 0

    lax.fori_loop(0, (local + 2 * EDGE) // ROW, grads, 0)

    def weights(i, _):
        w = pl.ds(pl.multiple_of(i * ROW, ROW), 2 * ROW)
        for s in range(seqs):
            for c in range(width // step):
                cols = slice(c * step, (c + 1) * step)
                win = xe[s, w, cols].astype(f32)
                g = gsp[s, pl.ds(pl.multiple_of(PAD + i * ROW, ROW), ROW), cols]
                for t in range(TAPS):
                    a = EDGE - TAPS // 2 + t
                    p = win[a : a + ROW] * g
                    gwd[t, :, cols] += p[:8] + p[8:]
        return 0

    lax.fori_loop(0, local // ROW, weights, 0)


def attend_back_block(b, h, keys, vals, kt, qh, stats, dbuf, dkv, local, first):
    f32, bf16 = jnp.float32, jnp.bfloat16
    scale = HEAD ** (-0.5)
    rows = pl.ds(pl.multiple_of(b * local, local), local)
    q = qh[h, rows]
    do = unpack(dbuf[b])[:, h * HEAD : (h + 1) * HEAD]
    st = dot_nt(keys, q * jnp.asarray(scale, bf16))
    p = jnp.exp(st - stats[h, b])
    dp = dot_nt(vals, do)
    delta = jnp.sum(p * dp, axis=0, keepdims=True)
    ds = (p * (dp - delta)).astype(bf16)
    dk = dot(ds, q)
    dv = dot(p.astype(bf16), do)
    if first:
        dkv[0] = dk
        dkv[1] = dv
    else:
        dkv[0] += dk
        dkv[1] += dv
    return (dot(kt, ds) * scale).T


def back_kernel(
    dp, seq, widths,
    dctx, qh, kh, vh, stats, gmix, convin, keyconv, mixed, qn, spread, xe, vec, wkx, bkx, w_kernel,
    vecg, gbup, gafter, gq0, gq1, gq2, gcp, gwdown, gwup, gwout,
    gx, o_proj, o_out, o_up, o_down, o_small, o_kernel,
    *rest,
):
    f32, bf16 = jnp.float32, jnp.bfloat16
    pieces = 9
    parts, rest = rest[:pieces], rest[pieces:]
    bufs, rest = rest[: 4 * pieces], rest[4 * pieces :]
    souts, rest = rest[:5], rest[5:]
    souts = (o_down, o_up, o_out) + souts + (o_small,)
    (
        dbuf, dsend, gsend, grecv, wq, wcp, grads, tw, gt, gl, gpad, gsp, gqm, gk, gci_ext, gcl,
        gdx_ext, gwd, gwk, gbk, gbpoint, wkp, hsend, hrecv, dqb, dkv, kall, bprow,
        ssem, rsem, gssem, grsem, lsem, asend, arecv, bsend, brecv, esend, erecv, wsem,
    ) = rest
    grid = Grid(dp, seq)
    z, Z = grid.z, seq
    N = dp * seq
    seqs = xe.shape[0]
    total = dctx.shape[0]
    local = total // seqs
    width = xe.shape[2]
    w1, wp, wu = widths

    loads = [
        pltpu.make_async_copy(src, dst, wsem.at[i])
        for i, (src, dst) in enumerate(
            (
                (gwdown, parts[0]), (gwup, parts[1]), (gwout, parts[2]),
                (gcp.reshape(wcp.shape), wcp),
                (gafter, gx),
                (gq0.reshape((width, 2 * PART)), wq.at[0]),
                (gq1.reshape((width, 2 * PART)), wq.at[1]),
                (gq2.reshape((width, 2 * PART)), wq.at[2]),
            )
        )
    ]
    for cp in loads:
        cp.start()
    for s in range(seqs):
        for h in range(2):
            dsend[2 * s + h] = pack(
                dctx[s * local : (s + 1) * local, h * PART : (h + 1) * PART]
            )
    entry_barrier(grid)
    sends = []
    for o in range(1, Z):
        to = (z + o) % Z
        cp = pltpu.make_async_remote_copy(
            src_ref=dsend.at[to], dst_ref=dbuf.at[z], send_sem=bsend.at[o - 1],
            recv_sem=brecv.at[o - 1], device_id=grid.dev(z=o), device_id_type=MESH,
        )
        cp.start()
        sends.append(cp)
    dbuf[z] = dsend[z]
    orders = ("zxyc", "zyxc", "zxyc", "zyxc", "zxyc", "zyxc", "zxyc", "zxyc", "zyxc")
    sc = [
        Scatter(
            grid, parts[i], orders[i], bufs[4 * i : 4 * i + 4], souts[i], ssem.at[i], rsem.at[i]
        )
        for i in range(pieces)
    ]
    sdown, sup, sout, scp, sq0, sq1, sq2, skern, svec = sc
    for i in range(3):
        loads[i].wait()
        sc[i].start()

    wk = w_kernel[...]
    wkp[...] = dot(
        (iota((128, wk.shape[0]), 0) == iota((128, wk.shape[0]), 1)).astype(bf16), wk
    ).astype(bf16)
    gwk[...] = jnp.zeros_like(gwk)
    gbk[...] = jnp.zeros_like(gbk)
    gwd[...] = jnp.zeros_like(gwd)
    gbpoint[...] = jnp.zeros_like(gbpoint)
    gpad[...] = jnp.zeros_like(gpad)
    zeros = jnp.zeros((PAD, CHAN), f32)
    for t in range(TAPS):
        tw[t, :PAD] = zeros
        tw[t, PAD + local :] = zeros
    zeros = jnp.zeros((PAD, width), f32)
    for s in range(seqs):
        gsp[s, :PAD] = zeros
        gsp[s, PAD + local :] = zeros
    loads[3].wait()
    wpt = wcp[:, CHAN:]

    def conv(s):
        conv_back(
            s, local, gmix, convin, keyconv, mixed, qn, wkx, bkx, wkp, wpt,
            tw, gt, gl, gpad, gsp, gqm, gk, gci_ext, gwk, gbk, gbpoint,
        )

    for s in range(seqs - 1):
        conv(s)
    sdown.step1()
    sup.step1()
    sout.step1()

    scale = HEAD ** (-0.5)
    back = []
    for h in range(HEADS_PER):
        keys, vals = kh[h], vh[h]
        kt = keys.T
        for o in range(Z):
            b = (z + Z - o) % Z
            if o and h == 0:
                sends[o - 1].wait_recv()
            dqb[b] = attend_back_block(
                b, h, keys, vals, kt, qh, stats, dbuf, dkv, local, o == 0
            ).astype(bf16)
        for o in list(range(1, Z)) + [0]:
            b = (z + o) % Z
            r = pl.ds(pl.multiple_of(b * local, local), local)
            val = pack(
                jnp.concatenate(
                    [dqb[b], (dkv[0, r] * scale).astype(bf16), dkv[1, r].astype(bf16)], axis=1
                )
            )
            if o:
                gsend[h, o - 1] = val
                cp = pltpu.make_async_remote_copy(
                    src_ref=gsend.at[h, o - 1], dst_ref=grecv.at[h, z],
                    send_sem=asend.at[h, o - 1], recv_sem=arecv.at[h, o - 1],
                    device_id=grid.dev(z=o), device_id_type=MESH,
                )
                cp.start()
                back.append(cp)
            else:
                grecv[h, z] = val

    conv(seqs - 1)
    sdown.step2()
    sup.step2()
    sout.step2()
    depth_back(local, seqs, gsp, xe, vec, gdx_ext, gwd)
    for i, at in ((0, 0), (1, EDGE + local)):
        for s in range(seqs):
            hsend[i, s, :, :CHAN] = gci_ext[s, at : at + EDGE]
            hsend[i, s, :, CHAN:] = gdx_ext[s, at : at + EDGE]
    hops = []
    for i, o in ((0, seq - 1), (1, 1)):
        cp = pltpu.make_async_remote_copy(
            src_ref=hsend.at[i], dst_ref=hrecv.at[i], send_sem=esend.at[i],
            recv_sem=erecv.at[i], device_id=grid.dev(z=o), device_id_type=MESH,
        )
        cp.start()
        hops.append(cp)
    gw = dot_tn(spread[...], gk[...])
    gate = lambda v: v.reshape(parts[3].shape[:3] + (CHAN,)).astype(bf16)
    parts[3][:, :, :, CHAN:] = gate(gw)
    bias_row = jnp.zeros((1, 128), f32)
    for t in range(TAPS):
        pick = (
            (iota((CHAN, 128), 0) == iota((CHAN, 128), 1) // TAPS * HEAD)
            & (iota((CHAN, 128), 1) % TAPS == t)
            & (iota((CHAN, 128), 1) < HEADS * TAPS)
        ).astype(f32)
        bias_row = bias_row + jnp.dot(
            rows_sum(gbk[t]), pick, precision=lax.Precision.HIGHEST, preferred_element_type=f32
        )
    parts[7][...] = jnp.zeros_like(parts[7])
    for c in range(CHAN // 128):
        tile = gwk[:TALL, c * 128 : (c + 1) * 128]
        if c == 0:
            tile = jnp.where(iota((TALL, 128), 0) == HEADS * TAPS, bias_row, tile)
        n = TALL // 8
        parts[7][c * n : (c + 1) * n, 0] = tile.reshape(n, 8, 128)
    skern.start()
    qsum, vsum = {}, {}

    def gather_grads(j):
        for o in range(1, Z):
            back[j * (Z - 1) + o - 1].wait_recv()
        gw = jnp.zeros((width, 2 * PART), f32)
        for s in range(seqs):
            r = slice(s * local, (s + 1) * local)
            vals = []
            for h in range(2):
                n = h * HEADS_PER + j
                val = unpack(grecv[j, 2 * s + h])
                q = (val[:, :HEAD].astype(f32) + gqm[r, n * HEAD : (n + 1) * HEAD]).astype(bf16)
                qsum[n] = qsum.get(n, 0.0) + rows_sum(q.astype(f32))
                vsum[n] = vsum.get(n, 0.0) + rows_sum(val[:, 2 * HEAD :].astype(f32))
                vals += [q, val[:, HEAD:]]
            low = jnp.concatenate(vals, axis=1)
            grads[j, r] = low
            gw = gw + dot_tn(xe[s, EDGE : EDGE + local], low)
        parts[4 + j][...] = gw.reshape(parts[4 + j].shape).astype(bf16)
        sc[4 + j].start()

    gather_grads(0)

    for cp in hops:
        cp.wait_recv()
    gbconv = jnp.zeros((1, CHAN), f32)
    for s in range(seqs):
        for i, at, ok in ((0, local, z < Z - 1), (1, EDGE, z > 0)):
            add = jnp.where(ok, hrecv[i, s], 0.0)
            gci_ext[s, at : at + EDGE] += add[:, :CHAN]
            gdx_ext[s, at : at + EDGE] += add[:, CHAN:]
        own = gci_ext[s, EDGE : EDGE + local]
        gbconv = gbconv + rows_sum(own)
        gcl[s * local : (s + 1) * local] = own.astype(bf16)
    gw = jnp.zeros((width, CHAN), f32)
    for s in range(seqs):
        gw = gw + dot_tn(xe[s, EDGE : EDGE + local], gcl[s * local : (s + 1) * local])
    parts[3][:, :, :, :CHAN] = gate(gw)
    scp.start()
    skern.step1()
    sq0.step1()
    loads[4].wait()
    for s in range(seqs):
        r = slice(s * local, (s + 1) * local)
        gx[r] += gdx_ext[s, EDGE : EDGE + local] + dot_nt(gcl[r], wcp[:, :CHAN])
    gather_grads(1)
    sdown.step3()
    sup.step3()
    sout.step3()
    scp.step1()
    skern.step2()
    sq0.step2()
    taps = jnp.concatenate([rows_sum(gwd[t]) for t in range(TAPS)], axis=0)
    head = jnp.concatenate([taps, vecg[TAPS:16]], axis=0)
    own = to_owners(head, w1, N)
    parts[8][:, 0] = own[:, :8]
    parts[8][:, 1] = own[:, 8:]
    up_rows = to_owners(jnp.where(iota((8, FF), 0) == 1, gbup[...], 0.0), wu, N)
    sq1.step1()
    scp.step2()
    gather_grads(2)
    bprow[...] = jnp.concatenate(
        [qsum[n] for n in range(HEADS)] + [vsum[n] for n in range(HEADS)] + [gbconv, gbpoint[...]],
        axis=1,
    )
    own = to_owners(jnp.where(iota((8, 4 * CHAN), 0) == 0, bprow[...], 0.0), wp, N)
    parts[8][:, 2] = own + up_rows
    svec.start()
    skern.step3()
    sq0.step3()
    sq1.step2()
    sq2.step1()
    svec.step1()
    skern.step4()
    gk_tail = Gather(grid, souts[7], kall, "zxyc", gssem, grsem, lsem)
    gk_tail.start()
    scp.step3()
    for i in range(HEADS_PER):
        loads[5 + i].wait()
    for s in range(seqs):
        r = slice(s * local, (s + 1) * local)
        acc = gx[r]
        for j in range(HEADS_PER):
            acc = acc + dot_nt(grads[j, r], wq[j])
        gx[r] = acc
    sq1.step3()
    sq2.step2()
    svec.step2()
    gk_tail.step1()
    sdown.step4()
    sup.step4()
    sout.step4()
    sq2.step3()
    svec.step3()
    gk_tail.step2()
    scp.step4()
    sq0.step4()
    sq1.step4()
    gk_tail.step3()
    gk_tail.step4()
    n = TALL // 8
    o_kernel[...] = jnp.concatenate(
        [kall[c * n : (c + 1) * n, 0].reshape(TALL, 128) for c in range(CHAN // 128)], axis=1
    )
    sq2.step4()
    svec.step4()
    flat = [souts[4 + j][...].reshape(w1, 2 * PART) for j in range(HEADS_PER)]
    cols = []
    for p in range(3):
        for n in range(HEADS):
            at = n // HEADS_PER * PART + p * HEAD
            cols.append(flat[n % HEADS_PER][:, at : at + HEAD])
    o_proj[:, : 3 * CHAN] = jnp.concatenate(cols, axis=1)
    o_proj[:, 3 * CHAN :] = souts[3][...].reshape(w1, 2 * CHAN)
    for cp in sends + back + hops:
        cp.wait_send()
    for g in sc:
        g.finish()
    gk_tail.finish()


TALL = -(-(HEADS * TAPS + 1) // 8) * 8


def back(dp, seq, widths, values, gathered, wgrads, shards):
    f32, bf16 = jnp.float32, jnp.bfloat16
    (
        dctx, qh, kh, vh, stats, gmix, convin, keyconv, mixed, qn, spread, xe, vec, wkx, bkx,
        w_kernel, vecg, gbup,
    ) = values
    N = dp * seq
    w1, wp, wu = widths
    seqs, ext, width = xe.shape
    total = dctx.shape[0]
    local = total // seqs
    length = kh.shape[1]
    sizes = sizes_of(dp, seq)
    shape = jax.ShapeDtypeStruct
    vm = pl.BlockSpec(memory_space=pltpu.VMEM)
    hb = pl.BlockSpec(memory_space=pl.ANY)
    t_down, t_up, t_out = [tiled(a).shape for a in shards]
    lead = t_out[:2]
    piece = [
        (t_down, bf16), (t_up, bf16), (t_out, bf16), (lead + (2 * CHAN,), bf16),
    ]
    piece += [(lead + (2 * PART,), bf16)] * HEADS_PER
    piece += [((1, 8, 128), f32), ((3, 8, 128), f32)]
    wgrads = [g.reshape((N,) + p[0]) for g, p in zip(wgrads, piece)]
    scratch = [pltpu.VMEM((N,) + p, d) for p, d in piece]
    for p, d in piece:
        scratch += scatter_scratch(sizes, p, d, "zxyc")
    scratch += [pltpu.VMEM(p, f32) for p, d in piece[3:8]]
    V = pltpu.VMEM
    scratch += [
        V((seq, local // 2, 2 * PART), bf16),
        V((seq, local // 2, 2 * PART), bf16),
        V((HEADS_PER, seq - 1, local // 2, 2 * PART), bf16),
        V((HEADS_PER, seq, local // 2, 2 * PART), bf16),
        V((HEADS_PER, width, 2 * PART), bf16),
        V((width, 2 * CHAN), bf16),
        V((HEADS_PER, total, 2 * PART), bf16),
        V((TAPS, local + 2 * PAD, CHAN), f32),
        V((TAPS, local, CHAN), f32),
        V((TAPS, local, CHAN), bf16),
        V((local + 2 * PAD, CHAN), f32),
        V((seqs, local + 2 * PAD, width), f32),
        V((total, CHAN), f32),
        V((total, CHAN), bf16),
        V((seqs, ext, CHAN), f32),
        V((total, CHAN), bf16),
        V((seqs, ext, width), f32),
        V((TAPS, 8, width), f32),
        V((128, CHAN), f32),
        V((TAPS, 8, CHAN), f32),
        V((1, CHAN), f32),
        V((128, CHAN), bf16),
        V((2, seqs, EDGE, CHAN + width), f32),
        V((2, seqs, EDGE, CHAN + width), f32),
        V((seq, local, HEAD), bf16),
        V((2, length, HEAD), f32),
        V((N, 1, 8, 128), f32),
        V((1, 4 * CHAN), f32),
    ]
    sem = lambda *s: pltpu.SemaphoreType.DMA(s)
    n = len(piece)
    scratch += [
        sem(n, N - 1), sem(n, N - 1), sem(N - 1), sem(N - 1), sem(),
        sem(HEADS_PER, seq - 1), sem(HEADS_PER, seq - 1), sem(seq - 1), sem(seq - 1),
        sem(2), sem(2), sem(8),
    ]
    outs = [
        shape((total, width), f32),
        shape((w1, 5 * CHAN), f32),
        shape(t_out, f32),
        shape(t_up, f32),
        shape(t_down, f32),
        shape((3, 8, 128), f32),
        shape((TALL, CHAN), f32),
    ]
    return pl.pallas_call(
        partial(back_kernel, dp, seq, widths),
        out_shape=outs,
        in_specs=[vm] * len(values) + [hb] * 8,
        out_specs=[vm] * len(outs),
        scratch_shapes=scratch,
        compiler_params=pltpu.CompilerParams(
            collective_id=3, has_side_effects=True, vmem_limit_bytes=62 << 20
        ),
        name="back",
    )(*values, *gathered, *wgrads)


def finish_kernel(gx, proj, out, up, down, small, kern, *rest):
    outs, held, sem = rest[:-6], rest[-6:-1], rest[-1]
    copies = [
        pltpu.make_async_copy(a, b, sem.at[0, i])
        for i, (a, b) in enumerate(zip((gx, proj, out, up, down), held))
    ]
    for cp in copies:
        cp.start()
    stores = [
        pltpu.make_async_copy(a, b, sem.at[1, i])
        for i, (a, b) in enumerate(zip(held, outs[:5]))
    ]
    for a, b in zip(copies, stores):
        a.wait()
        b.start()
    depth, kernel_t, bkernel, bproj, bup = outs[5:10]
    s = small[...]
    depth[...] = s[:2].reshape(16, 128)[: depth.shape[0], : depth.shape[1]]
    kernel_t[...] = kern[: kernel_t.shape[0]]
    bkernel[...] = kern[HEADS * TAPS : HEADS * TAPS + 1, : HEADS * TAPS]
    bproj[...] = s[2, 0:1, : bproj.shape[1]]
    bup[...] = s[2, 1:2, : bup.shape[1]]
    for i, v in zip(range(V_BOUT, V_S2 + 1), outs[10:]):
        v[...] = s[i // 8, i % 8 : i % 8 + 1, : v.shape[1]]
    for cp in stores:
        cp.wait()


def finish(widths, arrays):
    f32 = jnp.float32
    w1, wp, wu = widths
    shape = jax.ShapeDtypeStruct
    vm = pl.BlockSpec(memory_space=pltpu.VMEM)
    hb = pl.BlockSpec(memory_space=pl.ANY)
    outs = [shape(a.shape, f32) for a in arrays[:5]]
    outs += [
        shape((TAPS, w1), f32), shape((HEADS * TAPS, CHAN), f32), shape((1, HEADS * TAPS), f32),
        shape((1, wp), f32), shape((1, wu), f32),
    ]
    outs += [shape((1, w1), f32)] * 6
    return pl.pallas_call(
        finish_kernel,
        out_shape=outs,
        in_specs=[hb] * 5 + [vm] * 2,
        out_specs=[hb] * 5 + [vm] * 11,
        scratch_shapes=[pltpu.VMEM(a.shape, f32) for a in arrays[:5]]
        + [pltpu.SemaphoreType.DMA((2, 5))],
        name="finish",
    )(*arrays)


def fast_body(
    hidden, cotangent, w_proj, w_depth, w_kernel, b_kernel, w_out, w_up, w_down, b_proj, b_up,
    b_out, ln1_gain, ln1_bias, b_down, ln2_gain, ln2_bias,
):
    dp, seq = lax.axis_size("dp"), lax.axis_size("seq")
    seqs, local, width = hidden.shape
    total = seqs * local
    widths = (w_out.shape[0], b_proj.shape[0], b_up.shape[0])
    small = pack_small(
        w_depth, (b_out, ln1_gain, ln1_bias, b_down, ln2_gain, ln2_bias), b_proj, b_up
    )
    w_kernel = w_kernel.T
    (
        gq0, gq1, gq2, gcp, gout, gup, gdown, qh, kh, vh, stats, joined, qn, xe, convin, keyconv, mixed,
        spread, vec, bup, wkx, bkx,
    ) = front(
        dp, seq, hidden, w_proj, w_out, w_up, w_down, small, w_kernel, b_kernel[None], widths
    )
    out, gafter, dctx, gmix, gwout, gwup, gwdown, vecg, gbup = ffn(
        joined, hidden.reshape(total, width), cotangent.reshape(total, width),
        gout.reshape(-1, w_out.shape[1]), gup.reshape(-1, w_up.shape[1]),
        gdown.reshape(-1, w_down.shape[1]), vec, bup,
    )
    res = back(
        dp, seq, widths,
        (
            dctx, qh, kh, vh, stats, gmix, convin, keyconv, mixed, qn, spread, xe, vec, wkx, bkx,
            w_kernel, vecg, gbup,
        ),
        (gafter, gq0, gq1, gq2, gcp), (gwdown, gwup, gwout), (w_down, w_up, w_out),
    )
    (
        gx, g_proj, g_out, g_up, g_down, g_depth, g_kernel, g_bkernel, g_bproj, g_bup, *g_vecs,
    ) = finish(widths, res)
    return (
        out.reshape(hidden.shape),
        gx.reshape(hidden.shape),
        g_proj,
        g_depth.T,
        g_kernel.T,
        g_bkernel[0],
        g_out.reshape(w_out.shape),
        g_up.reshape(w_up.shape),
        g_down.reshape(w_down.shape),
        g_bproj[0],
        g_bup[0],
    ) + tuple(v[0] for v in g_vecs)


def fits(mesh):
    return mesh.shape["seq"] == 4 and mesh.shape["dp"] == 8


def body(
    hidden,
    cotangent,
    w_proj,
    w_depth,
    w_kernel,
    b_kernel,
    w_out,
    w_up,
    w_down,
    b_proj,
    b_up,
    b_out,
    ln1_gain,
    ln1_bias,
    b_down,
    ln2_gain,
    ln2_bias,
):
    seq_count, local_rows, model_width = hidden.shape
    total_rows = seq_count * local_rows
    head_count = HEADS
    head_size = HEAD
    all_width = head_count * head_size
    tap_count = KERNEL
    half_kernel = KERNEL // 2
    group_count = GROUPS
    hidden_units = FF
    ext_rows = local_rows + 2 * half_kernel
    score_scale = head_size ** (-0.5)
    dp, seq = lax.axis_size("dp"), lax.axis_size("seq")
    devices = dp * seq
    vectors = (b_proj, b_up, b_out, ln1_gain, ln1_bias, b_down, ln2_gain, ln2_bias)
    widths = [w_depth.shape[0] * KERNEL] + [v.shape[0] for v in vectors]
    small = jnp.concatenate([w_depth.reshape(-1)] + list(vectors))
    small = jnp.pad(small, (0, 1024 - small.shape[0])).reshape(8, 128)
    full_proj, full_out, full_up, full_down, small = gather_all(
        dp, seq, [w_proj, w_out, w_up, w_down, small]
    )
    small = cut(small.reshape(devices, 1024), widths)
    full_depth = small[0].reshape(-1, KERNEL)
    (
        full_bproj,
        full_bup,
        full_bout,
        gain_one,
        shift_one,
        full_bdown,
        gain_two,
        shift_two,
    ) = [v.reshape(-1) for v in small[1:]]
    bias_proj = full_bproj.astype(jnp.float32)
    gain_first = gain_one.astype(jnp.float32)
    shift_first = shift_one.astype(jnp.float32)
    gain_second = gain_two.astype(jnp.float32)
    shift_second = shift_two.astype(jnp.float32)
    tokens_flat = hidden.reshape(total_rows, model_width)
    first_proj = jnp.dot(
        tokens_flat, full_proj[:, : 3 * all_width], preferred_element_type=jnp.float32
    )
    queries = (first_proj[:, :all_width] + bias_proj[:all_width]).astype(jnp.bfloat16)
    key_rows = first_proj[:, all_width : 2 * all_width].astype(jnp.bfloat16)
    value_rows = (first_proj[:, 2 * all_width :] + bias_proj[all_width : 2 * all_width]).astype(
        jnp.bfloat16
    )
    extended = with_halo(hidden, (("seq", 1),), half_kernel)
    position = lax.axis_index("seq") * local_rows + jnp.arange(ext_rows) - half_kernel
    inside = ((position >= 0) & (position < local_rows * lax.axis_size("seq"))).astype(jnp.float32)
    conv_input = jnp.dot(
        extended.reshape(seq_count * ext_rows, model_width),
        full_proj[:, 3 * all_width : 4 * all_width],
        preferred_element_type=jnp.float32,
    )
    conv_input = (conv_input + bias_proj[2 * all_width : 3 * all_width]).reshape(
        seq_count, ext_rows, all_width
    ) * inside[None, :, None]
    depth_weights = full_depth.astype(jnp.float32)
    depth_sum = jnp.zeros((seq_count, local_rows, model_width), jnp.float32)
    for tap_index in range(tap_count):
        depth_sum = (
            depth_sum
            + extended[:, tap_index : tap_index + local_rows].astype(jnp.float32)
            * depth_weights[:, tap_index]
        )
    spread = depth_sum.astype(jnp.bfloat16).reshape(total_rows, model_width)
    key_conv = (
        jnp.dot(spread, full_proj[:, 4 * all_width :], preferred_element_type=jnp.float32)
        + bias_proj[3 * all_width :]
    )
    mixed_key = (key_conv * queries.astype(jnp.float32)).astype(jnp.bfloat16)
    logits = jnp.dot(mixed_key, w_kernel, preferred_element_type=jnp.float32) + b_kernel.astype(
        jnp.float32
    )
    tap_weights = jax.nn.softmax(
        logits.reshape(seq_count, local_rows, head_count, tap_count), axis=-1
    )
    conv_heads = conv_input.reshape(seq_count, ext_rows, head_count, head_size)
    conv_mix = jnp.zeros((seq_count, local_rows, head_count, head_size), jnp.float32)
    for tap_index in range(tap_count):
        conv_mix = (
            conv_mix
            + tap_weights[..., tap_index, None] * conv_heads[:, tap_index : tap_index + local_rows]
        )
    queries_seq = queries.reshape(seq_count, local_rows, all_width)
    all_keys, all_values = (
        lax.all_gather(
            key_rows.reshape(seq_count, local_rows, all_width), "seq", axis=1, tiled=True
        ),
        lax.all_gather(
            value_rows.reshape(seq_count, local_rows, all_width), "seq", axis=1, tiled=True
        ),
    )
    full_length = all_keys.shape[1]

    def forward_one(item_set):
        query_seq, key_seq, value_seq = item_set
        return attend(
            query_seq.reshape(local_rows, head_count, head_size),
            key_seq.reshape(full_length, head_count, head_size),
            value_seq.reshape(full_length, head_count, head_size),
            score_scale,
        )

    context, norm_log = lax.map(forward_one, (queries_seq, all_keys, all_values))
    joined = jnp.concatenate(
        [
            context.reshape(total_rows, all_width),
            conv_mix.reshape(total_rows, all_width).astype(jnp.bfloat16),
        ],
        axis=-1,
    )
    after_mix = (
        jnp.dot(joined, full_out, preferred_element_type=jnp.float32)
        + full_bout.astype(jnp.float32)
        + tokens_flat.astype(jnp.float32)
    )
    first_norm, first_pull = jax.vjp(layer_norm, after_mix, gain_first, shift_first)
    grouped_in = first_norm.astype(jnp.bfloat16).reshape(
        total_rows, group_count, model_width // group_count
    )
    up_groups = full_up.reshape(
        group_count, model_width // group_count, hidden_units // group_count
    )
    pre_act = jnp.einsum(
        "ngd,gdf->ngf", grouped_in, up_groups, preferred_element_type=jnp.float32
    ).reshape(total_rows, hidden_units) + full_bup.astype(jnp.float32)
    activated, gelu_pull = jax.vjp(partial(jax.nn.gelu, approximate=False), pre_act)
    act_low = activated.astype(jnp.bfloat16).reshape(
        total_rows, group_count, hidden_units // group_count
    )
    down_groups = full_down.reshape(
        group_count, hidden_units // group_count, model_width // group_count
    )
    summed = jnp.einsum(
        "ngf,gfd->ngd", act_low, down_groups, preferred_element_type=jnp.float32
    ).reshape(total_rows, model_width)
    summed = summed + full_bdown.astype(jnp.float32) + first_norm
    out_value, second_pull = jax.vjp(layer_norm, summed, gain_second, shift_second)
    output = out_value.astype(jnp.bfloat16).reshape(seq_count, local_rows, model_width)
    back_proj = full_proj
    back_depth = full_depth.astype(jnp.float32)
    back_out = full_out
    back_up = up_groups
    back_down = down_groups
    grad_summed, grad_gain_two, grad_shift_two = second_pull(
        cotangent.reshape(total_rows, model_width).astype(jnp.float32)
    )
    grad_bdown = jnp.sum(grad_summed, axis=0)
    summed_low = grad_summed.astype(jnp.bfloat16).reshape(
        total_rows, group_count, model_width // group_count
    )
    grad_activ = jnp.einsum(
        "ngd,gfd->ngf", summed_low, back_down, preferred_element_type=jnp.float32
    ).reshape(total_rows, hidden_units)
    grad_wdown = jnp.einsum(
        "ngf,ngd->gfd", act_low, summed_low, preferred_element_type=jnp.float32
    ).reshape(hidden_units, model_width // group_count)
    grad_pre = gelu_pull(grad_activ)[0]
    grad_bup = jnp.sum(grad_pre, axis=0)
    pre_low = grad_pre.astype(jnp.bfloat16).reshape(
        total_rows, group_count, hidden_units // group_count
    )
    grad_wup = jnp.einsum(
        "ngd,ngf->gdf", grouped_in, pre_low, preferred_element_type=jnp.float32
    ).reshape(model_width, hidden_units // group_count)
    grad_first = grad_summed + jnp.einsum(
        "ngf,gdf->ngd", pre_low, back_up, preferred_element_type=jnp.float32
    ).reshape(total_rows, model_width)
    grad_after, grad_gain_one, grad_shift_one = first_pull(grad_first)
    grad_bout = jnp.sum(grad_after, axis=0)
    after_low = grad_after.astype(jnp.bfloat16)
    grad_wout = jnp.dot(joined.T, after_low, preferred_element_type=jnp.float32)
    grad_joined = jnp.dot(after_low, back_out.T, preferred_element_type=jnp.float32)
    grad_context = (
        grad_joined[:, :all_width].astype(jnp.bfloat16).reshape(seq_count, local_rows, all_width)
    )
    grad_mix = grad_joined[:, all_width:].reshape(seq_count, local_rows, head_count, head_size)

    def back_one(item_set):
        query_seq, grad_seq, norm_seq, key_seq, value_seq = item_set
        grad_query, grad_key, grad_value, unused_delta = attend_back(
            query_seq.reshape(local_rows, head_count, head_size),
            grad_seq.reshape(local_rows, head_count, head_size),
            norm_seq,
            key_seq.reshape(full_length, head_count, head_size),
            value_seq.reshape(full_length, head_count, head_size),
            None,
            score_scale,
        )
        key_value = jnp.concatenate(
            [grad_key.reshape(full_length, all_width), grad_value.reshape(full_length, all_width)],
            axis=-1,
        )
        return (grad_query.reshape(local_rows, all_width), key_value)

    grad_query_att, kv_terms = lax.map(
        back_one, (queries_seq, grad_context, norm_log, all_keys, all_values)
    )
    own_kv = lax.psum_scatter(
        kv_terms.astype(jnp.bfloat16), "seq", scatter_dimension=1, tiled=True
    ).astype(jnp.float32)
    grad_keys_low = own_kv[..., :all_width].reshape(total_rows, all_width).astype(jnp.bfloat16)
    grad_values_low = own_kv[..., all_width:].reshape(total_rows, all_width).astype(jnp.bfloat16)
    grad_taps = jnp.stack(
        [
            jnp.sum(grad_mix * conv_heads[:, tap_index : tap_index + local_rows], axis=-1)
            for tap_index in range(tap_count)
        ],
        axis=-1,
    )
    grad_conv_ext = jnp.zeros((seq_count, ext_rows, head_count, head_size), jnp.float32)
    for tap_index in range(tap_count):
        grad_conv_ext = grad_conv_ext + jnp.pad(
            tap_weights[..., tap_index, None] * grad_mix,
            ((0, 0), (tap_index, 2 * half_kernel - tap_index), (0, 0), (0, 0)),
        )
    grad_logits = tap_weights * (
        grad_taps - jnp.sum(tap_weights * grad_taps, axis=-1, keepdims=True)
    )
    grad_logits = grad_logits.reshape(total_rows, head_count * tap_count)
    grad_bkernel = jnp.sum(grad_logits, axis=0)
    logits_low = grad_logits.astype(jnp.bfloat16)
    grad_wkernel = jnp.dot(mixed_key.T, logits_low, preferred_element_type=jnp.float32)
    grad_mixed = jnp.dot(logits_low, w_kernel.T, preferred_element_type=jnp.float32)
    grad_queries = (grad_query_att.reshape(total_rows, all_width) + grad_mixed * key_conv).astype(
        jnp.bfloat16
    )
    grad_key_conv = grad_mixed * queries.astype(jnp.float32)
    grad_bpt = jnp.sum(grad_key_conv, axis=0)
    key_conv_low = grad_key_conv.astype(jnp.bfloat16)
    grad_wpt = jnp.dot(spread.T, key_conv_low, preferred_element_type=jnp.float32)
    grad_spread = jnp.dot(
        key_conv_low, back_proj[:, 4 * all_width :].T, preferred_element_type=jnp.float32
    ).reshape(seq_count, local_rows, model_width)
    grad_wdepth = jnp.stack(
        [
            jnp.sum(
                extended[:, tap_index : tap_index + local_rows].astype(jnp.float32) * grad_spread,
                axis=(0, 1),
            )
            for tap_index in range(tap_count)
        ],
        axis=-1,
    )
    grad_ext_depth = jnp.zeros((seq_count, ext_rows, model_width), jnp.float32)
    for tap_index in range(tap_count):
        grad_ext_depth = grad_ext_depth + jnp.pad(
            back_depth[:, tap_index] * grad_spread,
            ((0, 0), (tap_index, 2 * half_kernel - tap_index), (0, 0)),
        )
    combined = jnp.concatenate(
        [grad_conv_ext.reshape(seq_count, ext_rows, all_width), grad_ext_depth], axis=-1
    )
    received = with_halo(combined.astype(jnp.bfloat16), (("seq", 1),), half_kernel).astype(
        combined.dtype
    )
    own_part = combined[:, half_kernel : half_kernel + local_rows]
    own_part = own_part.at[:, :half_kernel].add(received[:, :half_kernel])
    own_part = own_part.at[:, local_rows - half_kernel :].add(
        received[:, received.shape[1] - half_kernel :]
    )
    grad_conv_own = own_part[..., :all_width].reshape(total_rows, all_width)
    grad_depth_x = own_part[..., all_width:].reshape(total_rows, model_width)
    grad_bconv = jnp.sum(grad_conv_own, axis=0)
    conv_low = grad_conv_own.astype(jnp.bfloat16)
    stacked = jnp.concatenate([grad_queries, grad_keys_low, grad_values_low, conv_low], axis=-1)
    grad_wfirst = jnp.dot(tokens_flat.T, stacked, preferred_element_type=jnp.float32)
    grad_tokens = (
        grad_after
        + jnp.dot(stacked, back_proj[:, : 4 * all_width].T, preferred_element_type=jnp.float32)
        + grad_depth_x
    )
    grad_wproj = jnp.concatenate([grad_wfirst, grad_wpt], axis=1)
    grad_bproj = jnp.concatenate(
        [
            jnp.sum(grad_queries.astype(jnp.float32), axis=0),
            jnp.sum(grad_values_low.astype(jnp.float32), axis=0),
            grad_bconv,
            grad_bpt,
        ]
    )
    def blocks(grad, shard):
        return grad.astype(jnp.bfloat16).reshape((devices,) + tiled(shard).shape)

    per_device = [
        g.reshape(devices, -1)
        for g in (
            grad_wdepth, grad_bproj, grad_bup, grad_bout, grad_gain_one, grad_shift_one,
            grad_bdown, grad_gain_two, grad_shift_two,
        )
    ]
    kernel_flat = jnp.concatenate([grad_wkernel.reshape(-1), grad_bkernel])
    kernel_len = kernel_flat.shape[0]
    kernel_each = -(-kernel_len // devices)
    kernel_flat = jnp.pad(kernel_flat, (0, kernel_each * devices - kernel_len))
    small_grad = jnp.concatenate(
        [
            lanes(jnp.concatenate(per_device, axis=1), 1),
            lanes(kernel_flat.reshape(devices, kernel_each), 1),
        ],
        axis=1,
    )
    sum_down, sum_up, sum_out, sum_proj, sum_small, sum_kernel = scatter_all(
        dp,
        seq,
        [
            blocks(grad_wdown, w_down), blocks(grad_wup, w_up), blocks(grad_wout, w_out),
            blocks(grad_wproj, w_proj), small_grad,
        ],
        ("zxyc", "zyxc", "zxyc", "zyxc", "zxyc"),
    )
    mine = cut(sum_small[:1].reshape(1, 1024), widths)
    shards = [sum_proj.reshape(w_proj.shape), mine[0].reshape(w_depth.shape)]
    shards += [
        sum_out.reshape(w_out.shape), sum_up.reshape(w_up.shape), sum_down.reshape(w_down.shape),
    ]
    shards += [m.reshape(-1) for m in mine[1:]]
    kernel_sum = sum_kernel.reshape(devices, 1024)[:, :kernel_each].reshape(-1)
    kernel_total = (
        kernel_sum[: grad_wkernel.size].reshape(grad_wkernel.shape),
        kernel_sum[grad_wkernel.size : kernel_len],
    )
    return (
        output,
        grad_tokens.reshape(seq_count, local_rows, model_width),
        shards[0],
        shards[1],
        kernel_total[0],
        kernel_total[1],
        shards[2],
        shards[3],
        shards[4],
        shards[5],
        shards[6],
        shards[7],
        shards[8],
        shards[9],
        shards[10],
        shards[11],
        shards[12],
    )


def solution(mesh):
    placed = (
        P("dp", "seq", None),
        P("dp", "seq", None),
        P(("dp", "seq"), None),
        P(("dp", "seq"), None),
        P(),
        P(),
        P(("dp", "seq"), None),
        P(("dp", "seq"), None),
        P(("dp", "seq"), None),
        P(("dp", "seq")),
        P(("dp", "seq")),
        P(("dp", "seq")),
        P(("dp", "seq")),
        P(("dp", "seq")),
        P(("dp", "seq")),
        P(("dp", "seq")),
        P(("dp", "seq")),
    )
    return jax.shard_map(
        fast_body if fits(mesh) else body,
        mesh=mesh,
        in_specs=placed,
        out_specs=(
            P("dp", "seq", None),
            P("dp", "seq", None),
            P(("dp", "seq"), None),
            P(("dp", "seq"), None),
            P(),
            P(),
            P(("dp", "seq"), None),
            P(("dp", "seq"), None),
            P(("dp", "seq"), None),
            P(("dp", "seq")),
            P(("dp", "seq")),
            P(("dp", "seq")),
            P(("dp", "seq")),
            P(("dp", "seq")),
            P(("dp", "seq")),
            P(("dp", "seq")),
            P(("dp", "seq")),
        ),
        check_vma=False,
    )
```

```python
from functools import partial

import jax
import jax.numpy as jnp
from jax import lax
from jax.experimental import pallas as pl
from jax.experimental.pallas import tpu as pltpu
from jax.sharding import PartitionSpec as P

MESH = pl.DeviceIdType.MESH


class Grid:
    def __init__(self, dp, seq):
        self.C = 2 if dp % 2 == 0 else 1
        rest = dp // self.C
        y = 1
        while (2 * y) * (2 * y) <= rest and rest % (2 * y) == 0:
            y *= 2
        self.Y, self.X, self.Z = y, rest // y, seq
        d = lax.axis_index("dp")
        self.z = lax.axis_index("seq")
        self.c = d % self.C
        self.x = (d // self.C) % self.X
        self.y = d // (self.C * self.X)
        self.dp = d
    def size(self, ax):
        return getattr(self, ax.upper())
    def at(self, **off):
        g = {a: (getattr(self, a) + off.get(a, 0)) % self.size(a) if off.get(a, 0) else getattr(self, a) for a in "yxcz"}
        return g
    def dpof(self, g):
        return (g["y"] * self.X + g["x"]) * self.C + g["c"]
    def dev(self, **off):
        g = self.at(**off)
        return (self.dpof(g), g["z"])


def peers(grid):
    out = []
    for a in "zxyc":
        for o in range(1, grid.size(a)):
            out.append(grid.dev(**{a: o}))
    return out


def greet(grid):
    for p in peers(grid):
        pl.semaphore_signal(
            pltpu.get_barrier_semaphore(), inc=1, device_id=p, device_id_type=MESH
        )


def meet(grid):
    pl.semaphore_wait(pltpu.get_barrier_semaphore(), len(peers(grid)))


def entry_barrier(grid):
    greet(grid)
    meet(grid)


def pick(ref, axes, at):
    return ref.at[tuple(at[a] if a in axes else slice(None) for a in "yxc")]


def shards(ref, n):
    size = ref.shape[0] * ref.shape[1] * ref.shape[2] * ref.shape[3]
    return ref.reshape((size,) + tuple(ref.shape[4:])).at[pl.ds(0, n)]


def remote(src, dst, ssem, rsem, dev):
    return pltpu.make_async_remote_copy(
        src_ref=src, dst_ref=dst, send_sem=ssem, recv_sem=rsem, device_id=dev, device_id_type=MESH
    )


class Gather:
    def __init__(self, grid, src, buf, order, ssem, rsem, lsem):
        self.g, self.src, self.buf, self.ssem, self.rsem, self.lsem = grid, src, buf, ssem, rsem, lsem
        self.u, self.v = order[1], order[2]
        self.sent = 0

    def _send(self, src, dst, stage, n, **off):
        remote(src, dst, self.ssem, self.rsem.at[stage], self.g.dev(**off)).start()
        self.sent += n

    def _wait(self, stage, n):
        ref = shards(self.buf, n)
        remote(ref, ref, self.ssem, self.rsem.at[stage], self.g.dev(c=1)).wait_recv()

    def _block(self, uo=0):
        return pick(self.buf, "yxc", self.g.at(**{self.u: uo}))

    def start(self):
        g = self.g
        own = self.buf.at[g.y, g.x, g.c, g.z]
        self.local = pltpu.make_async_copy(self.src, own, self.lsem)
        self.local.start()
        for o in range(1, g.Z):
            self._send(self.src, own, 0, 1, z=o)

    def step1(self):
        g = self.g
        self.local.wait()
        self._wait(0, g.Z - 1)
        own = self._block()
        for o in range(1, g.size(self.u)):
            self._send(own, own, 1, g.Z, **{self.u: o})
        for o in range(1, g.size(self.v)):
            self._send(own, own, 2, g.Z, **{self.v: o})

    def step2(self):
        g = self.g
        U, V = g.size(self.u), g.size(self.v)
        if U > 1:
            self._wait(1, (U - 1) * g.Z)
        for q in range(1, U):
            for o in range(1, V):
                self._send(self._block(q), self._block(q), 2, g.Z, **{self.v: o})

    def step3(self):
        g = self.g
        U, V = g.size(self.u), g.size(self.v)
        if V > 1:
            self._wait(2, U * (V - 1) * g.Z)
        mine = pick(self.buf, "c", g.at())
        for o in range(1, g.C):
            self._send(mine, mine, 3, U * V * g.Z, c=o)

    def step4(self):
        g = self.g
        if g.C > 1:
            self._wait(3, (g.C - 1) * g.Y * g.X * g.Z)

    def finish(self):
        ref = shards(self.buf, self.sent)
        remote(ref, ref, self.ssem, self.rsem.at[0], self.g.dev(c=1)).wait_send()


def run_gathers(gs):
    n = len(gs)
    for g in gs:
        g.start()
    steps = [lambda g: g.step1(), lambda g: g.step2(), lambda g: g.step3(), lambda g: g.step4()]
    for t in range(n + 3):
        for s in range(4):
            i = t - s
            if 0 <= i < n:
                steps[s](gs[i])
    for g in gs:
        g.finish()


class Scatter:
    def __init__(self, grid, part, order, bufs, out, ssem, rsem):
        self.g, self.part, self.out, self.ssem, self.rsem = grid, part, out, ssem, rsem
        self.rc, self.rv, self.ru, self.rz = bufs
        self.u, self.v = order[1], order[2]
        self.U, self.V = grid.size(self.u), grid.size(self.v)
        self.sent = 0

    def _send(self, src, dst, stage, n, **off):
        remote(src, dst, self.ssem, self.rsem.at[stage], self.g.dev(**off)).start()
        self.sent += n

    def _wait(self, stage, ref):
        remote(ref, ref, self.ssem, self.rsem.at[stage], self.g.dev(c=1)).wait_recv()

    def _yx(self, u, v):
        return (v, u) if self.v == "y" else (u, v)

    def _total(self, u, v, i, stage):
        f = jnp.float32
        y, x = self._yx(u, v)
        s = self.part[y, x, self.g.c, i].astype(f)
        for o in range(self.g.C - 1):
            s = s + self.rc[o, y, x, i].astype(f)
        if stage > 1:
            for k in range(self.V - 1):
                s = s + self.rv[k, u, i].astype(f)
        if stage > 2:
            for k in range(self.U - 1):
                s = s + self.ru[k, i].astype(f)
        return s

    def start(self):
        g = self.g
        for o in range(1, g.C):
            self._send(pick(self.part, "c", g.at(c=o)), self.rc.at[o - 1], 0, g.Y * g.X * g.Z, c=o)

    def step1(self):
        g = self.g
        if g.C > 1:
            self._wait(0, self.rc)
        for w in range(1, self.V):
            to = g.at(**{self.v: w})

            def body(i, _):
                u, k = i // g.Z, i % g.Z
                y, x = self._yx(u, to[self.v])
                self.part[y, x, g.c, k] = self._total(u, to[self.v], k, 1).astype(self.part.dtype)
                return 0

            lax.fori_loop(0, self.U * g.Z, body, 0)
            self._send(
                pick(self.part, self.v + "c", to), self.rv.at[w - 1], 1, self.U * g.Z, **{self.v: w}
            )

    def step2(self):
        g = self.g
        here = g.at()
        if self.V > 1:
            self._wait(1, self.rv)
        for q in range(1, self.U):
            to = g.at(**{self.u: q})

            def body(k, _):
                u, v = to[self.u], here[self.v]
                y, x = self._yx(u, v)
                self.part[y, x, g.c, k] = self._total(u, v, k, 2).astype(self.part.dtype)
                return 0

            lax.fori_loop(0, g.Z, body, 0)
            self._send(pick(self.part, "yxc", to), self.ru.at[q - 1], 2, g.Z, **{self.u: q})

    def step3(self):
        g = self.g
        here = g.at()
        if self.U > 1:
            self._wait(2, self.ru)
        for o in range(1, g.Z):
            i = (g.z + o) % g.Z
            self.part[g.y, g.x, g.c, i] = self._total(here[self.u], here[self.v], i, 3).astype(
                self.part.dtype
            )
            self._send(self.part.at[g.y, g.x, g.c, i], self.rz.at[o - 1], 3, 1, z=o)

    def step4(self):
        g = self.g
        here = g.at()
        s = self._total(here[self.u], here[self.v], g.z, 3)
        if g.Z > 1:
            self._wait(3, self.rz)
        for o in range(g.Z - 1):
            s = s + self.rz[o].astype(jnp.float32)
        self.out[...] = s

    def finish(self):
        ref = shards(self.part, self.sent)
        remote(ref, ref, self.ssem, self.rsem.at[0], self.g.dev(c=1)).wait_send()


def scatter_scratch(sizes, shape, dtype, order):
    Z, C, U, V = sizes["z"], sizes["c"], sizes[order[1]], sizes[order[2]]
    t = tuple(shape)
    m = lambda n: max(n, 1)
    return [
        pltpu.VMEM((m(C - 1), sizes["y"], sizes["x"], Z) + t, dtype),
        pltpu.VMEM((m(V - 1), U, Z) + t, dtype),
        pltpu.VMEM((m(U - 1), Z) + t, dtype),
        pltpu.VMEM((m(Z - 1),) + t, dtype),
    ]


def run_scatters(gs):
    n = len(gs)
    for g in gs:
        g.start()
    for t in range(n + 3):
        for s in range(4):
            i = t - s
            if 0 <= i < n:
                [gs[i].step1, gs[i].step2, gs[i].step3, gs[i].step4][s]()
    for g in gs:
        g.finish()


ORDERS = ("zxyc", "zyxc", "zyxc", "zxyc", "zyxc", "zxyc")
VMEM_CAP = 60 << 20


def sizes_of(dp, seq):
    C = 2 if dp % 2 == 0 else 1
    rest = dp // C
    y = 1
    while (2 * y) * (2 * y) <= rest and rest % (2 * y) == 0:
        y *= 2
    return dict(y=y, x=rest // y, c=C, z=seq)


def mesh_lead(dp, seq):
    s = sizes_of(dp, seq)
    return (s["y"], s["x"], s["c"], s["z"])


def tiled(shard):
    rows, cols = shard.shape
    return shard.reshape((rows // 8, 8, cols) if rows % 8 == 0 else (1, rows, cols))


def gather_kernel(dp, seq, orders, *refs):
    n = len(orders)
    ins, outs = refs[:n], refs[n : 2 * n]
    ssem, rsem, lsem = refs[2 * n :]
    grid = Grid(dp, seq)
    entry_barrier(grid)
    run_gathers(
        [
            Gather(grid, ins[i], outs[i], orders[i], ssem.at[i], rsem.at[i], lsem.at[i])
            for i in range(n)
        ]
    )


def gather_all(dp, seq, shards):
    n = len(shards)
    lead = mesh_lead(dp, seq)
    blocks = [tiled(s) for s in shards]
    outs = pl.pallas_call(
        partial(gather_kernel, dp, seq, ORDERS[:n]),
        out_shape=[jax.ShapeDtypeStruct(lead + b.shape, b.dtype) for b in blocks],
        in_specs=[pl.BlockSpec(memory_space=pl.ANY)] * n,
        out_specs=[pl.BlockSpec(memory_space=pl.ANY)] * n,
        scratch_shapes=[
            pltpu.SemaphoreType.DMA((n,)), pltpu.SemaphoreType.DMA((n, 4)),
            pltpu.SemaphoreType.DMA((n,)),
        ],
        compiler_params=pltpu.CompilerParams(collective_id=0, has_side_effects=True),
        name="gather",
    )(*blocks)
    return [o.reshape((-1, s.shape[1])) for o, s in zip(outs, shards)]


def scatter_kernel(dp, seq, orders, count, *refs):
    n = len(orders)
    ins, outs, total, rest = refs[:n], refs[n : 2 * n], refs[2 * n], refs[2 * n + 1 :]
    parts, rest = rest[:n], rest[n:]
    ssem, rsem, lsem, gs, gr = rest[-5:]
    tail = rest[-6]
    grid = Grid(dp, seq)
    copies = [pltpu.make_async_copy(ins[i], parts[i], lsem.at[i]) for i in range(n)]
    for c in copies:
        c.start()
    entry_barrier(grid)
    for c in copies:
        c.wait()
    run_scatters(
        [
            Scatter(
                grid, parts[i], orders[i], rest[4 * i : 4 * i + 4], outs[i],
                ssem.at[i], rsem.at[i],
            )
            for i in range(n)
        ]
    )
    tail[...] = outs[n - 1][1:]
    run_gathers([Gather(grid, tail, total, "zxyc", gs, gr, lsem.at[n])])


def scatter_all(dp, seq, parts, orders):
    n = len(parts)
    N = dp * seq
    sizes = sizes_of(dp, seq)
    lead = mesh_lead(dp, seq)
    parts = [p.reshape(lead + p.shape[1:]) for p in parts]
    scratch = [pltpu.VMEM(p.shape, p.dtype) for p in parts]
    for p, o in zip(parts, orders):
        scratch += scatter_scratch(sizes, p.shape[4:], p.dtype, o)
    last = parts[-1].shape[4:]
    tail = (last[0] - 1,) + last[1:]
    return pl.pallas_call(
        partial(scatter_kernel, dp, seq, orders, n),
        out_shape=[jax.ShapeDtypeStruct(p.shape[4:], jnp.float32) for p in parts]
        + [jax.ShapeDtypeStruct(lead + tail, jnp.float32)],
        in_specs=[pl.BlockSpec(memory_space=pl.ANY)] * n,
        out_specs=[pl.BlockSpec(memory_space=pltpu.VMEM)] * (n + 1),
        scratch_shapes=scratch
        + [
            pltpu.VMEM(tail, jnp.float32), pltpu.SemaphoreType.DMA((n,)),
            pltpu.SemaphoreType.DMA((n, 4)), pltpu.SemaphoreType.DMA((n + 1,)),
            pltpu.SemaphoreType.DMA(()), pltpu.SemaphoreType.DMA((4,)),
        ],
        compiler_params=pltpu.CompilerParams(
            collective_id=1, has_side_effects=True, vmem_limit_bytes=VMEM_CAP
        ),
        name="scatter",
    )(*parts)


def lanes(flat, rows):
    return jnp.pad(flat, ((0, 0), (0, rows * 1024 - flat.shape[1]))).reshape(-1, rows, 8, 128)


def cut(rows, widths):
    out, at = [], 0
    for w in widths:
        out.append(rows[:, at : at + w])
        at += w
    return out


HEADS = 6
HEAD = 64
KERNEL = 9
FF = 3072
GROUPS = 2


norm_eps = 1e-12


def with_halo(cells, sides, width):
    for axis, dim in sides:
        count = lax.axis_size(axis)
        ends = count - 1
        head = lax.slice_in_dim(cells, 0, width, axis=dim)
        tail = lax.slice_in_dim(cells, cells.shape[dim] - width, cells.shape[dim], axis=dim)
        cells = jnp.concatenate(
            [
                lax.ppermute(tail, axis, [(i, (i + 1) % count) for i in range(ends)]),
                cells,
                lax.ppermute(head, axis, [((i + 1) % count, i) for i in range(ends)]),
            ],
            axis=dim,
        )
    return cells


def layer_norm(inputs, gain_vec, shift_vec):
    centre = inputs - jnp.mean(inputs, axis=-1, keepdims=True)
    variance = jnp.mean(centre * centre, axis=-1, keepdims=True)
    return centre * lax.rsqrt(variance + norm_eps) * gain_vec + shift_vec


def attend(queries, key_rows, value_rows, score_scale):
    scores = (
        jnp.einsum("ihe,jhe->hij", queries, key_rows, preferred_element_type=jnp.float32)
        * score_scale
    )
    row_max = jnp.max(scores, axis=-1, keepdims=True)
    norm_log = row_max + jnp.log(jnp.sum(jnp.exp(scores - row_max), axis=-1, keepdims=True))
    weights_low = jnp.exp(scores - norm_log).astype(jnp.bfloat16)
    context = jnp.einsum(
        "hij,jhe->ihe", weights_low, value_rows, preferred_element_type=jnp.float32
    )
    return (context.astype(jnp.bfloat16), norm_log[..., 0])


def attend_back(queries, grad_context, norm_log, key_rows, value_rows, row_delta, score_scale):
    scores = (
        jnp.einsum("ihe,jhe->hij", queries, key_rows, preferred_element_type=jnp.float32)
        * score_scale
    )
    soft_rows = jnp.exp(scores - norm_log[..., None])
    grad_soft = jnp.einsum(
        "ihe,jhe->hij", grad_context, value_rows, preferred_element_type=jnp.float32
    )
    row_delta = jnp.sum(soft_rows * grad_soft, axis=-1)
    grad_scores = (soft_rows * (grad_soft - row_delta[..., None])).astype(jnp.bfloat16)
    grad_queries = (
        jnp.einsum("hij,jhe->ihe", grad_scores, key_rows, preferred_element_type=jnp.float32)
        * score_scale
    )
    grad_keys = (
        jnp.einsum("hij,ihe->jhe", grad_scores, queries, preferred_element_type=jnp.float32)
        * score_scale
    )
    grad_values = jnp.einsum(
        "hij,ihe->jhe",
        soft_rows.astype(jnp.bfloat16),
        grad_context,
        preferred_element_type=jnp.float32,
    )
    return (grad_queries, grad_keys, grad_values, row_delta)


def dot(a, b):
    return jnp.dot(a, b, preferred_element_type=jnp.float32)


def dot_nt(a, b):
    return lax.dot_general(a, b, (((1,), (1,)), ((), ())), preferred_element_type=jnp.float32)


def dot_tn(a, b):
    return lax.dot_general(a, b, (((0,), (0,)), ((), ())), preferred_element_type=jnp.float32)


def centred(v):
    centre = v - jnp.mean(v, axis=-1, keepdims=True)
    inv = lax.rsqrt(jnp.mean(centre * centre, axis=-1, keepdims=True) + norm_eps)
    return centre * inv, inv


def norm_back(grad, normed, inv):
    return inv * (
        grad
        - jnp.mean(grad, axis=-1, keepdims=True)
        - normed * jnp.mean(grad * normed, axis=-1, keepdims=True)
    )


def rows_sum(v):
    return jnp.sum(v, axis=0, keepdims=True)


V_BOUT, V_G1, V_S1, V_BDOWN, V_G2, V_S2 = range(9, 15)
HALF_GELU = 0.7071067811865476
PDF = 0.3989422804014327
BLOCK = 128
CHUNK = 512


def ffn_kernel(
    joined, x, cot, wout, h_wup, h_wdown, vec, bup,
    h_out, h_gafter, h_dctx, h_gmix, h_gwout, h_gwup, h_gwdown, vecg, gbup,
    wup, wdown, out, gafter, dctx, gmix, gwout, gwup, gwdown,
    act, slope, gp, fnb, gsb, gab, lsem, bsem, wsem,
):
    f32, bf16 = jnp.float32, jnp.bfloat16
    total = x.shape[0]
    width = x.shape[1]
    chan = width // 2
    gw = width // GROUPS
    gf = FF // GROUPS
    loads = [
        pltpu.make_async_copy(h_wup, wup, lsem.at[0]),
        pltpu.make_async_copy(h_wdown, wdown, lsem.at[1]),
    ]
    for cp in loads:
        cp.start()

    def stores(r):
        rows = pl.ds(pl.multiple_of(r * BLOCK, BLOCK), BLOCK)
        return [
            pltpu.make_async_copy(a.at[rows], b.at[rows], bsem.at[i, r])
            for i, (a, b) in enumerate(
                ((out, h_out), (gafter, h_gafter), (dctx, h_dctx), (gmix, h_gmix))
            )
        ]

    vecg[...] = jnp.zeros_like(vecg)
    gbup[...] = jnp.zeros_like(gbup)

    def block(r, _):
        rows = pl.ds(pl.multiple_of(r * BLOCK, BLOCK), BLOCK)
        row = lambda i: vec[i : i + 1, :]
        after = dot(joined[rows], wout[...]) + row(V_BOUT) + x[rows].astype(f32)
        n1, inv1 = centred(after)
        first = n1 * row(V_G1) + row(V_S1)
        low = first.astype(bf16)
        fnb[rows] = low

        @pl.when(r == 0)
        def _():
            for cp in loads:
                cp.wait()

        parts = []
        for g in range(GROUPS):
            acc = jnp.zeros((BLOCK, gw), f32)
            for j in range(gf // CHUNK):
                cols = slice(g * gf + j * CHUNK, g * gf + (j + 1) * CHUNK)
                pre = dot(
                    low[:, g * gw : (g + 1) * gw],
                    wup[g * gw : (g + 1) * gw, j * CHUNK : (j + 1) * CHUNK],
                ) + bup[:, cols]
                cdf = 0.5 + 0.5 * lax.erf(pre * HALF_GELU)
                a = (pre * cdf).astype(bf16)
                act[rows, cols] = a
                slope[:, cols] = cdf + pre * (PDF * jnp.exp(pre * pre * -0.5))
                acc = acc + dot(a, wdown[cols])
            parts.append(acc)
        summed = jnp.concatenate(parts, axis=-1) + row(V_BDOWN) + first
        n2, inv2 = centred(summed)
        out[rows] = (n2 * row(V_G2) + row(V_S2)).astype(bf16)
        c = cot[rows].astype(f32)
        gs = norm_back(c * row(V_G2), n2, inv2)
        glow = gs.astype(bf16)
        gsb[rows] = glow
        parts = []
        for g in range(GROUPS):
            acc = jnp.zeros((BLOCK, gw), f32)
            for j in range(gf // CHUNK):
                cols = slice(g * gf + j * CHUNK, g * gf + (j + 1) * CHUNK)
                pre = dot_nt(glow[:, g * gw : (g + 1) * gw], wdown[cols]) * slope[:, cols]
                gbup[:, cols] += rows_sum(pre)
                p = pre.astype(bf16)
                gp[rows, cols] = p
                acc = acc + dot_nt(
                    p, wup[g * gw : (g + 1) * gw, j * CHUNK : (j + 1) * CHUNK]
                )
            parts.append(acc)
        gfirst = gs + jnp.concatenate(parts, axis=-1)
        ga = norm_back(gfirst * row(V_G1), n1, inv1)
        gafter[rows] = ga
        alow = ga.astype(bf16)
        gab[rows] = alow
        gj = dot_nt(alow, wout[...])
        dctx[rows] = gj[:, :chan].astype(bf16)
        gmix[rows] = gj[:, chan:]
        for i, v in (
            (V_BOUT, ga), (V_G1, gfirst * n1), (V_S1, gfirst), (V_BDOWN, gs), (V_G2, c * n2),
            (V_S2, c),
        ):
            vecg[i : i + 1, :] += rows_sum(v)
        for cp in stores(r):
            cp.start()
        return 0

    lax.fori_loop(0, total // BLOCK, block, 0)
    gwout[...] = dot_tn(joined[...], gab[...]).astype(bf16)
    ends = [pltpu.make_async_copy(gwout, h_gwout, wsem.at[0, 0])]
    ends[0].start()
    chunks = gf // CHUNK
    for g in range(GROUPS):

        def weights(j, _, g=g):
            cols = pl.ds(pl.multiple_of(g * gf + j * CHUNK, CHUNK), CHUNK)
            gwdown[cols] = dot_tn(act[:, cols], gsb[:, g * gw : (g + 1) * gw]).astype(bf16)
            gwup[g * gw : (g + 1) * gw, pl.ds(pl.multiple_of(j * CHUNK, CHUNK), CHUNK)] = dot_tn(
                fnb[:, g * gw : (g + 1) * gw], gp[:, cols]
            ).astype(bf16)
            return 0

        lax.fori_loop(0, chunks, weights, 0, unroll=True)
        for i, (a, b, rows) in enumerate(
            (
                (gwdown, h_gwdown, slice(g * gf, (g + 1) * gf)),
                (gwup, h_gwup, slice(g * gw, (g + 1) * gw)),
            )
        ):
            cp = pltpu.make_async_copy(a.at[rows], b.at[rows], wsem.at[1 + i, g])
            cp.start()
            ends.append(cp)
    for r in range(total // BLOCK):
        ends += stores(r)
    for cp in ends:
        cp.wait()


def ffn(joined, x, cot, wout, wup, wdown, vec, bup):
    f32, bf16 = jnp.float32, jnp.bfloat16
    total, width = x.shape
    shape = jax.ShapeDtypeStruct
    return pl.pallas_call(
        ffn_kernel,
        out_shape=[
            shape((total, width), bf16),
            shape((total, width), f32),
            shape((total, width // 2), bf16),
            shape((total, width // 2), f32),
            shape(wout.shape, bf16),
            shape(wup.shape, bf16),
            shape(wdown.shape, bf16),
            shape(vec.shape, f32),
            shape(bup.shape, f32),
        ],
        in_specs=[pl.BlockSpec(memory_space=pltpu.VMEM)] * 4
        + [pl.BlockSpec(memory_space=pl.ANY)] * 2
        + [pl.BlockSpec(memory_space=pltpu.VMEM)] * 2,
        out_specs=[pl.BlockSpec(memory_space=pl.ANY)] * 7
        + [pl.BlockSpec(memory_space=pltpu.VMEM)] * 2,
        scratch_shapes=[
            pltpu.VMEM(wup.shape, bf16),
            pltpu.VMEM(wdown.shape, bf16),
            pltpu.VMEM((total, width), bf16),
            pltpu.VMEM((total, width), f32),
            pltpu.VMEM((total, width // 2), bf16),
            pltpu.VMEM((total, width // 2), f32),
            pltpu.VMEM(wout.shape, bf16),
            pltpu.VMEM(wup.shape, bf16),
            pltpu.VMEM(wdown.shape, bf16),
            pltpu.VMEM((total, FF), bf16),
            pltpu.VMEM((BLOCK, FF), f32),
            pltpu.VMEM((total, FF), bf16),
            pltpu.VMEM((total, width), bf16),
            pltpu.VMEM((total, width), bf16),
            pltpu.VMEM((total, width), bf16),
            pltpu.SemaphoreType.DMA((2,)),
            pltpu.SemaphoreType.DMA((4, total // BLOCK)),
            pltpu.SemaphoreType.DMA((3, GROUPS)),
        ],
        compiler_params=pltpu.CompilerParams(vmem_limit_bytes=VMEM_CAP),
        name="ffn",
    )(joined, x, cot, wout, wup, wdown, vec, bup)


HEADS_PER = HEADS // 2
PART = HEADS_PER * HEAD
EDGE = 8
TAPS = KERNEL
CHAN = HEADS * HEAD


def iota(shape, dim):
    return lax.broadcasted_iota(jnp.int32, shape, dim)


def expander(rows, cols, width):
    return (iota((rows, cols), 1) % width == iota((rows, cols), 0)).astype(jnp.bfloat16)


def owned(stack, width):
    keep = iota(stack.shape, 2) // width == iota(stack.shape, 0)
    return jnp.sum(jnp.where(keep, stack, 0.0), axis=0)


def unpack_small(gsmall, vec, bproj, bup, widths):
    n = gsmall.shape[0] * gsmall.shape[1] * gsmall.shape[2] * gsmall.shape[3]
    gsmall = gsmall[...].reshape((n,) + gsmall.shape[4:])
    w, wp, wu = widths
    flat = gsmall[:, :2].reshape(n * 16, 128).astype(jnp.bfloat16)
    cols = vec.shape[1]
    vec[...] = owned(dot(flat, expander(128, cols, w)).reshape(n, 16, cols), w)
    flat = gsmall[:, 2].reshape(n * 8, 128).astype(jnp.bfloat16)
    cols = bproj.shape[1]
    bproj[...] = owned(dot(flat, expander(128, cols, wp)).reshape(n, 8, cols), wp)[:1]
    cols = bup.shape[1]
    bup[...] = owned(dot(flat, expander(128, cols, wu)).reshape(n, 8, cols), wu)[1:2]


def pack(v):
    r = v.shape[0] // 2
    return jnp.concatenate([v[:r], v[r:]], axis=1)


def unpack(v):
    c = v.shape[1] // 2
    return jnp.concatenate([v[:, :c], v[:, c:]], axis=0)


def tap_logits(mixed, wkx, bkx, logits, at=0):
    rows = pl.ds(at, mixed.shape[0])

    def tap(t, _):
        logits[t, rows] = dot(mixed, wkx[t]) + bkx[pl.ds(t, 1)]
        return 0

    lax.fori_loop(0, TAPS, tap, 0, unroll=True)


def softmax_taps(logits, rows):
    ls = [logits[t, rows] for t in range(TAPS)]
    top = ls[0]
    for v in ls[1:]:
        top = jnp.maximum(top, v)
    es = [jnp.exp(v - top) for v in ls]
    total = es[0]
    for v in es[1:]:
        total = total + v
    inv = 1.0 / total
    return [e * inv for e in es]


def expand_kernel_weights(w_kernel, b_kernel, wkx, bkx):
    cols = wkx.shape[2]
    wk, bk = w_kernel[...], b_kernel[...]
    for t in range(TAPS):
        k = wk.shape[0]
        pick = (iota((k, cols), 0) == iota((k, cols), 1) // HEAD * TAPS + t).astype(jnp.bfloat16)
        wkx[t] = dot_tn(wk, pick).astype(jnp.bfloat16)
        bkx[t : t + 1] = dot(bk, pick)


ROW = 16


def front_kernel(
    dp, seq, widths,
    x, wproj, wout, wup, wdown, small, w_kernel, b_kernel,
    gq0, gq1, gq2, gcp, gout, gup, gdown,
    h_qh, h_kh, h_vh, h_joined, h_qn, h_xe, h_convin, h_keyconv, h_mixed, h_spread, h_wkx,
    stats, vec, bup, bkx,
    qh, kh, vh, joined, qn, xe, convin, keyconv, mixed, spread, wkx,
    pq, pcp, gsmall, wq, wcp, xf, edges, inedge, qkv, abuf, csend, cbuf, logits, bproj,
    ssem, rsem, lsem, asend, arecv, bsend, brecv, esend, erecv, wsem, osem,
):
    f32, bf16 = jnp.float32, jnp.bfloat16
    grid = Grid(dp, seq)
    z, Z = grid.z, seq
    seqs, local, width = x.shape
    total = seqs * local

    greet(grid)
    outs = (
        (qh, h_qh), (kh, h_kh), (vh, h_vh), (joined, h_joined), (qn, h_qn), (xe, h_xe),
        (convin, h_convin), (keyconv, h_keyconv), (mixed, h_mixed), (spread, h_spread),
        (wkx, h_wkx),
    )
    ends = []

    def store(*refs):
        for i, (a, b) in enumerate(outs):
            if any(a is r for r in refs):
                cp = pltpu.make_async_copy(a, b, osem.at[i])
                cp.start()
                ends.append(cp)

    w = wproj[...].astype(f32)
    for j in range(HEADS_PER):
        cols = []
        for n in (j, HEADS_PER + j):
            for p in range(3):
                at = p * CHAN + n * HEAD
                cols.append(w[:, at : at + HEAD])
        pq[j] = jnp.concatenate(cols, axis=1).reshape(pq.shape[1:]).astype(bf16)
    pcp[...] = w[:, 3 * CHAN :].reshape(pcp.shape).astype(bf16)
    for s in range(seqs):
        edges[0, s] = x[s, :EDGE].astype(f32)
        edges[1, s] = x[s, local - EDGE :].astype(f32)

    expand_kernel_weights(w_kernel, b_kernel, wkx, bkx)
    store(wkx)
    meet(grid)
    mk = lambda i, src, buf, order: Gather(
        grid, src, buf, order, ssem.at[i], rsem.at[i], lsem.at[i]
    )
    gs = mk(0, small, gsmall, "zxyc")
    gq = [
        mk(1, pq.at[0], gq0, "zxyc"), mk(2, pq.at[1], gq1, "zyxc"), mk(3, pq.at[2], gq2, "zxyc")
    ]
    g2 = mk(4, pcp, gcp, "zyxc")
    g3 = mk(5, wout, gout, "zxyc")
    g4 = mk(6, wup, gup, "zyxc")
    g5 = mk(7, wdown, gdown, "zxyc")
    large = (g4, g5, g3)
    whole_q = [
        pltpu.make_async_copy(g.reshape((width, 2 * PART)), wq.at[j], wsem.at[j])
        for j, g in enumerate((gq0, gq1, gq2))
    ]
    whole_cp = pltpu.make_async_copy(gcp.reshape(wcp.shape), wcp, wsem.at[HEADS_PER])
    hops = [
        pltpu.make_async_remote_copy(
            src_ref=edges.at[i], dst_ref=inedge.at[i], send_sem=esend.at[i],
            recv_sem=erecv.at[i], device_id=grid.dev(z=o), device_id_type=MESH,
        )
        for i, o in ((0, seq - 1), (1, 1))
    ]
    sends = {}
    heads = {}

    def qkv_unit(j):
        gq[j].step4()
        whole_q[j].start()
        whole_q[j].wait()
        zero = jnp.zeros((1, HEAD), f32)
        cols = []
        for n in (j, HEADS_PER + j):
            at = n * HEAD
            cols += [bproj[:, at : at + HEAD], zero, bproj[:, CHAN + at : CHAN + at + HEAD]]
        qkv_bias = jnp.concatenate(cols, axis=1)
        for s in range(seqs):
            val = (dot(x[s], wq[j]) + qkv_bias).astype(bf16)
            for h in range(2):
                qkv[2 * s + h, j] = pack(val[:, h * PART : (h + 1) * PART])
                heads[s, h * HEADS_PER + j] = val[:, h * PART : h * PART + HEAD]
        for o in range(1, Z):
            to = (z + o) % Z
            cp = pltpu.make_async_remote_copy(
                src_ref=qkv.at[to, j], dst_ref=abuf.at[j, z], send_sem=asend.at[j, o - 1],
                recv_sem=arecv.at[j, o - 1], device_id=grid.dev(z=o), device_id_type=MESH,
            )
            cp.start()
            sends[j, o] = cp
        abuf[j, z] = qkv[z, j]

    def extend():
        for cp in hops:
            cp.wait_recv()
        for s in range(seqs):
            top = jnp.where(z > 0, inedge[1, s], 0.0)
            low = jnp.where(z < Z - 1, inedge[0, s], 0.0)
            xf[s, :EDGE] = top
            xf[s, EDGE : EDGE + local] = x[s].astype(f32)
            xf[s, EDGE + local :] = low
            xe[s] = xf[s].astype(bf16)
        spread_rows(xf, vec, spread, seqs, local)
        store(xe, spread)

    def conv_inputs():
        whole_cp.start()
        for s in range(seqs):
            qn[s * local : (s + 1) * local] = jnp.concatenate(
                [heads[s, n] for n in range(HEADS)], axis=1
            )
        store(qn)
        whole_cp.wait()
        bias = bproj[...]
        ext = local + 2 * EDGE
        at = iota((ext, 1), 0)
        inside = ((at >= EDGE) | (z > 0)) & ((at < EDGE + local) | (z < Z - 1))
        for s in range(seqs):
            val = dot(xe[s], wcp[:, :CHAN]) + bias[:, 2 * CHAN : 3 * CHAN]
            convin[s] = jnp.where(inside, val, 0.0)
        for s in range(seqs):
            rows = slice(s * local, (s + 1) * local)
            kc = dot(spread[rows], wcp[:, CHAN:]) + bias[:, 3 * CHAN :]
            keyconv[rows] = kc
            mixed[rows] = (kc * qn[rows].astype(f32)).astype(bf16)
        store(convin, keyconv, mixed)

    def conv_mix(s):
        tap_logits(mixed[s * local : (s + 1) * local], wkx, bkx, logits)

        def mix(i, _):
            r = pl.ds(pl.multiple_of(i * ROW, ROW), ROW)
            win = convin[s, pl.ds(pl.multiple_of(i * ROW, ROW), 2 * ROW)]
            tw = softmax_taps(logits, r)
            acc = jnp.zeros((ROW, CHAN), f32)
            for t in range(TAPS):
                a = EDGE - TAPS // 2 + t
                acc = acc + tw[t] * win[a : a + ROW]
            joined[pl.ds(pl.multiple_of(s * local + i * ROW, ROW), ROW), CHAN:] = acc.astype(bf16)
            return 0

        lax.fori_loop(0, local // ROW, mix, 0)

    returns = []

    def attention(j):
        for o in range(1, Z):
            sends[j, o].wait_recv()
        for b in range(Z):
            val = unpack(abuf[j, b])
            rows = slice(b * local, (b + 1) * local)
            for p, ref in enumerate((qh, kh, vh)):
                ref[j, rows] = val[:, p * HEAD : (p + 1) * HEAD]
        if j == HEADS_PER - 1:
            store(qh, kh, vh)
        returns.extend(attend_unit(grid, j, qh, kh, vh, stats, csend, cbuf, bsend, brecv))

    gs.start()
    for g in gq:
        g.start()
    g2.start()
    for cp in hops:
        cp.start()
    gs.step1()
    for g in gq:
        g.step1()
    g2.step1()
    for g in large:
        g.start()
    gs.step2()
    for g in gq:
        g.step2()
    g2.step2()
    gs.step3()
    for g in gq:
        g.step3()
    g2.step3()
    gs.step4()
    unpack_small(gsmall, vec, bproj, bup, widths)
    qkv_unit(0)
    qkv_unit(1)
    qkv_unit(2)
    for g in large:
        g.step1()
    extend()
    g2.step4()
    conv_inputs()
    conv_mix(0)
    attention(0)
    for g in large:
        g.step2()
    conv_mix(1)
    attention(1)
    for g in large:
        g.step3()
    attention(2)
    for g in large:
        g.step4()
    for cp in returns:
        cp.wait_recv()
    for s in range(seqs):
        pieces = []
        for n in range(HEADS):
            v = cbuf[n % HEADS_PER, 2 * s + n // HEADS_PER]
            pieces.append(unpack(unpack(v)))
        joined[s * local : (s + 1) * local, :CHAN] = jnp.concatenate(pieces, axis=1)
    store(joined)
    for cp in list(sends.values()) + returns + hops:
        cp.wait_send()
    for g in [gs] + gq + [g2, g3, g4, g5]:
        g.finish()
    for cp in ends:
        cp.wait()


def spread_rows(xf, vec, spread, seqs, local):
    width = xf.shape[2]
    step = 256

    def body(i, _):
        for s in range(seqs):
            for c in range(width // step):
                cols = slice(c * step, (c + 1) * step)
                win = xf[s, pl.ds(pl.multiple_of(i * ROW, ROW), 2 * ROW), cols]
                acc = jnp.zeros((ROW, step), jnp.float32)
                for t in range(TAPS):
                    a = EDGE - TAPS // 2 + t
                    acc = acc + win[a : a + ROW] * vec[t : t + 1, cols]
                r = pl.ds(pl.multiple_of(s * local + i * ROW, ROW), ROW)
                spread[r, cols] = acc.astype(spread.dtype)
        return 0

    lax.fori_loop(0, local // ROW, body, 0)


def attend_unit(grid, h, qh, kh, vh, stats, csend, cbuf, bsend, brecv):
    f32, bf16 = jnp.float32, jnp.bfloat16
    z, Z = grid.z, grid.Z
    local = qh.shape[1] // Z
    sends = []
    scale = jnp.asarray(HEAD ** (-0.5), bf16)
    keys = kh[h]
    vt = vh[h].T
    def send(i):
        return pltpu.make_async_remote_copy(
            src_ref=csend.at[h, i], dst_ref=cbuf.at[h, z], send_sem=bsend.at[h, i],
            recv_sem=brecv.at[h, i], device_id=(grid.dp, (z + i + 1) % Z), device_id_type=MESH,
        )

    def block(i, _):
        b = (z + i + 1) % Z
        rows = pl.ds(pl.multiple_of(b * local, local), local)
        st = dot_nt(keys, qh[h, rows] * scale)
        top = jnp.max(st, axis=0, keepdims=True)
        e = jnp.exp(st - top)
        den = jnp.sum(e, axis=0, keepdims=True)
        stats[h, b] = top + jnp.log(den)
        ct = dot(vt, e.astype(bf16)) / den
        csend[h, i] = pack(pack(ct.T.astype(bf16)))

        @pl.when(i < Z - 1)
        def _():
            send(i).start()

        return 0

    lax.fori_loop(0, Z, block, 0, unroll=True)
    cbuf[h, z] = csend[h, Z - 1]
    return [send(i) for i in range(Z - 1)]


def front(dp, seq, x, w_proj, w_out, w_up, w_down, small, w_kernel, b_kernel, widths):
    f32, bf16 = jnp.float32, jnp.bfloat16
    seqs, local, width = x.shape
    total = seqs * local
    length = seq * local
    N = dp * seq
    rows = w_proj.shape[0]
    lead = tiled(w_proj).shape[:2]
    place = mesh_lead(dp, seq)
    shape = jax.ShapeDtypeStruct
    wide = 6 * PART
    ext = local + 2 * EDGE
    vm = pl.BlockSpec(memory_space=pltpu.VMEM)
    hb = pl.BlockSpec(memory_space=pl.ANY)
    other = [tiled(a) for a in (w_out, w_up, w_down)]
    hbm_out = [
        shape(place + lead + (c,), bf16) for c in (2 * PART,) * HEADS_PER + (2 * CHAN,)
    ]
    hbm_out += [shape(place + a.shape, bf16) for a in other]
    big_out = [
        shape((HEADS_PER, length, HEAD), bf16),
        shape((HEADS_PER, length, HEAD), bf16),
        shape((HEADS_PER, length, HEAD), bf16),
        shape((total, width), bf16),
        shape((total, CHAN), bf16),
        shape((seqs, ext, width), bf16),
        shape((seqs, ext, CHAN), f32),
        shape((total, CHAN), f32),
        shape((total, CHAN), bf16),
        shape((total, width), bf16),
        shape((TAPS, CHAN, CHAN), bf16),
    ]
    vm_out = [
        shape((HEADS_PER, seq, 1, local), f32),
        shape((16, width), f32),
        shape((1, FF), f32),
        shape((16, CHAN), f32),
    ]
    hbm_out += big_out
    sem = lambda *s: pltpu.SemaphoreType.DMA(s)
    return pl.pallas_call(
        partial(front_kernel, dp, seq, widths),
        out_shape=hbm_out + vm_out,
        in_specs=[vm] * 8,
        out_specs=[hb] * len(hbm_out) + [vm] * len(vm_out),
        scratch_shapes=[pltpu.VMEM(o.shape, o.dtype) for o in big_out]
        + [
            pltpu.VMEM((HEADS_PER,) + lead + (2 * PART,), bf16),
            pltpu.VMEM(lead + (2 * CHAN,), bf16),
            pltpu.VMEM(place + small.shape, f32),
            pltpu.VMEM((HEADS_PER, width, 2 * PART), bf16),
            pltpu.VMEM((width, 2 * CHAN), bf16),
            pltpu.VMEM((seqs, ext, width), f32),
            pltpu.VMEM((2, seqs, EDGE, width), f32),
            pltpu.VMEM((2, seqs, EDGE, width), f32),
            pltpu.VMEM((seq, HEADS_PER, local // 2, 2 * PART), bf16),
            pltpu.VMEM((HEADS_PER, seq, local // 2, 2 * PART), bf16),
            pltpu.VMEM((HEADS_PER, seq, local // 4, 4 * HEAD), bf16),
            pltpu.VMEM((HEADS_PER, seq, local // 4, 4 * HEAD), bf16),
            pltpu.VMEM((TAPS, local, CHAN), f32),
            pltpu.VMEM((1, 4 * CHAN), f32),
            sem(8), sem(8, 4), sem(8),
            sem(HEADS_PER, seq - 1), sem(HEADS_PER, seq - 1),
            sem(HEADS_PER, seq - 1), sem(HEADS_PER, seq - 1), sem(2), sem(2), sem(HEADS_PER + 1),
            sem(len(big_out)),
        ],
        compiler_params=pltpu.CompilerParams(
            collective_id=2, has_side_effects=True, vmem_limit_bytes=VMEM_CAP
        ),
        name="front",
    )(x, w_proj, *other, small, w_kernel, b_kernel)


def pack_small(w_depth, vectors, b_proj, b_up):
    rows = [(i, v) for i, v in enumerate([w_depth[:, t] for t in range(TAPS)] + list(vectors))]
    rows += [(16, b_proj), (17, b_up)]
    out = jnp.zeros((24, 128), jnp.float32)
    for i, v in rows:
        out = out + jnp.pad(v.astype(jnp.float32)[None], ((i, 23 - i), (0, 128 - v.shape[0])))
    return out.reshape(3, 8, 128)


def unhalve(w):
    w = w.reshape(w.shape[:-1] + (2, 3, PART))
    return jnp.swapaxes(w, -3, -2).reshape(w.shape[:-3] + (3 * CHAN,))


PAD = 16


def dot_pick(v, picks):
    bf16 = jnp.bfloat16
    hi = v.astype(bf16)
    rest = v - hi.astype(jnp.float32)
    mid = rest.astype(bf16)
    lo = (rest - mid.astype(jnp.float32)).astype(bf16)
    return dot_nt(hi, picks) + dot_nt(mid, picks) + dot_nt(lo, picks)


def to_owners(v, width, n):
    r, cols = v.shape
    picks = expander(128, cols, width)
    if r == 1:
        keep = iota((n, cols), 1) // width == iota((n, cols), 0)
        return dot_pick(jnp.where(keep, v, 0.0), picks)
    keep = iota((n, r, cols), 2) // width == iota((n, r, cols), 0)
    stack = jnp.where(keep, v[None], 0.0).reshape(n * r, cols)
    return dot_pick(stack, picks).reshape(n, r, 128)


def conv_back(
    s, local, gmix, convin, keyconv, mixed, qn, wkx, bkx, wkp, wpt,
    tw, gt, gl, gpad, gsp, gqm, gk, gci_ext, gwk, gbk, gbpoint,
):
    f32, bf16 = jnp.float32, jnp.bfloat16
    rows = slice(s * local, (s + 1) * local)
    body_rows = slice(PAD, PAD + local)
    tap_logits(mixed[rows], wkx, bkx, tw, PAD)
    gpad[body_rows] = gmix[rows]
    same = (iota((CHAN, CHAN), 0) // HEAD == iota((CHAN, CHAN), 1) // HEAD).astype(bf16)
    for t in range(TAPS):
        a = EDGE - TAPS // 2 + t
        p = gmix[rows] * convin[s, a : a + local]
        hi = p.astype(bf16)
        lo = (p - hi.astype(f32)).astype(bf16)
        gt[t] = dot(hi, same) + dot(lo, same)

    def taps(i, _):
        r = pl.ds(pl.multiple_of(i * ROW, ROW), ROW)
        rp = pl.ds(pl.multiple_of(PAD + i * ROW, ROW), ROW)
        ws = softmax_taps(tw, rp)
        gs = [gt[t, r] for t in range(TAPS)]
        mean = ws[0] * gs[0]
        for t in range(1, TAPS):
            mean = mean + ws[t] * gs[t]
        for t in range(TAPS):
            tw[t, rp] = ws[t]
            g = ws[t] * (gs[t] - mean)
            gl[t, r] = g.astype(bf16)
            gbk[t] += g[:8] + g[8:]
        return 0

    lax.fori_loop(0, local // ROW, taps, 0)

    def spread_back(i, _):
        w = pl.ds(pl.multiple_of(i * ROW, ROW), 2 * ROW)
        g = gpad[w]
        acc = jnp.zeros((ROW, CHAN), f32)
        for t in range(TAPS):
            a = PAD - TAPS // 2 - t
            acc = acc + (tw[t, w] * g)[a : a + ROW]
        gci_ext[s, pl.ds(pl.multiple_of(i * ROW, ROW), ROW)] = acc
        return 0

    lax.fori_loop(0, (local + 2 * EDGE) // ROW, spread_back, 0)
    compact = jnp.zeros((local, 128), f32)
    for t in range(TAPS):
        pick = (
            (iota((CHAN, 128), 0) == iota((CHAN, 128), 1) // TAPS * HEAD)
            & (iota((CHAN, 128), 1) % TAPS == t)
            & (iota((CHAN, 128), 1) < HEADS * TAPS)
        ).astype(bf16)
        compact = compact + dot(gl[t], pick)
    low = compact.astype(bf16)
    gwk[...] += dot_tn(low, mixed[rows])
    gmixed = dot(low, wkp[...])
    gqm[rows] = gmixed * keyconv[rows]
    gkc = gmixed * qn[rows].astype(f32)
    gbpoint[...] += rows_sum(gkc)
    glow = gkc.astype(bf16)
    gk[rows] = glow
    gsp[s, body_rows] = dot_nt(glow, wpt)


def depth_back(local, seqs, gsp, xe, vec, gdx_ext, gwd):
    f32 = jnp.float32
    width = gsp.shape[2]
    step = 256

    def grads(i, _):
        w = pl.ds(pl.multiple_of(i * ROW, ROW), 2 * ROW)
        for s in range(seqs):
            for c in range(width // step):
                cols = slice(c * step, (c + 1) * step)
                g = gsp[s, w, cols]
                acc = jnp.zeros((ROW, step), f32)
                for t in range(TAPS):
                    a = PAD - TAPS // 2 - t
                    acc = acc + g[a : a + ROW] * vec[t : t + 1, cols]
                gdx_ext[s, pl.ds(pl.multiple_of(i * ROW, ROW), ROW), cols] = acc
        return 0

    lax.fori_loop(0, (local + 2 * EDGE) // ROW, grads, 0)

    def weights(i, _):
        w = pl.ds(pl.multiple_of(i * ROW, ROW), 2 * ROW)
        for s in range(seqs):
            for c in range(width // step):
                cols = slice(c * step, (c + 1) * step)
                win = xe[s, w, cols].astype(f32)
                g = gsp[s, pl.ds(pl.multiple_of(PAD + i * ROW, ROW), ROW), cols]
                for t in range(TAPS):
                    a = EDGE - TAPS // 2 + t
                    p = win[a : a + ROW] * g
                    gwd[t, :, cols] += p[:8] + p[8:]
        return 0

    lax.fori_loop(0, local // ROW, weights, 0)


def attend_back_block(b, h, keys, vals, kt, qh, stats, dbuf, dkv, local):
    f32, bf16 = jnp.float32, jnp.bfloat16
    scale = HEAD ** (-0.5)
    rows = pl.ds(pl.multiple_of(b * local, local), local)
    q = qh[h, rows]
    do = unpack(dbuf[b])[:, h * HEAD : (h + 1) * HEAD]
    st = dot_nt(keys, q * jnp.asarray(scale, bf16))
    p = jnp.exp(st - stats[h, b])
    dp = dot_nt(vals, do)
    delta = jnp.sum(p * dp, axis=0, keepdims=True)
    ds = (p * (dp - delta)).astype(bf16)
    dk = dot(ds, q)
    dv = dot(p.astype(bf16), do)
    dkv[0] += dk
    dkv[1] += dv
    return (dot(kt, ds) * scale).T


def back_kernel(
    dp, seq, widths,
    dctx, stats, vec, bkx, w_kernel, vecg, gbup,
    h_gmix, h_convin, h_keyconv, h_mixed, h_qn, h_wkx, h_qh, h_kh, h_vh, h_spread, h_xe,
    gafter, gq0, gq1, gq2, gcp, gwdown, gwup, gwout,
    h_gx, o_proj, o_out, o_up, o_down, o_small, o_kernel,
    gmix, convin, keyconv, mixed, qn, wkx, qh, kh, vh, spread, xe, gx, xt,
    *rest,
):
    f32, bf16 = jnp.float32, jnp.bfloat16
    pieces = 9
    parts, rest = rest[:pieces], rest[pieces:]
    bufs, rest = rest[: 4 * pieces], rest[4 * pieces :]
    souts, rest = rest[:5], rest[5:]
    souts = (o_down, o_up, o_out) + souts + (o_small,)
    (
        dbuf, dsend, gsend, grecv, wq, wcp, grads, tw, gt, gl, gpad, gsp, gqm, gk, gci_ext, gcl,
        gdx_ext, gwd, gwk, gbk, gbpoint, wkp, hsend, hrecv, dqb, dkv, kall, bprow,
        ssem, rsem, gssem, grsem, lsem, asend, arecv, bsend, brecv, esend, erecv, wsem,
    ) = rest
    grid = Grid(dp, seq)
    z, Z = grid.z, seq
    N = dp * seq
    seqs = xe.shape[0]
    total = dctx.shape[0]
    local = total // seqs
    width = xe.shape[2]
    w1, wp, wu = widths

    loads = [
        pltpu.make_async_copy(src, dst, wsem.at[i])
        for i, (src, dst) in enumerate(
            (
                (gwdown, parts[0]), (gwup, parts[1]), (gwout, parts[2]),
                (gcp.reshape(wcp.shape), wcp),
                (gafter, gx),
                (gq0.reshape((width, 2 * PART)), wq.at[0]),
                (gq1.reshape((width, 2 * PART)), wq.at[1]),
                (gq2.reshape((width, 2 * PART)), wq.at[2]),
            )
        )
    ]
    greet(grid)
    ins = [
        pltpu.make_async_copy(src, dst, wsem.at[8 + i])
        for i, (src, dst) in enumerate(
            (
                (h_gmix, gmix), (h_convin, convin), (h_keyconv, keyconv), (h_mixed, mixed),
                (h_qn, qn), (h_wkx, wkx), (h_qh, qh), (h_kh, kh), (h_vh, vh), (h_spread, spread),
                (h_xe, xe),
            )
        )
    ]
    for cp in loads[:3] + ins + loads[3:]:
        cp.start()
    for s in range(seqs):
        for h in range(2):
            dsend[2 * s + h] = pack(
                dctx[s * local : (s + 1) * local, h * PART : (h + 1) * PART]
            )
    wk = w_kernel[...]
    wkp[...] = dot(
        (iota((128, wk.shape[0]), 0) == iota((128, wk.shape[0]), 1)).astype(bf16), wk
    ).astype(bf16)
    gwk[...] = jnp.zeros_like(gwk)
    gbk[...] = jnp.zeros_like(gbk)
    gwd[...] = jnp.zeros_like(gwd)
    gbpoint[...] = jnp.zeros_like(gbpoint)
    gpad[...] = jnp.zeros_like(gpad)
    zeros = jnp.zeros((PAD, CHAN), f32)
    for t in range(TAPS):
        tw[t, :PAD] = zeros
        tw[t, PAD + local :] = zeros
    zeros = jnp.zeros((PAD, width), f32)
    for s in range(seqs):
        gsp[s, :PAD] = zeros
        gsp[s, PAD + local :] = zeros
    parts[8][...] = jnp.zeros_like(parts[8])
    parts[8][:, :, :, :, 2, 1:2] = to_owners(gbup[...], wu, N).reshape(parts[8].shape[:4] + (1, 128))
    meet(grid)
    sends = []
    for o in range(1, Z):
        to = (z + o) % Z
        cp = pltpu.make_async_remote_copy(
            src_ref=dsend.at[to], dst_ref=dbuf.at[z], send_sem=bsend.at[o - 1],
            recv_sem=brecv.at[o - 1], device_id=grid.dev(z=o), device_id_type=MESH,
        )
        cp.start()
        sends.append(cp)
    dbuf[z] = dsend[z]
    orders = ("zxyc", "zyxc", "zxyc", "zyxc", "zxyc", "zyxc", "zxyc", "zxyc", "zyxc")
    sc = [
        Scatter(
            grid, parts[i], orders[i], bufs[4 * i : 4 * i + 4], souts[i], ssem.at[i], rsem.at[i]
        )
        for i in range(pieces)
    ]
    sdown, sup, sout, scp, sq0, sq1, sq2, skern, svec = sc
    for i in range(3):
        loads[i].wait()
        sc[i].start()

    for cp in ins[:6]:
        cp.wait()
    loads[3].wait()
    wpt = wcp[:, CHAN:]

    def conv(s):
        conv_back(
            s, local, gmix, convin, keyconv, mixed, qn, wkx, bkx, wkp, wpt,
            tw, gt, gl, gpad, gsp, gqm, gk, gci_ext, gwk, gbk, gbpoint,
        )

    for s in range(seqs - 1):
        conv(s)
    sdown.step1()
    sup.step1()
    sout.step1()

    scale = HEAD ** (-0.5)
    back = []
    for cp in ins[6:]:
        cp.wait()
    for s in range(seqs):
        xt[:, s * local : (s + 1) * local] = xe[s, EDGE : EDGE + local].T
    for cp in sends:
        cp.wait_recv()
    for h in range(HEADS_PER):
        keys, vals = kh[h], vh[h]
        kt = keys.T
        dkv[...] = jnp.zeros_like(dkv)

        def block(o, _, h=h, keys=keys, vals=vals, kt=kt):
            b = (z + Z - o) % Z
            dqb[b] = attend_back_block(
                b, h, keys, vals, kt, qh, stats, dbuf, dkv, local
            ).astype(bf16)
            return 0

        lax.fori_loop(0, Z, block, 0, unroll=True)
        for o in list(range(1, Z)) + [0]:
            b = (z + o) % Z
            r = pl.ds(pl.multiple_of(b * local, local), local)
            val = pack(
                jnp.concatenate(
                    [dqb[b], (dkv[0, r] * scale).astype(bf16), dkv[1, r].astype(bf16)], axis=1
                )
            )
            if o:
                gsend[h, o - 1] = val
                cp = pltpu.make_async_remote_copy(
                    src_ref=gsend.at[h, o - 1], dst_ref=grecv.at[h, z],
                    send_sem=asend.at[h, o - 1], recv_sem=arecv.at[h, o - 1],
                    device_id=grid.dev(z=o), device_id_type=MESH,
                )
                cp.start()
                back.append(cp)
            else:
                grecv[h, z] = val

    conv(seqs - 1)
    sdown.step2()
    sup.step2()
    sout.step2()
    depth_back(local, seqs, gsp, xe, vec, gdx_ext, gwd)
    for i, at in ((0, 0), (1, EDGE + local)):
        for s in range(seqs):
            hsend[i, s, :, :CHAN] = gci_ext[s, at : at + EDGE]
            hsend[i, s, :, CHAN:] = gdx_ext[s, at : at + EDGE]
    hops = []
    for i, o in ((0, seq - 1), (1, 1)):
        cp = pltpu.make_async_remote_copy(
            src_ref=hsend.at[i], dst_ref=hrecv.at[i], send_sem=esend.at[i],
            recv_sem=erecv.at[i], device_id=grid.dev(z=o), device_id_type=MESH,
        )
        cp.start()
        hops.append(cp)
    gw = dot_tn(spread[...], gk[...])
    gate = lambda v: v.reshape(parts[3].shape[:-1] + (CHAN,)).astype(bf16)
    parts[3][..., CHAN:] = gate(gw)
    bias_row = jnp.zeros((1, 128), f32)
    for t in range(TAPS):
        pick = (
            (iota((128, CHAN), 1) == iota((128, CHAN), 0) // TAPS * HEAD)
            & (iota((128, CHAN), 0) % TAPS == t)
            & (iota((128, CHAN), 0) < HEADS * TAPS)
        ).astype(bf16)
        bias_row = bias_row + dot_pick(rows_sum(gbk[t]), pick)
    tiles = []
    for c in range(CHAN // 128):
        tile = gwk[:TALL, c * 128 : (c + 1) * 128]
        if c == 0:
            tile = jnp.where(iota((TALL, 128), 0) == HEADS * TAPS, bias_row, tile)
        tiles.append(tile.reshape(TALL // 8, 8, 128))
    count = CHAN // 128 * TALL // 8
    tiles.append(jnp.zeros((N - count, 8, 128), f32))
    parts[7][...] = jnp.concatenate(tiles, axis=0).reshape(parts[7].shape)
    skern.start()
    qsum, vsum = {}, {}

    def gather_grads(j):
        for o in range(1, Z):
            back[j * (Z - 1) + o - 1].wait_recv()
        for s in range(seqs):
            r = slice(s * local, (s + 1) * local)
            vals = []
            for h in range(2):
                n = h * HEADS_PER + j
                val = unpack(grecv[j, 2 * s + h])
                q = (val[:, :HEAD].astype(f32) + gqm[r, n * HEAD : (n + 1) * HEAD]).astype(bf16)
                qsum[n] = qsum.get(n, 0.0) + rows_sum(q.astype(f32))
                vsum[n] = vsum.get(n, 0.0) + rows_sum(val[:, 2 * HEAD :].astype(f32))
                vals += [q, val[:, HEAD:]]
            low = jnp.concatenate(vals, axis=1)
            grads[j, r] = low
        gw = dot(xt[...], grads[j])
        parts[4 + j][...] = gw.reshape(parts[4 + j].shape).astype(bf16)
        sc[4 + j].start()

    gather_grads(0)

    for cp in hops:
        cp.wait_recv()
    gbconv = jnp.zeros((1, CHAN), f32)
    for s in range(seqs):
        for i, at, ok in ((0, local, z < Z - 1), (1, EDGE, z > 0)):
            add = jnp.where(ok, hrecv[i, s], 0.0)
            gci_ext[s, at : at + EDGE] += add[:, :CHAN]
            gdx_ext[s, at : at + EDGE] += add[:, CHAN:]
        own = gci_ext[s, EDGE : EDGE + local]
        gbconv = gbconv + rows_sum(own)
        gcl[s * local : (s + 1) * local] = own.astype(bf16)
    gw = dot(xt[...], gcl[...])
    parts[3][..., :CHAN] = gate(gw)
    scp.start()
    skern.step1()
    sq0.step1()
    loads[4].wait()
    for s in range(seqs):
        r = slice(s * local, (s + 1) * local)
        gx[r] += gdx_ext[s, EDGE : EDGE + local] + dot_nt(gcl[r], wcp[:, :CHAN])
    gather_grads(1)
    sdown.step3()
    sup.step3()
    sout.step3()
    scp.step1()
    skern.step2()
    sq0.step2()
    taps = jnp.concatenate([rows_sum(gwd[t]) for t in range(TAPS)], axis=0)
    head = jnp.concatenate([taps, vecg[TAPS:16]], axis=0)
    own = to_owners(head, w1, N)
    place = parts[8].shape[:4]
    parts[8][:, :, :, :, 0] = own[:, :8].reshape(place + (8, 128))
    parts[8][:, :, :, :, 1] = own[:, 8:].reshape(place + (8, 128))
    sq1.step1()
    scp.step2()
    gather_grads(2)
    bprow[...] = jnp.concatenate(
        [qsum[n] for n in range(HEADS)] + [vsum[n] for n in range(HEADS)] + [gbconv, gbpoint[...]],
        axis=1,
    )
    own = to_owners(bprow[...], wp, N)
    parts[8][:, :, :, :, 2, 0:1] = own.reshape(place + (1, 128))
    svec.start()
    skern.step3()
    sq0.step3()
    sq1.step2()
    sq2.step1()
    svec.step1()
    skern.step4()
    gk_tail = Gather(grid, souts[7], kall, "zxyc", gssem, grsem, lsem)
    gk_tail.start()
    scp.step3()
    for i in range(HEADS_PER):
        loads[5 + i].wait()
    for s in range(seqs):
        r = slice(s * local, (s + 1) * local)
        acc = gx[r]
        for j in range(HEADS_PER):
            acc = acc + dot_nt(grads[j, r], wq[j])
        gx[r] = acc
    last = pltpu.make_async_copy(gx, h_gx, wsem.at[19])
    last.start()
    sq1.step3()
    sq2.step2()
    svec.step2()
    gk_tail.step1()
    sdown.step4()
    sup.step4()
    sout.step4()
    sq2.step3()
    svec.step3()
    gk_tail.step2()
    scp.step4()
    sq0.step4()
    sq1.step4()
    gk_tail.step3()
    gk_tail.step4()
    n = TALL // 8
    every = kall[...].reshape(N, 8, 128)
    o_kernel[...] = jnp.concatenate(
        [every[c * n : (c + 1) * n].reshape(TALL, 128) for c in range(CHAN // 128)], axis=1
    )
    sq2.step4()
    svec.step4()
    flat = [souts[4 + j][...].reshape(w1, 2 * PART) for j in range(HEADS_PER)]
    cols = []
    for p in range(3):
        for n in range(HEADS):
            at = n // HEADS_PER * PART + p * HEAD
            cols.append(flat[n % HEADS_PER][:, at : at + HEAD])
    o_proj[:, : 3 * CHAN] = jnp.concatenate(cols, axis=1)
    o_proj[:, 3 * CHAN :] = souts[3][...].reshape(w1, 2 * CHAN)
    for cp in sends + back + hops:
        cp.wait_send()
    for g in sc:
        g.finish()
    gk_tail.finish()
    last.wait()


TALL = -(-(HEADS * TAPS + 1) // 8) * 8


def back(dp, seq, widths, values, streamed, gathered, wgrads, shards):
    f32, bf16 = jnp.float32, jnp.bfloat16
    dctx = values[0]
    qh, xe = streamed[6], streamed[10]
    N = dp * seq
    w1, wp, wu = widths
    seqs, ext, width = xe.shape
    total = dctx.shape[0]
    local = total // seqs
    length = qh.shape[1]
    sizes = sizes_of(dp, seq)
    shape = jax.ShapeDtypeStruct
    vm = pl.BlockSpec(memory_space=pltpu.VMEM)
    hb = pl.BlockSpec(memory_space=pl.ANY)
    t_down, t_up, t_out = [tiled(a).shape for a in shards]
    lead = t_out[:2]
    piece = [
        (t_down, bf16), (t_up, bf16), (t_out, bf16), (lead + (2 * CHAN,), bf16),
    ]
    piece += [(lead + (2 * PART,), bf16)] * HEADS_PER
    piece += [((1, 8, 128), f32), ((3, 8, 128), f32)]
    place = mesh_lead(dp, seq)
    wgrads = [g.reshape(place + p[0]) for g, p in zip(wgrads, piece)]
    scratch = [pltpu.VMEM(a.shape, a.dtype) for a in streamed]
    scratch += [pltpu.VMEM((total, width), f32), pltpu.VMEM((width, total), bf16)]
    scratch += [pltpu.VMEM(place + p, d) for p, d in piece]
    for p, d in piece:
        scratch += scatter_scratch(sizes, p, d, "zxyc")
    scratch += [pltpu.VMEM(p, f32) for p, d in piece[3:8]]
    V = pltpu.VMEM
    scratch += [
        V((seq, local // 2, 2 * PART), bf16),
        V((seq, local // 2, 2 * PART), bf16),
        V((HEADS_PER, seq - 1, local // 2, 2 * PART), bf16),
        V((HEADS_PER, seq, local // 2, 2 * PART), bf16),
        V((HEADS_PER, width, 2 * PART), bf16),
        V((width, 2 * CHAN), bf16),
        V((HEADS_PER, total, 2 * PART), bf16),
        V((TAPS, local + 2 * PAD, CHAN), f32),
        V((TAPS, local, CHAN), f32),
        V((TAPS, local, CHAN), bf16),
        V((local + 2 * PAD, CHAN), f32),
        V((seqs, local + 2 * PAD, width), f32),
        V((total, CHAN), f32),
        V((total, CHAN), bf16),
        V((seqs, ext, CHAN), f32),
        V((total, CHAN), bf16),
        V((seqs, ext, width), f32),
        V((TAPS, 8, width), f32),
        V((128, CHAN), f32),
        V((TAPS, 8, CHAN), f32),
        V((1, CHAN), f32),
        V((128, CHAN), bf16),
        V((2, seqs, EDGE, CHAN + width), f32),
        V((2, seqs, EDGE, CHAN + width), f32),
        V((seq, local, HEAD), bf16),
        V((2, length, HEAD), f32),
        V(place + (1, 8, 128), f32),
        V((1, 4 * CHAN), f32),
    ]
    sem = lambda *s: pltpu.SemaphoreType.DMA(s)
    n = len(piece)
    scratch += [
        sem(n), sem(n, 4), sem(), sem(4), sem(),
        sem(HEADS_PER, seq - 1), sem(HEADS_PER, seq - 1), sem(seq - 1), sem(seq - 1),
        sem(2), sem(2), sem(20),
    ]
    outs = [
        shape((total, width), f32),
        shape((w1, 5 * CHAN), f32),
        shape(t_out, f32),
        shape(t_up, f32),
        shape(t_down, f32),
        shape((3, 8, 128), f32),
        shape((TALL, CHAN), f32),
    ]
    return pl.pallas_call(
        partial(back_kernel, dp, seq, widths),
        out_shape=outs,
        in_specs=[vm] * len(values) + [hb] * (8 + len(streamed)),
        out_specs=[hb] + [vm] * (len(outs) - 1),
        scratch_shapes=scratch,
        compiler_params=pltpu.CompilerParams(
            collective_id=3, has_side_effects=True, vmem_limit_bytes=62 << 20
        ),
        name="back",
    )(*values, *streamed, *gathered, *wgrads)


def finish_kernel(gx, proj, out, up, down, small, kern, *rest):
    outs, held, sem = rest[:-6], rest[-6:-1], rest[-1]
    copies = [
        pltpu.make_async_copy(a, b, sem.at[0, i])
        for i, (a, b) in enumerate(zip((gx, proj, out, up, down), held))
    ]
    for cp in copies:
        cp.start()
    stores = [
        pltpu.make_async_copy(a, b, sem.at[1, i])
        for i, (a, b) in enumerate(zip(held, outs[:5]))
    ]
    for a, b in zip(copies, stores):
        a.wait()
        b.start()
    depth, kernel_t, bkernel, bproj, bup = outs[5:10]
    s = small[...]
    depth[...] = s[:2].reshape(16, 128)[: depth.shape[0], : depth.shape[1]]
    kernel_t[...] = kern[: kernel_t.shape[0]]
    bkernel[...] = kern[HEADS * TAPS : HEADS * TAPS + 1, : HEADS * TAPS]
    bproj[...] = s[2, 0:1, : bproj.shape[1]]
    bup[...] = s[2, 1:2, : bup.shape[1]]
    for i, v in zip(range(V_BOUT, V_S2 + 1), outs[10:]):
        v[...] = s[i // 8, i % 8 : i % 8 + 1, : v.shape[1]]
    for cp in stores:
        cp.wait()


def finish(widths, arrays):
    f32 = jnp.float32
    w1, wp, wu = widths
    shape = jax.ShapeDtypeStruct
    vm = pl.BlockSpec(memory_space=pltpu.VMEM)
    hb = pl.BlockSpec(memory_space=pl.ANY)
    outs = [shape(a.shape, f32) for a in arrays[:5]]
    outs += [
        shape((TAPS, w1), f32), shape((HEADS * TAPS, CHAN), f32), shape((1, HEADS * TAPS), f32),
        shape((1, wp), f32), shape((1, wu), f32),
    ]
    outs += [shape((1, w1), f32)] * 6
    return pl.pallas_call(
        finish_kernel,
        out_shape=outs,
        in_specs=[hb] * 5 + [vm] * 2,
        out_specs=[hb] * 5 + [vm] * 11,
        scratch_shapes=[pltpu.VMEM(a.shape, f32) for a in arrays[:5]]
        + [pltpu.SemaphoreType.DMA((2, 5))],
        name="finish",
    )(*arrays)


def fast_body(
    hidden, cotangent, w_proj, w_depth, w_kernel, b_kernel, w_out, w_up, w_down, b_proj, b_up,
    b_out, ln1_gain, ln1_bias, b_down, ln2_gain, ln2_bias,
):
    dp, seq = lax.axis_size("dp"), lax.axis_size("seq")
    seqs, local, width = hidden.shape
    total = seqs * local
    widths = (w_out.shape[0], b_proj.shape[0], b_up.shape[0])
    small = pack_small(
        w_depth, (b_out, ln1_gain, ln1_bias, b_down, ln2_gain, ln2_bias), b_proj, b_up
    )
    w_kernel = w_kernel.T
    (
        gq0, gq1, gq2, gcp, gout, gup, gdown, qh, kh, vh, joined, qn, xe, convin, keyconv, mixed,
        spread, wkx, stats, vec, bup, bkx,
    ) = front(
        dp, seq, hidden, w_proj, w_out, w_up, w_down, small, w_kernel, b_kernel[None], widths
    )
    out, gafter, dctx, gmix, gwout, gwup, gwdown, vecg, gbup = ffn(
        joined, hidden.reshape(total, width), cotangent.reshape(total, width),
        gout.reshape(-1, w_out.shape[1]), gup.reshape(-1, w_up.shape[1]),
        gdown.reshape(-1, w_down.shape[1]), vec, bup,
    )
    res = back(
        dp, seq, widths,
        (dctx, stats, vec, bkx, w_kernel, vecg, gbup),
        (gmix, convin, keyconv, mixed, qn, wkx, qh, kh, vh, spread, xe),
        (gafter, gq0, gq1, gq2, gcp), (gwdown, gwup, gwout), (w_down, w_up, w_out),
    )
    (
        gx, g_proj, g_out, g_up, g_down, g_depth, g_kernel, g_bkernel, g_bproj, g_bup, *g_vecs,
    ) = finish(widths, res)
    return (
        out.reshape(hidden.shape),
        gx.reshape(hidden.shape),
        g_proj,
        g_depth.T,
        g_kernel.T,
        g_bkernel[0],
        g_out.reshape(w_out.shape),
        g_up.reshape(w_up.shape),
        g_down.reshape(w_down.shape),
        g_bproj[0],
        g_bup[0],
    ) + tuple(v[0] for v in g_vecs)


def fits(mesh):
    return mesh.shape["seq"] == 4 and mesh.shape["dp"] == 8


def body(
    hidden,
    cotangent,
    w_proj,
    w_depth,
    w_kernel,
    b_kernel,
    w_out,
    w_up,
    w_down,
    b_proj,
    b_up,
    b_out,
    ln1_gain,
    ln1_bias,
    b_down,
    ln2_gain,
    ln2_bias,
):
    seq_count, local_rows, model_width = hidden.shape
    total_rows = seq_count * local_rows
    head_count = HEADS
    head_size = HEAD
    all_width = head_count * head_size
    tap_count = KERNEL
    half_kernel = KERNEL // 2
    group_count = GROUPS
    hidden_units = FF
    ext_rows = local_rows + 2 * half_kernel
    score_scale = head_size ** (-0.5)
    dp, seq = lax.axis_size("dp"), lax.axis_size("seq")
    devices = dp * seq
    vectors = (b_proj, b_up, b_out, ln1_gain, ln1_bias, b_down, ln2_gain, ln2_bias)
    widths = [w_depth.shape[0] * KERNEL] + [v.shape[0] for v in vectors]
    small = jnp.concatenate([w_depth.reshape(-1)] + list(vectors))
    small = jnp.pad(small, (0, 1024 - small.shape[0])).reshape(8, 128)
    full_proj, full_out, full_up, full_down, small = gather_all(
        dp, seq, [w_proj, w_out, w_up, w_down, small]
    )
    small = cut(small.reshape(devices, 1024), widths)
    full_depth = small[0].reshape(-1, KERNEL)
    (
        full_bproj,
        full_bup,
        full_bout,
        gain_one,
        shift_one,
        full_bdown,
        gain_two,
        shift_two,
    ) = [v.reshape(-1) for v in small[1:]]
    bias_proj = full_bproj.astype(jnp.float32)
    gain_first = gain_one.astype(jnp.float32)
    shift_first = shift_one.astype(jnp.float32)
    gain_second = gain_two.astype(jnp.float32)
    shift_second = shift_two.astype(jnp.float32)
    tokens_flat = hidden.reshape(total_rows, model_width)
    first_proj = jnp.dot(
        tokens_flat, full_proj[:, : 3 * all_width], preferred_element_type=jnp.float32
    )
    queries = (first_proj[:, :all_width] + bias_proj[:all_width]).astype(jnp.bfloat16)
    key_rows = first_proj[:, all_width : 2 * all_width].astype(jnp.bfloat16)
    value_rows = (first_proj[:, 2 * all_width :] + bias_proj[all_width : 2 * all_width]).astype(
        jnp.bfloat16
    )
    extended = with_halo(hidden, (("seq", 1),), half_kernel)
    position = lax.axis_index("seq") * local_rows + jnp.arange(ext_rows) - half_kernel
    inside = ((position >= 0) & (position < local_rows * lax.axis_size("seq"))).astype(jnp.float32)
    conv_input = jnp.dot(
        extended.reshape(seq_count * ext_rows, model_width),
        full_proj[:, 3 * all_width : 4 * all_width],
        preferred_element_type=jnp.float32,
    )
    conv_input = (conv_input + bias_proj[2 * all_width : 3 * all_width]).reshape(
        seq_count, ext_rows, all_width
    ) * inside[None, :, None]
    depth_weights = full_depth.astype(jnp.float32)
    depth_sum = jnp.zeros((seq_count, local_rows, model_width), jnp.float32)
    for tap_index in range(tap_count):
        depth_sum = (
            depth_sum
            + extended[:, tap_index : tap_index + local_rows].astype(jnp.float32)
            * depth_weights[:, tap_index]
        )
    spread = depth_sum.astype(jnp.bfloat16).reshape(total_rows, model_width)
    key_conv = (
        jnp.dot(spread, full_proj[:, 4 * all_width :], preferred_element_type=jnp.float32)
        + bias_proj[3 * all_width :]
    )
    mixed_key = (key_conv * queries.astype(jnp.float32)).astype(jnp.bfloat16)
    logits = jnp.dot(mixed_key, w_kernel, preferred_element_type=jnp.float32) + b_kernel.astype(
        jnp.float32
    )
    tap_weights = jax.nn.softmax(
        logits.reshape(seq_count, local_rows, head_count, tap_count), axis=-1
    )
    conv_heads = conv_input.reshape(seq_count, ext_rows, head_count, head_size)
    conv_mix = jnp.zeros((seq_count, local_rows, head_count, head_size), jnp.float32)
    for tap_index in range(tap_count):
        conv_mix = (
            conv_mix
            + tap_weights[..., tap_index, None] * conv_heads[:, tap_index : tap_index + local_rows]
        )
    queries_seq = queries.reshape(seq_count, local_rows, all_width)
    all_keys, all_values = (
        lax.all_gather(
            key_rows.reshape(seq_count, local_rows, all_width), "seq", axis=1, tiled=True
        ),
        lax.all_gather(
            value_rows.reshape(seq_count, local_rows, all_width), "seq", axis=1, tiled=True
        ),
    )
    full_length = all_keys.shape[1]

    def forward_one(item_set):
        query_seq, key_seq, value_seq = item_set
        return attend(
            query_seq.reshape(local_rows, head_count, head_size),
            key_seq.reshape(full_length, head_count, head_size),
            value_seq.reshape(full_length, head_count, head_size),
            score_scale,
        )

    context, norm_log = lax.map(forward_one, (queries_seq, all_keys, all_values))
    joined = jnp.concatenate(
        [
            context.reshape(total_rows, all_width),
            conv_mix.reshape(total_rows, all_width).astype(jnp.bfloat16),
        ],
        axis=-1,
    )
    after_mix = (
        jnp.dot(joined, full_out, preferred_element_type=jnp.float32)
        + full_bout.astype(jnp.float32)
        + tokens_flat.astype(jnp.float32)
    )
    first_norm, first_pull = jax.vjp(layer_norm, after_mix, gain_first, shift_first)
    grouped_in = first_norm.astype(jnp.bfloat16).reshape(
        total_rows, group_count, model_width // group_count
    )
    up_groups = full_up.reshape(
        group_count, model_width // group_count, hidden_units // group_count
    )
    pre_act = jnp.einsum(
        "ngd,gdf->ngf", grouped_in, up_groups, preferred_element_type=jnp.float32
    ).reshape(total_rows, hidden_units) + full_bup.astype(jnp.float32)
    activated, gelu_pull = jax.vjp(partial(jax.nn.gelu, approximate=False), pre_act)
    act_low = activated.astype(jnp.bfloat16).reshape(
        total_rows, group_count, hidden_units // group_count
    )
    down_groups = full_down.reshape(
        group_count, hidden_units // group_count, model_width // group_count
    )
    summed = jnp.einsum(
        "ngf,gfd->ngd", act_low, down_groups, preferred_element_type=jnp.float32
    ).reshape(total_rows, model_width)
    summed = summed + full_bdown.astype(jnp.float32) + first_norm
    out_value, second_pull = jax.vjp(layer_norm, summed, gain_second, shift_second)
    output = out_value.astype(jnp.bfloat16).reshape(seq_count, local_rows, model_width)
    back_proj = full_proj
    back_depth = full_depth.astype(jnp.float32)
    back_out = full_out
    back_up = up_groups
    back_down = down_groups
    grad_summed, grad_gain_two, grad_shift_two = second_pull(
        cotangent.reshape(total_rows, model_width).astype(jnp.float32)
    )
    grad_bdown = jnp.sum(grad_summed, axis=0)
    summed_low = grad_summed.astype(jnp.bfloat16).reshape(
        total_rows, group_count, model_width // group_count
    )
    grad_activ = jnp.einsum(
        "ngd,gfd->ngf", summed_low, back_down, preferred_element_type=jnp.float32
    ).reshape(total_rows, hidden_units)
    grad_wdown = jnp.einsum(
        "ngf,ngd->gfd", act_low, summed_low, preferred_element_type=jnp.float32
    ).reshape(hidden_units, model_width // group_count)
    grad_pre = gelu_pull(grad_activ)[0]
    grad_bup = jnp.sum(grad_pre, axis=0)
    pre_low = grad_pre.astype(jnp.bfloat16).reshape(
        total_rows, group_count, hidden_units // group_count
    )
    grad_wup = jnp.einsum(
        "ngd,ngf->gdf", grouped_in, pre_low, preferred_element_type=jnp.float32
    ).reshape(model_width, hidden_units // group_count)
    grad_first = grad_summed + jnp.einsum(
        "ngf,gdf->ngd", pre_low, back_up, preferred_element_type=jnp.float32
    ).reshape(total_rows, model_width)
    grad_after, grad_gain_one, grad_shift_one = first_pull(grad_first)
    grad_bout = jnp.sum(grad_after, axis=0)
    after_low = grad_after.astype(jnp.bfloat16)
    grad_wout = jnp.dot(joined.T, after_low, preferred_element_type=jnp.float32)
    grad_joined = jnp.dot(after_low, back_out.T, preferred_element_type=jnp.float32)
    grad_context = (
        grad_joined[:, :all_width].astype(jnp.bfloat16).reshape(seq_count, local_rows, all_width)
    )
    grad_mix = grad_joined[:, all_width:].reshape(seq_count, local_rows, head_count, head_size)

    def back_one(item_set):
        query_seq, grad_seq, norm_seq, key_seq, value_seq = item_set
        grad_query, grad_key, grad_value, unused_delta = attend_back(
            query_seq.reshape(local_rows, head_count, head_size),
            grad_seq.reshape(local_rows, head_count, head_size),
            norm_seq,
            key_seq.reshape(full_length, head_count, head_size),
            value_seq.reshape(full_length, head_count, head_size),
            None,
            score_scale,
        )
        key_value = jnp.concatenate(
            [grad_key.reshape(full_length, all_width), grad_value.reshape(full_length, all_width)],
            axis=-1,
        )
        return (grad_query.reshape(local_rows, all_width), key_value)

    grad_query_att, kv_terms = lax.map(
        back_one, (queries_seq, grad_context, norm_log, all_keys, all_values)
    )
    own_kv = lax.psum_scatter(
        kv_terms.astype(jnp.bfloat16), "seq", scatter_dimension=1, tiled=True
    ).astype(jnp.float32)
    grad_keys_low = own_kv[..., :all_width].reshape(total_rows, all_width).astype(jnp.bfloat16)
    grad_values_low = own_kv[..., all_width:].reshape(total_rows, all_width).astype(jnp.bfloat16)
    grad_taps = jnp.stack(
        [
            jnp.sum(grad_mix * conv_heads[:, tap_index : tap_index + local_rows], axis=-1)
            for tap_index in range(tap_count)
        ],
        axis=-1,
    )
    grad_conv_ext = jnp.zeros((seq_count, ext_rows, head_count, head_size), jnp.float32)
    for tap_index in range(tap_count):
        grad_conv_ext = grad_conv_ext + jnp.pad(
            tap_weights[..., tap_index, None] * grad_mix,
            ((0, 0), (tap_index, 2 * half_kernel - tap_index), (0, 0), (0, 0)),
        )
    grad_logits = tap_weights * (
        grad_taps - jnp.sum(tap_weights * grad_taps, axis=-1, keepdims=True)
    )
    grad_logits = grad_logits.reshape(total_rows, head_count * tap_count)
    grad_bkernel = jnp.sum(grad_logits, axis=0)
    logits_low = grad_logits.astype(jnp.bfloat16)
    grad_wkernel = jnp.dot(mixed_key.T, logits_low, preferred_element_type=jnp.float32)
    grad_mixed = jnp.dot(logits_low, w_kernel.T, preferred_element_type=jnp.float32)
    grad_queries = (grad_query_att.reshape(total_rows, all_width) + grad_mixed * key_conv).astype(
        jnp.bfloat16
    )
    grad_key_conv = grad_mixed * queries.astype(jnp.float32)
    grad_bpt = jnp.sum(grad_key_conv, axis=0)
    key_conv_low = grad_key_conv.astype(jnp.bfloat16)
    grad_wpt = jnp.dot(spread.T, key_conv_low, preferred_element_type=jnp.float32)
    grad_spread = jnp.dot(
        key_conv_low, back_proj[:, 4 * all_width :].T, preferred_element_type=jnp.float32
    ).reshape(seq_count, local_rows, model_width)
    grad_wdepth = jnp.stack(
        [
            jnp.sum(
                extended[:, tap_index : tap_index + local_rows].astype(jnp.float32) * grad_spread,
                axis=(0, 1),
            )
            for tap_index in range(tap_count)
        ],
        axis=-1,
    )
    grad_ext_depth = jnp.zeros((seq_count, ext_rows, model_width), jnp.float32)
    for tap_index in range(tap_count):
        grad_ext_depth = grad_ext_depth + jnp.pad(
            back_depth[:, tap_index] * grad_spread,
            ((0, 0), (tap_index, 2 * half_kernel - tap_index), (0, 0)),
        )
    combined = jnp.concatenate(
        [grad_conv_ext.reshape(seq_count, ext_rows, all_width), grad_ext_depth], axis=-1
    )
    received = with_halo(combined.astype(jnp.bfloat16), (("seq", 1),), half_kernel).astype(
        combined.dtype
    )
    own_part = combined[:, half_kernel : half_kernel + local_rows]
    own_part = own_part.at[:, :half_kernel].add(received[:, :half_kernel])
    own_part = own_part.at[:, local_rows - half_kernel :].add(
        received[:, received.shape[1] - half_kernel :]
    )
    grad_conv_own = own_part[..., :all_width].reshape(total_rows, all_width)
    grad_depth_x = own_part[..., all_width:].reshape(total_rows, model_width)
    grad_bconv = jnp.sum(grad_conv_own, axis=0)
    conv_low = grad_conv_own.astype(jnp.bfloat16)
    stacked = jnp.concatenate([grad_queries, grad_keys_low, grad_values_low, conv_low], axis=-1)
    grad_wfirst = jnp.dot(tokens_flat.T, stacked, preferred_element_type=jnp.float32)
    grad_tokens = (
        grad_after
        + jnp.dot(stacked, back_proj[:, : 4 * all_width].T, preferred_element_type=jnp.float32)
        + grad_depth_x
    )
    grad_wproj = jnp.concatenate([grad_wfirst, grad_wpt], axis=1)
    grad_bproj = jnp.concatenate(
        [
            jnp.sum(grad_queries.astype(jnp.float32), axis=0),
            jnp.sum(grad_values_low.astype(jnp.float32), axis=0),
            grad_bconv,
            grad_bpt,
        ]
    )
    def blocks(grad, shard):
        return grad.astype(jnp.bfloat16).reshape((devices,) + tiled(shard).shape)

    per_device = [
        g.reshape(devices, -1)
        for g in (
            grad_wdepth, grad_bproj, grad_bup, grad_bout, grad_gain_one, grad_shift_one,
            grad_bdown, grad_gain_two, grad_shift_two,
        )
    ]
    kernel_flat = jnp.concatenate([grad_wkernel.reshape(-1), grad_bkernel])
    kernel_len = kernel_flat.shape[0]
    kernel_each = -(-kernel_len // devices)
    kernel_flat = jnp.pad(kernel_flat, (0, kernel_each * devices - kernel_len))
    small_grad = jnp.concatenate(
        [
            lanes(jnp.concatenate(per_device, axis=1), 1),
            lanes(kernel_flat.reshape(devices, kernel_each), 1),
        ],
        axis=1,
    )
    sum_down, sum_up, sum_out, sum_proj, sum_small, sum_kernel = scatter_all(
        dp,
        seq,
        [
            blocks(grad_wdown, w_down), blocks(grad_wup, w_up), blocks(grad_wout, w_out),
            blocks(grad_wproj, w_proj), small_grad,
        ],
        ("zxyc", "zyxc", "zxyc", "zyxc", "zxyc"),
    )
    mine = cut(sum_small[:1].reshape(1, 1024), widths)
    shards = [sum_proj.reshape(w_proj.shape), mine[0].reshape(w_depth.shape)]
    shards += [
        sum_out.reshape(w_out.shape), sum_up.reshape(w_up.shape), sum_down.reshape(w_down.shape),
    ]
    shards += [m.reshape(-1) for m in mine[1:]]
    kernel_sum = sum_kernel.reshape(devices, 1024)[:, :kernel_each].reshape(-1)
    kernel_total = (
        kernel_sum[: grad_wkernel.size].reshape(grad_wkernel.shape),
        kernel_sum[grad_wkernel.size : kernel_len],
    )
    return (
        output,
        grad_tokens.reshape(seq_count, local_rows, model_width),
        shards[0],
        shards[1],
        kernel_total[0],
        kernel_total[1],
        shards[2],
        shards[3],
        shards[4],
        shards[5],
        shards[6],
        shards[7],
        shards[8],
        shards[9],
        shards[10],
        shards[11],
        shards[12],
    )


def solution(mesh):
    placed = (
        P("dp", "seq", None),
        P("dp", "seq", None),
        P(("dp", "seq"), None),
        P(("dp", "seq"), None),
        P(),
        P(),
        P(("dp", "seq"), None),
        P(("dp", "seq"), None),
        P(("dp", "seq"), None),
        P(("dp", "seq")),
        P(("dp", "seq")),
        P(("dp", "seq")),
        P(("dp", "seq")),
        P(("dp", "seq")),
        P(("dp", "seq")),
        P(("dp", "seq")),
        P(("dp", "seq")),
    )
    return jax.shard_map(
        fast_body if fits(mesh) else body,
        mesh=mesh,
        in_specs=placed,
        out_specs=(
            P("dp", "seq", None),
            P("dp", "seq", None),
            P(("dp", "seq"), None),
            P(("dp", "seq"), None),
            P(),
            P(),
            P(("dp", "seq"), None),
            P(("dp", "seq"), None),
            P(("dp", "seq"), None),
            P(("dp", "seq")),
            P(("dp", "seq")),
            P(("dp", "seq")),
            P(("dp", "seq")),
            P(("dp", "seq")),
            P(("dp", "seq")),
            P(("dp", "seq")),
            P(("dp", "seq")),
        ),
        check_vma=False,
    )
```

```python
from functools import partial

import jax
import jax.numpy as jnp
from jax import lax
from jax.experimental import pallas as pl
from jax.experimental.pallas import tpu as pltpu
from jax.sharding import PartitionSpec as P

MESH = pl.DeviceIdType.MESH


class Grid:
    def __init__(self, dp, seq):
        self.C = 2 if dp % 2 == 0 else 1
        rest = dp // self.C
        y = 1
        while (2 * y) * (2 * y) <= rest and rest % (2 * y) == 0:
            y *= 2
        self.Y, self.X, self.Z = y, rest // y, seq
        d = lax.axis_index("dp")
        self.z = lax.axis_index("seq")
        self.c = d % self.C
        self.x = (d // self.C) % self.X
        self.y = d // (self.C * self.X)
        self.dp = d
    def size(self, ax):
        return getattr(self, ax.upper())
    def at(self, **off):
        g = {a: (getattr(self, a) + off.get(a, 0)) % self.size(a) if off.get(a, 0) else getattr(self, a) for a in "yxcz"}
        return g
    def dpof(self, g):
        return (g["y"] * self.X + g["x"]) * self.C + g["c"]
    def dev(self, **off):
        g = self.at(**off)
        return (self.dpof(g), g["z"])


def peers(grid):
    out = []
    for a in "zxyc":
        for o in range(1, grid.size(a)):
            out.append(grid.dev(**{a: o}))
    return out


def greet(grid):
    for p in peers(grid):
        pl.semaphore_signal(
            pltpu.get_barrier_semaphore(), inc=1, device_id=p, device_id_type=MESH
        )


def meet(grid):
    pl.semaphore_wait(pltpu.get_barrier_semaphore(), len(peers(grid)))


def entry_barrier(grid):
    greet(grid)
    meet(grid)


def pick(ref, axes, at):
    return ref.at[tuple(at[a] if a in axes else slice(None) for a in "yxc")]


def shards(ref, n):
    size = ref.shape[0] * ref.shape[1] * ref.shape[2] * ref.shape[3]
    return ref.reshape((size,) + tuple(ref.shape[4:])).at[pl.ds(0, n)]


def remote(src, dst, ssem, rsem, dev):
    return pltpu.make_async_remote_copy(
        src_ref=src, dst_ref=dst, send_sem=ssem, recv_sem=rsem, device_id=dev, device_id_type=MESH
    )


class Gather:
    def __init__(self, grid, src, buf, order, ssem, rsem, lsem):
        self.g, self.src, self.buf, self.ssem, self.rsem, self.lsem = grid, src, buf, ssem, rsem, lsem
        self.u, self.v = order[1], order[2]
        self.sent = 0

    def _send(self, src, dst, stage, n, **off):
        remote(src, dst, self.ssem, self.rsem.at[stage], self.g.dev(**off)).start()
        self.sent += n

    def _wait(self, stage, n):
        ref = shards(self.buf, n)
        remote(ref, ref, self.ssem, self.rsem.at[stage], self.g.dev(c=1)).wait_recv()

    def _block(self, uo=0):
        return pick(self.buf, "yxc", self.g.at(**{self.u: uo}))

    def start(self):
        g = self.g
        own = self.buf.at[g.y, g.x, g.c, g.z]
        self.local = pltpu.make_async_copy(self.src, own, self.lsem)
        self.local.start()
        for o in range(1, g.Z):
            self._send(self.src, own, 0, 1, z=o)

    def step1(self):
        g = self.g
        self.local.wait()
        self._wait(0, g.Z - 1)
        own = self._block()
        for o in range(1, g.size(self.u)):
            self._send(own, own, 1, g.Z, **{self.u: o})
        for o in range(1, g.size(self.v)):
            self._send(own, own, 2, g.Z, **{self.v: o})

    def step2(self):
        g = self.g
        U, V = g.size(self.u), g.size(self.v)
        if U > 1:
            self._wait(1, (U - 1) * g.Z)
        for q in range(1, U):
            for o in range(1, V):
                self._send(self._block(q), self._block(q), 2, g.Z, **{self.v: o})

    def step3(self):
        g = self.g
        U, V = g.size(self.u), g.size(self.v)
        if V > 1:
            self._wait(2, U * (V - 1) * g.Z)
        mine = pick(self.buf, "c", g.at())
        for o in range(1, g.C):
            self._send(mine, mine, 3, U * V * g.Z, c=o)

    def step4(self):
        g = self.g
        if g.C > 1:
            self._wait(3, (g.C - 1) * g.Y * g.X * g.Z)

    def finish(self):
        ref = shards(self.buf, self.sent)
        remote(ref, ref, self.ssem, self.rsem.at[0], self.g.dev(c=1)).wait_send()


def run_gathers(gs):
    n = len(gs)
    for g in gs:
        g.start()
    steps = [lambda g: g.step1(), lambda g: g.step2(), lambda g: g.step3(), lambda g: g.step4()]
    for t in range(n + 3):
        for s in range(4):
            i = t - s
            if 0 <= i < n:
                steps[s](gs[i])
    for g in gs:
        g.finish()


class Scatter:
    def __init__(self, grid, part, order, bufs, out, ssem, rsem):
        self.g, self.part, self.out, self.ssem, self.rsem = grid, part, out, ssem, rsem
        self.rc, self.rv, self.ru, self.rz = bufs
        self.u, self.v = order[1], order[2]
        self.U, self.V = grid.size(self.u), grid.size(self.v)
        self.sent = 0

    def _send(self, src, dst, stage, n, **off):
        remote(src, dst, self.ssem, self.rsem.at[stage], self.g.dev(**off)).start()
        self.sent += n

    def _wait(self, stage, ref):
        remote(ref, ref, self.ssem, self.rsem.at[stage], self.g.dev(c=1)).wait_recv()

    def _yx(self, u, v):
        return (v, u) if self.v == "y" else (u, v)

    def _total(self, u, v, i, stage):
        f = jnp.float32
        y, x = self._yx(u, v)
        s = self.part[y, x, self.g.c, i].astype(f)
        for o in range(self.g.C - 1):
            s = s + self.rc[o, y, x, i].astype(f)
        if stage > 1:
            for k in range(self.V - 1):
                s = s + self.rv[k, u, i].astype(f)
        if stage > 2:
            for k in range(self.U - 1):
                s = s + self.ru[k, i].astype(f)
        return s

    def start(self):
        g = self.g
        for o in range(1, g.C):
            self._send(pick(self.part, "c", g.at(c=o)), self.rc.at[o - 1], 0, g.Y * g.X * g.Z, c=o)

    def step1(self):
        g = self.g
        if g.C > 1:
            self._wait(0, self.rc)
        for w in range(1, self.V):
            to = g.at(**{self.v: w})

            def body(i, _):
                u, k = i // g.Z, i % g.Z
                y, x = self._yx(u, to[self.v])
                self.part[y, x, g.c, k] = self._total(u, to[self.v], k, 1).astype(self.part.dtype)
                return 0

            lax.fori_loop(0, self.U * g.Z, body, 0)
            self._send(
                pick(self.part, self.v + "c", to), self.rv.at[w - 1], 1, self.U * g.Z, **{self.v: w}
            )

    def step2(self):
        g = self.g
        here = g.at()
        if self.V > 1:
            self._wait(1, self.rv)
        for q in range(1, self.U):
            to = g.at(**{self.u: q})

            def body(k, _):
                u, v = to[self.u], here[self.v]
                y, x = self._yx(u, v)
                self.part[y, x, g.c, k] = self._total(u, v, k, 2).astype(self.part.dtype)
                return 0

            lax.fori_loop(0, g.Z, body, 0)
            self._send(pick(self.part, "yxc", to), self.ru.at[q - 1], 2, g.Z, **{self.u: q})

    def step3(self):
        g = self.g
        here = g.at()
        if self.U > 1:
            self._wait(2, self.ru)
        for o in range(1, g.Z):
            i = (g.z + o) % g.Z
            self.part[g.y, g.x, g.c, i] = self._total(here[self.u], here[self.v], i, 3).astype(
                self.part.dtype
            )
            self._send(self.part.at[g.y, g.x, g.c, i], self.rz.at[o - 1], 3, 1, z=o)

    def step4(self):
        g = self.g
        here = g.at()
        s = self._total(here[self.u], here[self.v], g.z, 3)
        if g.Z > 1:
            self._wait(3, self.rz)
        for o in range(g.Z - 1):
            s = s + self.rz[o].astype(jnp.float32)
        self.out[...] = s

    def finish(self):
        ref = shards(self.part, self.sent)
        remote(ref, ref, self.ssem, self.rsem.at[0], self.g.dev(c=1)).wait_send()


def scatter_scratch(sizes, shape, dtype, order):
    Z, C, U, V = sizes["z"], sizes["c"], sizes[order[1]], sizes[order[2]]
    t = tuple(shape)
    m = lambda n: max(n, 1)
    return [
        pltpu.VMEM((m(C - 1), sizes["y"], sizes["x"], Z) + t, dtype),
        pltpu.VMEM((m(V - 1), U, Z) + t, dtype),
        pltpu.VMEM((m(U - 1), Z) + t, dtype),
        pltpu.VMEM((m(Z - 1),) + t, dtype),
    ]


def run_scatters(gs):
    n = len(gs)
    for g in gs:
        g.start()
    for t in range(n + 3):
        for s in range(4):
            i = t - s
            if 0 <= i < n:
                [gs[i].step1, gs[i].step2, gs[i].step3, gs[i].step4][s]()
    for g in gs:
        g.finish()


ORDERS = ("zxyc", "zyxc", "zyxc", "zxyc", "zyxc", "zxyc")
VMEM_CAP = 60 << 20


def sizes_of(dp, seq):
    C = 2 if dp % 2 == 0 else 1
    rest = dp // C
    y = 1
    while (2 * y) * (2 * y) <= rest and rest % (2 * y) == 0:
        y *= 2
    return dict(y=y, x=rest // y, c=C, z=seq)


def mesh_lead(dp, seq):
    s = sizes_of(dp, seq)
    return (s["y"], s["x"], s["c"], s["z"])


def tiled(shard):
    rows, cols = shard.shape
    return shard.reshape((rows // 8, 8, cols) if rows % 8 == 0 else (1, rows, cols))


def gather_kernel(dp, seq, orders, *refs):
    n = len(orders)
    ins, outs = refs[:n], refs[n : 2 * n]
    ssem, rsem, lsem = refs[2 * n :]
    grid = Grid(dp, seq)
    entry_barrier(grid)
    run_gathers(
        [
            Gather(grid, ins[i], outs[i], orders[i], ssem.at[i], rsem.at[i], lsem.at[i])
            for i in range(n)
        ]
    )


def gather_all(dp, seq, shards):
    n = len(shards)
    lead = mesh_lead(dp, seq)
    blocks = [tiled(s) for s in shards]
    outs = pl.pallas_call(
        partial(gather_kernel, dp, seq, ORDERS[:n]),
        out_shape=[jax.ShapeDtypeStruct(lead + b.shape, b.dtype) for b in blocks],
        in_specs=[pl.BlockSpec(memory_space=pl.ANY)] * n,
        out_specs=[pl.BlockSpec(memory_space=pl.ANY)] * n,
        scratch_shapes=[
            pltpu.SemaphoreType.DMA((n,)), pltpu.SemaphoreType.DMA((n, 4)),
            pltpu.SemaphoreType.DMA((n,)),
        ],
        compiler_params=pltpu.CompilerParams(collective_id=0, has_side_effects=True),
        name="gather",
    )(*blocks)
    return [o.reshape((-1, s.shape[1])) for o, s in zip(outs, shards)]


def scatter_kernel(dp, seq, orders, count, *refs):
    n = len(orders)
    ins, outs, total, rest = refs[:n], refs[n : 2 * n], refs[2 * n], refs[2 * n + 1 :]
    parts, rest = rest[:n], rest[n:]
    ssem, rsem, lsem, gs, gr = rest[-5:]
    tail = rest[-6]
    grid = Grid(dp, seq)
    copies = [pltpu.make_async_copy(ins[i], parts[i], lsem.at[i]) for i in range(n)]
    for c in copies:
        c.start()
    entry_barrier(grid)
    for c in copies:
        c.wait()
    run_scatters(
        [
            Scatter(
                grid, parts[i], orders[i], rest[4 * i : 4 * i + 4], outs[i],
                ssem.at[i], rsem.at[i],
            )
            for i in range(n)
        ]
    )
    tail[...] = outs[n - 1][1:]
    run_gathers([Gather(grid, tail, total, "zxyc", gs, gr, lsem.at[n])])


def scatter_all(dp, seq, parts, orders):
    n = len(parts)
    N = dp * seq
    sizes = sizes_of(dp, seq)
    lead = mesh_lead(dp, seq)
    parts = [p.reshape(lead + p.shape[1:]) for p in parts]
    scratch = [pltpu.VMEM(p.shape, p.dtype) for p in parts]
    for p, o in zip(parts, orders):
        scratch += scatter_scratch(sizes, p.shape[4:], p.dtype, o)
    last = parts[-1].shape[4:]
    tail = (last[0] - 1,) + last[1:]
    return pl.pallas_call(
        partial(scatter_kernel, dp, seq, orders, n),
        out_shape=[jax.ShapeDtypeStruct(p.shape[4:], jnp.float32) for p in parts]
        + [jax.ShapeDtypeStruct(lead + tail, jnp.float32)],
        in_specs=[pl.BlockSpec(memory_space=pl.ANY)] * n,
        out_specs=[pl.BlockSpec(memory_space=pltpu.VMEM)] * (n + 1),
        scratch_shapes=scratch
        + [
            pltpu.VMEM(tail, jnp.float32), pltpu.SemaphoreType.DMA((n,)),
            pltpu.SemaphoreType.DMA((n, 4)), pltpu.SemaphoreType.DMA((n + 1,)),
            pltpu.SemaphoreType.DMA(()), pltpu.SemaphoreType.DMA((4,)),
        ],
        compiler_params=pltpu.CompilerParams(
            collective_id=1, has_side_effects=True, vmem_limit_bytes=VMEM_CAP
        ),
        name="scatter",
    )(*parts)


def lanes(flat, rows):
    return jnp.pad(flat, ((0, 0), (0, rows * 1024 - flat.shape[1]))).reshape(-1, rows, 8, 128)


def cut(rows, widths):
    out, at = [], 0
    for w in widths:
        out.append(rows[:, at : at + w])
        at += w
    return out


HEADS = 6
HEAD = 64
KERNEL = 9
FF = 3072
GROUPS = 2


norm_eps = 1e-12


def with_halo(cells, sides, width):
    for axis, dim in sides:
        count = lax.axis_size(axis)
        ends = count - 1
        head = lax.slice_in_dim(cells, 0, width, axis=dim)
        tail = lax.slice_in_dim(cells, cells.shape[dim] - width, cells.shape[dim], axis=dim)
        cells = jnp.concatenate(
            [
                lax.ppermute(tail, axis, [(i, (i + 1) % count) for i in range(ends)]),
                cells,
                lax.ppermute(head, axis, [((i + 1) % count, i) for i in range(ends)]),
            ],
            axis=dim,
        )
    return cells


def layer_norm(inputs, gain_vec, shift_vec):
    centre = inputs - jnp.mean(inputs, axis=-1, keepdims=True)
    variance = jnp.mean(centre * centre, axis=-1, keepdims=True)
    return centre * lax.rsqrt(variance + norm_eps) * gain_vec + shift_vec


def attend(queries, key_rows, value_rows, score_scale):
    scores = (
        jnp.einsum("ihe,jhe->hij", queries, key_rows, preferred_element_type=jnp.float32)
        * score_scale
    )
    row_max = jnp.max(scores, axis=-1, keepdims=True)
    norm_log = row_max + jnp.log(jnp.sum(jnp.exp(scores - row_max), axis=-1, keepdims=True))
    weights_low = jnp.exp(scores - norm_log).astype(jnp.bfloat16)
    context = jnp.einsum(
        "hij,jhe->ihe", weights_low, value_rows, preferred_element_type=jnp.float32
    )
    return (context.astype(jnp.bfloat16), norm_log[..., 0])


def attend_back(queries, grad_context, norm_log, key_rows, value_rows, row_delta, score_scale):
    scores = (
        jnp.einsum("ihe,jhe->hij", queries, key_rows, preferred_element_type=jnp.float32)
        * score_scale
    )
    soft_rows = jnp.exp(scores - norm_log[..., None])
    grad_soft = jnp.einsum(
        "ihe,jhe->hij", grad_context, value_rows, preferred_element_type=jnp.float32
    )
    row_delta = jnp.sum(soft_rows * grad_soft, axis=-1)
    grad_scores = (soft_rows * (grad_soft - row_delta[..., None])).astype(jnp.bfloat16)
    grad_queries = (
        jnp.einsum("hij,jhe->ihe", grad_scores, key_rows, preferred_element_type=jnp.float32)
        * score_scale
    )
    grad_keys = (
        jnp.einsum("hij,ihe->jhe", grad_scores, queries, preferred_element_type=jnp.float32)
        * score_scale
    )
    grad_values = jnp.einsum(
        "hij,ihe->jhe",
        soft_rows.astype(jnp.bfloat16),
        grad_context,
        preferred_element_type=jnp.float32,
    )
    return (grad_queries, grad_keys, grad_values, row_delta)


def dot(a, b):
    return jnp.dot(a, b, preferred_element_type=jnp.float32)


def dot_nt(a, b):
    return lax.dot_general(a, b, (((1,), (1,)), ((), ())), preferred_element_type=jnp.float32)


def dot_tn(a, b):
    return lax.dot_general(a, b, (((0,), (0,)), ((), ())), preferred_element_type=jnp.float32)


def centred(v):
    centre = v - jnp.mean(v, axis=-1, keepdims=True)
    inv = lax.rsqrt(jnp.mean(centre * centre, axis=-1, keepdims=True) + norm_eps)
    return centre * inv, inv


def norm_back(grad, normed, inv):
    return inv * (
        grad
        - jnp.mean(grad, axis=-1, keepdims=True)
        - normed * jnp.mean(grad * normed, axis=-1, keepdims=True)
    )


def rows_sum(v):
    return jnp.sum(v, axis=0, keepdims=True)


V_BOUT, V_G1, V_S1, V_BDOWN, V_G2, V_S2 = range(9, 15)
HALF_GELU = 0.7071067811865476
PDF = 0.3989422804014327
BLOCK = 512
CHUNK = 768


def ffn_kernel(
    joined, x, cot, wout, h_wup, h_wdown, vec, bup,
    h_out, h_gafter, h_dctx, h_gmix, h_gwout, h_gwup, h_gwdown, vecg, gbup,
    wup, wdown, out, gafter, dctx, gmix, gwout, gwup, gwdown,
    act, slope, gp, fnb, gsb, gab, lsem, bsem, wsem,
):
    f32, bf16 = jnp.float32, jnp.bfloat16
    total = x.shape[0]
    width = x.shape[1]
    chan = width // 2
    gw = width // GROUPS
    gf = FF // GROUPS
    loads = [
        pltpu.make_async_copy(h_wup, wup, lsem.at[0]),
        pltpu.make_async_copy(h_wdown, wdown, lsem.at[1]),
    ]
    for cp in loads:
        cp.start()

    def stores(r):
        rows = pl.ds(pl.multiple_of(r * BLOCK, BLOCK), BLOCK)
        return [
            pltpu.make_async_copy(a.at[rows], b.at[rows], bsem.at[i, r])
            for i, (a, b) in enumerate(
                ((out, h_out), (gafter, h_gafter), (dctx, h_dctx), (gmix, h_gmix))
            )
        ]

    vecg[...] = jnp.zeros_like(vecg)
    gbup[...] = jnp.zeros_like(gbup)

    def block(r, _):
        rows = pl.ds(pl.multiple_of(r * BLOCK, BLOCK), BLOCK)
        row = lambda i: vec[i : i + 1, :]
        after = dot(joined[rows], wout[...]) + row(V_BOUT) + x[rows].astype(f32)
        n1, inv1 = centred(after)
        first = n1 * row(V_G1) + row(V_S1)
        low = first.astype(bf16)
        fnb[rows] = low

        @pl.when(r == 0)
        def _():
            for cp in loads:
                cp.wait()

        parts = []
        for g in range(GROUPS):
            acc = jnp.zeros((BLOCK, gw), f32)
            for j in range(gf // CHUNK):
                cols = slice(g * gf + j * CHUNK, g * gf + (j + 1) * CHUNK)
                pre = dot(
                    low[:, g * gw : (g + 1) * gw],
                    wup[g * gw : (g + 1) * gw, j * CHUNK : (j + 1) * CHUNK],
                ) + bup[:, cols]
                cdf = 0.5 + 0.5 * lax.erf(pre * HALF_GELU)
                a = (pre * cdf).astype(bf16)
                act[rows, cols] = a
                slope[:, cols] = cdf + pre * (PDF * jnp.exp(pre * pre * -0.5))
                acc = acc + dot(a, wdown[cols])
            parts.append(acc)
        summed = jnp.concatenate(parts, axis=-1) + row(V_BDOWN) + first
        n2, inv2 = centred(summed)
        out[rows] = (n2 * row(V_G2) + row(V_S2)).astype(bf16)
        c = cot[rows].astype(f32)
        gs = norm_back(c * row(V_G2), n2, inv2)
        glow = gs.astype(bf16)
        gsb[rows] = glow
        parts = []
        for g in range(GROUPS):
            acc = jnp.zeros((BLOCK, gw), f32)
            for j in range(gf // CHUNK):
                cols = slice(g * gf + j * CHUNK, g * gf + (j + 1) * CHUNK)
                pre = dot_nt(glow[:, g * gw : (g + 1) * gw], wdown[cols]) * slope[:, cols]
                gbup[:, cols] += rows_sum(pre)
                p = pre.astype(bf16)
                gp[rows, cols] = p
                acc = acc + dot_nt(
                    p, wup[g * gw : (g + 1) * gw, j * CHUNK : (j + 1) * CHUNK]
                )
            parts.append(acc)
        gfirst = gs + jnp.concatenate(parts, axis=-1)
        ga = norm_back(gfirst * row(V_G1), n1, inv1)
        gafter[rows] = ga
        alow = ga.astype(bf16)
        gab[rows] = alow
        gj = dot_nt(alow, wout[...])
        dctx[rows] = gj[:, :chan].astype(bf16)
        gmix[rows] = gj[:, chan:]
        for i, v in (
            (V_BOUT, ga), (V_G1, gfirst * n1), (V_S1, gfirst), (V_BDOWN, gs), (V_G2, c * n2),
            (V_S2, c),
        ):
            vecg[i : i + 1, :] += rows_sum(v)
        for cp in stores(r):
            cp.start()
        return 0

    lax.fori_loop(0, total // BLOCK, block, 0)
    gwout[...] = dot_tn(joined[...], gab[...]).astype(bf16)
    ends = [pltpu.make_async_copy(gwout, h_gwout, wsem.at[0, 0])]
    ends[0].start()
    chunks = gf // CHUNK
    for g in range(GROUPS):

        def weights(j, _, g=g):
            cols = pl.ds(pl.multiple_of(g * gf + j * CHUNK, CHUNK), CHUNK)
            gwdown[cols] = dot_tn(act[:, cols], gsb[:, g * gw : (g + 1) * gw]).astype(bf16)
            gwup[g * gw : (g + 1) * gw, pl.ds(pl.multiple_of(j * CHUNK, CHUNK), CHUNK)] = dot_tn(
                fnb[:, g * gw : (g + 1) * gw], gp[:, cols]
            ).astype(bf16)
            return 0

        lax.fori_loop(0, chunks, weights, 0, unroll=True)
        for i, (a, b, rows) in enumerate(
            (
                (gwdown, h_gwdown, slice(g * gf, (g + 1) * gf)),
                (gwup, h_gwup, slice(g * gw, (g + 1) * gw)),
            )
        ):
            cp = pltpu.make_async_copy(a.at[rows], b.at[rows], wsem.at[1 + i, g])
            cp.start()
            ends.append(cp)
    for r in range(total // BLOCK):
        ends += stores(r)
    for cp in ends:
        cp.wait()


def ffn(joined, x, cot, wout, wup, wdown, vec, bup):
    f32, bf16 = jnp.float32, jnp.bfloat16
    total, width = x.shape
    shape = jax.ShapeDtypeStruct
    return pl.pallas_call(
        ffn_kernel,
        out_shape=[
            shape((total, width), bf16),
            shape((total, width), f32),
            shape((total, width // 2), bf16),
            shape((total, width // 2), f32),
            shape(wout.shape, bf16),
            shape(wup.shape, bf16),
            shape(wdown.shape, bf16),
            shape(vec.shape, f32),
            shape(bup.shape, f32),
        ],
        in_specs=[pl.BlockSpec(memory_space=pltpu.VMEM)] * 4
        + [pl.BlockSpec(memory_space=pl.ANY)] * 2
        + [pl.BlockSpec(memory_space=pltpu.VMEM)] * 2,
        out_specs=[pl.BlockSpec(memory_space=pl.ANY)] * 7
        + [pl.BlockSpec(memory_space=pltpu.VMEM)] * 2,
        scratch_shapes=[
            pltpu.VMEM(wup.shape, bf16),
            pltpu.VMEM(wdown.shape, bf16),
            pltpu.VMEM((total, width), bf16),
            pltpu.VMEM((total, width), f32),
            pltpu.VMEM((total, width // 2), bf16),
            pltpu.VMEM((total, width // 2), f32),
            pltpu.VMEM(wout.shape, bf16),
            pltpu.VMEM(wup.shape, bf16),
            pltpu.VMEM(wdown.shape, bf16),
            pltpu.VMEM((total, FF), bf16),
            pltpu.VMEM((BLOCK, FF), f32),
            pltpu.VMEM((total, FF), bf16),
            pltpu.VMEM((total, width), bf16),
            pltpu.VMEM((total, width), bf16),
            pltpu.VMEM((total, width), bf16),
            pltpu.SemaphoreType.DMA((2,)),
            pltpu.SemaphoreType.DMA((4, total // BLOCK)),
            pltpu.SemaphoreType.DMA((3, GROUPS)),
        ],
        compiler_params=pltpu.CompilerParams(vmem_limit_bytes=VMEM_CAP),
        name="ffn",
    )(joined, x, cot, wout, wup, wdown, vec, bup)


HEADS_PER = HEADS // 2
PART = HEADS_PER * HEAD
EDGE = 8
TAPS = KERNEL
CHAN = HEADS * HEAD


def iota(shape, dim):
    return lax.broadcasted_iota(jnp.int32, shape, dim)


def expander(rows, cols, width):
    return (iota((rows, cols), 1) % width == iota((rows, cols), 0)).astype(jnp.bfloat16)


def owned(stack, width):
    keep = iota(stack.shape, 2) // width == iota(stack.shape, 0)
    return jnp.sum(jnp.where(keep, stack, 0.0), axis=0)


def unpack_small(gsmall, vec, bproj, bup, widths):
    n = gsmall.shape[0] * gsmall.shape[1] * gsmall.shape[2] * gsmall.shape[3]
    gsmall = gsmall[...].reshape((n,) + gsmall.shape[4:])
    w, wp, wu = widths
    flat = gsmall[:, :2].reshape(n * 16, 128).astype(jnp.bfloat16)
    cols = vec.shape[1]
    vec[...] = owned(dot(flat, expander(128, cols, w)).reshape(n, 16, cols), w)
    flat = gsmall[:, 2].reshape(n * 8, 128).astype(jnp.bfloat16)
    cols = bproj.shape[1]
    bproj[...] = owned(dot(flat, expander(128, cols, wp)).reshape(n, 8, cols), wp)[:1]
    cols = bup.shape[1]
    bup[...] = owned(dot(flat, expander(128, cols, wu)).reshape(n, 8, cols), wu)[1:2]


def pack(v):
    r = v.shape[0] // 2
    return jnp.concatenate([v[:r], v[r:]], axis=1)


def unpack(v):
    c = v.shape[1] // 2
    return jnp.concatenate([v[:, :c], v[:, c:]], axis=0)


def tap_logits(mixed, wkx, bkx, logits, at=0):
    rows = pl.ds(at, mixed.shape[0])

    def tap(t, _):
        logits[t, rows] = dot(mixed, wkx[t]) + bkx[pl.ds(t, 1)]
        return 0

    lax.fori_loop(0, TAPS, tap, 0, unroll=True)


def softmax_taps(logits, rows):
    ls = [logits[t, rows] for t in range(TAPS)]
    top = ls[0]
    for v in ls[1:]:
        top = jnp.maximum(top, v)
    es = [jnp.exp(v - top) for v in ls]
    total = es[0]
    for v in es[1:]:
        total = total + v
    inv = 1.0 / total
    return [e * inv for e in es]


def expand_kernel_weights(w_kernel, b_kernel, wkx, bkx):
    cols = wkx.shape[2]
    wk, bk = w_kernel[...], b_kernel[...]
    for t in range(TAPS):
        k = wk.shape[0]
        pick = (iota((k, cols), 0) == iota((k, cols), 1) // HEAD * TAPS + t).astype(jnp.bfloat16)
        wkx[t] = dot_tn(wk, pick).astype(jnp.bfloat16)
        bkx[t : t + 1] = dot(bk, pick)


ROW = 16


def front_kernel(
    dp, seq, widths,
    x, wproj, wout, wup, wdown, small, w_kernel, b_kernel,
    gq0, gq1, gq2, gcp, gout, gup, gdown,
    h_qh, h_kh, h_vh, h_joined, h_qn, h_xe, h_convin, h_keyconv, h_mixed, h_spread, h_wkx,
    stats, vec, bup, bkx,
    qh, kh, vh, joined, qn, xe, convin, keyconv, mixed, spread, wkx,
    pq, pcp, gsmall, wq, wcp, xf, edges, inedge, qkv, abuf, csend, cbuf, logits, bproj,
    ssem, rsem, lsem, asend, arecv, bsend, brecv, esend, erecv, wsem, osem,
):
    f32, bf16 = jnp.float32, jnp.bfloat16
    grid = Grid(dp, seq)
    z, Z = grid.z, seq
    seqs, local, width = x.shape
    total = seqs * local

    greet(grid)
    outs = (
        (qh, h_qh), (kh, h_kh), (vh, h_vh), (joined, h_joined), (qn, h_qn), (xe, h_xe),
        (convin, h_convin), (keyconv, h_keyconv), (mixed, h_mixed), (spread, h_spread),
        (wkx, h_wkx),
    )
    ends = []

    def store(*refs):
        for i, (a, b) in enumerate(outs):
            if any(a is r for r in refs):
                cp = pltpu.make_async_copy(a, b, osem.at[i])
                cp.start()
                ends.append(cp)

    w = wproj[...].astype(f32)
    for j in range(HEADS_PER):
        cols = []
        for n in (j, HEADS_PER + j):
            for p in range(3):
                at = p * CHAN + n * HEAD
                cols.append(w[:, at : at + HEAD])
        pq[j] = jnp.concatenate(cols, axis=1).reshape(pq.shape[1:]).astype(bf16)
    pcp[...] = w[:, 3 * CHAN :].reshape(pcp.shape).astype(bf16)
    for s in range(seqs):
        edges[0, s] = x[s, :EDGE].astype(f32)
        edges[1, s] = x[s, local - EDGE :].astype(f32)

    expand_kernel_weights(w_kernel, b_kernel, wkx, bkx)
    store(wkx)
    meet(grid)
    mk = lambda i, src, buf, order: Gather(
        grid, src, buf, order, ssem.at[i], rsem.at[i], lsem.at[i]
    )
    gs = mk(0, small, gsmall, "zxyc")
    gq = [
        mk(1, pq.at[0], gq0, "zxyc"), mk(2, pq.at[1], gq1, "zyxc"), mk(3, pq.at[2], gq2, "zxyc")
    ]
    g2 = mk(4, pcp, gcp, "zyxc")
    g3 = mk(5, wout, gout, "zxyc")
    g4 = mk(6, wup, gup, "zyxc")
    g5 = mk(7, wdown, gdown, "zxyc")
    large = (g4, g5, g3)
    whole_q = [
        pltpu.make_async_copy(g.reshape((width, 2 * PART)), wq.at[j], wsem.at[j])
        for j, g in enumerate((gq0, gq1, gq2))
    ]
    whole_cp = pltpu.make_async_copy(gcp.reshape(wcp.shape), wcp, wsem.at[HEADS_PER])
    hops = [
        pltpu.make_async_remote_copy(
            src_ref=edges.at[i], dst_ref=inedge.at[i], send_sem=esend.at[i],
            recv_sem=erecv.at[i], device_id=grid.dev(z=o), device_id_type=MESH,
        )
        for i, o in ((0, seq - 1), (1, 1))
    ]
    sends = {}
    heads = {}

    def qkv_unit(j):
        gq[j].step4()
        whole_q[j].start()
        whole_q[j].wait()
        zero = jnp.zeros((1, HEAD), f32)
        cols = []
        for n in (j, HEADS_PER + j):
            at = n * HEAD
            cols += [bproj[:, at : at + HEAD], zero, bproj[:, CHAN + at : CHAN + at + HEAD]]
        qkv_bias = jnp.concatenate(cols, axis=1)
        for s in range(seqs):
            val = (dot(x[s], wq[j]) + qkv_bias).astype(bf16)
            for h in range(2):
                qkv[2 * s + h, j] = pack(val[:, h * PART : (h + 1) * PART])
                heads[s, h * HEADS_PER + j] = val[:, h * PART : h * PART + HEAD]
        for o in range(1, Z):
            to = (z + o) % Z
            cp = pltpu.make_async_remote_copy(
                src_ref=qkv.at[to, j], dst_ref=abuf.at[j, z], send_sem=asend.at[j, o - 1],
                recv_sem=arecv.at[j, o - 1], device_id=grid.dev(z=o), device_id_type=MESH,
            )
            cp.start()
            sends[j, o] = cp
        abuf[j, z] = qkv[z, j]

    def extend():
        for cp in hops:
            cp.wait_recv()
        for s in range(seqs):
            top = jnp.where(z > 0, inedge[1, s], 0.0)
            low = jnp.where(z < Z - 1, inedge[0, s], 0.0)
            xf[s, :EDGE] = top
            xf[s, EDGE : EDGE + local] = x[s].astype(f32)
            xf[s, EDGE + local :] = low
            xe[s] = xf[s].astype(bf16)
        spread_rows(xf, vec, spread, seqs, local)
        store(xe, spread)

    def conv_inputs():
        whole_cp.start()
        for s in range(seqs):
            qn[s * local : (s + 1) * local] = jnp.concatenate(
                [heads[s, n] for n in range(HEADS)], axis=1
            )
        store(qn)
        whole_cp.wait()
        bias = bproj[...]
        ext = local + 2 * EDGE
        at = iota((ext, 1), 0)
        inside = ((at >= EDGE) | (z > 0)) & ((at < EDGE + local) | (z < Z - 1))
        for s in range(seqs):
            val = dot(xe[s], wcp[:, :CHAN]) + bias[:, 2 * CHAN : 3 * CHAN]
            convin[s] = jnp.where(inside, val, 0.0)
        for s in range(seqs):
            rows = slice(s * local, (s + 1) * local)
            kc = dot(spread[rows], wcp[:, CHAN:]) + bias[:, 3 * CHAN :]
            keyconv[rows] = kc
            mixed[rows] = (kc * qn[rows].astype(f32)).astype(bf16)
        store(convin, keyconv, mixed)

    def conv_mix(s):
        tap_logits(mixed[s * local : (s + 1) * local], wkx, bkx, logits)

        def mix(i, _):
            r = pl.ds(pl.multiple_of(i * ROW, ROW), ROW)
            win = convin[s, pl.ds(pl.multiple_of(i * ROW, ROW), 2 * ROW)]
            tw = softmax_taps(logits, r)
            acc = jnp.zeros((ROW, CHAN), f32)
            for t in range(TAPS):
                a = EDGE - TAPS // 2 + t
                acc = acc + tw[t] * win[a : a + ROW]
            joined[pl.ds(pl.multiple_of(s * local + i * ROW, ROW), ROW), CHAN:] = acc.astype(bf16)
            return 0

        lax.fori_loop(0, local // ROW, mix, 0)

    returns = []

    def attention(j):
        for o in range(1, Z):
            sends[j, o].wait_recv()
        for b in range(Z):
            val = unpack(abuf[j, b])
            rows = slice(b * local, (b + 1) * local)
            for p, ref in enumerate((qh, kh, vh)):
                ref[j, rows] = val[:, p * HEAD : (p + 1) * HEAD]
        if j == HEADS_PER - 1:
            store(qh, kh, vh)
        returns.extend(attend_unit(grid, j, qh, kh, vh, stats, csend, cbuf, bsend, brecv))

    gs.start()
    for g in gq:
        g.start()
    g2.start()
    for cp in hops:
        cp.start()
    gs.step1()
    for g in gq:
        g.step1()
    g2.step1()
    for g in large:
        g.start()
    gs.step2()
    for g in gq:
        g.step2()
    g2.step2()
    gs.step3()
    for g in gq:
        g.step3()
    g2.step3()
    gs.step4()
    unpack_small(gsmall, vec, bproj, bup, widths)
    qkv_unit(0)
    qkv_unit(1)
    qkv_unit(2)
    for g in large:
        g.step1()
    extend()
    g2.step4()
    conv_inputs()
    conv_mix(0)
    attention(0)
    for g in large:
        g.step2()
    conv_mix(1)
    attention(1)
    for g in large:
        g.step3()
    attention(2)
    for g in large:
        g.step4()
    for cp in returns:
        cp.wait_recv()
    for s in range(seqs):
        pieces = []
        for n in range(HEADS):
            v = cbuf[n % HEADS_PER, 2 * s + n // HEADS_PER]
            pieces.append(unpack(unpack(v)))
        joined[s * local : (s + 1) * local, :CHAN] = jnp.concatenate(pieces, axis=1)
    store(joined)
    for cp in list(sends.values()) + returns + hops:
        cp.wait_send()
    for g in [gs] + gq + [g2, g3, g4, g5]:
        g.finish()
    for cp in ends:
        cp.wait()


def spread_rows(xf, vec, spread, seqs, local):
    width = xf.shape[2]
    step = 256

    def body(i, _):
        for s in range(seqs):
            for c in range(width // step):
                cols = slice(c * step, (c + 1) * step)
                win = xf[s, pl.ds(pl.multiple_of(i * ROW, ROW), 2 * ROW), cols]
                acc = jnp.zeros((ROW, step), jnp.float32)
                for t in range(TAPS):
                    a = EDGE - TAPS // 2 + t
                    acc = acc + win[a : a + ROW] * vec[t : t + 1, cols]
                r = pl.ds(pl.multiple_of(s * local + i * ROW, ROW), ROW)
                spread[r, cols] = acc.astype(spread.dtype)
        return 0

    lax.fori_loop(0, local // ROW, body, 0)


def attend_unit(grid, h, qh, kh, vh, stats, csend, cbuf, bsend, brecv):
    f32, bf16 = jnp.float32, jnp.bfloat16
    z, Z = grid.z, grid.Z
    local = qh.shape[1] // Z
    sends = []
    scale = jnp.asarray(HEAD ** (-0.5), bf16)
    keys = kh[h]
    vt = vh[h].T
    def send(i):
        return pltpu.make_async_remote_copy(
            src_ref=csend.at[h, i], dst_ref=cbuf.at[h, z], send_sem=bsend.at[h, i],
            recv_sem=brecv.at[h, i], device_id=(grid.dp, (z + i + 1) % Z), device_id_type=MESH,
        )

    def block(i, _):
        b = (z + i + 1) % Z
        rows = pl.ds(pl.multiple_of(b * local, local), local)
        st = dot_nt(keys, qh[h, rows] * scale)
        top = jnp.max(st, axis=0, keepdims=True)
        e = jnp.exp(st - top)
        den = jnp.sum(e, axis=0, keepdims=True)
        stats[h, b] = top + jnp.log(den)
        ct = dot(vt, e.astype(bf16)) / den
        csend[h, i] = pack(pack(ct.T.astype(bf16)))

        @pl.when(i < Z - 1)
        def _():
            send(i).start()

        return 0

    lax.fori_loop(0, Z, block, 0)
    cbuf[h, z] = csend[h, Z - 1]
    return [send(i) for i in range(Z - 1)]


def front(dp, seq, x, w_proj, w_out, w_up, w_down, small, w_kernel, b_kernel, widths):
    f32, bf16 = jnp.float32, jnp.bfloat16
    seqs, local, width = x.shape
    total = seqs * local
    length = seq * local
    N = dp * seq
    rows = w_proj.shape[0]
    lead = tiled(w_proj).shape[:2]
    place = mesh_lead(dp, seq)
    shape = jax.ShapeDtypeStruct
    wide = 6 * PART
    ext = local + 2 * EDGE
    vm = pl.BlockSpec(memory_space=pltpu.VMEM)
    hb = pl.BlockSpec(memory_space=pl.ANY)
    other = [tiled(a) for a in (w_out, w_up, w_down)]
    hbm_out = [
        shape(place + lead + (c,), bf16) for c in (2 * PART,) * HEADS_PER + (2 * CHAN,)
    ]
    hbm_out += [shape(place + a.shape, bf16) for a in other]
    big_out = [
        shape((HEADS_PER, length, HEAD), bf16),
        shape((HEADS_PER, length, HEAD), bf16),
        shape((HEADS_PER, length, HEAD), bf16),
        shape((total, width), bf16),
        shape((total, CHAN), bf16),
        shape((seqs, ext, width), bf16),
        shape((seqs, ext, CHAN), f32),
        shape((total, CHAN), f32),
        shape((total, CHAN), bf16),
        shape((total, width), bf16),
        shape((TAPS, CHAN, CHAN), bf16),
    ]
    vm_out = [
        shape((HEADS_PER, seq, 1, local), f32),
        shape((16, width), f32),
        shape((1, FF), f32),
        shape((16, CHAN), f32),
    ]
    hbm_out += big_out
    sem = lambda *s: pltpu.SemaphoreType.DMA(s)
    return pl.pallas_call(
        partial(front_kernel, dp, seq, widths),
        out_shape=hbm_out + vm_out,
        in_specs=[vm] * 8,
        out_specs=[hb] * len(hbm_out) + [vm] * len(vm_out),
        scratch_shapes=[pltpu.VMEM(o.shape, o.dtype) for o in big_out]
        + [
            pltpu.VMEM((HEADS_PER,) + lead + (2 * PART,), bf16),
            pltpu.VMEM(lead + (2 * CHAN,), bf16),
            pltpu.VMEM(place + small.shape, f32),
            pltpu.VMEM((HEADS_PER, width, 2 * PART), bf16),
            pltpu.VMEM((width, 2 * CHAN), bf16),
            pltpu.VMEM((seqs, ext, width), f32),
            pltpu.VMEM((2, seqs, EDGE, width), f32),
            pltpu.VMEM((2, seqs, EDGE, width), f32),
            pltpu.VMEM((seq, HEADS_PER, local // 2, 2 * PART), bf16),
            pltpu.VMEM((HEADS_PER, seq, local // 2, 2 * PART), bf16),
            pltpu.VMEM((HEADS_PER, seq, local // 4, 4 * HEAD), bf16),
            pltpu.VMEM((HEADS_PER, seq, local // 4, 4 * HEAD), bf16),
            pltpu.VMEM((TAPS, local, CHAN), f32),
            pltpu.VMEM((1, 4 * CHAN), f32),
            sem(8), sem(8, 4), sem(8),
            sem(HEADS_PER, seq - 1), sem(HEADS_PER, seq - 1),
            sem(HEADS_PER, seq - 1), sem(HEADS_PER, seq - 1), sem(2), sem(2), sem(HEADS_PER + 1),
            sem(len(big_out)),
        ],
        compiler_params=pltpu.CompilerParams(
            collective_id=2, has_side_effects=True, vmem_limit_bytes=VMEM_CAP
        ),
        name="front",
    )(x, w_proj, *other, small, w_kernel, b_kernel)


def pack_small(w_depth, vectors, b_proj, b_up):
    rows = [(i, v) for i, v in enumerate([w_depth[:, t] for t in range(TAPS)] + list(vectors))]
    rows += [(16, b_proj), (17, b_up)]
    out = jnp.zeros((24, 128), jnp.float32)
    for i, v in rows:
        out = out + jnp.pad(v.astype(jnp.float32)[None], ((i, 23 - i), (0, 128 - v.shape[0])))
    return out.reshape(3, 8, 128)


def unhalve(w):
    w = w.reshape(w.shape[:-1] + (2, 3, PART))
    return jnp.swapaxes(w, -3, -2).reshape(w.shape[:-3] + (3 * CHAN,))


PAD = 16


def dot_pick(v, picks):
    bf16 = jnp.bfloat16
    hi = v.astype(bf16)
    rest = v - hi.astype(jnp.float32)
    mid = rest.astype(bf16)
    lo = (rest - mid.astype(jnp.float32)).astype(bf16)
    return dot_nt(hi, picks) + dot_nt(mid, picks) + dot_nt(lo, picks)


def to_owners(v, width, n):
    r, cols = v.shape
    picks = expander(128, cols, width)
    if r == 1:
        keep = iota((n, cols), 1) // width == iota((n, cols), 0)
        return dot_pick(jnp.where(keep, v, 0.0), picks)
    keep = iota((n, r, cols), 2) // width == iota((n, r, cols), 0)
    stack = jnp.where(keep, v[None], 0.0).reshape(n * r, cols)
    return dot_pick(stack, picks).reshape(n, r, 128)


def conv_back(
    s, local, gmix, convin, keyconv, mixed, qn, wkx, bkx, wkp, wpt,
    tw, gt, gl, gpad, gsp, gqm, gk, gci_ext, gwk, gbk, gbpoint,
):
    f32, bf16 = jnp.float32, jnp.bfloat16
    rows = slice(s * local, (s + 1) * local)
    body_rows = slice(PAD, PAD + local)
    tap_logits(mixed[rows], wkx, bkx, tw, PAD)
    gpad[body_rows] = gmix[rows]
    same = (iota((CHAN, CHAN), 0) // HEAD == iota((CHAN, CHAN), 1) // HEAD).astype(bf16)
    for t in range(TAPS):
        a = EDGE - TAPS // 2 + t
        p = gmix[rows] * convin[s, a : a + local]
        hi = p.astype(bf16)
        lo = (p - hi.astype(f32)).astype(bf16)
        gt[t] = dot(hi, same) + dot(lo, same)

    def taps(i, _):
        r = pl.ds(pl.multiple_of(i * ROW, ROW), ROW)
        rp = pl.ds(pl.multiple_of(PAD + i * ROW, ROW), ROW)
        ws = softmax_taps(tw, rp)
        gs = [gt[t, r] for t in range(TAPS)]
        mean = ws[0] * gs[0]
        for t in range(1, TAPS):
            mean = mean + ws[t] * gs[t]
        for t in range(TAPS):
            tw[t, rp] = ws[t]
            g = ws[t] * (gs[t] - mean)
            gl[t, r] = g.astype(bf16)
            gbk[t] += g[:8] + g[8:]
        return 0

    lax.fori_loop(0, local // ROW, taps, 0)

    def spread_back(i, _):
        w = pl.ds(pl.multiple_of(i * ROW, ROW), 2 * ROW)
        g = gpad[w]
        acc = jnp.zeros((ROW, CHAN), f32)
        for t in range(TAPS):
            a = PAD - TAPS // 2 - t
            acc = acc + (tw[t, w] * g)[a : a + ROW]
        gci_ext[s, pl.ds(pl.multiple_of(i * ROW, ROW), ROW)] = acc
        return 0

    lax.fori_loop(0, (local + 2 * EDGE) // ROW, spread_back, 0)
    compact = jnp.zeros((local, 128), f32)
    for t in range(TAPS):
        pick = (
            (iota((CHAN, 128), 0) == iota((CHAN, 128), 1) // TAPS * HEAD)
            & (iota((CHAN, 128), 1) % TAPS == t)
            & (iota((CHAN, 128), 1) < HEADS * TAPS)
        ).astype(bf16)
        compact = compact + dot(gl[t], pick)
    low = compact.astype(bf16)
    gwk[...] += dot_tn(low, mixed[rows])
    gmixed = dot(low, wkp[...])
    gqm[rows] = gmixed * keyconv[rows]
    gkc = gmixed * qn[rows].astype(f32)
    gbpoint[...] += rows_sum(gkc)
    glow = gkc.astype(bf16)
    gk[rows] = glow
    gsp[s, body_rows] = dot_nt(glow, wpt)


def depth_back(local, seqs, gsp, xe, vec, gdx_ext, gwd):
    f32 = jnp.float32
    width = gsp.shape[2]
    step = 256

    def grads(i, _):
        w = pl.ds(pl.multiple_of(i * ROW, ROW), 2 * ROW)
        for s in range(seqs):
            for c in range(width // step):
                cols = slice(c * step, (c + 1) * step)
                g = gsp[s, w, cols]
                acc = jnp.zeros((ROW, step), f32)
                for t in range(TAPS):
                    a = PAD - TAPS // 2 - t
                    acc = acc + g[a : a + ROW] * vec[t : t + 1, cols]
                gdx_ext[s, pl.ds(pl.multiple_of(i * ROW, ROW), ROW), cols] = acc
        return 0

    lax.fori_loop(0, (local + 2 * EDGE) // ROW, grads, 0)

    def weights(i, _):
        w = pl.ds(pl.multiple_of(i * ROW, ROW), 2 * ROW)
        for s in range(seqs):
            for c in range(width // step):
                cols = slice(c * step, (c + 1) * step)
                win = xe[s, w, cols].astype(f32)
                g = gsp[s, pl.ds(pl.multiple_of(PAD + i * ROW, ROW), ROW), cols]
                for t in range(TAPS):
                    a = EDGE - TAPS // 2 + t
                    p = win[a : a + ROW] * g
                    gwd[t, :, cols] += p[:8] + p[8:]
        return 0

    lax.fori_loop(0, local // ROW, weights, 0)


def attend_back_block(b, h, keys, vals, kt, qh, stats, dbuf, dkv, local):
    f32, bf16 = jnp.float32, jnp.bfloat16
    scale = HEAD ** (-0.5)
    rows = pl.ds(pl.multiple_of(b * local, local), local)
    q = qh[h, rows]
    do = unpack(dbuf[b])[:, h * HEAD : (h + 1) * HEAD]
    st = dot_nt(keys, q * jnp.asarray(scale, bf16))
    p = jnp.exp(st - stats[h, b])
    dp = dot_nt(vals, do)
    delta = jnp.sum(p * dp, axis=0, keepdims=True)
    ds = (p * (dp - delta)).astype(bf16)
    dk = dot(ds, q)
    dv = dot(p.astype(bf16), do)
    dkv[0] += dk
    dkv[1] += dv
    return (dot(kt, ds) * scale).T


def back_kernel(
    dp, seq, widths,
    dctx, stats, vec, bkx, w_kernel, vecg, gbup,
    h_gmix, h_convin, h_keyconv, h_mixed, h_qn, h_wkx, h_qh, h_kh, h_vh, h_spread, h_xe,
    gafter, gq0, gq1, gq2, gcp, gwdown, gwup, gwout,
    h_gx, o_proj, o_out, o_up, o_down, o_small, o_kernel,
    gmix, convin, keyconv, mixed, qn, wkx, qh, kh, vh, spread, xe, gx, xt,
    *rest,
):
    f32, bf16 = jnp.float32, jnp.bfloat16
    pieces = 9
    parts, rest = rest[:pieces], rest[pieces:]
    bufs, rest = rest[: 4 * pieces], rest[4 * pieces :]
    souts, rest = rest[:5], rest[5:]
    souts = (o_down, o_up, o_out) + souts + (o_small,)
    (
        dbuf, dsend, gsend, grecv, wq, wcp, grads, tw, gt, gl, gpad, gsp, gqm, gk, gci_ext, gcl,
        gdx_ext, gwd, gwk, gbk, gbpoint, wkp, hsend, hrecv, dqb, dkv, kall, bprow,
        ssem, rsem, gssem, grsem, lsem, asend, arecv, bsend, brecv, esend, erecv, wsem,
    ) = rest
    grid = Grid(dp, seq)
    z, Z = grid.z, seq
    N = dp * seq
    seqs = xe.shape[0]
    total = dctx.shape[0]
    local = total // seqs
    width = xe.shape[2]
    w1, wp, wu = widths

    loads = [
        pltpu.make_async_copy(src, dst, wsem.at[i])
        for i, (src, dst) in enumerate(
            (
                (gwdown, parts[0]), (gwup, parts[1]), (gwout, parts[2]),
                (gcp.reshape(wcp.shape), wcp),
                (gafter, gx),
                (gq0.reshape((width, 2 * PART)), wq.at[0]),
                (gq1.reshape((width, 2 * PART)), wq.at[1]),
                (gq2.reshape((width, 2 * PART)), wq.at[2]),
            )
        )
    ]
    greet(grid)
    ins = [
        pltpu.make_async_copy(src, dst, wsem.at[8 + i])
        for i, (src, dst) in enumerate(
            (
                (h_gmix, gmix), (h_convin, convin), (h_keyconv, keyconv), (h_mixed, mixed),
                (h_qn, qn), (h_wkx, wkx), (h_qh, qh), (h_kh, kh), (h_vh, vh), (h_spread, spread),
                (h_xe, xe),
            )
        )
    ]
    for cp in loads[:3] + ins + loads[3:]:
        cp.start()
    for s in range(seqs):
        for h in range(2):
            dsend[2 * s + h] = pack(
                dctx[s * local : (s + 1) * local, h * PART : (h + 1) * PART]
            )
    wk = w_kernel[...]
    wkp[...] = dot(
        (iota((128, wk.shape[0]), 0) == iota((128, wk.shape[0]), 1)).astype(bf16), wk
    ).astype(bf16)
    gwk[...] = jnp.zeros_like(gwk)
    gbk[...] = jnp.zeros_like(gbk)
    gwd[...] = jnp.zeros_like(gwd)
    gbpoint[...] = jnp.zeros_like(gbpoint)
    gpad[...] = jnp.zeros_like(gpad)
    zeros = jnp.zeros((PAD, CHAN), f32)
    for t in range(TAPS):
        tw[t, :PAD] = zeros
        tw[t, PAD + local :] = zeros
    zeros = jnp.zeros((PAD, width), f32)
    for s in range(seqs):
        gsp[s, :PAD] = zeros
        gsp[s, PAD + local :] = zeros
    parts[8][...] = jnp.zeros_like(parts[8])
    parts[8][:, :, :, :, 2, 1:2] = to_owners(gbup[...], wu, N).reshape(parts[8].shape[:4] + (1, 128))
    meet(grid)
    sends = []
    for o in range(1, Z):
        to = (z + o) % Z
        cp = pltpu.make_async_remote_copy(
            src_ref=dsend.at[to], dst_ref=dbuf.at[z], send_sem=bsend.at[o - 1],
            recv_sem=brecv.at[o - 1], device_id=grid.dev(z=o), device_id_type=MESH,
        )
        cp.start()
        sends.append(cp)
    dbuf[z] = dsend[z]
    orders = ("zxyc", "zyxc", "zxyc", "zyxc", "zxyc", "zyxc", "zxyc", "zxyc", "zyxc")
    sc = [
        Scatter(
            grid, parts[i], orders[i], bufs[4 * i : 4 * i + 4], souts[i], ssem.at[i], rsem.at[i]
        )
        for i in range(pieces)
    ]
    sdown, sup, sout, scp, sq0, sq1, sq2, skern, svec = sc
    for i in range(3):
        loads[i].wait()
        sc[i].start()

    for cp in ins[:6]:
        cp.wait()
    loads[3].wait()
    wpt = wcp[:, CHAN:]

    def conv(s):
        conv_back(
            s, local, gmix, convin, keyconv, mixed, qn, wkx, bkx, wkp, wpt,
            tw, gt, gl, gpad, gsp, gqm, gk, gci_ext, gwk, gbk, gbpoint,
        )

    for s in range(seqs - 1):
        conv(s)
    sdown.step1()
    sup.step1()
    sout.step1()

    scale = HEAD ** (-0.5)
    back = []
    for cp in ins[6:]:
        cp.wait()
    for s in range(seqs):
        xt[:, s * local : (s + 1) * local] = xe[s, EDGE : EDGE + local].T
    for cp in sends:
        cp.wait_recv()
    for h in range(HEADS_PER):
        keys, vals = kh[h], vh[h]
        kt = keys.T
        dkv[...] = jnp.zeros_like(dkv)

        def block(o, _, h=h, keys=keys, vals=vals, kt=kt):
            b = (z + Z - o) % Z
            dqb[b] = attend_back_block(
                b, h, keys, vals, kt, qh, stats, dbuf, dkv, local
            ).astype(bf16)
            return 0

        lax.fori_loop(0, Z, block, 0, unroll=2)
        for o in list(range(1, Z)) + [0]:
            b = (z + o) % Z
            r = pl.ds(pl.multiple_of(b * local, local), local)
            val = pack(
                jnp.concatenate(
                    [dqb[b], (dkv[0, r] * scale).astype(bf16), dkv[1, r].astype(bf16)], axis=1
                )
            )
            if o:
                gsend[h, o - 1] = val
                cp = pltpu.make_async_remote_copy(
                    src_ref=gsend.at[h, o - 1], dst_ref=grecv.at[h, z],
                    send_sem=asend.at[h, o - 1], recv_sem=arecv.at[h, o - 1],
                    device_id=grid.dev(z=o), device_id_type=MESH,
                )
                cp.start()
                back.append(cp)
            else:
                grecv[h, z] = val

    conv(seqs - 1)
    sdown.step2()
    sup.step2()
    sout.step2()
    depth_back(local, seqs, gsp, xe, vec, gdx_ext, gwd)
    for i, at in ((0, 0), (1, EDGE + local)):
        for s in range(seqs):
            hsend[i, s, :, :CHAN] = gci_ext[s, at : at + EDGE]
            hsend[i, s, :, CHAN:] = gdx_ext[s, at : at + EDGE]
    hops = []
    for i, o in ((0, seq - 1), (1, 1)):
        cp = pltpu.make_async_remote_copy(
            src_ref=hsend.at[i], dst_ref=hrecv.at[i], send_sem=esend.at[i],
            recv_sem=erecv.at[i], device_id=grid.dev(z=o), device_id_type=MESH,
        )
        cp.start()
        hops.append(cp)
    gw = dot_tn(spread[...], gk[...])
    gate = lambda v: v.reshape(parts[3].shape[:-1] + (CHAN,)).astype(bf16)
    parts[3][..., CHAN:] = gate(gw)
    bias_row = jnp.zeros((1, 128), f32)
    for t in range(TAPS):
        pick = (
            (iota((128, CHAN), 1) == iota((128, CHAN), 0) // TAPS * HEAD)
            & (iota((128, CHAN), 0) % TAPS == t)
            & (iota((128, CHAN), 0) < HEADS * TAPS)
        ).astype(bf16)
        bias_row = bias_row + dot_pick(rows_sum(gbk[t]), pick)
    tiles = []
    for c in range(CHAN // 128):
        tile = gwk[:TALL, c * 128 : (c + 1) * 128]
        if c == 0:
            tile = jnp.where(iota((TALL, 128), 0) == HEADS * TAPS, bias_row, tile)
        tiles.append(tile.reshape(TALL // 8, 8, 128))
    count = CHAN // 128 * TALL // 8
    tiles.append(jnp.zeros((N - count, 8, 128), f32))
    parts[7][...] = jnp.concatenate(tiles, axis=0).reshape(parts[7].shape)
    skern.start()
    qsum, vsum = {}, {}

    def gather_grads(j):
        for o in range(1, Z):
            back[j * (Z - 1) + o - 1].wait_recv()
        for s in range(seqs):
            r = slice(s * local, (s + 1) * local)
            vals = []
            for h in range(2):
                n = h * HEADS_PER + j
                val = unpack(grecv[j, 2 * s + h])
                q = (val[:, :HEAD].astype(f32) + gqm[r, n * HEAD : (n + 1) * HEAD]).astype(bf16)
                qsum[n] = qsum.get(n, 0.0) + rows_sum(q.astype(f32))
                vsum[n] = vsum.get(n, 0.0) + rows_sum(val[:, 2 * HEAD :].astype(f32))
                vals += [q, val[:, HEAD:]]
            low = jnp.concatenate(vals, axis=1)
            grads[j, r] = low
        gw = dot(xt[...], grads[j])
        parts[4 + j][...] = gw.reshape(parts[4 + j].shape).astype(bf16)
        sc[4 + j].start()

    gather_grads(0)

    for cp in hops:
        cp.wait_recv()
    gbconv = jnp.zeros((1, CHAN), f32)
    for s in range(seqs):
        for i, at, ok in ((0, local, z < Z - 1), (1, EDGE, z > 0)):
            add = jnp.where(ok, hrecv[i, s], 0.0)
            gci_ext[s, at : at + EDGE] += add[:, :CHAN]
            gdx_ext[s, at : at + EDGE] += add[:, CHAN:]
        own = gci_ext[s, EDGE : EDGE + local]
        gbconv = gbconv + rows_sum(own)
        gcl[s * local : (s + 1) * local] = own.astype(bf16)
    gw = dot(xt[...], gcl[...])
    parts[3][..., :CHAN] = gate(gw)
    scp.start()
    skern.step1()
    sq0.step1()
    loads[4].wait()
    for s in range(seqs):
        r = slice(s * local, (s + 1) * local)
        gx[r] += gdx_ext[s, EDGE : EDGE + local] + dot_nt(gcl[r], wcp[:, :CHAN])
    gather_grads(1)
    sdown.step3()
    sup.step3()
    sout.step3()
    scp.step1()
    skern.step2()
    sq0.step2()
    taps = jnp.concatenate([rows_sum(gwd[t]) for t in range(TAPS)], axis=0)
    head = jnp.concatenate([taps, vecg[TAPS:16]], axis=0)
    own = to_owners(head, w1, N)
    place = parts[8].shape[:4]
    parts[8][:, :, :, :, 0] = own[:, :8].reshape(place + (8, 128))
    parts[8][:, :, :, :, 1] = own[:, 8:].reshape(place + (8, 128))
    sq1.step1()
    scp.step2()
    gather_grads(2)
    bprow[...] = jnp.concatenate(
        [qsum[n] for n in range(HEADS)] + [vsum[n] for n in range(HEADS)] + [gbconv, gbpoint[...]],
        axis=1,
    )
    own = to_owners(bprow[...], wp, N)
    parts[8][:, :, :, :, 2, 0:1] = own.reshape(place + (1, 128))
    svec.start()
    skern.step3()
    sq0.step3()
    sq1.step2()
    sq2.step1()
    svec.step1()
    skern.step4()
    gk_tail = Gather(grid, souts[7], kall, "zxyc", gssem, grsem, lsem)
    gk_tail.start()
    scp.step3()
    for i in range(HEADS_PER):
        loads[5 + i].wait()
    for s in range(seqs):
        r = slice(s * local, (s + 1) * local)
        acc = gx[r]
        for j in range(HEADS_PER):
            acc = acc + dot_nt(grads[j, r], wq[j])
        gx[r] = acc
    last = pltpu.make_async_copy(gx, h_gx, wsem.at[19])
    last.start()
    sq1.step3()
    sq2.step2()
    svec.step2()
    gk_tail.step1()
    sdown.step4()
    sup.step4()
    sout.step4()
    sq2.step3()
    svec.step3()
    gk_tail.step2()
    scp.step4()
    sq0.step4()
    sq1.step4()
    gk_tail.step3()
    gk_tail.step4()
    n = TALL // 8
    every = kall[...].reshape(N, 8, 128)
    o_kernel[...] = jnp.concatenate(
        [every[c * n : (c + 1) * n].reshape(TALL, 128) for c in range(CHAN // 128)], axis=1
    )
    sq2.step4()
    svec.step4()
    flat = [souts[4 + j][...].reshape(w1, 2 * PART) for j in range(HEADS_PER)]
    cols = []
    for p in range(3):
        for n in range(HEADS):
            at = n // HEADS_PER * PART + p * HEAD
            cols.append(flat[n % HEADS_PER][:, at : at + HEAD])
    o_proj[:, : 3 * CHAN] = jnp.concatenate(cols, axis=1)
    o_proj[:, 3 * CHAN :] = souts[3][...].reshape(w1, 2 * CHAN)
    for cp in sends + back + hops:
        cp.wait_send()
    for g in sc:
        g.finish()
    gk_tail.finish()
    last.wait()


TALL = -(-(HEADS * TAPS + 1) // 8) * 8


def back(dp, seq, widths, values, streamed, gathered, wgrads, shards):
    f32, bf16 = jnp.float32, jnp.bfloat16
    dctx = values[0]
    qh, xe = streamed[6], streamed[10]
    N = dp * seq
    w1, wp, wu = widths
    seqs, ext, width = xe.shape
    total = dctx.shape[0]
    local = total // seqs
    length = qh.shape[1]
    sizes = sizes_of(dp, seq)
    shape = jax.ShapeDtypeStruct
    vm = pl.BlockSpec(memory_space=pltpu.VMEM)
    hb = pl.BlockSpec(memory_space=pl.ANY)
    t_down, t_up, t_out = [tiled(a).shape for a in shards]
    lead = t_out[:2]
    piece = [
        (t_down, bf16), (t_up, bf16), (t_out, bf16), (lead + (2 * CHAN,), bf16),
    ]
    piece += [(lead + (2 * PART,), bf16)] * HEADS_PER
    piece += [((1, 8, 128), f32), ((3, 8, 128), f32)]
    place = mesh_lead(dp, seq)
    wgrads = [g.reshape(place + p[0]) for g, p in zip(wgrads, piece)]
    scratch = [pltpu.VMEM(a.shape, a.dtype) for a in streamed]
    scratch += [pltpu.VMEM((total, width), f32), pltpu.VMEM((width, total), bf16)]
    scratch += [pltpu.VMEM(place + p, d) for p, d in piece]
    for p, d in piece:
        scratch += scatter_scratch(sizes, p, d, "zxyc")
    scratch += [pltpu.VMEM(p, f32) for p, d in piece[3:8]]
    V = pltpu.VMEM
    scratch += [
        V((seq, local // 2, 2 * PART), bf16),
        V((seq, local // 2, 2 * PART), bf16),
        V((HEADS_PER, seq - 1, local // 2, 2 * PART), bf16),
        V((HEADS_PER, seq, local // 2, 2 * PART), bf16),
        V((HEADS_PER, width, 2 * PART), bf16),
        V((width, 2 * CHAN), bf16),
        V((HEADS_PER, total, 2 * PART), bf16),
        V((TAPS, local + 2 * PAD, CHAN), f32),
        V((TAPS, local, CHAN), f32),
        V((TAPS, local, CHAN), bf16),
        V((local + 2 * PAD, CHAN), f32),
        V((seqs, local + 2 * PAD, width), f32),
        V((total, CHAN), f32),
        V((total, CHAN), bf16),
        V((seqs, ext, CHAN), f32),
        V((total, CHAN), bf16),
        V((seqs, ext, width), f32),
        V((TAPS, 8, width), f32),
        V((128, CHAN), f32),
        V((TAPS, 8, CHAN), f32),
        V((1, CHAN), f32),
        V((128, CHAN), bf16),
        V((2, seqs, EDGE, CHAN + width), f32),
        V((2, seqs, EDGE, CHAN + width), f32),
        V((seq, local, HEAD), bf16),
        V((2, length, HEAD), f32),
        V(place + (1, 8, 128), f32),
        V((1, 4 * CHAN), f32),
    ]
    sem = lambda *s: pltpu.SemaphoreType.DMA(s)
    n = len(piece)
    scratch += [
        sem(n), sem(n, 4), sem(), sem(4), sem(),
        sem(HEADS_PER, seq - 1), sem(HEADS_PER, seq - 1), sem(seq - 1), sem(seq - 1),
        sem(2), sem(2), sem(20),
    ]
    outs = [
        shape((total, width), f32),
        shape((w1, 5 * CHAN), f32),
        shape(t_out, f32),
        shape(t_up, f32),
        shape(t_down, f32),
        shape((3, 8, 128), f32),
        shape((TALL, CHAN), f32),
    ]
    return pl.pallas_call(
        partial(back_kernel, dp, seq, widths),
        out_shape=outs,
        in_specs=[vm] * len(values) + [hb] * (8 + len(streamed)),
        out_specs=[hb] + [vm] * (len(outs) - 1),
        scratch_shapes=scratch,
        compiler_params=pltpu.CompilerParams(
            collective_id=3, has_side_effects=True, vmem_limit_bytes=63 << 20
        ),
        name="back",
    )(*values, *streamed, *gathered, *wgrads)


def finish_kernel(gx, proj, out, up, down, small, kern, *rest):
    outs, held, sem = rest[:-6], rest[-6:-1], rest[-1]
    copies = [
        pltpu.make_async_copy(a, b, sem.at[0, i])
        for i, (a, b) in enumerate(zip((gx, proj, out, up, down), held))
    ]
    for cp in copies:
        cp.start()
    stores = [
        pltpu.make_async_copy(a, b, sem.at[1, i])
        for i, (a, b) in enumerate(zip(held, outs[:5]))
    ]
    for a, b in zip(copies, stores):
        a.wait()
        b.start()
    depth, kernel_t, bkernel, bproj, bup = outs[5:10]
    s = small[...]
    depth[...] = s[:2].reshape(16, 128)[: depth.shape[0], : depth.shape[1]]
    kernel_t[...] = kern[: kernel_t.shape[0]]
    bkernel[...] = kern[HEADS * TAPS : HEADS * TAPS + 1, : HEADS * TAPS]
    bproj[...] = s[2, 0:1, : bproj.shape[1]]
    bup[...] = s[2, 1:2, : bup.shape[1]]
    for i, v in zip(range(V_BOUT, V_S2 + 1), outs[10:]):
        v[...] = s[i // 8, i % 8 : i % 8 + 1, : v.shape[1]]
    for cp in stores:
        cp.wait()


def finish(widths, arrays):
    f32 = jnp.float32
    w1, wp, wu = widths
    shape = jax.ShapeDtypeStruct
    vm = pl.BlockSpec(memory_space=pltpu.VMEM)
    hb = pl.BlockSpec(memory_space=pl.ANY)
    outs = [shape(a.shape, f32) for a in arrays[:5]]
    outs += [
        shape((TAPS, w1), f32), shape((HEADS * TAPS, CHAN), f32), shape((1, HEADS * TAPS), f32),
        shape((1, wp), f32), shape((1, wu), f32),
    ]
    outs += [shape((1, w1), f32)] * 6
    return pl.pallas_call(
        finish_kernel,
        out_shape=outs,
        in_specs=[hb] * 5 + [vm] * 2,
        out_specs=[hb] * 5 + [vm] * 11,
        scratch_shapes=[pltpu.VMEM(a.shape, f32) for a in arrays[:5]]
        + [pltpu.SemaphoreType.DMA((2, 5))],
        name="finish",
    )(*arrays)


def fast_body(
    hidden, cotangent, w_proj, w_depth, w_kernel, b_kernel, w_out, w_up, w_down, b_proj, b_up,
    b_out, ln1_gain, ln1_bias, b_down, ln2_gain, ln2_bias,
):
    dp, seq = lax.axis_size("dp"), lax.axis_size("seq")
    seqs, local, width = hidden.shape
    total = seqs * local
    widths = (w_out.shape[0], b_proj.shape[0], b_up.shape[0])
    small = pack_small(
        w_depth, (b_out, ln1_gain, ln1_bias, b_down, ln2_gain, ln2_bias), b_proj, b_up
    )
    w_kernel = w_kernel.T
    (
        gq0, gq1, gq2, gcp, gout, gup, gdown, qh, kh, vh, joined, qn, xe, convin, keyconv, mixed,
        spread, wkx, stats, vec, bup, bkx,
    ) = front(
        dp, seq, hidden, w_proj, w_out, w_up, w_down, small, w_kernel, b_kernel[None], widths
    )
    out, gafter, dctx, gmix, gwout, gwup, gwdown, vecg, gbup = ffn(
        joined, hidden.reshape(total, width), cotangent.reshape(total, width),
        gout.reshape(-1, w_out.shape[1]), gup.reshape(-1, w_up.shape[1]),
        gdown.reshape(-1, w_down.shape[1]), vec, bup,
    )
    res = back(
        dp, seq, widths,
        (dctx, stats, vec, bkx, w_kernel, vecg, gbup),
        (gmix, convin, keyconv, mixed, qn, wkx, qh, kh, vh, spread, xe),
        (gafter, gq0, gq1, gq2, gcp), (gwdown, gwup, gwout), (w_down, w_up, w_out),
    )
    (
        gx, g_proj, g_out, g_up, g_down, g_depth, g_kernel, g_bkernel, g_bproj, g_bup, *g_vecs,
    ) = finish(widths, res)
    return (
        out.reshape(hidden.shape),
        gx.reshape(hidden.shape),
        g_proj,
        g_depth.T,
        g_kernel.T,
        g_bkernel[0],
        g_out.reshape(w_out.shape),
        g_up.reshape(w_up.shape),
        g_down.reshape(w_down.shape),
        g_bproj[0],
        g_bup[0],
    ) + tuple(v[0] for v in g_vecs)


def fits(mesh):
    return mesh.shape["seq"] == 4 and mesh.shape["dp"] == 8


def body(
    hidden,
    cotangent,
    w_proj,
    w_depth,
    w_kernel,
    b_kernel,
    w_out,
    w_up,
    w_down,
    b_proj,
    b_up,
    b_out,
    ln1_gain,
    ln1_bias,
    b_down,
    ln2_gain,
    ln2_bias,
):
    seq_count, local_rows, model_width = hidden.shape
    total_rows = seq_count * local_rows
    head_count = HEADS
    head_size = HEAD
    all_width = head_count * head_size
    tap_count = KERNEL
    half_kernel = KERNEL // 2
    group_count = GROUPS
    hidden_units = FF
    ext_rows = local_rows + 2 * half_kernel
    score_scale = head_size ** (-0.5)
    dp, seq = lax.axis_size("dp"), lax.axis_size("seq")
    devices = dp * seq
    vectors = (b_proj, b_up, b_out, ln1_gain, ln1_bias, b_down, ln2_gain, ln2_bias)
    widths = [w_depth.shape[0] * KERNEL] + [v.shape[0] for v in vectors]
    small = jnp.concatenate([w_depth.reshape(-1)] + list(vectors))
    small = jnp.pad(small, (0, 1024 - small.shape[0])).reshape(8, 128)
    full_proj, full_out, full_up, full_down, small = gather_all(
        dp, seq, [w_proj, w_out, w_up, w_down, small]
    )
    small = cut(small.reshape(devices, 1024), widths)
    full_depth = small[0].reshape(-1, KERNEL)
    (
        full_bproj,
        full_bup,
        full_bout,
        gain_one,
        shift_one,
        full_bdown,
        gain_two,
        shift_two,
    ) = [v.reshape(-1) for v in small[1:]]
    bias_proj = full_bproj.astype(jnp.float32)
    gain_first = gain_one.astype(jnp.float32)
    shift_first = shift_one.astype(jnp.float32)
    gain_second = gain_two.astype(jnp.float32)
    shift_second = shift_two.astype(jnp.float32)
    tokens_flat = hidden.reshape(total_rows, model_width)
    first_proj = jnp.dot(
        tokens_flat, full_proj[:, : 3 * all_width], preferred_element_type=jnp.float32
    )
    queries = (first_proj[:, :all_width] + bias_proj[:all_width]).astype(jnp.bfloat16)
    key_rows = first_proj[:, all_width : 2 * all_width].astype(jnp.bfloat16)
    value_rows = (first_proj[:, 2 * all_width :] + bias_proj[all_width : 2 * all_width]).astype(
        jnp.bfloat16
    )
    extended = with_halo(hidden, (("seq", 1),), half_kernel)
    position = lax.axis_index("seq") * local_rows + jnp.arange(ext_rows) - half_kernel
    inside = ((position >= 0) & (position < local_rows * lax.axis_size("seq"))).astype(jnp.float32)
    conv_input = jnp.dot(
        extended.reshape(seq_count * ext_rows, model_width),
        full_proj[:, 3 * all_width : 4 * all_width],
        preferred_element_type=jnp.float32,
    )
    conv_input = (conv_input + bias_proj[2 * all_width : 3 * all_width]).reshape(
        seq_count, ext_rows, all_width
    ) * inside[None, :, None]
    depth_weights = full_depth.astype(jnp.float32)
    depth_sum = jnp.zeros((seq_count, local_rows, model_width), jnp.float32)
    for tap_index in range(tap_count):
        depth_sum = (
            depth_sum
            + extended[:, tap_index : tap_index + local_rows].astype(jnp.float32)
            * depth_weights[:, tap_index]
        )
    spread = depth_sum.astype(jnp.bfloat16).reshape(total_rows, model_width)
    key_conv = (
        jnp.dot(spread, full_proj[:, 4 * all_width :], preferred_element_type=jnp.float32)
        + bias_proj[3 * all_width :]
    )
    mixed_key = (key_conv * queries.astype(jnp.float32)).astype(jnp.bfloat16)
    logits = jnp.dot(mixed_key, w_kernel, preferred_element_type=jnp.float32) + b_kernel.astype(
        jnp.float32
    )
    tap_weights = jax.nn.softmax(
        logits.reshape(seq_count, local_rows, head_count, tap_count), axis=-1
    )
    conv_heads = conv_input.reshape(seq_count, ext_rows, head_count, head_size)
    conv_mix = jnp.zeros((seq_count, local_rows, head_count, head_size), jnp.float32)
    for tap_index in range(tap_count):
        conv_mix = (
            conv_mix
            + tap_weights[..., tap_index, None] * conv_heads[:, tap_index : tap_index + local_rows]
        )
    queries_seq = queries.reshape(seq_count, local_rows, all_width)
    all_keys, all_values = (
        lax.all_gather(
            key_rows.reshape(seq_count, local_rows, all_width), "seq", axis=1, tiled=True
        ),
        lax.all_gather(
            value_rows.reshape(seq_count, local_rows, all_width), "seq", axis=1, tiled=True
        ),
    )
    full_length = all_keys.shape[1]

    def forward_one(item_set):
        query_seq, key_seq, value_seq = item_set
        return attend(
            query_seq.reshape(local_rows, head_count, head_size),
            key_seq.reshape(full_length, head_count, head_size),
            value_seq.reshape(full_length, head_count, head_size),
            score_scale,
        )

    context, norm_log = lax.map(forward_one, (queries_seq, all_keys, all_values))
    joined = jnp.concatenate(
        [
            context.reshape(total_rows, all_width),
            conv_mix.reshape(total_rows, all_width).astype(jnp.bfloat16),
        ],
        axis=-1,
    )
    after_mix = (
        jnp.dot(joined, full_out, preferred_element_type=jnp.float32)
        + full_bout.astype(jnp.float32)
        + tokens_flat.astype(jnp.float32)
    )
    first_norm, first_pull = jax.vjp(layer_norm, after_mix, gain_first, shift_first)
    grouped_in = first_norm.astype(jnp.bfloat16).reshape(
        total_rows, group_count, model_width // group_count
    )
    up_groups = full_up.reshape(
        group_count, model_width // group_count, hidden_units // group_count
    )
    pre_act = jnp.einsum(
        "ngd,gdf->ngf", grouped_in, up_groups, preferred_element_type=jnp.float32
    ).reshape(total_rows, hidden_units) + full_bup.astype(jnp.float32)
    activated, gelu_pull = jax.vjp(partial(jax.nn.gelu, approximate=False), pre_act)
    act_low = activated.astype(jnp.bfloat16).reshape(
        total_rows, group_count, hidden_units // group_count
    )
    down_groups = full_down.reshape(
        group_count, hidden_units // group_count, model_width // group_count
    )
    summed = jnp.einsum(
        "ngf,gfd->ngd", act_low, down_groups, preferred_element_type=jnp.float32
    ).reshape(total_rows, model_width)
    summed = summed + full_bdown.astype(jnp.float32) + first_norm
    out_value, second_pull = jax.vjp(layer_norm, summed, gain_second, shift_second)
    output = out_value.astype(jnp.bfloat16).reshape(seq_count, local_rows, model_width)
    back_proj = full_proj
    back_depth = full_depth.astype(jnp.float32)
    back_out = full_out
    back_up = up_groups
    back_down = down_groups
    grad_summed, grad_gain_two, grad_shift_two = second_pull(
        cotangent.reshape(total_rows, model_width).astype(jnp.float32)
    )
    grad_bdown = jnp.sum(grad_summed, axis=0)
    summed_low = grad_summed.astype(jnp.bfloat16).reshape(
        total_rows, group_count, model_width // group_count
    )
    grad_activ = jnp.einsum(
        "ngd,gfd->ngf", summed_low, back_down, preferred_element_type=jnp.float32
    ).reshape(total_rows, hidden_units)
    grad_wdown = jnp.einsum(
        "ngf,ngd->gfd", act_low, summed_low, preferred_element_type=jnp.float32
    ).reshape(hidden_units, model_width // group_count)
    grad_pre = gelu_pull(grad_activ)[0]
    grad_bup = jnp.sum(grad_pre, axis=0)
    pre_low = grad_pre.astype(jnp.bfloat16).reshape(
        total_rows, group_count, hidden_units // group_count
    )
    grad_wup = jnp.einsum(
        "ngd,ngf->gdf", grouped_in, pre_low, preferred_element_type=jnp.float32
    ).reshape(model_width, hidden_units // group_count)
    grad_first = grad_summed + jnp.einsum(
        "ngf,gdf->ngd", pre_low, back_up, preferred_element_type=jnp.float32
    ).reshape(total_rows, model_width)
    grad_after, grad_gain_one, grad_shift_one = first_pull(grad_first)
    grad_bout = jnp.sum(grad_after, axis=0)
    after_low = grad_after.astype(jnp.bfloat16)
    grad_wout = jnp.dot(joined.T, after_low, preferred_element_type=jnp.float32)
    grad_joined = jnp.dot(after_low, back_out.T, preferred_element_type=jnp.float32)
    grad_context = (
        grad_joined[:, :all_width].astype(jnp.bfloat16).reshape(seq_count, local_rows, all_width)
    )
    grad_mix = grad_joined[:, all_width:].reshape(seq_count, local_rows, head_count, head_size)

    def back_one(item_set):
        query_seq, grad_seq, norm_seq, key_seq, value_seq = item_set
        grad_query, grad_key, grad_value, unused_delta = attend_back(
            query_seq.reshape(local_rows, head_count, head_size),
            grad_seq.reshape(local_rows, head_count, head_size),
            norm_seq,
            key_seq.reshape(full_length, head_count, head_size),
            value_seq.reshape(full_length, head_count, head_size),
            None,
            score_scale,
        )
        key_value = jnp.concatenate(
            [grad_key.reshape(full_length, all_width), grad_value.reshape(full_length, all_width)],
            axis=-1,
        )
        return (grad_query.reshape(local_rows, all_width), key_value)

    grad_query_att, kv_terms = lax.map(
        back_one, (queries_seq, grad_context, norm_log, all_keys, all_values)
    )
    own_kv = lax.psum_scatter(
        kv_terms.astype(jnp.bfloat16), "seq", scatter_dimension=1, tiled=True
    ).astype(jnp.float32)
    grad_keys_low = own_kv[..., :all_width].reshape(total_rows, all_width).astype(jnp.bfloat16)
    grad_values_low = own_kv[..., all_width:].reshape(total_rows, all_width).astype(jnp.bfloat16)
    grad_taps = jnp.stack(
        [
            jnp.sum(grad_mix * conv_heads[:, tap_index : tap_index + local_rows], axis=-1)
            for tap_index in range(tap_count)
        ],
        axis=-1,
    )
    grad_conv_ext = jnp.zeros((seq_count, ext_rows, head_count, head_size), jnp.float32)
    for tap_index in range(tap_count):
        grad_conv_ext = grad_conv_ext + jnp.pad(
            tap_weights[..., tap_index, None] * grad_mix,
            ((0, 0), (tap_index, 2 * half_kernel - tap_index), (0, 0), (0, 0)),
        )
    grad_logits = tap_weights * (
        grad_taps - jnp.sum(tap_weights * grad_taps, axis=-1, keepdims=True)
    )
    grad_logits = grad_logits.reshape(total_rows, head_count * tap_count)
    grad_bkernel = jnp.sum(grad_logits, axis=0)
    logits_low = grad_logits.astype(jnp.bfloat16)
    grad_wkernel = jnp.dot(mixed_key.T, logits_low, preferred_element_type=jnp.float32)
    grad_mixed = jnp.dot(logits_low, w_kernel.T, preferred_element_type=jnp.float32)
    grad_queries = (grad_query_att.reshape(total_rows, all_width) + grad_mixed * key_conv).astype(
        jnp.bfloat16
    )
    grad_key_conv = grad_mixed * queries.astype(jnp.float32)
    grad_bpt = jnp.sum(grad_key_conv, axis=0)
    key_conv_low = grad_key_conv.astype(jnp.bfloat16)
    grad_wpt = jnp.dot(spread.T, key_conv_low, preferred_element_type=jnp.float32)
    grad_spread = jnp.dot(
        key_conv_low, back_proj[:, 4 * all_width :].T, preferred_element_type=jnp.float32
    ).reshape(seq_count, local_rows, model_width)
    grad_wdepth = jnp.stack(
        [
            jnp.sum(
                extended[:, tap_index : tap_index + local_rows].astype(jnp.float32) * grad_spread,
                axis=(0, 1),
            )
            for tap_index in range(tap_count)
        ],
        axis=-1,
    )
    grad_ext_depth = jnp.zeros((seq_count, ext_rows, model_width), jnp.float32)
    for tap_index in range(tap_count):
        grad_ext_depth = grad_ext_depth + jnp.pad(
            back_depth[:, tap_index] * grad_spread,
            ((0, 0), (tap_index, 2 * half_kernel - tap_index), (0, 0)),
        )
    combined = jnp.concatenate(
        [grad_conv_ext.reshape(seq_count, ext_rows, all_width), grad_ext_depth], axis=-1
    )
    received = with_halo(combined.astype(jnp.bfloat16), (("seq", 1),), half_kernel).astype(
        combined.dtype
    )
    own_part = combined[:, half_kernel : half_kernel + local_rows]
    own_part = own_part.at[:, :half_kernel].add(received[:, :half_kernel])
    own_part = own_part.at[:, local_rows - half_kernel :].add(
        received[:, received.shape[1] - half_kernel :]
    )
    grad_conv_own = own_part[..., :all_width].reshape(total_rows, all_width)
    grad_depth_x = own_part[..., all_width:].reshape(total_rows, model_width)
    grad_bconv = jnp.sum(grad_conv_own, axis=0)
    conv_low = grad_conv_own.astype(jnp.bfloat16)
    stacked = jnp.concatenate([grad_queries, grad_keys_low, grad_values_low, conv_low], axis=-1)
    grad_wfirst = jnp.dot(tokens_flat.T, stacked, preferred_element_type=jnp.float32)
    grad_tokens = (
        grad_after
        + jnp.dot(stacked, back_proj[:, : 4 * all_width].T, preferred_element_type=jnp.float32)
        + grad_depth_x
    )
    grad_wproj = jnp.concatenate([grad_wfirst, grad_wpt], axis=1)
    grad_bproj = jnp.concatenate(
        [
            jnp.sum(grad_queries.astype(jnp.float32), axis=0),
            jnp.sum(grad_values_low.astype(jnp.float32), axis=0),
            grad_bconv,
            grad_bpt,
        ]
    )
    def blocks(grad, shard):
        return grad.astype(jnp.bfloat16).reshape((devices,) + tiled(shard).shape)

    per_device = [
        g.reshape(devices, -1)
        for g in (
            grad_wdepth, grad_bproj, grad_bup, grad_bout, grad_gain_one, grad_shift_one,
            grad_bdown, grad_gain_two, grad_shift_two,
        )
    ]
    kernel_flat = jnp.concatenate([grad_wkernel.reshape(-1), grad_bkernel])
    kernel_len = kernel_flat.shape[0]
    kernel_each = -(-kernel_len // devices)
    kernel_flat = jnp.pad(kernel_flat, (0, kernel_each * devices - kernel_len))
    small_grad = jnp.concatenate(
        [
            lanes(jnp.concatenate(per_device, axis=1), 1),
            lanes(kernel_flat.reshape(devices, kernel_each), 1),
        ],
        axis=1,
    )
    sum_down, sum_up, sum_out, sum_proj, sum_small, sum_kernel = scatter_all(
        dp,
        seq,
        [
            blocks(grad_wdown, w_down), blocks(grad_wup, w_up), blocks(grad_wout, w_out),
            blocks(grad_wproj, w_proj), small_grad,
        ],
        ("zxyc", "zyxc", "zxyc", "zyxc", "zxyc"),
    )
    mine = cut(sum_small[:1].reshape(1, 1024), widths)
    shards = [sum_proj.reshape(w_proj.shape), mine[0].reshape(w_depth.shape)]
    shards += [
        sum_out.reshape(w_out.shape), sum_up.reshape(w_up.shape), sum_down.reshape(w_down.shape),
    ]
    shards += [m.reshape(-1) for m in mine[1:]]
    kernel_sum = sum_kernel.reshape(devices, 1024)[:, :kernel_each].reshape(-1)
    kernel_total = (
        kernel_sum[: grad_wkernel.size].reshape(grad_wkernel.shape),
        kernel_sum[grad_wkernel.size : kernel_len],
    )
    return (
        output,
        grad_tokens.reshape(seq_count, local_rows, model_width),
        shards[0],
        shards[1],
        kernel_total[0],
        kernel_total[1],
        shards[2],
        shards[3],
        shards[4],
        shards[5],
        shards[6],
        shards[7],
        shards[8],
        shards[9],
        shards[10],
        shards[11],
        shards[12],
    )


def solution(mesh):
    placed = (
        P("dp", "seq", None),
        P("dp", "seq", None),
        P(("dp", "seq"), None),
        P(("dp", "seq"), None),
        P(),
        P(),
        P(("dp", "seq"), None),
        P(("dp", "seq"), None),
        P(("dp", "seq"), None),
        P(("dp", "seq")),
        P(("dp", "seq")),
        P(("dp", "seq")),
        P(("dp", "seq")),
        P(("dp", "seq")),
        P(("dp", "seq")),
        P(("dp", "seq")),
        P(("dp", "seq")),
    )
    return jax.shard_map(
        fast_body if fits(mesh) else body,
        mesh=mesh,
        in_specs=placed,
        out_specs=(
            P("dp", "seq", None),
            P("dp", "seq", None),
            P(("dp", "seq"), None),
            P(("dp", "seq"), None),
            P(),
            P(),
            P(("dp", "seq"), None),
            P(("dp", "seq"), None),
            P(("dp", "seq"), None),
            P(("dp", "seq")),
            P(("dp", "seq")),
            P(("dp", "seq")),
            P(("dp", "seq")),
            P(("dp", "seq")),
            P(("dp", "seq")),
            P(("dp", "seq")),
            P(("dp", "seq")),
        ),
        check_vma=False,
    )
```

```python
from functools import partial

import jax
import jax.numpy as jnp
from jax import lax
from jax.experimental import pallas as pl
from jax.experimental.pallas import tpu as pltpu
from jax.sharding import PartitionSpec as P

MESH = pl.DeviceIdType.MESH


class Grid:
    def __init__(self, dp, seq):
        self.C = 2 if dp % 2 == 0 else 1
        rest = dp // self.C
        y = 1
        while (2 * y) * (2 * y) <= rest and rest % (2 * y) == 0:
            y *= 2
        self.Y, self.X, self.Z = y, rest // y, seq
        d = lax.axis_index("dp")
        self.z = lax.axis_index("seq")
        self.c = d % self.C
        self.x = (d // self.C) % self.X
        self.y = d // (self.C * self.X)
        self.dp = d
    def size(self, ax):
        return getattr(self, ax.upper())
    def at(self, **off):
        g = {a: (getattr(self, a) + off.get(a, 0)) % self.size(a) if off.get(a, 0) else getattr(self, a) for a in "yxcz"}
        return g
    def dpof(self, g):
        return (g["y"] * self.X + g["x"]) * self.C + g["c"]
    def dev(self, **off):
        g = self.at(**off)
        return (self.dpof(g), g["z"])


def peers(grid):
    out = []
    for a in "zxyc":
        for o in range(1, grid.size(a)):
            out.append(grid.dev(**{a: o}))
    return out


def greet(grid):
    for p in peers(grid):
        pl.semaphore_signal(
            pltpu.get_barrier_semaphore(), inc=1, device_id=p, device_id_type=MESH
        )


def meet(grid):
    pl.semaphore_wait(pltpu.get_barrier_semaphore(), len(peers(grid)))


def entry_barrier(grid):
    greet(grid)
    meet(grid)


def pick(ref, axes, at):
    return ref.at[tuple(at[a] if a in axes else slice(None) for a in "yxc")]


def shards(ref, n):
    size = ref.shape[0] * ref.shape[1] * ref.shape[2] * ref.shape[3]
    return ref.reshape((size,) + tuple(ref.shape[4:])).at[pl.ds(0, n)]


def remote(src, dst, ssem, rsem, dev):
    return pltpu.make_async_remote_copy(
        src_ref=src, dst_ref=dst, send_sem=ssem, recv_sem=rsem, device_id=dev, device_id_type=MESH
    )


class Gather:
    def __init__(self, grid, src, buf, order, ssem, rsem, lsem):
        self.g, self.src, self.buf, self.ssem, self.rsem, self.lsem = grid, src, buf, ssem, rsem, lsem
        self.u, self.v = order[1], order[2]
        self.sent = 0

    def _send(self, src, dst, stage, n, **off):
        remote(src, dst, self.ssem, self.rsem.at[stage], self.g.dev(**off)).start()
        self.sent += n

    def _wait(self, stage, n):
        ref = shards(self.buf, n)
        remote(ref, ref, self.ssem, self.rsem.at[stage], self.g.dev(c=1)).wait_recv()

    def _block(self, uo=0):
        return pick(self.buf, "yxc", self.g.at(**{self.u: uo}))

    def start(self):
        g = self.g
        own = self.buf.at[g.y, g.x, g.c, g.z]
        self.local = pltpu.make_async_copy(self.src, own, self.lsem)
        self.local.start()
        for o in range(1, g.Z):
            self._send(self.src, own, 0, 1, z=o)

    def step1(self):
        g = self.g
        self.local.wait()
        self._wait(0, g.Z - 1)
        own = self._block()
        for o in range(1, g.size(self.u)):
            self._send(own, own, 1, g.Z, **{self.u: o})
        for o in range(1, g.size(self.v)):
            self._send(own, own, 2, g.Z, **{self.v: o})

    def step2(self):
        g = self.g
        U, V = g.size(self.u), g.size(self.v)
        if U > 1:
            self._wait(1, (U - 1) * g.Z)
        for q in range(1, U):
            for o in range(1, V):
                self._send(self._block(q), self._block(q), 2, g.Z, **{self.v: o})

    def step3(self):
        g = self.g
        U, V = g.size(self.u), g.size(self.v)
        if V > 1:
            self._wait(2, U * (V - 1) * g.Z)
        mine = pick(self.buf, "c", g.at())
        for o in range(1, g.C):
            self._send(mine, mine, 3, U * V * g.Z, c=o)

    def step4(self):
        g = self.g
        if g.C > 1:
            self._wait(3, (g.C - 1) * g.Y * g.X * g.Z)

    def finish(self):
        ref = shards(self.buf, self.sent)
        remote(ref, ref, self.ssem, self.rsem.at[0], self.g.dev(c=1)).wait_send()


def run_gathers(gs):
    n = len(gs)
    for g in gs:
        g.start()
    steps = [lambda g: g.step1(), lambda g: g.step2(), lambda g: g.step3(), lambda g: g.step4()]
    for t in range(n + 3):
        for s in range(4):
            i = t - s
            if 0 <= i < n:
                steps[s](gs[i])
    for g in gs:
        g.finish()


class Scatter:
    def __init__(self, grid, part, order, bufs, out, ssem, rsem):
        self.g, self.part, self.out, self.ssem, self.rsem = grid, part, out, ssem, rsem
        self.rc, self.rv, self.ru, self.rz = bufs
        self.u, self.v = order[1], order[2]
        self.U, self.V = grid.size(self.u), grid.size(self.v)
        self.sent = 0

    def _send(self, src, dst, stage, n, **off):
        remote(src, dst, self.ssem, self.rsem.at[stage], self.g.dev(**off)).start()
        self.sent += n

    def _wait(self, stage, ref):
        remote(ref, ref, self.ssem, self.rsem.at[stage], self.g.dev(c=1)).wait_recv()

    def _yx(self, u, v):
        return (v, u) if self.v == "y" else (u, v)

    def _total(self, u, v, i, stage):
        f = jnp.float32
        y, x = self._yx(u, v)
        s = self.part[y, x, self.g.c, i].astype(f)
        for o in range(self.g.C - 1):
            s = s + self.rc[o, y, x, i].astype(f)
        if stage > 1:
            for k in range(self.V - 1):
                s = s + self.rv[k, u, i].astype(f)
        if stage > 2:
            for k in range(self.U - 1):
                s = s + self.ru[k, i].astype(f)
        return s

    def start(self):
        g = self.g
        for o in range(1, g.C):
            self._send(pick(self.part, "c", g.at(c=o)), self.rc.at[o - 1], 0, g.Y * g.X * g.Z, c=o)

    def step1(self):
        g = self.g
        if g.C > 1:
            self._wait(0, self.rc)
        for w in range(1, self.V):
            to = g.at(**{self.v: w})

            def body(i, _):
                u, k = i // g.Z, i % g.Z
                y, x = self._yx(u, to[self.v])
                self.part[y, x, g.c, k] = self._total(u, to[self.v], k, 1).astype(self.part.dtype)
                return 0

            lax.fori_loop(0, self.U * g.Z, body, 0)
            self._send(
                pick(self.part, self.v + "c", to), self.rv.at[w - 1], 1, self.U * g.Z, **{self.v: w}
            )

    def step2(self):
        g = self.g
        here = g.at()
        if self.V > 1:
            self._wait(1, self.rv)
        for q in range(1, self.U):
            to = g.at(**{self.u: q})

            def body(k, _):
                u, v = to[self.u], here[self.v]
                y, x = self._yx(u, v)
                self.part[y, x, g.c, k] = self._total(u, v, k, 2).astype(self.part.dtype)
                return 0

            lax.fori_loop(0, g.Z, body, 0)
            self._send(pick(self.part, "yxc", to), self.ru.at[q - 1], 2, g.Z, **{self.u: q})

    def step3(self):
        g = self.g
        here = g.at()
        if self.U > 1:
            self._wait(2, self.ru)
        for o in range(1, g.Z):
            i = (g.z + o) % g.Z
            self.part[g.y, g.x, g.c, i] = self._total(here[self.u], here[self.v], i, 3).astype(
                self.part.dtype
            )
            self._send(self.part.at[g.y, g.x, g.c, i], self.rz.at[o - 1], 3, 1, z=o)

    def step4(self):
        g = self.g
        here = g.at()
        s = self._total(here[self.u], here[self.v], g.z, 3)
        if g.Z > 1:
            self._wait(3, self.rz)
        for o in range(g.Z - 1):
            s = s + self.rz[o].astype(jnp.float32)
        self.out[...] = s

    def finish(self):
        ref = shards(self.part, self.sent)
        remote(ref, ref, self.ssem, self.rsem.at[0], self.g.dev(c=1)).wait_send()


def scatter_scratch(sizes, shape, dtype, order):
    Z, C, U, V = sizes["z"], sizes["c"], sizes[order[1]], sizes[order[2]]
    t = tuple(shape)
    m = lambda n: max(n, 1)
    return [
        pltpu.VMEM((m(C - 1), sizes["y"], sizes["x"], Z) + t, dtype),
        pltpu.VMEM((m(V - 1), U, Z) + t, dtype),
        pltpu.VMEM((m(U - 1), Z) + t, dtype),
        pltpu.VMEM((m(Z - 1),) + t, dtype),
    ]


def run_scatters(gs):
    n = len(gs)
    for g in gs:
        g.start()
    for t in range(n + 3):
        for s in range(4):
            i = t - s
            if 0 <= i < n:
                [gs[i].step1, gs[i].step2, gs[i].step3, gs[i].step4][s]()
    for g in gs:
        g.finish()


ORDERS = ("zxyc", "zyxc", "zyxc", "zxyc", "zyxc", "zxyc")
VMEM_CAP = 60 << 20


def sizes_of(dp, seq):
    C = 2 if dp % 2 == 0 else 1
    rest = dp // C
    y = 1
    while (2 * y) * (2 * y) <= rest and rest % (2 * y) == 0:
        y *= 2
    return dict(y=y, x=rest // y, c=C, z=seq)


def mesh_lead(dp, seq):
    s = sizes_of(dp, seq)
    return (s["y"], s["x"], s["c"], s["z"])


def tiled(shard):
    rows, cols = shard.shape
    return shard.reshape((rows // 8, 8, cols) if rows % 8 == 0 else (1, rows, cols))


def gather_kernel(dp, seq, orders, *refs):
    n = len(orders)
    ins, outs = refs[:n], refs[n : 2 * n]
    ssem, rsem, lsem = refs[2 * n :]
    grid = Grid(dp, seq)
    entry_barrier(grid)
    run_gathers(
        [
            Gather(grid, ins[i], outs[i], orders[i], ssem.at[i], rsem.at[i], lsem.at[i])
            for i in range(n)
        ]
    )


def gather_all(dp, seq, shards):
    n = len(shards)
    lead = mesh_lead(dp, seq)
    blocks = [tiled(s) for s in shards]
    outs = pl.pallas_call(
        partial(gather_kernel, dp, seq, ORDERS[:n]),
        out_shape=[jax.ShapeDtypeStruct(lead + b.shape, b.dtype) for b in blocks],
        in_specs=[pl.BlockSpec(memory_space=pl.ANY)] * n,
        out_specs=[pl.BlockSpec(memory_space=pl.ANY)] * n,
        scratch_shapes=[
            pltpu.SemaphoreType.DMA((n,)), pltpu.SemaphoreType.DMA((n, 4)),
            pltpu.SemaphoreType.DMA((n,)),
        ],
        compiler_params=pltpu.CompilerParams(collective_id=0, has_side_effects=True),
        name="gather",
    )(*blocks)
    return [o.reshape((-1, s.shape[1])) for o, s in zip(outs, shards)]


def scatter_kernel(dp, seq, orders, count, *refs):
    n = len(orders)
    ins, outs, total, rest = refs[:n], refs[n : 2 * n], refs[2 * n], refs[2 * n + 1 :]
    parts, rest = rest[:n], rest[n:]
    ssem, rsem, lsem, gs, gr = rest[-5:]
    tail = rest[-6]
    grid = Grid(dp, seq)
    copies = [pltpu.make_async_copy(ins[i], parts[i], lsem.at[i]) for i in range(n)]
    for c in copies:
        c.start()
    entry_barrier(grid)
    for c in copies:
        c.wait()
    run_scatters(
        [
            Scatter(
                grid, parts[i], orders[i], rest[4 * i : 4 * i + 4], outs[i],
                ssem.at[i], rsem.at[i],
            )
            for i in range(n)
        ]
    )
    tail[...] = outs[n - 1][1:]
    run_gathers([Gather(grid, tail, total, "zxyc", gs, gr, lsem.at[n])])


def scatter_all(dp, seq, parts, orders):
    n = len(parts)
    N = dp * seq
    sizes = sizes_of(dp, seq)
    lead = mesh_lead(dp, seq)
    parts = [p.reshape(lead + p.shape[1:]) for p in parts]
    scratch = [pltpu.VMEM(p.shape, p.dtype) for p in parts]
    for p, o in zip(parts, orders):
        scratch += scatter_scratch(sizes, p.shape[4:], p.dtype, o)
    last = parts[-1].shape[4:]
    tail = (last[0] - 1,) + last[1:]
    return pl.pallas_call(
        partial(scatter_kernel, dp, seq, orders, n),
        out_shape=[jax.ShapeDtypeStruct(p.shape[4:], jnp.float32) for p in parts]
        + [jax.ShapeDtypeStruct(lead + tail, jnp.float32)],
        in_specs=[pl.BlockSpec(memory_space=pl.ANY)] * n,
        out_specs=[pl.BlockSpec(memory_space=pltpu.VMEM)] * (n + 1),
        scratch_shapes=scratch
        + [
            pltpu.VMEM(tail, jnp.float32), pltpu.SemaphoreType.DMA((n,)),
            pltpu.SemaphoreType.DMA((n, 4)), pltpu.SemaphoreType.DMA((n + 1,)),
            pltpu.SemaphoreType.DMA(()), pltpu.SemaphoreType.DMA((4,)),
        ],
        compiler_params=pltpu.CompilerParams(
            collective_id=1, has_side_effects=True, vmem_limit_bytes=VMEM_CAP
        ),
        name="scatter",
    )(*parts)


def lanes(flat, rows):
    return jnp.pad(flat, ((0, 0), (0, rows * 1024 - flat.shape[1]))).reshape(-1, rows, 8, 128)


def cut(rows, widths):
    out, at = [], 0
    for w in widths:
        out.append(rows[:, at : at + w])
        at += w
    return out


HEADS = 6
HEAD = 64
KERNEL = 9
FF = 3072
GROUPS = 2


norm_eps = 1e-12


def with_halo(cells, sides, width):
    for axis, dim in sides:
        count = lax.axis_size(axis)
        ends = count - 1
        head = lax.slice_in_dim(cells, 0, width, axis=dim)
        tail = lax.slice_in_dim(cells, cells.shape[dim] - width, cells.shape[dim], axis=dim)
        cells = jnp.concatenate(
            [
                lax.ppermute(tail, axis, [(i, (i + 1) % count) for i in range(ends)]),
                cells,
                lax.ppermute(head, axis, [((i + 1) % count, i) for i in range(ends)]),
            ],
            axis=dim,
        )
    return cells


def layer_norm(inputs, gain_vec, shift_vec):
    centre = inputs - jnp.mean(inputs, axis=-1, keepdims=True)
    variance = jnp.mean(centre * centre, axis=-1, keepdims=True)
    return centre * lax.rsqrt(variance + norm_eps) * gain_vec + shift_vec


def attend(queries, key_rows, value_rows, score_scale):
    scores = (
        jnp.einsum("ihe,jhe->hij", queries, key_rows, preferred_element_type=jnp.float32)
        * score_scale
    )
    row_max = jnp.max(scores, axis=-1, keepdims=True)
    norm_log = row_max + jnp.log(jnp.sum(jnp.exp(scores - row_max), axis=-1, keepdims=True))
    weights_low = jnp.exp(scores - norm_log).astype(jnp.bfloat16)
    context = jnp.einsum(
        "hij,jhe->ihe", weights_low, value_rows, preferred_element_type=jnp.float32
    )
    return (context.astype(jnp.bfloat16), norm_log[..., 0])


def attend_back(queries, grad_context, norm_log, key_rows, value_rows, row_delta, score_scale):
    scores = (
        jnp.einsum("ihe,jhe->hij", queries, key_rows, preferred_element_type=jnp.float32)
        * score_scale
    )
    soft_rows = jnp.exp(scores - norm_log[..., None])
    grad_soft = jnp.einsum(
        "ihe,jhe->hij", grad_context, value_rows, preferred_element_type=jnp.float32
    )
    row_delta = jnp.sum(soft_rows * grad_soft, axis=-1)
    grad_scores = (soft_rows * (grad_soft - row_delta[..., None])).astype(jnp.bfloat16)
    grad_queries = (
        jnp.einsum("hij,jhe->ihe", grad_scores, key_rows, preferred_element_type=jnp.float32)
        * score_scale
    )
    grad_keys = (
        jnp.einsum("hij,ihe->jhe", grad_scores, queries, preferred_element_type=jnp.float32)
        * score_scale
    )
    grad_values = jnp.einsum(
        "hij,ihe->jhe",
        soft_rows.astype(jnp.bfloat16),
        grad_context,
        preferred_element_type=jnp.float32,
    )
    return (grad_queries, grad_keys, grad_values, row_delta)


def dot(a, b):
    return jnp.dot(a, b, preferred_element_type=jnp.float32)


def dot_nt(a, b):
    return lax.dot_general(a, b, (((1,), (1,)), ((), ())), preferred_element_type=jnp.float32)


def dot_tn(a, b):
    return lax.dot_general(a, b, (((0,), (0,)), ((), ())), preferred_element_type=jnp.float32)


def centred(v):
    centre = v - jnp.mean(v, axis=-1, keepdims=True)
    inv = lax.rsqrt(jnp.mean(centre * centre, axis=-1, keepdims=True) + norm_eps)
    return centre * inv, inv


def norm_back(grad, normed, inv):
    return inv * (
        grad
        - jnp.mean(grad, axis=-1, keepdims=True)
        - normed * jnp.mean(grad * normed, axis=-1, keepdims=True)
    )


def rows_sum(v):
    return jnp.sum(v, axis=0, keepdims=True)


V_BOUT, V_G1, V_S1, V_BDOWN, V_G2, V_S2 = range(9, 15)
HALF_GELU = 0.7071067811865476
PDF = 0.3989422804014327
BLOCK = 512
CHUNK = 768


def ffn_kernel(
    joined, x, cot, wout, h_wup, h_wdown, vec, bup,
    h_out, h_gafter, h_dctx, h_gmix, h_gwout, h_gwup, h_gwdown, vecg, gbup,
    wup, wdown, out, gafter, dctx, gmix, gwout, gwup, gwdown,
    act, slope, gp, fnb, gsb, gab, lsem, bsem, wsem,
):
    f32, bf16 = jnp.float32, jnp.bfloat16
    total = x.shape[0]
    width = x.shape[1]
    chan = width // 2
    gw = width // GROUPS
    gf = FF // GROUPS
    loads = [
        pltpu.make_async_copy(h_wup, wup, lsem.at[0]),
        pltpu.make_async_copy(h_wdown, wdown, lsem.at[1]),
    ]
    for cp in loads:
        cp.start()

    def stores(r):
        rows = pl.ds(pl.multiple_of(r * BLOCK, BLOCK), BLOCK)
        return [
            pltpu.make_async_copy(a.at[rows], b.at[rows], bsem.at[i, r])
            for i, (a, b) in enumerate(
                ((out, h_out), (gafter, h_gafter), (dctx, h_dctx), (gmix, h_gmix))
            )
        ]

    vecg[...] = jnp.zeros_like(vecg)
    gbup[...] = jnp.zeros_like(gbup)

    def block(r, _):
        rows = pl.ds(pl.multiple_of(r * BLOCK, BLOCK), BLOCK)
        row = lambda i: vec[i : i + 1, :]
        after = dot(joined[rows], wout[...]) + row(V_BOUT) + x[rows].astype(f32)
        n1, inv1 = centred(after)
        first = n1 * row(V_G1) + row(V_S1)
        low = first.astype(bf16)
        fnb[rows] = low

        @pl.when(r == 0)
        def _():
            for cp in loads:
                cp.wait()

        parts = []
        for g in range(GROUPS):
            acc = jnp.zeros((BLOCK, gw), f32)
            for j in range(gf // CHUNK):
                cols = slice(g * gf + j * CHUNK, g * gf + (j + 1) * CHUNK)
                pre = dot(
                    low[:, g * gw : (g + 1) * gw],
                    wup[g * gw : (g + 1) * gw, j * CHUNK : (j + 1) * CHUNK],
                ) + bup[:, cols]
                cdf = 0.5 + 0.5 * lax.erf(pre * HALF_GELU)
                a = (pre * cdf).astype(bf16)
                act[rows, cols] = a
                slope[:, cols] = cdf + pre * (PDF * jnp.exp(pre * pre * -0.5))
                acc = acc + dot(a, wdown[cols])
            parts.append(acc)
        summed = jnp.concatenate(parts, axis=-1) + row(V_BDOWN) + first
        n2, inv2 = centred(summed)
        out[rows] = (n2 * row(V_G2) + row(V_S2)).astype(bf16)
        c = cot[rows].astype(f32)
        gs = norm_back(c * row(V_G2), n2, inv2)
        glow = gs.astype(bf16)
        gsb[rows] = glow
        parts = []
        for g in range(GROUPS):
            acc = jnp.zeros((BLOCK, gw), f32)
            for j in range(gf // CHUNK):
                cols = slice(g * gf + j * CHUNK, g * gf + (j + 1) * CHUNK)
                pre = dot_nt(glow[:, g * gw : (g + 1) * gw], wdown[cols]) * slope[:, cols]
                gbup[:, cols] += rows_sum(pre)
                p = pre.astype(bf16)
                gp[rows, cols] = p
                acc = acc + dot_nt(
                    p, wup[g * gw : (g + 1) * gw, j * CHUNK : (j + 1) * CHUNK]
                )
            parts.append(acc)
        gfirst = gs + jnp.concatenate(parts, axis=-1)
        ga = norm_back(gfirst * row(V_G1), n1, inv1)
        gafter[rows] = ga
        alow = ga.astype(bf16)
        gab[rows] = alow
        gj = dot_nt(alow, wout[...])
        dctx[rows] = gj[:, :chan].astype(bf16)
        gmix[rows] = gj[:, chan:]
        for i, v in (
            (V_BOUT, ga), (V_G1, gfirst * n1), (V_S1, gfirst), (V_BDOWN, gs), (V_G2, c * n2),
            (V_S2, c),
        ):
            vecg[i : i + 1, :] += rows_sum(v)
        for cp in stores(r):
            cp.start()
        return 0

    lax.fori_loop(0, total // BLOCK, block, 0)
    gwout[...] = dot_tn(joined[...], gab[...]).astype(bf16)
    ends = [pltpu.make_async_copy(gwout, h_gwout, wsem.at[0, 0])]
    ends[0].start()
    chunks = gf // CHUNK
    for g in range(GROUPS):

        def weights(j, _, g=g):
            cols = pl.ds(pl.multiple_of(g * gf + j * CHUNK, CHUNK), CHUNK)
            gwdown[cols] = dot_tn(act[:, cols], gsb[:, g * gw : (g + 1) * gw]).astype(bf16)
            gwup[g * gw : (g + 1) * gw, pl.ds(pl.multiple_of(j * CHUNK, CHUNK), CHUNK)] = dot_tn(
                fnb[:, g * gw : (g + 1) * gw], gp[:, cols]
            ).astype(bf16)
            return 0

        lax.fori_loop(0, chunks, weights, 0, unroll=True)
        for i, (a, b, rows) in enumerate(
            (
                (gwdown, h_gwdown, slice(g * gf, (g + 1) * gf)),
                (gwup, h_gwup, slice(g * gw, (g + 1) * gw)),
            )
        ):
            cp = pltpu.make_async_copy(a.at[rows], b.at[rows], wsem.at[1 + i, g])
            cp.start()
            ends.append(cp)
    for r in range(total // BLOCK):
        ends += stores(r)
    for cp in ends:
        cp.wait()


def ffn(joined, x, cot, wout, wup, wdown, vec, bup):
    f32, bf16 = jnp.float32, jnp.bfloat16
    total, width = x.shape
    shape = jax.ShapeDtypeStruct
    return pl.pallas_call(
        ffn_kernel,
        out_shape=[
            shape((total, width), bf16),
            shape((total, width), f32),
            shape((total, width // 2), bf16),
            shape((total, width // 2), f32),
            shape(wout.shape, bf16),
            shape(wup.shape, bf16),
            shape(wdown.shape, bf16),
            shape(vec.shape, f32),
            shape(bup.shape, f32),
        ],
        in_specs=[pl.BlockSpec(memory_space=pltpu.VMEM)] * 4
        + [pl.BlockSpec(memory_space=pl.ANY)] * 2
        + [pl.BlockSpec(memory_space=pltpu.VMEM)] * 2,
        out_specs=[pl.BlockSpec(memory_space=pl.ANY)] * 7
        + [pl.BlockSpec(memory_space=pltpu.VMEM)] * 2,
        scratch_shapes=[
            pltpu.VMEM(wup.shape, bf16),
            pltpu.VMEM(wdown.shape, bf16),
            pltpu.VMEM((total, width), bf16),
            pltpu.VMEM((total, width), f32),
            pltpu.VMEM((total, width // 2), bf16),
            pltpu.VMEM((total, width // 2), f32),
            pltpu.VMEM(wout.shape, bf16),
            pltpu.VMEM(wup.shape, bf16),
            pltpu.VMEM(wdown.shape, bf16),
            pltpu.VMEM((total, FF), bf16),
            pltpu.VMEM((BLOCK, FF), f32),
            pltpu.VMEM((total, FF), bf16),
            pltpu.VMEM((total, width), bf16),
            pltpu.VMEM((total, width), bf16),
            pltpu.VMEM((total, width), bf16),
            pltpu.SemaphoreType.DMA((2,)),
            pltpu.SemaphoreType.DMA((4, total // BLOCK)),
            pltpu.SemaphoreType.DMA((3, GROUPS)),
        ],
        compiler_params=pltpu.CompilerParams(vmem_limit_bytes=VMEM_CAP),
        name="ffn",
    )(joined, x, cot, wout, wup, wdown, vec, bup)


HEADS_PER = HEADS // 2
PART = HEADS_PER * HEAD
EDGE = 8
TAPS = KERNEL
CHAN = HEADS * HEAD


def iota(shape, dim):
    return lax.broadcasted_iota(jnp.int32, shape, dim)


def expander(rows, cols, width):
    return (iota((rows, cols), 1) % width == iota((rows, cols), 0)).astype(jnp.bfloat16)


def owned(stack, width):
    keep = iota(stack.shape, 2) // width == iota(stack.shape, 0)
    return jnp.sum(jnp.where(keep, stack, 0.0), axis=0)


def unpack_small(gsmall, vec, bproj, bup, widths):
    n = gsmall.shape[0] * gsmall.shape[1] * gsmall.shape[2] * gsmall.shape[3]
    gsmall = gsmall[...].reshape((n,) + gsmall.shape[4:])
    w, wp, wu = widths
    flat = gsmall[:, :2].reshape(n * 16, 128).astype(jnp.bfloat16)
    cols = vec.shape[1]
    vec[...] = owned(dot(flat, expander(128, cols, w)).reshape(n, 16, cols), w)
    flat = gsmall[:, 2].reshape(n * 8, 128).astype(jnp.bfloat16)
    cols = bproj.shape[1]
    bproj[...] = owned(dot(flat, expander(128, cols, wp)).reshape(n, 8, cols), wp)[:1]
    cols = bup.shape[1]
    bup[...] = owned(dot(flat, expander(128, cols, wu)).reshape(n, 8, cols), wu)[1:2]


def pack(v):
    r = v.shape[0] // 2
    return jnp.concatenate([v[:r], v[r:]], axis=1)


def unpack(v):
    c = v.shape[1] // 2
    return jnp.concatenate([v[:, :c], v[:, c:]], axis=0)


def tap_logits(mixed, wkx, bkx, logits, at=0):
    rows = pl.ds(at, mixed.shape[0])

    def tap(t, _):
        logits[t, rows] = dot(mixed, wkx[t]) + bkx[pl.ds(t, 1)]
        return 0

    lax.fori_loop(0, TAPS, tap, 0)


def softmax_taps(logits, rows):
    ls = [logits[t, rows] for t in range(TAPS)]
    top = ls[0]
    for v in ls[1:]:
        top = jnp.maximum(top, v)
    es = [jnp.exp(v - top) for v in ls]
    total = es[0]
    for v in es[1:]:
        total = total + v
    inv = 1.0 / total
    return [e * inv for e in es]


def expand_kernel_weights(w_kernel, b_kernel, wkx, bkx):
    cols = wkx.shape[2]
    wk, bk = w_kernel[...], b_kernel[...]
    for t in range(TAPS):
        k = wk.shape[0]
        pick = (iota((k, cols), 0) == iota((k, cols), 1) // HEAD * TAPS + t).astype(jnp.bfloat16)
        wkx[t] = dot_tn(wk, pick).astype(jnp.bfloat16)
        bkx[t : t + 1] = dot(bk, pick)


ROW = 16


def front_kernel(
    dp, seq, widths,
    x, wproj, wout, wup, wdown, small, w_kernel, b_kernel,
    gq0, gq1, gq2, gcp, gout, gup, gdown,
    h_qh, h_kh, h_vh, h_joined, h_qn, h_xe, h_convin, h_keyconv, h_mixed, h_spread, h_wkx,
    stats, vec, bup, bkx,
    qh, kh, vh, joined, qn, xe, convin, keyconv, mixed, spread, wkx,
    pq, pcp, gsmall, wq, wcp, xf, edges, inedge, qkv, abuf, csend, cbuf, logits, bproj,
    ssem, rsem, lsem, asend, arecv, bsend, brecv, esend, erecv, wsem, osem,
):
    f32, bf16 = jnp.float32, jnp.bfloat16
    grid = Grid(dp, seq)
    z, Z = grid.z, seq
    seqs, local, width = x.shape
    total = seqs * local

    greet(grid)
    outs = (
        (qh, h_qh), (kh, h_kh), (vh, h_vh), (joined, h_joined), (qn, h_qn), (xe, h_xe),
        (convin, h_convin), (keyconv, h_keyconv), (mixed, h_mixed), (spread, h_spread),
        (wkx, h_wkx),
    )
    ends = []

    def store(*refs):
        for i, (a, b) in enumerate(outs):
            if any(a is r for r in refs):
                cp = pltpu.make_async_copy(a, b, osem.at[i])
                cp.start()
                ends.append(cp)

    w = wproj[...].astype(f32)
    for j in range(HEADS_PER):
        cols = []
        for n in (j, HEADS_PER + j):
            for p in range(3):
                at = p * CHAN + n * HEAD
                cols.append(w[:, at : at + HEAD])
        pq[j] = jnp.concatenate(cols, axis=1).reshape(pq.shape[1:]).astype(bf16)
    pcp[...] = w[:, 3 * CHAN :].reshape(pcp.shape).astype(bf16)
    for s in range(seqs):
        edges[0, s] = x[s, :EDGE].astype(f32)
        edges[1, s] = x[s, local - EDGE :].astype(f32)

    expand_kernel_weights(w_kernel, b_kernel, wkx, bkx)
    store(wkx)
    meet(grid)
    mk = lambda i, src, buf, order: Gather(
        grid, src, buf, order, ssem.at[i], rsem.at[i], lsem.at[i]
    )
    gs = mk(0, small, gsmall, "zxyc")
    gq = [
        mk(1, pq.at[0], gq0, "zxyc"), mk(2, pq.at[1], gq1, "zyxc"), mk(3, pq.at[2], gq2, "zxyc")
    ]
    g2 = mk(4, pcp, gcp, "zyxc")
    g3 = mk(5, wout, gout, "zxyc")
    g4 = mk(6, wup, gup, "zyxc")
    g5 = mk(7, wdown, gdown, "zxyc")
    large = (g4, g5, g3)
    whole_q = [
        pltpu.make_async_copy(g.reshape((width, 2 * PART)), wq.at[j], wsem.at[j])
        for j, g in enumerate((gq0, gq1, gq2))
    ]
    whole_cp = pltpu.make_async_copy(gcp.reshape(wcp.shape), wcp, wsem.at[HEADS_PER])
    hops = [
        pltpu.make_async_remote_copy(
            src_ref=edges.at[i], dst_ref=inedge.at[i], send_sem=esend.at[i],
            recv_sem=erecv.at[i], device_id=grid.dev(z=o), device_id_type=MESH,
        )
        for i, o in ((0, seq - 1), (1, 1))
    ]
    sends = {}
    heads = {}

    def qkv_unit(j):
        gq[j].step4()
        whole_q[j].start()
        whole_q[j].wait()
        zero = jnp.zeros((1, HEAD), f32)
        cols = []
        for n in (j, HEADS_PER + j):
            at = n * HEAD
            cols += [bproj[:, at : at + HEAD], zero, bproj[:, CHAN + at : CHAN + at + HEAD]]
        qkv_bias = jnp.concatenate(cols, axis=1)
        for s in range(seqs):
            val = (dot(x[s], wq[j]) + qkv_bias).astype(bf16)
            for h in range(2):
                qkv[2 * s + h, j] = pack(val[:, h * PART : (h + 1) * PART])
                heads[s, h * HEADS_PER + j] = val[:, h * PART : h * PART + HEAD]
        for o in range(1, Z):
            to = (z + o) % Z
            cp = pltpu.make_async_remote_copy(
                src_ref=qkv.at[to, j], dst_ref=abuf.at[j, z], send_sem=asend.at[j, o - 1],
                recv_sem=arecv.at[j, o - 1], device_id=grid.dev(z=o), device_id_type=MESH,
            )
            cp.start()
            sends[j, o] = cp
        abuf[j, z] = qkv[z, j]

    def extend():
        for cp in hops:
            cp.wait_recv()
        for s in range(seqs):
            top = jnp.where(z > 0, inedge[1, s], 0.0)
            low = jnp.where(z < Z - 1, inedge[0, s], 0.0)
            xf[s, :EDGE] = top
            xf[s, EDGE : EDGE + local] = x[s].astype(f32)
            xf[s, EDGE + local :] = low
            xe[s] = xf[s].astype(bf16)
        spread_rows(xf, vec, spread, seqs, local)
        store(xe, spread)

    def conv_inputs():
        whole_cp.start()
        for s in range(seqs):
            qn[s * local : (s + 1) * local] = jnp.concatenate(
                [heads[s, n] for n in range(HEADS)], axis=1
            )
        store(qn)
        whole_cp.wait()
        bias = bproj[...]
        ext = local + 2 * EDGE
        at = iota((ext, 1), 0)
        inside = ((at >= EDGE) | (z > 0)) & ((at < EDGE + local) | (z < Z - 1))
        for s in range(seqs):
            val = dot(xe[s], wcp[:, :CHAN]) + bias[:, 2 * CHAN : 3 * CHAN]
            convin[s] = jnp.where(inside, val, 0.0)
        for s in range(seqs):
            rows = slice(s * local, (s + 1) * local)
            kc = dot(spread[rows], wcp[:, CHAN:]) + bias[:, 3 * CHAN :]
            keyconv[rows] = kc
            mixed[rows] = (kc * qn[rows].astype(f32)).astype(bf16)
        store(convin, keyconv, mixed)

    def conv_mix(s):
        tap_logits(mixed[s * local : (s + 1) * local], wkx, bkx, logits)

        def mix(i, _):
            r = pl.ds(pl.multiple_of(i * ROW, ROW), ROW)
            win = convin[s, pl.ds(pl.multiple_of(i * ROW, ROW), 2 * ROW)]
            tw = softmax_taps(logits, r)
            acc = jnp.zeros((ROW, CHAN), f32)
            for t in range(TAPS):
                a = EDGE - TAPS // 2 + t
                acc = acc + tw[t] * win[a : a + ROW]
            joined[pl.ds(pl.multiple_of(s * local + i * ROW, ROW), ROW), CHAN:] = acc.astype(bf16)
            return 0

        lax.fori_loop(0, local // ROW, mix, 0)

    returns = []

    def attention(j):
        for o in range(1, Z):
            sends[j, o].wait_recv()
        for b in range(Z):
            val = unpack(abuf[j, b])
            rows = slice(b * local, (b + 1) * local)
            for p, ref in enumerate((qh, kh, vh)):
                ref[j, rows] = val[:, p * HEAD : (p + 1) * HEAD]
        if j == HEADS_PER - 1:
            store(qh, kh, vh)
        returns.extend(attend_unit(grid, j, qh, kh, vh, stats, csend, cbuf, bsend, brecv))

    gs.start()
    for g in gq:
        g.start()
    g2.start()
    for cp in hops:
        cp.start()
    gs.step1()
    for g in gq:
        g.step1()
    g2.step1()
    for g in large:
        g.start()
    gs.step2()
    for g in gq:
        g.step2()
    g2.step2()
    gs.step3()
    for g in gq:
        g.step3()
    g2.step3()
    gs.step4()
    unpack_small(gsmall, vec, bproj, bup, widths)
    qkv_unit(0)
    qkv_unit(1)
    qkv_unit(2)
    for g in large:
        g.step1()
    extend()
    g2.step4()
    conv_inputs()
    conv_mix(0)
    attention(0)
    for g in large:
        g.step2()
    conv_mix(1)
    attention(1)
    for g in large:
        g.step3()
    attention(2)
    for g in large:
        g.step4()
    for cp in returns:
        cp.wait_recv()
    for s in range(seqs):
        pieces = []
        for n in range(HEADS):
            v = cbuf[n % HEADS_PER, 2 * s + n // HEADS_PER]
            pieces.append(unpack(unpack(v)))
        joined[s * local : (s + 1) * local, :CHAN] = jnp.concatenate(pieces, axis=1)
    store(joined)
    for cp in list(sends.values()) + returns + hops:
        cp.wait_send()
    for g in [gs] + gq + [g2, g3, g4, g5]:
        g.finish()
    for cp in ends:
        cp.wait()


def spread_rows(xf, vec, spread, seqs, local):
    width = xf.shape[2]
    step = 256

    def body(i, _):
        for s in range(seqs):
            for c in range(width // step):
                cols = slice(c * step, (c + 1) * step)
                win = xf[s, pl.ds(pl.multiple_of(i * ROW, ROW), 2 * ROW), cols]
                acc = jnp.zeros((ROW, step), jnp.float32)
                for t in range(TAPS):
                    a = EDGE - TAPS // 2 + t
                    acc = acc + win[a : a + ROW] * vec[t : t + 1, cols]
                r = pl.ds(pl.multiple_of(s * local + i * ROW, ROW), ROW)
                spread[r, cols] = acc.astype(spread.dtype)
        return 0

    lax.fori_loop(0, local // ROW, body, 0)


def attend_unit(grid, h, qh, kh, vh, stats, csend, cbuf, bsend, brecv):
    f32, bf16 = jnp.float32, jnp.bfloat16
    z, Z = grid.z, grid.Z
    local = qh.shape[1] // Z
    sends = []
    scale = jnp.asarray(HEAD ** (-0.5), bf16)
    keys = kh[h]
    vt = vh[h].T
    def send(i):
        return pltpu.make_async_remote_copy(
            src_ref=csend.at[h, i], dst_ref=cbuf.at[h, z], send_sem=bsend.at[h, i],
            recv_sem=brecv.at[h, i], device_id=(grid.dp, (z + i + 1) % Z), device_id_type=MESH,
        )

    def block(i, _):
        b = (z + i + 1) % Z
        rows = pl.ds(pl.multiple_of(b * local, local), local)
        st = dot_nt(keys, qh[h, rows] * scale)
        top = jnp.max(st, axis=0, keepdims=True)
        e = jnp.exp(st - top)
        den = jnp.sum(e, axis=0, keepdims=True)
        stats[h, b] = top + jnp.log(den)
        ct = dot(vt, e.astype(bf16)) / den
        csend[h, i] = pack(pack(ct.T.astype(bf16)))

        @pl.when(i < Z - 1)
        def _():
            send(i).start()

        return 0

    lax.fori_loop(0, Z, block, 0)
    cbuf[h, z] = csend[h, Z - 1]
    return [send(i) for i in range(Z - 1)]


def front(dp, seq, x, w_proj, w_out, w_up, w_down, small, w_kernel, b_kernel, widths):
    f32, bf16 = jnp.float32, jnp.bfloat16
    seqs, local, width = x.shape
    total = seqs * local
    length = seq * local
    N = dp * seq
    rows = w_proj.shape[0]
    lead = tiled(w_proj).shape[:2]
    place = mesh_lead(dp, seq)
    shape = jax.ShapeDtypeStruct
    wide = 6 * PART
    ext = local + 2 * EDGE
    vm = pl.BlockSpec(memory_space=pltpu.VMEM)
    hb = pl.BlockSpec(memory_space=pl.ANY)
    other = [tiled(a) for a in (w_out, w_up, w_down)]
    hbm_out = [
        shape(place + lead + (c,), bf16) for c in (2 * PART,) * HEADS_PER + (2 * CHAN,)
    ]
    hbm_out += [shape(place + a.shape, bf16) for a in other]
    big_out = [
        shape((HEADS_PER, length, HEAD), bf16),
        shape((HEADS_PER, length, HEAD), bf16),
        shape((HEADS_PER, length, HEAD), bf16),
        shape((total, width), bf16),
        shape((total, CHAN), bf16),
        shape((seqs, ext, width), bf16),
        shape((seqs, ext, CHAN), f32),
        shape((total, CHAN), f32),
        shape((total, CHAN), bf16),
        shape((total, width), bf16),
        shape((TAPS, CHAN, CHAN), bf16),
    ]
    vm_out = [
        shape((HEADS_PER, seq, 1, local), f32),
        shape((16, width), f32),
        shape((1, FF), f32),
        shape((16, CHAN), f32),
    ]
    hbm_out += big_out
    sem = lambda *s: pltpu.SemaphoreType.DMA(s)
    return pl.pallas_call(
        partial(front_kernel, dp, seq, widths),
        out_shape=hbm_out + vm_out,
        in_specs=[vm] * 8,
        out_specs=[hb] * len(hbm_out) + [vm] * len(vm_out),
        scratch_shapes=[pltpu.VMEM(o.shape, o.dtype) for o in big_out]
        + [
            pltpu.VMEM((HEADS_PER,) + lead + (2 * PART,), bf16),
            pltpu.VMEM(lead + (2 * CHAN,), bf16),
            pltpu.VMEM(place + small.shape, f32),
            pltpu.VMEM((HEADS_PER, width, 2 * PART), bf16),
            pltpu.VMEM((width, 2 * CHAN), bf16),
            pltpu.VMEM((seqs, ext, width), f32),
            pltpu.VMEM((2, seqs, EDGE, width), f32),
            pltpu.VMEM((2, seqs, EDGE, width), f32),
            pltpu.VMEM((seq, HEADS_PER, local // 2, 2 * PART), bf16),
            pltpu.VMEM((HEADS_PER, seq, local // 2, 2 * PART), bf16),
            pltpu.VMEM((HEADS_PER, seq, local // 4, 4 * HEAD), bf16),
            pltpu.VMEM((HEADS_PER, seq, local // 4, 4 * HEAD), bf16),
            pltpu.VMEM((TAPS, local, CHAN), f32),
            pltpu.VMEM((1, 4 * CHAN), f32),
            sem(8), sem(8, 4), sem(8),
            sem(HEADS_PER, seq - 1), sem(HEADS_PER, seq - 1),
            sem(HEADS_PER, seq - 1), sem(HEADS_PER, seq - 1), sem(2), sem(2), sem(HEADS_PER + 1),
            sem(len(big_out)),
        ],
        compiler_params=pltpu.CompilerParams(
            collective_id=2, has_side_effects=True, vmem_limit_bytes=VMEM_CAP
        ),
        name="front",
    )(x, w_proj, *other, small, w_kernel, b_kernel)


def pack_small(w_depth, vectors, b_proj, b_up):
    rows = [(i, v) for i, v in enumerate([w_depth[:, t] for t in range(TAPS)] + list(vectors))]
    rows += [(16, b_proj), (17, b_up)]
    out = jnp.zeros((24, 128), jnp.float32)
    for i, v in rows:
        out = out + jnp.pad(v.astype(jnp.float32)[None], ((i, 23 - i), (0, 128 - v.shape[0])))
    return out.reshape(3, 8, 128)


def unhalve(w):
    w = w.reshape(w.shape[:-1] + (2, 3, PART))
    return jnp.swapaxes(w, -3, -2).reshape(w.shape[:-3] + (3 * CHAN,))


PAD = 16


def dot_pick(v, picks):
    bf16 = jnp.bfloat16
    hi = v.astype(bf16)
    rest = v - hi.astype(jnp.float32)
    mid = rest.astype(bf16)
    lo = (rest - mid.astype(jnp.float32)).astype(bf16)
    return dot_nt(hi, picks) + dot_nt(mid, picks) + dot_nt(lo, picks)


def to_owners(v, width, n):
    r, cols = v.shape
    picks = expander(128, cols, width)
    if r == 1:
        keep = iota((n, cols), 1) // width == iota((n, cols), 0)
        return dot_pick(jnp.where(keep, v, 0.0), picks)
    keep = iota((n, r, cols), 2) // width == iota((n, r, cols), 0)
    stack = jnp.where(keep, v[None], 0.0).reshape(n * r, cols)
    return dot_pick(stack, picks).reshape(n, r, 128)


def conv_back(
    s, local, gmix, convin, keyconv, mixed, qn, wkx, bkx, wkp, wpt,
    tw, gt, gl, gpad, gsp, gqm, gk, gci_ext, gwk, gbk, gbpoint,
):
    f32, bf16 = jnp.float32, jnp.bfloat16
    rows = slice(s * local, (s + 1) * local)
    body_rows = slice(PAD, PAD + local)
    tap_logits(mixed[rows], wkx, bkx, tw, PAD)
    gpad[body_rows] = gmix[rows]
    same = (iota((CHAN, CHAN), 0) // HEAD == iota((CHAN, CHAN), 1) // HEAD).astype(bf16)
    for t in range(TAPS):
        a = EDGE - TAPS // 2 + t
        p = gmix[rows] * convin[s, a : a + local]
        hi = p.astype(bf16)
        lo = (p - hi.astype(f32)).astype(bf16)
        gt[t] = dot(hi, same) + dot(lo, same)

    def taps(i, _):
        r = pl.ds(pl.multiple_of(i * ROW, ROW), ROW)
        rp = pl.ds(pl.multiple_of(PAD + i * ROW, ROW), ROW)
        ws = softmax_taps(tw, rp)
        gs = [gt[t, r] for t in range(TAPS)]
        mean = ws[0] * gs[0]
        for t in range(1, TAPS):
            mean = mean + ws[t] * gs[t]
        for t in range(TAPS):
            tw[t, rp] = ws[t]
            g = ws[t] * (gs[t] - mean)
            gl[t, r] = g.astype(bf16)
            gbk[t] += g[:8] + g[8:]
        return 0

    lax.fori_loop(0, local // ROW, taps, 0)

    def spread_back(i, _):
        w = pl.ds(pl.multiple_of(i * ROW, ROW), 2 * ROW)
        g = gpad[w]
        acc = jnp.zeros((ROW, CHAN), f32)
        for t in range(TAPS):
            a = PAD - TAPS // 2 - t
            acc = acc + (tw[t, w] * g)[a : a + ROW]
        gci_ext[s, pl.ds(pl.multiple_of(i * ROW, ROW), ROW)] = acc
        return 0

    lax.fori_loop(0, (local + 2 * EDGE) // ROW, spread_back, 0)
    compact = jnp.zeros((local, 128), f32)
    for t in range(TAPS):
        pick = (
            (iota((CHAN, 128), 0) == iota((CHAN, 128), 1) // TAPS * HEAD)
            & (iota((CHAN, 128), 1) % TAPS == t)
            & (iota((CHAN, 128), 1) < HEADS * TAPS)
        ).astype(bf16)
        compact = compact + dot(gl[t], pick)
    low = compact.astype(bf16)
    gwk[...] += dot_tn(low, mixed[rows])
    gmixed = dot(low, wkp[...])
    gqm[rows] = gmixed * keyconv[rows]
    gkc = gmixed * qn[rows].astype(f32)
    gbpoint[...] += rows_sum(gkc)
    glow = gkc.astype(bf16)
    gk[rows] = glow
    gsp[s, body_rows] = dot_nt(glow, wpt)


def depth_back(local, seqs, gsp, xe, vec, gdx_ext, gwd):
    f32 = jnp.float32
    width = gsp.shape[2]
    step = 256

    def grads(i, _):
        w = pl.ds(pl.multiple_of(i * ROW, ROW), 2 * ROW)
        for s in range(seqs):
            for c in range(width // step):
                cols = slice(c * step, (c + 1) * step)
                g = gsp[s, w, cols]
                acc = jnp.zeros((ROW, step), f32)
                for t in range(TAPS):
                    a = PAD - TAPS // 2 - t
                    acc = acc + g[a : a + ROW] * vec[t : t + 1, cols]
                gdx_ext[s, pl.ds(pl.multiple_of(i * ROW, ROW), ROW), cols] = acc
        return 0

    lax.fori_loop(0, (local + 2 * EDGE) // ROW, grads, 0)

    def weights(i, _):
        w = pl.ds(pl.multiple_of(i * ROW, ROW), 2 * ROW)
        for s in range(seqs):
            for c in range(width // step):
                cols = slice(c * step, (c + 1) * step)
                win = xe[s, w, cols].astype(f32)
                g = gsp[s, pl.ds(pl.multiple_of(PAD + i * ROW, ROW), ROW), cols]
                for t in range(TAPS):
                    a = EDGE - TAPS // 2 + t
                    p = win[a : a + ROW] * g
                    gwd[t, :, cols] += p[:8] + p[8:]
        return 0

    lax.fori_loop(0, local // ROW, weights, 0)


def attend_back_block(b, h, keys, vals, kt, qh, stats, dbuf, dkv, local):
    f32, bf16 = jnp.float32, jnp.bfloat16
    scale = HEAD ** (-0.5)
    rows = pl.ds(pl.multiple_of(b * local, local), local)
    q = qh[h, rows]
    do = unpack(dbuf[b])[:, h * HEAD : (h + 1) * HEAD]
    st = dot_nt(keys, q * jnp.asarray(scale, bf16))
    p = jnp.exp(st - stats[h, b])
    dp = dot_nt(vals, do)
    delta = jnp.sum(p * dp, axis=0, keepdims=True)
    ds = (p * (dp - delta)).astype(bf16)
    dk = dot(ds, q)
    dv = dot(p.astype(bf16), do)
    dkv[0] += dk
    dkv[1] += dv
    return (dot(kt, ds) * scale).T


def back_kernel(
    dp, seq, widths,
    dctx, stats, vec, bkx, w_kernel, vecg, gbup,
    h_gmix, h_convin, h_keyconv, h_mixed, h_qn, h_wkx, h_qh, h_kh, h_vh, h_spread, h_xe,
    gafter, gq0, gq1, gq2, gcp, gwdown, gwup, gwout,
    h_gx, o_proj, o_out, o_up, o_down, o_small, o_kernel,
    gmix, convin, keyconv, mixed, qn, wkx, qh, kh, vh, spread, xe, gx, xt,
    *rest,
):
    f32, bf16 = jnp.float32, jnp.bfloat16
    pieces = 9
    parts, rest = rest[:pieces], rest[pieces:]
    bufs, rest = rest[: 4 * pieces], rest[4 * pieces :]
    souts, rest = rest[:5], rest[5:]
    souts = (o_down, o_up, o_out) + souts + (o_small,)
    (
        dbuf, dsend, gsend, grecv, wq, wcp, grads, tw, gt, gl, gpad, gsp, gqm, gk, gci_ext, gcl,
        gdx_ext, gwd, gwk, gbk, gbpoint, wkp, hsend, hrecv, dqb, dkv, kall, bprow,
        ssem, rsem, gssem, grsem, lsem, asend, arecv, bsend, brecv, esend, erecv, wsem,
    ) = rest
    grid = Grid(dp, seq)
    z, Z = grid.z, seq
    N = dp * seq
    seqs = xe.shape[0]
    total = dctx.shape[0]
    local = total // seqs
    width = xe.shape[2]
    w1, wp, wu = widths

    loads = [
        pltpu.make_async_copy(src, dst, wsem.at[i])
        for i, (src, dst) in enumerate(
            (
                (gwdown, parts[0]), (gwup, parts[1]), (gwout, parts[2]),
                (gcp.reshape(wcp.shape), wcp),
                (gafter, gx),
                (gq0.reshape((width, 2 * PART)), wq.at[0]),
                (gq1.reshape((width, 2 * PART)), wq.at[1]),
                (gq2.reshape((width, 2 * PART)), wq.at[2]),
            )
        )
    ]
    greet(grid)
    ins = [
        pltpu.make_async_copy(src, dst, wsem.at[8 + i])
        for i, (src, dst) in enumerate(
            (
                (h_gmix, gmix), (h_convin, convin), (h_keyconv, keyconv), (h_mixed, mixed),
                (h_qn, qn), (h_wkx, wkx), (h_qh, qh), (h_kh, kh), (h_vh, vh), (h_spread, spread),
                (h_xe, xe),
            )
        )
    ]
    for cp in loads[:3] + ins + loads[3:]:
        cp.start()
    for s in range(seqs):
        for h in range(2):
            dsend[2 * s + h] = pack(
                dctx[s * local : (s + 1) * local, h * PART : (h + 1) * PART]
            )
    wk = w_kernel[...]
    wkp[...] = dot(
        (iota((128, wk.shape[0]), 0) == iota((128, wk.shape[0]), 1)).astype(bf16), wk
    ).astype(bf16)
    gwk[...] = jnp.zeros_like(gwk)
    gbk[...] = jnp.zeros_like(gbk)
    gwd[...] = jnp.zeros_like(gwd)
    gbpoint[...] = jnp.zeros_like(gbpoint)
    gpad[...] = jnp.zeros_like(gpad)
    zeros = jnp.zeros((PAD, CHAN), f32)
    for t in range(TAPS):
        tw[t, :PAD] = zeros
        tw[t, PAD + local :] = zeros
    zeros = jnp.zeros((PAD, width), f32)
    for s in range(seqs):
        gsp[s, :PAD] = zeros
        gsp[s, PAD + local :] = zeros
    parts[8][...] = jnp.zeros_like(parts[8])
    parts[8][:, :, :, :, 2, 1:2] = to_owners(gbup[...], wu, N).reshape(parts[8].shape[:4] + (1, 128))
    meet(grid)
    sends = []
    for o in range(1, Z):
        to = (z + o) % Z
        cp = pltpu.make_async_remote_copy(
            src_ref=dsend.at[to], dst_ref=dbuf.at[z], send_sem=bsend.at[o - 1],
            recv_sem=brecv.at[o - 1], device_id=grid.dev(z=o), device_id_type=MESH,
        )
        cp.start()
        sends.append(cp)
    dbuf[z] = dsend[z]
    orders = ("zxyc", "zyxc", "zxyc", "zyxc", "zxyc", "zyxc", "zxyc", "zxyc", "zyxc")
    sc = [
        Scatter(
            grid, parts[i], orders[i], bufs[4 * i : 4 * i + 4], souts[i], ssem.at[i], rsem.at[i]
        )
        for i in range(pieces)
    ]
    sdown, sup, sout, scp, sq0, sq1, sq2, skern, svec = sc
    for i in range(3):
        loads[i].wait()
        sc[i].start()

    for cp in ins[:6]:
        cp.wait()
    loads[3].wait()
    wpt = wcp[:, CHAN:]

    def conv(s):
        conv_back(
            s, local, gmix, convin, keyconv, mixed, qn, wkx, bkx, wkp, wpt,
            tw, gt, gl, gpad, gsp, gqm, gk, gci_ext, gwk, gbk, gbpoint,
        )

    for s in range(seqs - 1):
        conv(s)
    sdown.step1()
    sup.step1()
    sout.step1()

    scale = HEAD ** (-0.5)
    back = []
    for cp in ins[6:]:
        cp.wait()
    for s in range(seqs):
        xt[:, s * local : (s + 1) * local] = xe[s, EDGE : EDGE + local].T
    for cp in sends:
        cp.wait_recv()
    for h in range(HEADS_PER):
        keys, vals = kh[h], vh[h]
        kt = keys.T
        dkv[...] = jnp.zeros_like(dkv)

        def block(o, _, h=h, keys=keys, vals=vals, kt=kt):
            b = (z + Z - o) % Z
            dqb[b] = attend_back_block(
                b, h, keys, vals, kt, qh, stats, dbuf, dkv, local
            ).astype(bf16)
            return 0

        lax.fori_loop(0, Z, block, 0, unroll=2)
        for o in list(range(1, Z)) + [0]:
            b = (z + o) % Z
            r = pl.ds(pl.multiple_of(b * local, local), local)
            val = pack(
                jnp.concatenate(
                    [dqb[b], (dkv[0, r] * scale).astype(bf16), dkv[1, r].astype(bf16)], axis=1
                )
            )
            if o:
                gsend[h, o - 1] = val
                cp = pltpu.make_async_remote_copy(
                    src_ref=gsend.at[h, o - 1], dst_ref=grecv.at[h, z],
                    send_sem=asend.at[h, o - 1], recv_sem=arecv.at[h, o - 1],
                    device_id=grid.dev(z=o), device_id_type=MESH,
                )
                cp.start()
                back.append(cp)
            else:
                grecv[h, z] = val

    conv(seqs - 1)
    sdown.step2()
    sup.step2()
    sout.step2()
    depth_back(local, seqs, gsp, xe, vec, gdx_ext, gwd)
    for i, at in ((0, 0), (1, EDGE + local)):
        for s in range(seqs):
            hsend[i, s, :, :CHAN] = gci_ext[s, at : at + EDGE]
            hsend[i, s, :, CHAN:] = gdx_ext[s, at : at + EDGE]
    hops = []
    for i, o in ((0, seq - 1), (1, 1)):
        cp = pltpu.make_async_remote_copy(
            src_ref=hsend.at[i], dst_ref=hrecv.at[i], send_sem=esend.at[i],
            recv_sem=erecv.at[i], device_id=grid.dev(z=o), device_id_type=MESH,
        )
        cp.start()
        hops.append(cp)
    gw = dot_tn(spread[...], gk[...])
    gate = lambda v: v.reshape(parts[3].shape[:-1] + (CHAN,)).astype(bf16)
    parts[3][..., CHAN:] = gate(gw)
    bias_row = jnp.zeros((1, 128), f32)
    for t in range(TAPS):
        pick = (
            (iota((128, CHAN), 1) == iota((128, CHAN), 0) // TAPS * HEAD)
            & (iota((128, CHAN), 0) % TAPS == t)
            & (iota((128, CHAN), 0) < HEADS * TAPS)
        ).astype(bf16)
        bias_row = bias_row + dot_pick(rows_sum(gbk[t]), pick)
    tiles = []
    for c in range(CHAN // 128):
        tile = gwk[:TALL, c * 128 : (c + 1) * 128]
        if c == 0:
            tile = jnp.where(iota((TALL, 128), 0) == HEADS * TAPS, bias_row, tile)
        tiles.append(tile.reshape(TALL // 8, 8, 128))
    count = CHAN // 128 * TALL // 8
    tiles.append(jnp.zeros((N - count, 8, 128), f32))
    parts[7][...] = jnp.concatenate(tiles, axis=0).reshape(parts[7].shape)
    skern.start()
    qsum, vsum = {}, {}

    def gather_grads(j):
        for o in range(1, Z):
            back[j * (Z - 1) + o - 1].wait_recv()
        for s in range(seqs):
            r = slice(s * local, (s + 1) * local)
            vals = []
            for h in range(2):
                n = h * HEADS_PER + j
                val = unpack(grecv[j, 2 * s + h])
                q = (val[:, :HEAD].astype(f32) + gqm[r, n * HEAD : (n + 1) * HEAD]).astype(bf16)
                qsum[n] = qsum.get(n, 0.0) + rows_sum(q.astype(f32))
                vsum[n] = vsum.get(n, 0.0) + rows_sum(val[:, 2 * HEAD :].astype(f32))
                vals += [q, val[:, HEAD:]]
            low = jnp.concatenate(vals, axis=1)
            grads[j, r] = low
        gw = dot(xt[...], grads[j])
        parts[4 + j][...] = gw.reshape(parts[4 + j].shape).astype(bf16)
        sc[4 + j].start()

    gather_grads(0)

    for cp in hops:
        cp.wait_recv()
    gbconv = jnp.zeros((1, CHAN), f32)
    for s in range(seqs):
        for i, at, ok in ((0, local, z < Z - 1), (1, EDGE, z > 0)):
            add = jnp.where(ok, hrecv[i, s], 0.0)
            gci_ext[s, at : at + EDGE] += add[:, :CHAN]
            gdx_ext[s, at : at + EDGE] += add[:, CHAN:]
        own = gci_ext[s, EDGE : EDGE + local]
        gbconv = gbconv + rows_sum(own)
        gcl[s * local : (s + 1) * local] = own.astype(bf16)
    gw = dot(xt[...], gcl[...])
    parts[3][..., :CHAN] = gate(gw)
    scp.start()
    skern.step1()
    sq0.step1()
    loads[4].wait()
    for s in range(seqs):
        r = slice(s * local, (s + 1) * local)
        gx[r] += gdx_ext[s, EDGE : EDGE + local] + dot_nt(gcl[r], wcp[:, :CHAN])
    gather_grads(1)
    sdown.step3()
    sup.step3()
    sout.step3()
    scp.step1()
    skern.step2()
    sq0.step2()
    taps = jnp.concatenate([rows_sum(gwd[t]) for t in range(TAPS)], axis=0)
    head = jnp.concatenate([taps, vecg[TAPS:16]], axis=0)
    own = to_owners(head, w1, N)
    place = parts[8].shape[:4]
    parts[8][:, :, :, :, 0] = own[:, :8].reshape(place + (8, 128))
    parts[8][:, :, :, :, 1] = own[:, 8:].reshape(place + (8, 128))
    sq1.step1()
    scp.step2()
    gather_grads(2)
    bprow[...] = jnp.concatenate(
        [qsum[n] for n in range(HEADS)] + [vsum[n] for n in range(HEADS)] + [gbconv, gbpoint[...]],
        axis=1,
    )
    own = to_owners(bprow[...], wp, N)
    parts[8][:, :, :, :, 2, 0:1] = own.reshape(place + (1, 128))
    svec.start()
    skern.step3()
    sq0.step3()
    sq1.step2()
    sq2.step1()
    svec.step1()
    skern.step4()
    gk_tail = Gather(grid, souts[7], kall, "zxyc", gssem, grsem, lsem)
    gk_tail.start()
    scp.step3()
    for i in range(HEADS_PER):
        loads[5 + i].wait()
    for s in range(seqs):
        r = slice(s * local, (s + 1) * local)
        acc = gx[r]
        for j in range(HEADS_PER):
            acc = acc + dot_nt(grads[j, r], wq[j])
        gx[r] = acc
    last = pltpu.make_async_copy(gx, h_gx, wsem.at[19])
    last.start()
    sq1.step3()
    sq2.step2()
    svec.step2()
    gk_tail.step1()
    sdown.step4()
    sup.step4()
    sout.step4()
    sq2.step3()
    svec.step3()
    gk_tail.step2()
    scp.step4()
    sq0.step4()
    sq1.step4()
    gk_tail.step3()
    gk_tail.step4()
    n = TALL // 8
    every = kall[...].reshape(N, 8, 128)
    o_kernel[...] = jnp.concatenate(
        [every[c * n : (c + 1) * n].reshape(TALL, 128) for c in range(CHAN // 128)], axis=1
    )
    sq2.step4()
    svec.step4()
    flat = [souts[4 + j][...].reshape(w1, 2 * PART) for j in range(HEADS_PER)]
    cols = []
    for p in range(3):
        for n in range(HEADS):
            at = n // HEADS_PER * PART + p * HEAD
            cols.append(flat[n % HEADS_PER][:, at : at + HEAD])
    o_proj[:, : 3 * CHAN] = jnp.concatenate(cols, axis=1)
    o_proj[:, 3 * CHAN :] = souts[3][...].reshape(w1, 2 * CHAN)
    for cp in sends + back + hops:
        cp.wait_send()
    for g in sc:
        g.finish()
    gk_tail.finish()
    last.wait()


TALL = -(-(HEADS * TAPS + 1) // 8) * 8


def back(dp, seq, widths, values, streamed, gathered, wgrads, shards):
    f32, bf16 = jnp.float32, jnp.bfloat16
    dctx = values[0]
    qh, xe = streamed[6], streamed[10]
    N = dp * seq
    w1, wp, wu = widths
    seqs, ext, width = xe.shape
    total = dctx.shape[0]
    local = total // seqs
    length = qh.shape[1]
    sizes = sizes_of(dp, seq)
    shape = jax.ShapeDtypeStruct
    vm = pl.BlockSpec(memory_space=pltpu.VMEM)
    hb = pl.BlockSpec(memory_space=pl.ANY)
    t_down, t_up, t_out = [tiled(a).shape for a in shards]
    lead = t_out[:2]
    piece = [
        (t_down, bf16), (t_up, bf16), (t_out, bf16), (lead + (2 * CHAN,), bf16),
    ]
    piece += [(lead + (2 * PART,), bf16)] * HEADS_PER
    piece += [((1, 8, 128), f32), ((3, 8, 128), f32)]
    place = mesh_lead(dp, seq)
    wgrads = [g.reshape(place + p[0]) for g, p in zip(wgrads, piece)]
    scratch = [pltpu.VMEM(a.shape, a.dtype) for a in streamed]
    scratch += [pltpu.VMEM((total, width), f32), pltpu.VMEM((width, total), bf16)]
    scratch += [pltpu.VMEM(place + p, d) for p, d in piece]
    for p, d in piece:
        scratch += scatter_scratch(sizes, p, d, "zxyc")
    scratch += [pltpu.VMEM(p, f32) for p, d in piece[3:8]]
    V = pltpu.VMEM
    scratch += [
        V((seq, local // 2, 2 * PART), bf16),
        V((seq, local // 2, 2 * PART), bf16),
        V((HEADS_PER, seq - 1, local // 2, 2 * PART), bf16),
        V((HEADS_PER, seq, local // 2, 2 * PART), bf16),
        V((HEADS_PER, width, 2 * PART), bf16),
        V((width, 2 * CHAN), bf16),
        V((HEADS_PER, total, 2 * PART), bf16),
        V((TAPS, local + 2 * PAD, CHAN), f32),
        V((TAPS, local, CHAN), f32),
        V((TAPS, local, CHAN), bf16),
        V((local + 2 * PAD, CHAN), f32),
        V((seqs, local + 2 * PAD, width), f32),
        V((total, CHAN), f32),
        V((total, CHAN), bf16),
        V((seqs, ext, CHAN), f32),
        V((total, CHAN), bf16),
        V((seqs, ext, width), f32),
        V((TAPS, 8, width), f32),
        V((128, CHAN), f32),
        V((TAPS, 8, CHAN), f32),
        V((1, CHAN), f32),
        V((128, CHAN), bf16),
        V((2, seqs, EDGE, CHAN + width), f32),
        V((2, seqs, EDGE, CHAN + width), f32),
        V((seq, local, HEAD), bf16),
        V((2, length, HEAD), f32),
        V(place + (1, 8, 128), f32),
        V((1, 4 * CHAN), f32),
    ]
    sem = lambda *s: pltpu.SemaphoreType.DMA(s)
    n = len(piece)
    scratch += [
        sem(n), sem(n, 4), sem(), sem(4), sem(),
        sem(HEADS_PER, seq - 1), sem(HEADS_PER, seq - 1), sem(seq - 1), sem(seq - 1),
        sem(2), sem(2), sem(20),
    ]
    outs = [
        shape((total, width), f32),
        shape((w1, 5 * CHAN), f32),
        shape(t_out, f32),
        shape(t_up, f32),
        shape(t_down, f32),
        shape((3, 8, 128), f32),
        shape((TALL, CHAN), f32),
    ]
    return pl.pallas_call(
        partial(back_kernel, dp, seq, widths),
        out_shape=outs,
        in_specs=[vm] * len(values) + [hb] * (8 + len(streamed)),
        out_specs=[hb] + [vm] * (len(outs) - 1),
        scratch_shapes=scratch,
        compiler_params=pltpu.CompilerParams(
            collective_id=3, has_side_effects=True, vmem_limit_bytes=63 << 20
        ),
        name="back",
    )(*values, *streamed, *gathered, *wgrads)


def finish_kernel(gx, proj, out, up, down, small, kern, *rest):
    outs, held, sem = rest[:-6], rest[-6:-1], rest[-1]
    copies = [
        pltpu.make_async_copy(a, b, sem.at[0, i])
        for i, (a, b) in enumerate(zip((gx, proj, out, up, down), held))
    ]
    for cp in copies:
        cp.start()
    stores = [
        pltpu.make_async_copy(a, b, sem.at[1, i])
        for i, (a, b) in enumerate(zip(held, outs[:5]))
    ]
    for a, b in zip(copies, stores):
        a.wait()
        b.start()
    depth, kernel_t, bkernel, bproj, bup = outs[5:10]
    s = small[...]
    depth[...] = s[:2].reshape(16, 128)[: depth.shape[0], : depth.shape[1]]
    kernel_t[...] = kern[: kernel_t.shape[0]]
    bkernel[...] = kern[HEADS * TAPS : HEADS * TAPS + 1, : HEADS * TAPS]
    bproj[...] = s[2, 0:1, : bproj.shape[1]]
    bup[...] = s[2, 1:2, : bup.shape[1]]
    for i, v in zip(range(V_BOUT, V_S2 + 1), outs[10:]):
        v[...] = s[i // 8, i % 8 : i % 8 + 1, : v.shape[1]]
    for cp in stores:
        cp.wait()


def finish(widths, arrays):
    f32 = jnp.float32
    w1, wp, wu = widths
    shape = jax.ShapeDtypeStruct
    vm = pl.BlockSpec(memory_space=pltpu.VMEM)
    hb = pl.BlockSpec(memory_space=pl.ANY)
    outs = [shape(a.shape, f32) for a in arrays[:5]]
    outs += [
        shape((TAPS, w1), f32), shape((HEADS * TAPS, CHAN), f32), shape((1, HEADS * TAPS), f32),
        shape((1, wp), f32), shape((1, wu), f32),
    ]
    outs += [shape((1, w1), f32)] * 6
    return pl.pallas_call(
        finish_kernel,
        out_shape=outs,
        in_specs=[hb] * 5 + [vm] * 2,
        out_specs=[hb] * 5 + [vm] * 11,
        scratch_shapes=[pltpu.VMEM(a.shape, f32) for a in arrays[:5]]
        + [pltpu.SemaphoreType.DMA((2, 5))],
        name="finish",
    )(*arrays)


def fast_body(
    hidden, cotangent, w_proj, w_depth, w_kernel, b_kernel, w_out, w_up, w_down, b_proj, b_up,
    b_out, ln1_gain, ln1_bias, b_down, ln2_gain, ln2_bias,
):
    dp, seq = lax.axis_size("dp"), lax.axis_size("seq")
    seqs, local, width = hidden.shape
    total = seqs * local
    widths = (w_out.shape[0], b_proj.shape[0], b_up.shape[0])
    small = pack_small(
        w_depth, (b_out, ln1_gain, ln1_bias, b_down, ln2_gain, ln2_bias), b_proj, b_up
    )
    w_kernel = w_kernel.T
    (
        gq0, gq1, gq2, gcp, gout, gup, gdown, qh, kh, vh, joined, qn, xe, convin, keyconv, mixed,
        spread, wkx, stats, vec, bup, bkx,
    ) = front(
        dp, seq, hidden, w_proj, w_out, w_up, w_down, small, w_kernel, b_kernel[None], widths
    )
    out, gafter, dctx, gmix, gwout, gwup, gwdown, vecg, gbup = ffn(
        joined, hidden.reshape(total, width), cotangent.reshape(total, width),
        gout.reshape(-1, w_out.shape[1]), gup.reshape(-1, w_up.shape[1]),
        gdown.reshape(-1, w_down.shape[1]), vec, bup,
    )
    res = back(
        dp, seq, widths,
        (dctx, stats, vec, bkx, w_kernel, vecg, gbup),
        (gmix, convin, keyconv, mixed, qn, wkx, qh, kh, vh, spread, xe),
        (gafter, gq0, gq1, gq2, gcp), (gwdown, gwup, gwout), (w_down, w_up, w_out),
    )
    (
        gx, g_proj, g_out, g_up, g_down, g_depth, g_kernel, g_bkernel, g_bproj, g_bup, *g_vecs,
    ) = finish(widths, res)
    return (
        out.reshape(hidden.shape),
        gx.reshape(hidden.shape),
        g_proj,
        g_depth.T,
        g_kernel.T,
        g_bkernel[0],
        g_out.reshape(w_out.shape),
        g_up.reshape(w_up.shape),
        g_down.reshape(w_down.shape),
        g_bproj[0],
        g_bup[0],
    ) + tuple(v[0] for v in g_vecs)


def fits(mesh):
    return mesh.shape["seq"] == 4 and mesh.shape["dp"] == 8


def body(
    hidden,
    cotangent,
    w_proj,
    w_depth,
    w_kernel,
    b_kernel,
    w_out,
    w_up,
    w_down,
    b_proj,
    b_up,
    b_out,
    ln1_gain,
    ln1_bias,
    b_down,
    ln2_gain,
    ln2_bias,
):
    seq_count, local_rows, model_width = hidden.shape
    total_rows = seq_count * local_rows
    head_count = HEADS
    head_size = HEAD
    all_width = head_count * head_size
    tap_count = KERNEL
    half_kernel = KERNEL // 2
    group_count = GROUPS
    hidden_units = FF
    ext_rows = local_rows + 2 * half_kernel
    score_scale = head_size ** (-0.5)
    dp, seq = lax.axis_size("dp"), lax.axis_size("seq")
    devices = dp * seq
    vectors = (b_proj, b_up, b_out, ln1_gain, ln1_bias, b_down, ln2_gain, ln2_bias)
    widths = [w_depth.shape[0] * KERNEL] + [v.shape[0] for v in vectors]
    small = jnp.concatenate([w_depth.reshape(-1)] + list(vectors))
    small = jnp.pad(small, (0, 1024 - small.shape[0])).reshape(8, 128)
    full_proj, full_out, full_up, full_down, small = gather_all(
        dp, seq, [w_proj, w_out, w_up, w_down, small]
    )
    small = cut(small.reshape(devices, 1024), widths)
    full_depth = small[0].reshape(-1, KERNEL)
    (
        full_bproj,
        full_bup,
        full_bout,
        gain_one,
        shift_one,
        full_bdown,
        gain_two,
        shift_two,
    ) = [v.reshape(-1) for v in small[1:]]
    bias_proj = full_bproj.astype(jnp.float32)
    gain_first = gain_one.astype(jnp.float32)
    shift_first = shift_one.astype(jnp.float32)
    gain_second = gain_two.astype(jnp.float32)
    shift_second = shift_two.astype(jnp.float32)
    tokens_flat = hidden.reshape(total_rows, model_width)
    first_proj = jnp.dot(
        tokens_flat, full_proj[:, : 3 * all_width], preferred_element_type=jnp.float32
    )
    queries = (first_proj[:, :all_width] + bias_proj[:all_width]).astype(jnp.bfloat16)
    key_rows = first_proj[:, all_width : 2 * all_width].astype(jnp.bfloat16)
    value_rows = (first_proj[:, 2 * all_width :] + bias_proj[all_width : 2 * all_width]).astype(
        jnp.bfloat16
    )
    extended = with_halo(hidden, (("seq", 1),), half_kernel)
    position = lax.axis_index("seq") * local_rows + jnp.arange(ext_rows) - half_kernel
    inside = ((position >= 0) & (position < local_rows * lax.axis_size("seq"))).astype(jnp.float32)
    conv_input = jnp.dot(
        extended.reshape(seq_count * ext_rows, model_width),
        full_proj[:, 3 * all_width : 4 * all_width],
        preferred_element_type=jnp.float32,
    )
    conv_input = (conv_input + bias_proj[2 * all_width : 3 * all_width]).reshape(
        seq_count, ext_rows, all_width
    ) * inside[None, :, None]
    depth_weights = full_depth.astype(jnp.float32)
    depth_sum = jnp.zeros((seq_count, local_rows, model_width), jnp.float32)
    for tap_index in range(tap_count):
        depth_sum = (
            depth_sum
            + extended[:, tap_index : tap_index + local_rows].astype(jnp.float32)
            * depth_weights[:, tap_index]
        )
    spread = depth_sum.astype(jnp.bfloat16).reshape(total_rows, model_width)
    key_conv = (
        jnp.dot(spread, full_proj[:, 4 * all_width :], preferred_element_type=jnp.float32)
        + bias_proj[3 * all_width :]
    )
    mixed_key = (key_conv * queries.astype(jnp.float32)).astype(jnp.bfloat16)
    logits = jnp.dot(mixed_key, w_kernel, preferred_element_type=jnp.float32) + b_kernel.astype(
        jnp.float32
    )
    tap_weights = jax.nn.softmax(
        logits.reshape(seq_count, local_rows, head_count, tap_count), axis=-1
    )
    conv_heads = conv_input.reshape(seq_count, ext_rows, head_count, head_size)
    conv_mix = jnp.zeros((seq_count, local_rows, head_count, head_size), jnp.float32)
    for tap_index in range(tap_count):
        conv_mix = (
            conv_mix
            + tap_weights[..., tap_index, None] * conv_heads[:, tap_index : tap_index + local_rows]
        )
    queries_seq = queries.reshape(seq_count, local_rows, all_width)
    all_keys, all_values = (
        lax.all_gather(
            key_rows.reshape(seq_count, local_rows, all_width), "seq", axis=1, tiled=True
        ),
        lax.all_gather(
            value_rows.reshape(seq_count, local_rows, all_width), "seq", axis=1, tiled=True
        ),
    )
    full_length = all_keys.shape[1]

    def forward_one(item_set):
        query_seq, key_seq, value_seq = item_set
        return attend(
            query_seq.reshape(local_rows, head_count, head_size),
            key_seq.reshape(full_length, head_count, head_size),
            value_seq.reshape(full_length, head_count, head_size),
            score_scale,
        )

    context, norm_log = lax.map(forward_one, (queries_seq, all_keys, all_values))
    joined = jnp.concatenate(
        [
            context.reshape(total_rows, all_width),
            conv_mix.reshape(total_rows, all_width).astype(jnp.bfloat16),
        ],
        axis=-1,
    )
    after_mix = (
        jnp.dot(joined, full_out, preferred_element_type=jnp.float32)
        + full_bout.astype(jnp.float32)
        + tokens_flat.astype(jnp.float32)
    )
    first_norm, first_pull = jax.vjp(layer_norm, after_mix, gain_first, shift_first)
    grouped_in = first_norm.astype(jnp.bfloat16).reshape(
        total_rows, group_count, model_width // group_count
    )
    up_groups = full_up.reshape(
        group_count, model_width // group_count, hidden_units // group_count
    )
    pre_act = jnp.einsum(
        "ngd,gdf->ngf", grouped_in, up_groups, preferred_element_type=jnp.float32
    ).reshape(total_rows, hidden_units) + full_bup.astype(jnp.float32)
    activated, gelu_pull = jax.vjp(partial(jax.nn.gelu, approximate=False), pre_act)
    act_low = activated.astype(jnp.bfloat16).reshape(
        total_rows, group_count, hidden_units // group_count
    )
    down_groups = full_down.reshape(
        group_count, hidden_units // group_count, model_width // group_count
    )
    summed = jnp.einsum(
        "ngf,gfd->ngd", act_low, down_groups, preferred_element_type=jnp.float32
    ).reshape(total_rows, model_width)
    summed = summed + full_bdown.astype(jnp.float32) + first_norm
    out_value, second_pull = jax.vjp(layer_norm, summed, gain_second, shift_second)
    output = out_value.astype(jnp.bfloat16).reshape(seq_count, local_rows, model_width)
    back_proj = full_proj
    back_depth = full_depth.astype(jnp.float32)
    back_out = full_out
    back_up = up_groups
    back_down = down_groups
    grad_summed, grad_gain_two, grad_shift_two = second_pull(
        cotangent.reshape(total_rows, model_width).astype(jnp.float32)
    )
    grad_bdown = jnp.sum(grad_summed, axis=0)
    summed_low = grad_summed.astype(jnp.bfloat16).reshape(
        total_rows, group_count, model_width // group_count
    )
    grad_activ = jnp.einsum(
        "ngd,gfd->ngf", summed_low, back_down, preferred_element_type=jnp.float32
    ).reshape(total_rows, hidden_units)
    grad_wdown = jnp.einsum(
        "ngf,ngd->gfd", act_low, summed_low, preferred_element_type=jnp.float32
    ).reshape(hidden_units, model_width // group_count)
    grad_pre = gelu_pull(grad_activ)[0]
    grad_bup = jnp.sum(grad_pre, axis=0)
    pre_low = grad_pre.astype(jnp.bfloat16).reshape(
        total_rows, group_count, hidden_units // group_count
    )
    grad_wup = jnp.einsum(
        "ngd,ngf->gdf", grouped_in, pre_low, preferred_element_type=jnp.float32
    ).reshape(model_width, hidden_units // group_count)
    grad_first = grad_summed + jnp.einsum(
        "ngf,gdf->ngd", pre_low, back_up, preferred_element_type=jnp.float32
    ).reshape(total_rows, model_width)
    grad_after, grad_gain_one, grad_shift_one = first_pull(grad_first)
    grad_bout = jnp.sum(grad_after, axis=0)
    after_low = grad_after.astype(jnp.bfloat16)
    grad_wout = jnp.dot(joined.T, after_low, preferred_element_type=jnp.float32)
    grad_joined = jnp.dot(after_low, back_out.T, preferred_element_type=jnp.float32)
    grad_context = (
        grad_joined[:, :all_width].astype(jnp.bfloat16).reshape(seq_count, local_rows, all_width)
    )
    grad_mix = grad_joined[:, all_width:].reshape(seq_count, local_rows, head_count, head_size)

    def back_one(item_set):
        query_seq, grad_seq, norm_seq, key_seq, value_seq = item_set
        grad_query, grad_key, grad_value, unused_delta = attend_back(
            query_seq.reshape(local_rows, head_count, head_size),
            grad_seq.reshape(local_rows, head_count, head_size),
            norm_seq,
            key_seq.reshape(full_length, head_count, head_size),
            value_seq.reshape(full_length, head_count, head_size),
            None,
            score_scale,
        )
        key_value = jnp.concatenate(
            [grad_key.reshape(full_length, all_width), grad_value.reshape(full_length, all_width)],
            axis=-1,
        )
        return (grad_query.reshape(local_rows, all_width), key_value)

    grad_query_att, kv_terms = lax.map(
        back_one, (queries_seq, grad_context, norm_log, all_keys, all_values)
    )
    own_kv = lax.psum_scatter(
        kv_terms.astype(jnp.bfloat16), "seq", scatter_dimension=1, tiled=True
    ).astype(jnp.float32)
    grad_keys_low = own_kv[..., :all_width].reshape(total_rows, all_width).astype(jnp.bfloat16)
    grad_values_low = own_kv[..., all_width:].reshape(total_rows, all_width).astype(jnp.bfloat16)
    grad_taps = jnp.stack(
        [
            jnp.sum(grad_mix * conv_heads[:, tap_index : tap_index + local_rows], axis=-1)
            for tap_index in range(tap_count)
        ],
        axis=-1,
    )
    grad_conv_ext = jnp.zeros((seq_count, ext_rows, head_count, head_size), jnp.float32)
    for tap_index in range(tap_count):
        grad_conv_ext = grad_conv_ext + jnp.pad(
            tap_weights[..., tap_index, None] * grad_mix,
            ((0, 0), (tap_index, 2 * half_kernel - tap_index), (0, 0), (0, 0)),
        )
    grad_logits = tap_weights * (
        grad_taps - jnp.sum(tap_weights * grad_taps, axis=-1, keepdims=True)
    )
    grad_logits = grad_logits.reshape(total_rows, head_count * tap_count)
    grad_bkernel = jnp.sum(grad_logits, axis=0)
    logits_low = grad_logits.astype(jnp.bfloat16)
    grad_wkernel = jnp.dot(mixed_key.T, logits_low, preferred_element_type=jnp.float32)
    grad_mixed = jnp.dot(logits_low, w_kernel.T, preferred_element_type=jnp.float32)
    grad_queries = (grad_query_att.reshape(total_rows, all_width) + grad_mixed * key_conv).astype(
        jnp.bfloat16
    )
    grad_key_conv = grad_mixed * queries.astype(jnp.float32)
    grad_bpt = jnp.sum(grad_key_conv, axis=0)
    key_conv_low = grad_key_conv.astype(jnp.bfloat16)
    grad_wpt = jnp.dot(spread.T, key_conv_low, preferred_element_type=jnp.float32)
    grad_spread = jnp.dot(
        key_conv_low, back_proj[:, 4 * all_width :].T, preferred_element_type=jnp.float32
    ).reshape(seq_count, local_rows, model_width)
    grad_wdepth = jnp.stack(
        [
            jnp.sum(
                extended[:, tap_index : tap_index + local_rows].astype(jnp.float32) * grad_spread,
                axis=(0, 1),
            )
            for tap_index in range(tap_count)
        ],
        axis=-1,
    )
    grad_ext_depth = jnp.zeros((seq_count, ext_rows, model_width), jnp.float32)
    for tap_index in range(tap_count):
        grad_ext_depth = grad_ext_depth + jnp.pad(
            back_depth[:, tap_index] * grad_spread,
            ((0, 0), (tap_index, 2 * half_kernel - tap_index), (0, 0)),
        )
    combined = jnp.concatenate(
        [grad_conv_ext.reshape(seq_count, ext_rows, all_width), grad_ext_depth], axis=-1
    )
    received = with_halo(combined.astype(jnp.bfloat16), (("seq", 1),), half_kernel).astype(
        combined.dtype
    )
    own_part = combined[:, half_kernel : half_kernel + local_rows]
    own_part = own_part.at[:, :half_kernel].add(received[:, :half_kernel])
    own_part = own_part.at[:, local_rows - half_kernel :].add(
        received[:, received.shape[1] - half_kernel :]
    )
    grad_conv_own = own_part[..., :all_width].reshape(total_rows, all_width)
    grad_depth_x = own_part[..., all_width:].reshape(total_rows, model_width)
    grad_bconv = jnp.sum(grad_conv_own, axis=0)
    conv_low = grad_conv_own.astype(jnp.bfloat16)
    stacked = jnp.concatenate([grad_queries, grad_keys_low, grad_values_low, conv_low], axis=-1)
    grad_wfirst = jnp.dot(tokens_flat.T, stacked, preferred_element_type=jnp.float32)
    grad_tokens = (
        grad_after
        + jnp.dot(stacked, back_proj[:, : 4 * all_width].T, preferred_element_type=jnp.float32)
        + grad_depth_x
    )
    grad_wproj = jnp.concatenate([grad_wfirst, grad_wpt], axis=1)
    grad_bproj = jnp.concatenate(
        [
            jnp.sum(grad_queries.astype(jnp.float32), axis=0),
            jnp.sum(grad_values_low.astype(jnp.float32), axis=0),
            grad_bconv,
            grad_bpt,
        ]
    )
    def blocks(grad, shard):
        return grad.astype(jnp.bfloat16).reshape((devices,) + tiled(shard).shape)

    per_device = [
        g.reshape(devices, -1)
        for g in (
            grad_wdepth, grad_bproj, grad_bup, grad_bout, grad_gain_one, grad_shift_one,
            grad_bdown, grad_gain_two, grad_shift_two,
        )
    ]
    kernel_flat = jnp.concatenate([grad_wkernel.reshape(-1), grad_bkernel])
    kernel_len = kernel_flat.shape[0]
    kernel_each = -(-kernel_len // devices)
    kernel_flat = jnp.pad(kernel_flat, (0, kernel_each * devices - kernel_len))
    small_grad = jnp.concatenate(
        [
            lanes(jnp.concatenate(per_device, axis=1), 1),
            lanes(kernel_flat.reshape(devices, kernel_each), 1),
        ],
        axis=1,
    )
    sum_down, sum_up, sum_out, sum_proj, sum_small, sum_kernel = scatter_all(
        dp,
        seq,
        [
            blocks(grad_wdown, w_down), blocks(grad_wup, w_up), blocks(grad_wout, w_out),
            blocks(grad_wproj, w_proj), small_grad,
        ],
        ("zxyc", "zyxc", "zxyc", "zyxc", "zxyc"),
    )
    mine = cut(sum_small[:1].reshape(1, 1024), widths)
    shards = [sum_proj.reshape(w_proj.shape), mine[0].reshape(w_depth.shape)]
    shards += [
        sum_out.reshape(w_out.shape), sum_up.reshape(w_up.shape), sum_down.reshape(w_down.shape),
    ]
    shards += [m.reshape(-1) for m in mine[1:]]
    kernel_sum = sum_kernel.reshape(devices, 1024)[:, :kernel_each].reshape(-1)
    kernel_total = (
        kernel_sum[: grad_wkernel.size].reshape(grad_wkernel.shape),
        kernel_sum[grad_wkernel.size : kernel_len],
    )
    return (
        output,
        grad_tokens.reshape(seq_count, local_rows, model_width),
        shards[0],
        shards[1],
        kernel_total[0],
        kernel_total[1],
        shards[2],
        shards[3],
        shards[4],
        shards[5],
        shards[6],
        shards[7],
        shards[8],
        shards[9],
        shards[10],
        shards[11],
        shards[12],
    )


def solution(mesh):
    placed = (
        P("dp", "seq", None),
        P("dp", "seq", None),
        P(("dp", "seq"), None),
        P(("dp", "seq"), None),
        P(),
        P(),
        P(("dp", "seq"), None),
        P(("dp", "seq"), None),
        P(("dp", "seq"), None),
        P(("dp", "seq")),
        P(("dp", "seq")),
        P(("dp", "seq")),
        P(("dp", "seq")),
        P(("dp", "seq")),
        P(("dp", "seq")),
        P(("dp", "seq")),
        P(("dp", "seq")),
    )
    return jax.shard_map(
        fast_body if fits(mesh) else body,
        mesh=mesh,
        in_specs=placed,
        out_specs=(
            P("dp", "seq", None),
            P("dp", "seq", None),
            P(("dp", "seq"), None),
            P(("dp", "seq"), None),
            P(),
            P(),
            P(("dp", "seq"), None),
            P(("dp", "seq"), None),
            P(("dp", "seq"), None),
            P(("dp", "seq")),
            P(("dp", "seq")),
            P(("dp", "seq")),
            P(("dp", "seq")),
            P(("dp", "seq")),
            P(("dp", "seq")),
            P(("dp", "seq")),
            P(("dp", "seq")),
        ),
        check_vma=False,
    )
```
